32 devices in a mesh: dp: 8 (over z, y), hid: 4 (over x, core).
Axes of the slice: x: 2, y: 2, z: 4, core: 2. Of those that a mesh axis runs over, the one named last changes fastest.
Arguments:
- tokens: bfloat16 [16384, 1024], P('dp', 'hid'), may hold values from -6 to 6
- query_weight: bfloat16 [1024, 1024], P(None, 'hid'), may hold values from -0.1875 to 0.1875
- query_bias: float32 [1024], P('hid'), may hold values from -4 to 4
- key_weight: bfloat16 [1024, 1024], P(None, 'hid'), may hold values from -0.1875 to 0.1875
- value_weight: bfloat16 [1024, 1024], P(None, 'hid'), may hold values from -0.1875 to 0.1875
- value_bias: float32 [1024], P('hid'), may hold values from -4 to 4
- output_weight: bfloat16 [1024, 1024], P('hid'), may hold values from -0.75 to 0.75
- output_bias: float32 [1024], P('hid'), may hold values from -4 to 4
- attention_gain: float32 [1024], P('hid'), may hold values from 0.5 to 1.5
- attention_shift: float32 [1024], P('hid'), may hold values from -4 to 4
- inner_weight: bfloat16 [1024, 4096], P(None, 'hid'), may hold values from -0.1875 to 0.1875
- inner_bias: float32 [4096], P('hid'), may hold values from -4 to 4
- down_weight: bfloat16 [4096, 1024], P('hid'), may hold values from -0.1875 to 0.1875
- down_bias: float32 [1024], P('hid'), may hold values from -4 to 4
- final_gain: float32 [1024], P('hid'), may hold values from 0.5 to 1.5
- final_shift: float32 [1024], P('hid'), may hold values from -4 to 4
- head_alpha: float32 [16], replicated, may hold values from -1 to 3
- unit_alpha: float32 [4096], replicated, may hold values from -1 to 3
- width_alpha: float32 [1024], replicated, may hold values from -1 to 3
- multipliers: float32 [2], replicated, may hold values from -1 to 1
- head_noise: float32 [16], P('hid'), may hold values from 0.02 to 0.98
- unit_noise: float32 [4096], P('hid'), may hold values from 0.02 to 0.98
- width_noise: float32 [1024], P('hid'), may hold values from 0.02 to 0.98
- lengths: int32 [32], replicated, may hold values from 64 to 512, as said below
- teacher: bfloat16 [16384, 1024], P('dp', 'hid'), may hold values from -6 to 6
- upstream: bfloat16 [16384, 1024], P('dp', 'hid'), may hold values from -6 to 6
Outputs:
- output: bfloat16 [16384, 1024], P('dp', 'hid')
- tokens_grad: float32 [16384, 1024], P('dp', 'hid')
- query_weight_grad: float32 [1024, 1024], P(None, 'hid')
- query_bias_grad: float32 [1024], P('hid')
- key_weight_grad: float32 [1024, 1024], P(None, 'hid')
- value_weight_grad: float32 [1024, 1024], P(None, 'hid')
- value_bias_grad: float32 [1024], P('hid')
- output_weight_grad: float32 [1024, 1024], P('hid')
- output_bias_grad: float32 [1024], P('hid')
- attention_gain_grad: float32 [1024], P('hid')
- attention_shift_grad: float32 [1024], P('hid')
- inner_weight_grad: float32 [1024, 4096], P(None, 'hid')
- inner_bias_grad: float32 [4096], P('hid')
- down_weight_grad: float32 [4096, 1024], P('hid')
- down_bias_grad: float32 [1024], P('hid')
- final_gain_grad: float32 [1024], P('hid')
- final_shift_grad: float32 [1024], P('hid')
- head_alpha_grad: float32 [16], P('hid')
- unit_alpha_grad: float32 [4096], P('hid')
- width_alpha_grad: float32 [1024], P('hid')
- distill_mse: float32 [], replicated
- multipliers_new: float32 [2], replicated
The draws below stay inside these ranges and needn't reach their ends.
Inputs may be any that keep to these rules, and one draw needn't show every extreme that they name: `lengths`: each sequence has 64 to 512 live tokens at its start; in every draw some sequence has 512 and some has 64.
All inputs are finite; a program needn't handle non-finite values.
Results may differ from the reference program's by a relative error of at most 0.02.
Values may be sent and summed in bfloat16 or wider, within the bound.
A program may use at most 192 MiB of HBM per device.

```python
import jax
import jax.numpy as jnp
from jax import lax

D = 1024
HEADS = 16
HD = 64
FF = 4096
SLOT = 512
SEQS = 32
TOKENS = 16384
N_HID = 4


def draw_lengths(key, part):
    key_body, key_full, key_short = jax.random.split(jax.random.fold_in(key, 7), 3)
    drawn_lengths = jax.random.randint(key_body, (SEQS,), SLOT // 8, SLOT + 1)
    full_place = jax.random.randint(key_full, (), 0, SEQS)
    short_place = (full_place + jax.random.randint(key_short, (), 1, SEQS)) % SEQS
    drawn_lengths = drawn_lengths.at[full_place].set(SLOT)
    return drawn_lengths.at[short_place].set(SLOT // 8).astype(jnp.int32)


def block_levels(own_key, shape, cuts, smallest, top_value):
    loudness = 1.0
    for position, shards_of in cuts:
        steps = jax.random.uniform(jax.random.fold_in(jax.random.fold_in(own_key, 6), position), (shards_of,), jnp.float32, smallest / len(cuts), top_value / len(cuts))
        loudness = loudness * jnp.repeat(jnp.exp(steps), shape[position] // shards_of).reshape((-1,) + (1,) * (len(shape) - 1 - position))
    return loudness


def centred(stream_key, dims, width, bound, cuts=(), held_as=jnp.bfloat16):
    drawn = width * jax.random.normal(stream_key, dims, jnp.float32)
    if cuts:
        drawn = drawn * block_levels(stream_key, dims, cuts, -0.22, 0.18)
    return jnp.clip(drawn, -bound, bound).astype(held_as)


def setup_inputs(seed: int = 0) -> dict:
    key_of = jax.random.split(jax.random.key(seed), 27)
    tokens = centred(key_of[0], (TOKENS, D), 1.0, 6.0, ((0, 8), (1, 4)))
    query_weight = centred(key_of[1], (D, D), D ** -0.5, 0.1875, ((1, 4),))
    query_bias = centred(key_of[2], (D,), 0.3, 4.0, ((0, 4),), jnp.float32)
    key_weight = centred(key_of[3], (D, D), D ** -0.5, 0.1875, ((1, 4),))
    value_weight = centred(key_of[4], (D, D), D ** -0.5, 0.1875, ((1, 4),))
    value_bias = centred(key_of[5], (D,), 0.3, 4.0, ((0, 4),), jnp.float32)
    output_weight = centred(key_of[6], (D, D), (D // 16) ** -0.5, 0.75, ((0, 4),))
    output_bias = centred(key_of[7], (D,), 0.3, 4.0, ((0, 4),), jnp.float32)
    attention_gain = jnp.clip(1.0 + 0.1 * jax.random.normal(key_of[8], (D,), jnp.float32), 0.5, 1.5)
    attention_shift = centred(key_of[9], (D,), 0.3, 4.0, ((0, 4),), jnp.float32)
    inner_weight = centred(key_of[10], (D, FF), D ** -0.5, 0.1875, ((1, 4),))
    inner_bias = centred(key_of[11], (FF,), 0.3, 4.0, ((0, 4),), jnp.float32)
    down_weight = centred(key_of[12], (FF, D), (FF // 4) ** -0.5, 0.1875, ((0, 4),))
    down_bias = centred(key_of[13], (D,), 0.3, 4.0, ((0, 4),), jnp.float32)
    final_gain = jnp.clip(1.0 + 0.1 * jax.random.normal(key_of[14], (D,), jnp.float32), 0.5, 1.5)
    final_shift = centred(key_of[15], (D,), 0.3, 4.0, ((0, 4),), jnp.float32)
    head_alpha = jnp.clip(jax.random.uniform(key_of[16], (HEADS,), jnp.float32, -1.0, 3.0), -1.0, 3.0)
    unit_alpha = jnp.clip(jax.random.uniform(key_of[17], (FF,), jnp.float32, -1.0, 3.0), -1.0, 3.0)
    width_alpha = jnp.clip(jax.random.uniform(key_of[18], (D,), jnp.float32, -1.0, 3.0), -1.0, 3.0)
    multipliers = jnp.clip(jax.random.uniform(key_of[19], (2,), jnp.float32, -1.0, 1.0), -1.0, 1.0)
    head_noise = jnp.clip(0.02 + 0.96000002 * jax.random.uniform(key_of[20], (HEADS,), jnp.float32) ** block_levels(key_of[20], (HEADS,), ((0, 4),), -0.2, 0.2), 0.02, 0.98)
    unit_noise = jnp.clip(0.02 + 0.96000002 * jax.random.uniform(key_of[21], (FF,), jnp.float32) ** block_levels(key_of[21], (FF,), ((0, 4),), -0.2, 0.2), 0.02, 0.98)
    width_noise = jnp.clip(0.02 + 0.96000002 * jax.random.uniform(key_of[22], (D,), jnp.float32) ** block_levels(key_of[22], (D,), ((0, 4),), -0.2, 0.2), 0.02, 0.98)
    lengths = draw_lengths(jax.random.fold_in(key_of[26], 71), 0)
    teacher = centred(key_of[24], (TOKENS, D), 1.0, 6.0, ((0, 8), (1, 4)))
    upstream = centred(key_of[25], (TOKENS, D), 1.0, 6.0, ((0, 8), (1, 4)))
    return {"tokens": tokens, "query_weight": query_weight, "query_bias": query_bias, "key_weight": key_weight, "value_weight": value_weight, "value_bias": value_bias, "output_weight": output_weight, "output_bias": output_bias, "attention_gain": attention_gain, "attention_shift": attention_shift, "inner_weight": inner_weight, "inner_bias": inner_bias, "down_weight": down_weight, "down_bias": down_bias, "final_gain": final_gain, "final_shift": final_shift, "head_alpha": head_alpha, "unit_alpha": unit_alpha, "width_alpha": width_alpha, "multipliers": multipliers, "head_noise": head_noise, "unit_noise": unit_noise, "width_noise": width_noise, "lengths": lengths, "teacher": teacher, "upstream": upstream}


@jax.custom_vjp
def low(v):
    return lax.optimization_barrier(v.astype(jnp.bfloat16)).astype(jnp.float32)

@jax.custom_vjp
def low_back(v):
    return v

def low_keep(v):
    return (low(v), None)

def low_pass(kept, grad):
    return (grad,)

def back_keep(v):
    return (v, None)

def back_low(kept, grad):
    return (low(grad),)
low.defvjp(low_keep, low_pass)
low_back.defvjp(back_keep, back_low)
BETA = 2.0 / 3.0
GAMMA = -0.1
ZETA = 1.1
TARGET = 0.7
ASCENT = 1.0
EPS = 1e-12
MASKED = -1000000000.0
HIGH = lax.Precision.HIGHEST

def erf_gelu(values):
    return 0.5 * values * (1.0 + lax.erf(values * 0.7071067811865476))

def gate_value(noise, alpha):
    logits = (jnp.log(noise) - jnp.log(1.0 - noise) + alpha) / BETA
    stretched = jax.nn.sigmoid(logits) * (ZETA - GAMMA) + GAMMA
    return jnp.clip(stretched, 0.0, 1.0)

def keep_prob(alpha):
    return jax.nn.sigmoid(alpha - BETA * jnp.log(-GAMMA / ZETA))

def lagrangian(head_alpha, unit_alpha, width_alpha, multipliers):
    heads_kept = jnp.sum(keep_prob(head_alpha))
    units_kept = jnp.sum(keep_prob(unit_alpha))
    dims_kept = jnp.sum(keep_prob(width_alpha))
    full_size = 4.0 * D * D + 2.0 * D * FF
    expected = (4.0 * HD * heads_kept * dims_kept + 2.0 * units_kept * dims_kept) / full_size
    gap_value = 1.0 - expected - TARGET
    return multipliers[0] * gap_value + multipliers[1] * gap_value * gap_value

def layer_norm(hidden, scale_gain, shift_bias):
    row_mean = lax.optimization_barrier(jnp.mean(hidden, axis=-1, keepdims=True))
    centered = hidden - row_mean
    variance = lax.optimization_barrier(jnp.mean(centered * centered, axis=-1, keepdims=True))
    return centered * lax.rsqrt(variance + EPS) * scale_gain + shift_bias

def attend(pieces):
    queries, keys_all, values, length_one = pieces
    raw_scores = jnp.einsum('qhd,khd->hqk', queries, keys_all, precision=HIGH) * HD ** (-0.5)
    valid_keys = jnp.arange(SLOT) < length_one
    scores = low_back(jnp.where(valid_keys[None, None, :], raw_scores, MASKED))
    highest = lax.optimization_barrier(jnp.max(scores, axis=-1, keepdims=True))
    exponent = jnp.exp(scores - highest)
    probabilities = exponent / lax.optimization_barrier(jnp.sum(exponent, axis=-1, keepdims=True))
    return jnp.einsum('hqk,khd->qhd', low(probabilities), values, precision=HIGH)

def block_forward(params, fixed):
    tokens, query_weight, query_bias, key_weight, value_weight, value_bias, output_weight, output_bias, attention_gain, attention_shift, inner_weight, inner_bias, down_weight, down_bias, final_gain, final_shift, head_alpha, unit_alpha, width_alpha, multipliers = params
    head_noise, unit_noise, width_noise, lengths, teacher, upstream = fixed
    shard_width = D // N_HID
    unit_width = FF // N_HID
    head_gate = gate_value(head_noise, head_alpha)
    unit_gate = gate_value(unit_noise, unit_alpha)
    width_gate = gate_value(width_noise, width_alpha)
    query_parts = []
    key_parts = []
    value_parts = []
    for section in range(N_HID):
        columns = slice(section * shard_width, (section + 1) * shard_width)
        entering = low_back(tokens)
        query_parts.append(jnp.dot(entering, query_weight[:, columns], precision=HIGH) + query_bias[columns])
        key_parts.append(jnp.dot(entering, key_weight[:, columns], precision=HIGH))
        value_parts.append(jnp.dot(entering, value_weight[:, columns], precision=HIGH) + value_bias[columns])
    queries = low(low_back(jnp.concatenate(query_parts, axis=1)))
    keys_all = low(low_back(jnp.concatenate(key_parts, axis=1)))
    values = low(low_back(jnp.concatenate(value_parts, axis=1)))
    shaped = (SEQS, SLOT, HEADS, HD)
    context = lax.map(jax.checkpoint(attend), (queries.reshape(shaped), keys_all.reshape(shaped), values.reshape(shaped), lengths))
    context = low_back(context.reshape(TOKENS, HEADS, HD))
    gated_low = low((context * head_gate[None, :, None]).reshape(TOKENS, D))
    summed = jnp.zeros((TOKENS, D), jnp.float32)
    for section in range(N_HID):
        rows_cut = slice(section * shard_width, (section + 1) * shard_width)
        summed = summed + low(jnp.dot(gated_low[:, rows_cut], output_weight[rows_cut, :], precision=HIGH))
    attention_pre = low_back(summed) + output_bias
    middle = layer_norm(tokens + attention_pre * width_gate, attention_gain, attention_shift)
    middle_low = low(middle)
    ffn_sum = jnp.zeros((TOKENS, D), jnp.float32)
    for section in range(N_HID):
        columns = slice(section * unit_width, (section + 1) * unit_width)
        entering = low_back(middle_low)
        pre_act = low_back(jnp.dot(entering, inner_weight[:, columns], precision=HIGH) + inner_bias[columns])
        inner_act = low(erf_gelu(pre_act) * unit_gate[columns])
        ffn_sum = ffn_sum + low(jnp.dot(inner_act, down_weight[columns, :], precision=HIGH))
    ffn_pre = low_back(ffn_sum) + down_bias
    final_out = layer_norm(middle + ffn_pre * width_gate, final_gain, final_shift)
    live_rows = (jnp.arange(SLOT)[None, :] < lengths[:, None]).reshape(TOKENS, 1).astype(jnp.float32)
    differ = final_out - teacher
    squared = jnp.sum(live_rows * differ * differ)
    objective = jnp.sum(live_rows * (upstream * final_out + 0.5 * differ * differ))
    objective = objective + lagrangian(head_alpha, unit_alpha, width_alpha, multipliers)
    return (objective, (final_out, squared))

def reference(tokens, query_weight, query_bias, key_weight, value_weight, value_bias, output_weight, output_bias, attention_gain, attention_shift, inner_weight, inner_bias, down_weight, down_bias, final_gain, final_shift, head_alpha, unit_alpha, width_alpha, multipliers, head_noise, unit_noise, width_noise, lengths, teacher, upstream):
    params = tuple((item.astype(jnp.float32) for item in (tokens, query_weight, query_bias, key_weight, value_weight, value_bias, output_weight, output_bias, attention_gain, attention_shift, inner_weight, inner_bias, down_weight, down_bias, final_gain, final_shift, head_alpha, unit_alpha, width_alpha, multipliers)))
    fixed = (head_noise, unit_noise, width_noise, lengths, teacher.astype(jnp.float32), upstream.astype(jnp.float32))
    objective, pullback, (final_out, squared) = jax.vjp(lambda *items: block_forward(items, fixed), *params, has_aux=True)
    grads = pullback(jnp.ones_like(objective))
    distill_mse = squared / (jnp.sum(lengths).astype(jnp.float32) * D)
    multipliers_new = params[19] + ASCENT * grads[19]
    return (final_out.astype(jnp.bfloat16), grads[0], grads[1], grads[2], grads[3], grads[4], grads[5], grads[6], grads[7], grads[8], grads[9], grads[10], grads[11], grads[12], grads[13], grads[14], grads[15], grads[16], grads[17], grads[18], distill_mse, multipliers_new)
```

```python
import functools

import jax
import jax.numpy as jnp
from jax import lax
from jax.experimental import pallas as pl
from jax.experimental.pallas import tpu as pltpu
from jax.sharding import PartitionSpec as P

D = 1024
HD = 64
FF = 4096
SLOT = 512

BETA = 2.0 / 3.0
GAMMA = -0.1
ZETA = 1.1
TARGET = 0.7
ASCENT = 1.0
EPS = 1e-12
MASKED = -1000000000.0
ROOT_HALF = 0.7071067811865476
ROOT_TWO_PI = 2.5066282746310002

MESH = pl.DeviceIdType.MESH
VMEM_LIMIT = 66_000_000
BF = jnp.bfloat16
F32 = jnp.float32
NB = 256
RB = 16


def gate_value(noise, alpha):
    logits = (jnp.log(noise) - jnp.log(1.0 - noise) + alpha) / BETA
    stretched = jax.nn.sigmoid(logits) * (ZETA - GAMMA) + GAMMA
    return jnp.clip(stretched, 0.0, 1.0)


def keep_prob(alpha):
    return jax.nn.sigmoid(alpha - BETA * jnp.log(-GAMMA / ZETA))


def lagrangian(head_alpha, unit_alpha, width_alpha, multipliers):
    heads_kept = jnp.sum(keep_prob(head_alpha))
    units_kept = jnp.sum(keep_prob(unit_alpha))
    dims_kept = jnp.sum(keep_prob(width_alpha))
    full_size = 4.0 * D * D + 2.0 * D * FF
    expected = (4.0 * HD * heads_kept * dims_kept + 2.0 * units_kept * dims_kept) / full_size
    gap_value = 1.0 - expected - TARGET
    return multipliers[0] * gap_value + multipliers[1] * gap_value * gap_value


def nn(a, b):
    return jnp.dot(a, b, preferred_element_type=F32)


def nt(a, b):
    return lax.dot_general(a, b, (((1,), (1,)), ((), ())), preferred_element_type=F32)


def tn(a, b):
    return lax.dot_general(a, b, (((0,), (0,)), ((), ())), preferred_element_type=F32)


def fold(values):
    return jnp.sum(values.reshape(values.shape[0] // 8, 8, values.shape[1]), axis=0)


class Group:
    def __init__(self, n):
        self.n = n
        self.nx = n // 2
        self.me = lax.axis_index("hid")
        self.x = lax.div(self.me, 2)
        self.c = lax.rem(self.me, 2)
        self.partner = 2 * self.x + 1 - self.c

    def chip_ahead(self, j):
        return lax.rem(self.x + 1 + j, self.nx)

    def chip_behind(self, j):
        return lax.rem(self.x - 1 - j + self.nx, self.nx)

    def slot(self, h):
        return lax.rem(h, 2) * self.nx + lax.div(h, 2)

    def all_peers(self):
        return [{"hid": lax.rem(self.me + 1 + i, self.n)} for i in range(self.n - 1)]

    def near_peers(self):
        near = [self.partner] + [2 * self.chip_ahead(j) + self.c for j in range(self.nx - 1)]
        return [{"hid": peer} for peer in near]


def remote(src, dst, send_sem, recv_sem, to):
    return pltpu.make_async_remote_copy(
        src_ref=src,
        dst_ref=dst,
        send_sem=send_sem,
        recv_sem=recv_sem,
        device_id=to if isinstance(to, dict) else {"hid": to},
        device_id_type=MESH,
    )


def gather_sems(seqs, nx):
    wide = pltpu.SemaphoreType.DMA((seqs, nx - 1))
    return [wide] * 4 + [pltpu.SemaphoreType.DMA((seqs,))] * 3


def reduce_sems(seqs, nx):
    wide = pltpu.SemaphoreType.DMA((seqs, nx - 1))
    return [wide] * 2 + [pltpu.SemaphoreType.DMA((seqs,))] * 2


class Gather:
    def __init__(self, group, sems, source, region):
        self.g, self.source, self.region = group, source, region
        self.xs, self.xr, self.rs, self.rr, self.ps, self.pr, self.os = sems

    def _own(self, s):
        return pltpu.make_async_copy(self.source(s), self.region(s, self.g.me), self.os.at[s])

    def _cross(self, s, j):
        to = 2 * self.g.chip_ahead(j) + self.g.c
        return remote(
            self.source(s), self.region(s, self.g.me), self.xs.at[s, j], self.xr.at[s, j], to
        )

    def _crossed(self, s, j):
        to = 2 * self.g.chip_ahead(j) + self.g.c
        block = self.region(s, 2 * self.g.chip_behind(j) + self.g.c)
        return remote(self.source(s), block, self.xs.at[s, j], self.xr.at[s, j], to)

    def _pair(self, s):
        return remote(
            self.source(s),
            self.region(s, self.g.me),
            self.ps.at[s],
            self.pr.at[s],
            self.g.partner,
        )

    def _paired(self, s):
        block = self.region(s, self.g.partner)
        return remote(self.source(s), block, self.ps.at[s], self.pr.at[s], self.g.partner)

    def _relay(self, s, j):
        block = self.region(s, 2 * self.g.chip_behind(j) + self.g.c)
        return remote(block, block, self.rs.at[s, j], self.rr.at[s, j], self.g.partner)

    def _relayed(self, s, j):
        block = self.region(s, 2 * self.g.chip_behind(j) + 1 - self.g.c)
        return remote(block, block, self.rs.at[s, j], self.rr.at[s, j], self.g.partner)

    def start(self, s):
        for j in range(self.g.nx - 1):
            self._cross(s, j).start()
        self._pair(s).start()
        self._own(s).start()

    def relay(self, s):
        for j in range(self.g.nx - 1):
            self._crossed(s, j).wait_recv()
            self._relay(s, j).start()

    def wait(self, s):
        self._own(s).wait()
        self._paired(s).wait_recv()
        for j in range(self.g.nx - 1):
            self._relayed(s, j).wait_recv()

    def drain(self, s):
        self._pair(s).wait_send()
        for j in range(self.g.nx - 1):
            self._cross(s, j).wait_send()
            self._relay(s, j).wait_send()


class Reduce:
    def __init__(self, group, sems, psend, precv, own, xsend, xrecv):
        self.g = group
        self.psend, self.precv, self.own, self.xsend, self.xrecv = psend, precv, own, xsend, xrecv
        self.xs, self.xr, self.ps, self.pr = sems

    def _pair(self, s):
        return remote(
            self.psend.at[s], self.precv.at[s], self.ps.at[s], self.pr.at[s], self.g.partner
        )

    def _cross(self, s, j):
        to = 2 * self.g.chip_ahead(j) + self.g.c
        return remote(
            self.xsend.at[s, j], self.xrecv.at[s, j], self.xs.at[s, j], self.xr.at[s, j], to
        )

    def start(self, s):
        self._pair(s).start()

    def cross(self, s):
        self._pair(s).wait()
        rows = self.own.shape[2]
        for j in range(self.g.nx - 1):
            chip = self.g.chip_ahead(j)

            def add(i, carry, chip=chip, j=j):
                at = pl.ds(pl.multiple_of(i * RB, RB), RB)
                total = self.own[s, chip, at, :] + self.precv[s, chip, at, :].astype(F32)
                self.xsend[s, j, at, :] = total.astype(BF)
                return carry

            lax.fori_loop(0, rows // RB, add, 0)
            self._cross(s, j).start()

    def arrive(self, s):
        for j in range(self.g.nx - 1):
            self._cross(s, j).wait()

    def total(self, s, at):
        total = self.own[s, self.g.x, at, :] + self.precv[s, self.g.x, at, :].astype(F32)
        for j in range(self.g.nx - 1):
            total = total + self.xrecv[s, j, at, :].astype(F32)
        return total


class Cycle:
    def __init__(self, size):
        self.size = size
        self.me = lax.axis_index("dp")
        self.length = size // 2
        line, column = lax.div(self.me, 2), lax.rem(self.me, 2)
        self.place = line + column * (size - 1 - 2 * line)

    def device(self, place):
        column = lax.div(place, self.length)
        line = place + column * (self.size - 1 - 2 * place)
        return 2 * line + column

    def beside(self, way):
        return self.device(lax.rem(self.place + way + self.size, self.size))


def split(shape, size):
    tall = max(16, shape[0] // (2 * size))
    across = 2 * size * tall // shape[0]
    return tall, shape[1] // across, across


def ring_scratch(shape, size):
    tall, broad, _ = split(shape, size)
    step = pltpu.SemaphoreType.DMA((size - 1,))
    return [
        pltpu.VMEM((size - 1, tall, broad), BF),
        pltpu.VMEM((2, tall, broad), F32),
        pltpu.SemaphoreType.DMA((2, 3)),
    ] + [step] * 4 + [pltpu.SemaphoreType.REGULAR]


class Ring:
    def __init__(self, cycle, data, outs, way, scratch):
        self.cycle, self.data, self.outs, self.way = cycle, data, outs, way
        self.size = cycle.size
        self.recv, self.stage, self.stage_sem, self.ss, self.sr, self.gs, self.gr, self.free = scratch
        self.tall, self.broad, self.across = split(data.shape, self.size)
        self.to, self.frm = {"dp": cycle.beside(way)}, {"dp": cycle.beside(-way)}
        self.ticks = 2 * self.size - 1

    def block(self, number):
        place = lax.rem(self.cycle.place + self.way * number + 2 * self.size, self.size)
        index = 2 * place + (0 if self.way > 0 else 1)
        if self.across == 1:
            return pl.multiple_of(index * self.tall, self.tall), 0
        row = lax.div(index, self.across)
        column = lax.rem(index, self.across)
        return (
            pl.multiple_of(row * self.tall, self.tall),
            pl.multiple_of(column * self.broad, self.broad),
        )

    def view(self, number):
        row, column = self.block(number)
        return self.data.at[pl.ds(row, self.tall), pl.ds(column, self.broad)]

    def _add(self, t):
        return remote(self.view(-t), self.recv.at[t], self.ss.at[t], self.sr.at[t], self.to)

    def _pass(self, t):
        block = self.view(1 - t)
        return remote(block, block, self.gs.at[t], self.gr.at[t], self.to)

    def _passed(self, t):
        block = self.view(-t)
        return remote(block, block, self.gs.at[t], self.gr.at[t], self.to)

    def _sum(self, t):
        row, column = self.block(-t)

        def part(i, carry):
            at = pl.ds(pl.multiple_of(row + i * RB, RB), RB)
            cols = pl.ds(column, self.broad)
            arrived = self.recv[t - 1, pl.ds(pl.multiple_of(i * RB, RB), RB), :].astype(F32)
            self.data[at, cols] = (self.data[at, cols].astype(F32) + arrived).astype(BF)
            return carry

        lax.fori_loop(0, self.tall // RB, part, 0)

    def _puts(self, number, slot):
        row, column = self.block(number)
        puts = []
        for k, (target, first, count) in enumerate(self.outs):
            if self.across == 1:
                source = self.stage.at[slot, :, pl.ds(first, count)]
                place = target.at[pl.ds(row, self.tall), :]
            else:
                source = self.stage.at[slot]
                place = target.at[pl.ds(row, self.tall), pl.ds(column, self.broad)]
            puts.append(pltpu.make_async_copy(source, place, self.stage_sem.at[slot, k]))
        return puts

    def _put(self, number, count):
        slot = lax.rem(count, 2)

        @pl.when(count >= 2)
        def _():
            for put in self._puts(number, slot):
                put.wait()

        row, column = self.block(number)

        def part(i, carry):
            at = pl.ds(pl.multiple_of(row + i * RB, RB), RB)
            value = self.data[at, pl.ds(column, self.broad)].astype(F32)
            self.stage[slot, pl.ds(pl.multiple_of(i * RB, RB), RB), :] = value
            return carry

        lax.fori_loop(0, self.tall // RB, part, 0)
        for put in self._puts(number, slot):
            put.start()

    def tick(self, t):
        size = self.size

        @pl.when(t == 0)
        def _():
            self._add(0).start()

        @pl.when((t >= 1) & (t <= size - 1))
        def _():
            self._add(t - 1).wait_recv()
            self._sum(t)

        @pl.when((t >= 1) & (t < size - 1))
        def _():
            self._add(t).start()

        @pl.when((t >= 1) & (t <= size - 1))
        def _():
            self._add(t - 1).wait_send()
            pl.semaphore_signal(self.free, inc=1, device_id=self.frm, device_id_type=MESH)

        @pl.when(t == size - 1)
        def _():
            pl.semaphore_wait(self.free, 1)
            self._pass(0).start()
            self._put(1, 0)

        @pl.when((t > size - 1) & (t < 2 * size - 1))
        def _():
            u = t - size
            self._passed(u).wait_recv()

            @pl.when(t < 2 * size - 2)
            def _():
                pl.semaphore_wait(self.free, 1)
                self._pass(u + 1).start()

            self._put(-u, u + 1)

    def drain(self):
        for slot in range(2):
            for put in self._puts(0, slot):
                put.wait()

        def step(t, carry):
            self._pass(t).wait_send()
            return carry

        lax.fori_loop(0, self.size - 1, step, 0)


def meet(peers):
    barrier = pltpu.get_barrier_semaphore()
    for peer in peers:
        pl.semaphore_signal(barrier, inc=1, device_id=peer, device_id_type=MESH)
    pl.semaphore_wait(barrier, len(peers))


def mean_of(values):
    return jnp.sum(values, axis=1, keepdims=True) * (1.0 / D)


def attend_kernel(n, seqs, heads, *refs):
    (
        len_ref, tok_ref, change_ref, par_ref, wq_ref, wk_ref, wv_ref, qb_ref, vb_ref, wo_ref, gate_ref,
        full_o, qkv_o, prob_o, ctx_o, gat_o, nrm_o, pre_o, rstd_o, mid_o, par_o, change_o,
        full, wqkv, wo, qkv, prob, ctx, gat, own, psend, precv, xsend, xrecv,
        nrm, pre, rstd, mid, par, score, in_sem, out_sem, vec_send, vec_recv, ch_send, ch_recv, *sems,
    ) = refs
    g = Group(n)
    width = heads * HD
    rows = SLOT // n
    gsems, rsems = sems[:7], sems[7:]
    cols = lambda h: pl.ds(pl.multiple_of(h * width, width), width)
    seq = lambda s: pl.ds(pl.multiple_of(s * SLOT, SLOT), SLOT)
    own_rows = lambda s: pl.ds(pl.multiple_of(s * rows, rows), rows)
    ga = Gather(g, gsems, lambda s: tok_ref.at[seq(s), :], lambda s, h: full.at[seq(s), cols(h)])
    re = Reduce(g, rsems, psend, precv, own, xsend, xrecv)

    def vec_to(i):
        to = lax.rem(g.me + 1 + i, n)
        return remote(par_ref, par.at[:, cols(g.me)], vec_send.at[i], vec_recv.at[i], to)

    def vec_from(i):
        to = lax.rem(g.me + 1 + i, n)
        frm = lax.rem(g.me - 1 - i + n, n)
        return remote(par_ref, par.at[:, cols(frm)], vec_send.at[i], vec_recv.at[i], to)

    def change_to(i):
        to = lax.rem(g.me + 1 + i, n)
        return remote(
            change_ref.at[:, g.slot(to)], change_o.at[:, :, cols(g.me)], ch_send.at[i], ch_recv.at[i], to
        )

    def change_from(i):
        to = lax.rem(g.me + 1 + i, n)
        frm = lax.rem(g.me - 1 - i + n, n)
        return remote(
            change_ref.at[:, g.slot(to)], change_o.at[:, :, cols(frm)], ch_send.at[i], ch_recv.at[i], to
        )

    loads = [
        pltpu.make_async_copy(wq_ref, wqkv.at[:, pl.ds(0, width)], in_sem.at[0]),
        pltpu.make_async_copy(wk_ref, wqkv.at[:, pl.ds(width, width)], in_sem.at[1]),
        pltpu.make_async_copy(wv_ref, wqkv.at[:, pl.ds(2 * width, width)], in_sem.at[2]),
        pltpu.make_async_copy(wo_ref, wo, in_sem.at[3]),
        pltpu.make_async_copy(par_ref, par.at[:, cols(g.me)], in_sem.at[4]),
        pltpu.make_async_copy(
            change_ref.at[:, g.slot(g.me)], change_o.at[:, :, cols(g.me)], in_sem.at[5]
        ),
    ]

    def sequence_outs(s):
        return [
            pltpu.make_async_copy(full.at[seq(s), :], full_o.at[seq(s), :], out_sem.at[s, 0]),
            pltpu.make_async_copy(qkv.at[seq(s), :], qkv_o.at[seq(s), :], out_sem.at[s, 1]),
            pltpu.make_async_copy(prob.at[s], prob_o.at[s], out_sem.at[s, 2]),
            pltpu.make_async_copy(ctx.at[seq(s), :], ctx_o.at[seq(s), :], out_sem.at[s, 3]),
            pltpu.make_async_copy(gat.at[seq(s), :], gat_o.at[seq(s), :], out_sem.at[s, 4]),
        ]

    def row_outs(s):
        return [
            pltpu.make_async_copy(nrm.at[own_rows(s), :], nrm_o.at[own_rows(s), :], out_sem.at[s, 5]),
            pltpu.make_async_copy(pre.at[own_rows(s), :], pre_o.at[own_rows(s), :], out_sem.at[s, 6]),
            pltpu.make_async_copy(rstd.at[own_rows(s), :], rstd_o.at[own_rows(s), :], out_sem.at[s, 7]),
            pltpu.make_async_copy(mid.at[own_rows(s), :], mid_o.at[own_rows(s), :], out_sem.at[s, 8]),
        ]

    meet(g.all_peers())

    def begin(s, carry):
        ga.start(s)
        return carry

    lax.fori_loop(0, seqs, begin, 0)
    for i in range(n - 1):
        vec_to(i).start()
    for load in loads:
        load.start()
    for i in range(n - 1):
        change_to(i).start()
    ga.relay(0)
    for load in loads[:5]:
        load.wait()
    for i in range(n - 1):
        vec_from(i).wait()
    par_o[...] = par[...]

    lanes = lax.broadcasted_iota(jnp.int32, (1, width), 1)
    head_lanes = [
        jnp.where((lanes >= h * HD) & (lanes < (h + 1) * HD), 1.0, 0.0).astype(BF) for h in range(heads)
    ]

    def finish(s):
        re.arrive(s)

        def block(i, carry):
            at = pl.ds(pl.multiple_of(i * RB, RB), RB)
            here = pl.ds(pl.multiple_of(s * rows + i * RB, RB), RB)
            token_row = pl.multiple_of(s * SLOT + g.slot(g.me) * rows + i * RB, RB)
            attention_pre = re.total(s, at) + par[0:1, :]
            residual = full[pl.ds(token_row, RB), :].astype(F32) + attention_pre * par[1:2, :]
            centered = residual - mean_of(residual)
            row_rstd = lax.rsqrt(mean_of(centered * centered) + EPS)
            normed = centered * row_rstd
            middle = normed * par[2:3, :] + par[3:4, :]
            nrm[here, :] = normed
            pre[here, :] = attention_pre
            rstd[here, :] = jnp.broadcast_to(row_rstd, (RB, 128))
            mid[here, :] = middle.astype(BF)
            return carry

        lax.fori_loop(0, rows // RB, block, 0)
        for copy in row_outs(s):
            copy.start()

    def sequence(s, carry):
        ga.wait(s)
        here = seq(s)
        projected = nn(full[here, :], wqkv[...])
        qkv[here, 0:width] = (projected[:, 0:width] + qb_ref[...]).astype(BF)
        qkv[here, width : 2 * width] = projected[:, width : 2 * width].astype(BF)
        qkv[here, 2 * width : 3 * width] = (projected[:, 2 * width : 3 * width] + vb_ref[...]).astype(BF)

        @pl.when(s + 1 < seqs)
        def _():
            ga.relay(s + 1)

        @pl.when(s > 0)
        def _():
            re.cross(s - 1)

        length = len_ref[s]
        for h in range(heads):
            score[...] = nt(qkv[here, 0:width] * head_lanes[h], qkv[here, width : 2 * width])

            def softmax(i, carry, h=h):
                at = pl.ds(pl.multiple_of(i * 64, 64), 64)
                places = lax.broadcasted_iota(jnp.int32, (64, SLOT), 1)
                scores = jnp.where(places < length, score[at, :] * (HD**-0.5), MASKED)
                exponent = jnp.exp(scores - jnp.max(scores, axis=1, keepdims=True))
                total = jnp.sum(exponent, axis=1, keepdims=True)
                prob[s, h, at, :] = (exponent * (1.0 / total)).astype(BF)
                return carry

            lax.fori_loop(0, SLOT // 64, softmax, 0)
            term = nn(prob[s, h], qkv[here, 2 * width : 3 * width] * head_lanes[h])
            ctx[here, :] = term if h == 0 else ctx[here, :] + term
        gat[here, :] = (ctx[here, :] * gate_ref[...]).astype(BF)
        for copy in sequence_outs(s):
            copy.start()
        half = SLOT // 2
        there = pl.ds(pl.multiple_of(s * SLOT + (1 - g.c) * half, half), half)
        psend[s] = nn(gat[there, :], wo[...]).astype(BF).reshape(n // 2, rows, D)
        re.start(s)
        mine = pl.ds(pl.multiple_of(s * SLOT + g.c * half, half), half)
        own[s] = nn(gat[mine, :], wo[...]).reshape(n // 2, rows, D)

        @pl.when(s > 0)
        def _():
            finish(s - 1)

        return carry

    lax.fori_loop(0, seqs, sequence, 0)
    re.cross(seqs - 1)
    finish(seqs - 1)
    loads[5].wait()
    for i in range(n - 1):
        change_from(i).wait()

    def end(s, carry):
        ga.drain(s)
        for copy in sequence_outs(s) + row_outs(s):
            copy.wait()
        return carry

    lax.fori_loop(0, seqs, end, 0)


def feed_kernel(n, seqs, units, *refs):
    (
        len_ref, mid_ref, nrm_ref, pre_ref, rstd_ref, par, change_ref, w1_ref, b1_ref, w2_ref, ugate_ref,
        out_o, dlow_o, dres_o, dw1_o, dw2_o, rowsum_o, unitsum_o,
        midf, dffn, w1, w2, act, inner, slope, own, psend, precv, xsend, xrecv,
        nrm, pre, rstd, change, dtwo, dsend, fout, dlow, dres, wide, grad, sums, unit_sums,
        in_sem, out_sem, grad_sem, *sems,
    ) = refs
    g = Group(n)
    rows = SLOT // n
    half = SLOT // 2
    g1, r1, g2, r2 = sems[:7], sems[7:11], sems[11:18], sems[18:]
    seq = lambda s: pl.ds(pl.multiple_of(s * SLOT, SLOT), SLOT)
    own_rows = lambda s: pl.ds(pl.multiple_of(s * rows, rows), rows)
    spot = lambda s, h: pl.ds(pl.multiple_of(s * SLOT + g.slot(h) * rows, rows), rows)
    gm = Gather(g, g1, lambda s: mid_ref.at[own_rows(s), :], lambda s, h: midf.at[spot(s, h), :])
    gd = Gather(g, g2, lambda s: dsend.at[own_rows(s), :], lambda s, h: dffn.at[spot(s, h), :])
    rf = Reduce(g, r1, psend, precv, own, xsend, xrecv)
    rb = Reduce(g, r2, psend, precv, own, xsend, xrecv)
    loads = [
        pltpu.make_async_copy(w1_ref, w1, in_sem.at[0]),
        pltpu.make_async_copy(w2_ref, w2, in_sem.at[1]),
        pltpu.make_async_copy(nrm_ref, nrm, in_sem.at[2]),
        pltpu.make_async_copy(change_ref, change, in_sem.at[3]),
        pltpu.make_async_copy(pre_ref, pre, in_sem.at[4]),
        pltpu.make_async_copy(rstd_ref, rstd, in_sem.at[5]),
    ]

    meet(g.near_peers())

    def begin(s, carry):
        gm.start(s)
        return carry

    lax.fori_loop(0, seqs, begin, 0)
    for load in loads:
        load.start()
    sums[...] = jnp.zeros_like(sums)
    unit_sums[...] = jnp.zeros_like(unit_sums)
    gm.relay(0)
    for load in loads:
        load.wait()

    def finish_forward(s):
        rf.arrive(s)
        length = len_ref[s]

        def block(i, carry):
            at = pl.ds(pl.multiple_of(i * RB, RB), RB)
            here = pl.ds(pl.multiple_of(s * rows + i * RB, RB), RB)
            ffn_pre = rf.total(s, at) + par[4:5, :]
            middle = nrm[here, :] * par[2:3, :] + par[3:4, :]
            residual = middle + ffn_pre * par[1:2, :]
            centered = residual - mean_of(residual)
            row_rstd = lax.rsqrt(mean_of(centered * centered) + EPS)
            normed = centered * row_rstd
            final = normed * par[5:6, :] + par[6:7, :]
            fout[here, :] = final.astype(BF)
            place = g.slot(g.me) * rows + i * RB + lax.broadcasted_iota(jnp.int32, (RB, 1), 0)
            live = jnp.where(place < length, 1.0, 0.0)
            d_final = live * (change[here, :].astype(F32) + final)
            sums[0] += fold(d_final * normed)
            sums[1] += fold(d_final)
            d_normed = d_final * par[5:6, :]
            d_two = row_rstd * (d_normed - mean_of(d_normed) - normed * mean_of(d_normed * normed))
            sums[2] += fold(d_two * ffn_pre)
            d_ffn = d_two * par[1:2, :]
            sums[3] += fold(d_ffn)
            dtwo[here, :] = d_two
            dsend[here, :] = d_ffn.astype(BF)
            return carry

        lax.fori_loop(0, rows // RB, block, 0)
        gd.start(s)

    def forward(s, carry):
        gm.wait(s)
        here = seq(s)

        def part(b, carry):
            cols = pl.ds(pl.multiple_of(b * NB, NB), NB)
            wide[...] = nn(midf[here, :], w1[:, cols])
            bias = b1_ref[:, cols]
            gate = ugate_ref[:, cols]

            def block(i, carry):
                at = pl.ds(pl.multiple_of(i * 32, 32), 32)
                row = pl.ds(pl.multiple_of(s * SLOT + i * 32, 32), 32)
                v = wide[at, :] + bias
                phi = 0.5 * (1.0 + lax.erf(v * ROOT_HALF))
                activated = v * phi
                act[row, cols] = activated.astype(BF)
                inner[row, cols] = (activated * gate).astype(BF)
                steep = phi + v * jnp.exp(-0.5 * v * v) * (1.0 / ROOT_TWO_PI)
                slope[row, cols] = (gate * steep).astype(BF)
                return carry

            lax.fori_loop(0, SLOT // 32, block, 0)
            return carry

        lax.fori_loop(0, units // NB, part, 0)

        @pl.when(s + 1 < seqs)
        def _():
            gm.relay(s + 1)

        @pl.when(s > 0)
        def _():
            rf.cross(s - 1)

        there = pl.ds(pl.multiple_of(s * SLOT + (1 - g.c) * half, half), half)
        psend[s] = nn(inner[there, :], w2[...]).astype(BF).reshape(n // 2, rows, D)
        rf.start(s)
        mine = pl.ds(pl.multiple_of(s * SLOT + g.c * half, half), half)
        own[s] = nn(inner[mine, :], w2[...]).reshape(n // 2, rows, D)

        @pl.when(s > 0)
        def _():
            finish_forward(s - 1)

        return carry

    lax.fori_loop(0, seqs, forward, 0)
    rf.cross(seqs - 1)
    gd.relay(0)
    finish_forward(seqs - 1)

    def row_outs(s):
        return [
            pltpu.make_async_copy(fout.at[own_rows(s), :], out_o.at[own_rows(s), :], out_sem.at[s, 0]),
            pltpu.make_async_copy(dlow.at[own_rows(s), :], dlow_o.at[own_rows(s), :], out_sem.at[s, 1]),
            pltpu.make_async_copy(dres.at[own_rows(s), :], dres_o.at[own_rows(s), :], out_sem.at[s, 2]),
        ]

    def finish_backward(s):
        rb.arrive(s)

        def block(i, carry):
            at = pl.ds(pl.multiple_of(i * RB, RB), RB)
            here = pl.ds(pl.multiple_of(s * rows + i * RB, RB), RB)
            normed = nrm[here, :]
            d_middle = dtwo[here, :] + rb.total(s, at)
            sums[4] += fold(d_middle * normed)
            sums[5] += fold(d_middle)
            d_normed = d_middle * par[2:3, :]
            d_one = rstd[here, 0:1] * (
                d_normed - mean_of(d_normed) - normed * mean_of(d_normed * normed)
            )
            sums[2] += fold(d_one * pre[here, :])
            d_attn = d_one * par[1:2, :]
            sums[6] += fold(d_attn)
            dres[here, :] = d_one
            dlow[here, :] = d_attn.astype(BF)
            return carry

        lax.fori_loop(0, rows // RB, block, 0)
        for copy in row_outs(s):
            copy.start()

    def backward(s, carry):
        gd.wait(s)
        here = seq(s)

        def part(b, carry):
            cols = pl.ds(pl.multiple_of(b * NB, NB), NB)
            wide[...] = nt(dffn[here, :], w2[cols, :])

            def block(i, sums_here):
                unit_part, bias_part = sums_here
                at = pl.ds(pl.multiple_of(i * 32, 32), 32)
                row = pl.ds(pl.multiple_of(s * SLOT + i * 32, 32), 32)
                d_inner = wide[at, :]
                d_pre = (d_inner * slope[row, cols].astype(F32)).astype(BF)
                unit_part = unit_part + fold(d_inner * act[row, cols].astype(F32))
                bias_part = bias_part + fold(d_pre.astype(F32))
                slope[row, cols] = d_pre
                return (unit_part, bias_part)

            zero = jnp.zeros((8, NB), F32)
            unit_part, bias_part = lax.fori_loop(0, SLOT // 32, block, (zero, zero))
            unit_sums[0, :, cols] += unit_part
            unit_sums[1, :, cols] += bias_part
            return carry

        lax.fori_loop(0, units // NB, part, 0)

        @pl.when(s + 1 < seqs)
        def _():
            gd.relay(s + 1)

        @pl.when(s > 0)
        def _():
            rb.cross(s - 1)

        there = pl.ds(pl.multiple_of(s * SLOT + (1 - g.c) * half, half), half)
        psend[s] = nt(slope[there, :], w1[...]).astype(BF).reshape(n // 2, rows, D)
        rb.start(s)
        mine = pl.ds(pl.multiple_of(s * SLOT + g.c * half, half), half)
        own[s] = nt(slope[mine, :], w1[...]).reshape(n // 2, rows, D)

        @pl.when(s > 0)
        def _():
            finish_backward(s - 1)

        return carry

    lax.fori_loop(0, seqs, backward, 0)
    rb.cross(seqs - 1)

    def grad_out(k, b):
        target = (dw2_o, dw1_o)[k]
        at = pl.ds(pl.multiple_of(b * NB, NB), NB)
        return pltpu.make_async_copy(grad.at[b], target.at[at, :], grad_sem.at[k, b])

    def down_grad(b, carry):
        cols = pl.ds(pl.multiple_of(b * NB, NB), NB)
        grad[b] = tn(inner[:, cols], dffn[...]).astype(BF)
        grad_out(0, b).start()
        return carry

    lax.fori_loop(0, units // NB, down_grad, 0)
    finish_backward(seqs - 1)
    for b in range(units // NB):
        grad_out(0, b).wait()

    def inner_grad(b, carry):
        cols = pl.ds(pl.multiple_of(b * NB, NB), NB)
        grad[b, :, 0:units] = tn(midf[:, cols], slope[...]).astype(BF)
        pltpu.make_async_copy(
            grad.at[b, :, pl.ds(0, units)], dw1_o.at[cols, :], grad_sem.at[1, b]
        ).start()
        return carry

    lax.fori_loop(0, D // NB, inner_grad, 0)
    for k in range(7):
        rowsum_o[k : k + 1, :] = jnp.sum(sums[k], axis=0, keepdims=True)
    rowsum_o[7:8, :] = jnp.zeros((1, D), F32)
    for k in range(2):
        unitsum_o[k : k + 1, :] = jnp.sum(unit_sums[k], axis=0, keepdims=True)
    for b in range(D // NB):
        at = pl.ds(b * NB, NB)
        pltpu.make_async_copy(
            grad.at[b, :, pl.ds(0, units)], dw1_o.at[at, :], grad_sem.at[1, b]
        ).wait()

    def end(s, carry):
        gm.drain(s)
        gd.drain(s)
        for copy in row_outs(s):
            copy.wait()
        return carry

    lax.fori_loop(0, seqs, end, 0)


def attend_back_kernel(n, seqs, heads, size, *refs):
    (
        dlow_ref, dres_ref, full_ref, qkv_ref, prob_ref, ctx_ref, gat_ref,
        wq_ref, wk_ref, wv_ref, wo_ref, dw1_ref, dw2_ref, out_ref, gate_ref,
        tgrad_o, dwqkv_o, dwo_o, dw1_o, dw2_o, output_o, sums_o,
        dattn, dres, full, qkv, prob, ctx, gat, wqkv, wo, dctx, dqkv, dprob, dscore, acc,
        block_f, own, psend, precv, xsend, xrecv, tgrad, grad, gwo, sums, dw1, dw2,
        in_sem, out_sem, grad_sem, move_send, move_recv, *sems,
    ) = refs
    g = Group(n)
    cycle = Cycle(size)
    rings = []
    for k, (data, target) in enumerate(((dw1, dw1_o), (dw2, dw2_o))):
        for way in (1, -1):
            i = 11 + 8 * len(rings)
            outs = [(target, 0, data.shape[1])]
            rings.append(Ring(cycle, data, outs, way, sems[i : i + 8]))
    ticks = rings[0].ticks

    def tick(t):
        for ring in rings:
            ring.tick(t)

    def move_to(i):
        to = lax.rem(g.me + 1 + i, n)
        return remote(
            out_ref.at[:, :, cols_of(to)], output_o.at[:, g.slot(g.me)], move_send.at[i], move_recv.at[i], to
        )

    def move_from(i):
        to = lax.rem(g.me + 1 + i, n)
        frm = lax.rem(g.me - 1 - i + n, n)
        return remote(
            out_ref.at[:, :, cols_of(to)], output_o.at[:, g.slot(frm)], move_send.at[i], move_recv.at[i], to
        )

    width = heads * HD
    rows = SLOT // n
    gsems, rsems = sems[:7], sems[7:11]
    cols_of = lambda h: pl.ds(pl.multiple_of(h * width, width), width)
    seq = lambda s: pl.ds(pl.multiple_of(s * SLOT, SLOT), SLOT)
    own_rows = lambda s: pl.ds(pl.multiple_of(s * rows, rows), rows)
    spot = lambda s, h: pl.ds(pl.multiple_of(s * SLOT + g.slot(h) * rows, rows), rows)
    ga = Gather(g, gsems, lambda s: dlow_ref.at[own_rows(s), :], lambda s, h: dattn.at[spot(s, h), :])
    re = Reduce(g, rsems, psend, precv, own, xsend, xrecv)
    loads = [
        pltpu.make_async_copy(wo_ref, wo, in_sem.at[0]),
        pltpu.make_async_copy(ctx_ref, ctx, in_sem.at[1]),
        pltpu.make_async_copy(qkv_ref, qkv, in_sem.at[2]),
        pltpu.make_async_copy(prob_ref, prob, in_sem.at[3]),
        pltpu.make_async_copy(wq_ref, wqkv.at[:, pl.ds(0, width)], in_sem.at[4]),
        pltpu.make_async_copy(wk_ref, wqkv.at[:, pl.ds(width, width)], in_sem.at[5]),
        pltpu.make_async_copy(wv_ref, wqkv.at[:, pl.ds(2 * width, width)], in_sem.at[6]),
        pltpu.make_async_copy(dres_ref, dres, in_sem.at[7]),
        pltpu.make_async_copy(full_ref, full, in_sem.at[8]),
        pltpu.make_async_copy(gat_ref, gat, in_sem.at[9]),
        pltpu.make_async_copy(
            out_ref.at[:, :, cols_of(g.me)], output_o.at[:, g.slot(g.me)], in_sem.at[11]
        ),
    ]
    grads_in = [
        pltpu.make_async_copy(dw1_ref, dw1, in_sem.at[12]),
        pltpu.make_async_copy(dw2_ref, dw2, in_sem.at[13]),
    ]
    meet(g.all_peers() + [{"dp": cycle.beside(1)}, {"dp": cycle.beside(-1)}])
    for load in grads_in:
        load.start()

    def begin(s, carry):
        ga.start(s)
        return carry

    lax.fori_loop(0, seqs, begin, 0)
    for load in loads:
        load.start()
    sums[...] = jnp.zeros_like(sums)
    for load in grads_in:
        load.wait()
    tick(0)
    ga.relay(0)
    for load in loads[:8]:
        load.wait()

    lanes = lax.broadcasted_iota(jnp.int32, (1, width), 1)
    head_lanes = [
        jnp.where((lanes >= h * HD) & (lanes < (h + 1) * HD), 1.0, 0.0).astype(BF) for h in range(heads)
    ]

    def out(s):
        return pltpu.make_async_copy(tgrad.at[seq(s), :], tgrad_o.at[seq(s), :], out_sem.at[s])

    def finish(s):
        re.arrive(s)

        def block(i, carry):
            at = pl.ds(pl.multiple_of(i * 32, 32), 32)
            tgrad[pl.ds(pl.multiple_of(s * SLOT + i * 32, 32), 32), :] = re.total(s, at)
            return carry

        lax.fori_loop(0, SLOT // 32, block, 0)
        out(s).start()

    def token_block(s, h):
        cols = pl.ds(pl.multiple_of(h * width, width), width)
        block_f[...] = nt(dqkv[seq(s), :], wqkv[cols, :])
        mine = pl.ds(pl.multiple_of(g.slot(g.me) * rows, rows), rows)
        block_f[mine, :] += dres[own_rows(s), cols]

    def sequence(s, carry):
        ga.wait(s)
        here = seq(s)
        d_gated = nt(dattn[here, :], wo[...])
        sums[0] += fold(d_gated * ctx[here, :])
        dctx[...] = (d_gated * gate_ref[...]).astype(BF)

        @pl.when(s + 1 < seqs)
        def _():
            ga.relay(s + 1)

        @pl.when(s > 0)
        def _():
            re.cross(s - 1)

        for h in range(heads):
            d_context = dctx[...] * head_lanes[h]
            dprob[...] = nt(d_context, qkv[here, 2 * width : 3 * width])

            def softmax(i, carry, h=h):
                at = pl.ds(pl.multiple_of(i * 64, 64), 64)
                p = prob[s, h, at, :].astype(F32)
                weighted = p * dprob[at, :]
                total = jnp.sum(weighted, axis=1, keepdims=True)
                dscore[at, :] = (weighted - p * total).astype(BF)
                return carry

            lax.fori_loop(0, SLOT // 64, softmax, 0)
            terms = (
                nn(dscore[...], qkv[here, width : 2 * width] * head_lanes[h]),
                tn(dscore[...], qkv[here, 0:width] * head_lanes[h]),
                tn(prob[s, h], d_context),
            )
            for k in range(3):
                acc[k] = terms[k] if h == 0 else acc[k] + terms[k]
            tick(s * heads + h + 1)
        scales = (HD**-0.5, HD**-0.5, 1.0)
        for k in range(3):
            rounded = (acc[k] * scales[k]).astype(BF)
            dqkv[here, k * width : (k + 1) * width] = rounded
            sums[1 + k] += fold(rounded.astype(F32))
        for chip in range(n // 2):
            token_block(s, 2 * chip + 1 - g.c)
            psend[s, chip] = block_f[...].astype(BF)
        re.start(s)
        for chip in range(n // 2):
            token_block(s, 2 * chip + g.c)
            own[s, chip] = block_f[...]

        @pl.when(s > 0)
        def _():
            finish(s - 1)

        return carry

    lax.fori_loop(0, seqs, sequence, 0)
    re.cross(seqs - 1)
    for i in range(n - 1):
        move_to(i).start()
    for load in loads[8:]:
        load.wait()

    def grad_out(b):
        at = pl.ds(pl.multiple_of(b * NB, NB), NB)
        return pltpu.make_async_copy(grad.at[b], dwqkv_o.at[at, :], grad_sem.at[b])

    def token_grad(b, carry):
        cols = pl.ds(pl.multiple_of(b * NB, NB), NB)
        grad[b] = tn(full[:, cols], dqkv[...]).astype(BF)
        grad_out(b).start()
        return carry

    lax.fori_loop(0, D // NB, token_grad, 0)
    gwo[...] = tn(gat[...], dattn[...]).astype(BF)
    gwo_out = pltpu.make_async_copy(gwo, dwo_o, in_sem.at[10])
    gwo_out.start()
    finish(seqs - 1)
    for k in range(4):
        sums_o[k : k + 1, :] = jnp.sum(sums[k], axis=0, keepdims=True)
    sums_o[4:8, :] = jnp.zeros((4, width), F32)
    gwo_out.wait()

    def rest(t, carry):
        tick(t)
        return carry

    lax.fori_loop(seqs * heads + 1, ticks, rest, 0)
    for ring in rings:
        ring.drain()
    for i in range(n - 1):
        move_from(i).wait()

    def end_grad(b, carry):
        grad_out(b).wait()
        return carry

    lax.fori_loop(0, D // NB, end_grad, 0)

    def end(s, carry):
        ga.drain(s)
        out(s).wait()
        return carry

    lax.fori_loop(0, seqs, end, 0)


def settle_kernel(n, size, seqs, *refs):
    (
        len_ref, dwqkv_ref, dwo_ref, output_ref, teacher_ref, row_ref, unit_ref, head_ref,
        dwq_o, dwk_o, dwv_o, dwo_o, small_o, units_o,
        dwqkv, dwo, output, teacher, parts, small, rbuf, sbuf, ubuf,
        in_sem, r_send, r_recv, s_send, s_recv, u_send, u_recv, *sems,
    ) = refs
    g = Group(n)
    cycle = Cycle(size)
    width = head_ref.shape[1]
    cols = lambda h: pl.ds(pl.multiple_of(h * width, width), width)
    outs = [(dwq_o, 0, width), (dwk_o, width, width), (dwv_o, 2 * width, width)]
    rings = []
    for data, targets in ((dwqkv, outs), (dwo, [(dwo_o, 0, D)])):
        for way in (1, -1):
            i = 8 * len(rings)
            rings.append(Ring(cycle, data, targets, way, sems[i : i + 8]))

    def tick(t):
        for ring in rings:
            ring.tick(t)

    def row_to(i):
        to = lax.rem(g.me + 1 + i, n)
        return remote(parts.at[:, cols(to)], rbuf.at[i], r_send.at[i], r_recv.at[i], to)

    def small_to(i):
        to = {"dp": lax.rem(cycle.me + 1 + i, size)}
        return remote(small, sbuf.at[i], s_send.at[i], s_recv.at[i], to)

    def units_to(i):
        to = {"dp": lax.rem(cycle.me + 1 + i, size)}
        return remote(unit_ref, ubuf.at[i], u_send.at[i], u_recv.at[i], to)

    loads = [
        pltpu.make_async_copy(dwqkv_ref, dwqkv, in_sem.at[0]),
        pltpu.make_async_copy(dwo_ref, dwo, in_sem.at[1]),
        pltpu.make_async_copy(output_ref, output, in_sem.at[2]),
        pltpu.make_async_copy(teacher_ref, teacher, in_sem.at[3]),
    ]
    for load in loads:
        load.start()
    meet(g.all_peers() + [{"dp": lax.rem(cycle.me + 1 + i, size)} for i in range(size - 1)])
    for load in loads[:2]:
        load.wait()
    tick(0)
    for load in loads[2:]:
        load.wait()
    for i in range(size - 1):
        units_to(i).start()

    def sequence(s, total):
        length = len_ref[s]

        def block(i, total):
            at = pl.ds(pl.multiple_of(s * SLOT + i * 32, 32), 32)
            place = i * 32 + lax.broadcasted_iota(jnp.int32, (32, 1), 0)
            differ = output[at, :].astype(F32) - teacher[at, :].astype(F32)
            return total + fold(jnp.where(place < length, differ * differ, 0.0))

        return lax.fori_loop(0, SLOT // 32, block, total)

    squares = lax.fori_loop(0, seqs, sequence, jnp.zeros((8, width), F32))
    parts[...] = row_ref[...]
    for h in range(n):
        parts[7:8, h * width : (h + 1) * width] = jnp.sum(squares, axis=0, keepdims=True)
    for i in range(n - 1):
        row_to(i).start()
    tick(1)
    total = parts[:, cols(g.me)]
    for i in range(n - 1):
        row_to(i).wait()
        total = total + rbuf[i]
    small[:, 0:width] = total
    small[:, width : 2 * width] = head_ref[...]
    for i in range(size - 1):
        small_to(i).start()

    def rest(t, carry):
        tick(t)
        return carry

    lax.fori_loop(2, rings[0].ticks, rest, 0)
    small_sum = small[...]
    unit_sum = unit_ref[...]
    for i in range(size - 1):
        small_to(i).wait()
        units_to(i).wait()
        small_sum = small_sum + sbuf[i]
        unit_sum = unit_sum + ubuf[i]
    small_o[...] = small_sum
    units_o[...] = unit_sum
    for ring in rings:
        ring.drain()


def hbm():
    return pl.BlockSpec(memory_space=pl.ANY)


def vmem():
    return pl.BlockSpec(memory_space=pltpu.VMEM)


def smem():
    return pl.BlockSpec(memory_space=pltpu.SMEM)


def call(kernel, name, ident, ins, outs, scratch, flops):
    return pl.pallas_call(
        kernel,
        name=name,
        out_shape=[jax.ShapeDtypeStruct(shape, dtype) for shape, dtype, _ in outs],
        in_specs=ins,
        out_specs=[spec for _, _, spec in outs],
        scratch_shapes=scratch,
        compiler_params=pltpu.CompilerParams(
            collective_id=ident, has_side_effects=True, vmem_limit_bytes=VMEM_LIMIT
        ),
        cost_estimate=pl.CostEstimate(flops=flops, bytes_accessed=30_000_000, transcendentals=0),
    )


def attend(n, seqs, heads, args):
    width, rows, nx, half = heads * HD, SLOT // n, n // 2, SLOT // 2
    tokens, owned = seqs * SLOT, seqs * rows
    v, dma = pltpu.VMEM, pltpu.SemaphoreType.DMA
    return call(
        functools.partial(attend_kernel, n, seqs, heads),
        "attend",
        0,
        [smem(), hbm(), hbm(), vmem(), hbm(), hbm(), hbm(), vmem(), vmem(), hbm(), vmem()],
        [
            ((tokens, D), BF, hbm()),
            ((tokens, 3 * width), BF, hbm()),
            ((seqs, heads, SLOT, SLOT), BF, hbm()),
            ((tokens, width), F32, hbm()),
            ((tokens, width), BF, hbm()),
            ((owned, D), F32, hbm()),
            ((owned, D), F32, hbm()),
            ((owned, 128), F32, hbm()),
            ((owned, D), BF, hbm()),
            ((8, D), F32, vmem()),
            ((seqs, rows, D), BF, hbm()),
        ],
        [
            v((tokens, D), BF),
            v((D, 3 * width), BF),
            v((width, D), BF),
            v((tokens, 3 * width), BF),
            v((seqs, heads, SLOT, SLOT), BF),
            v((tokens, width), F32),
            v((tokens, width), BF),
            v((seqs, nx, rows, D), F32),
            v((seqs, nx, rows, D), BF),
            v((seqs, nx, rows, D), BF),
            v((seqs, nx - 1, rows, D), BF),
            v((seqs, nx - 1, rows, D), BF),
            v((owned, D), F32),
            v((owned, D), F32),
            v((owned, 128), F32),
            v((owned, D), BF),
            v((8, D), F32),
            v((SLOT, SLOT), F32),
            dma((6,)),
            dma((seqs, 9)),
            dma((n - 1,)),
            dma((n - 1,)),
            dma((n - 1,)),
            dma((n - 1,)),
        ]
        + gather_sems(seqs, nx)
        + reduce_sems(seqs, nx),
        10_000_000_000,
    )(*args)


def feed(n, seqs, units, args):
    rows, nx = SLOT // n, n // 2
    tokens, owned = seqs * SLOT, seqs * rows
    v, dma = pltpu.VMEM, pltpu.SemaphoreType.DMA
    return call(
        functools.partial(feed_kernel, n, seqs, units),
        "feed",
        1,
        [smem(), hbm(), hbm(), hbm(), hbm(), vmem(), hbm(), hbm(), vmem(), hbm(), vmem()],
        [
            ((owned, D), BF, hbm()),
            ((owned, D), BF, hbm()),
            ((owned, D), F32, hbm()),
            ((D, units), BF, hbm()),
            ((units, D), BF, hbm()),
            ((8, D), F32, vmem()),
            ((2, units), F32, vmem()),
        ],
        [
            v((tokens, D), BF),
            v((tokens, D), BF),
            v((D, units), BF),
            v((units, D), BF),
            v((tokens, units), BF),
            v((tokens, units), BF),
            v((tokens, units), BF),
            v((seqs, nx, rows, D), F32),
            v((seqs, nx, rows, D), BF),
            v((seqs, nx, rows, D), BF),
            v((seqs, nx - 1, rows, D), BF),
            v((seqs, nx - 1, rows, D), BF),
            v((owned, D), F32),
            v((owned, D), F32),
            v((owned, 128), F32),
            v((owned, D), BF),
            v((owned, D), F32),
            v((owned, D), BF),
            v((owned, D), BF),
            v((owned, D), BF),
            v((owned, D), F32),
            v((SLOT, NB), F32),
            v((D // NB, NB, D), BF),
            v((7, 8, D), F32),
            v((2, 8, units), F32),
            dma((6,)),
            dma((seqs, 3)),
            dma((2, D // NB)),
        ]
        + (gather_sems(seqs, nx) + reduce_sems(seqs, nx)) * 2,
        30_000_000_000,
    )(*args)


def attend_back(n, seqs, heads, units, size, args):
    width, rows, nx = heads * HD, SLOT // n, n // 2
    tokens, owned = seqs * SLOT, seqs * rows
    v, dma = pltpu.VMEM, pltpu.SemaphoreType.DMA
    return call(
        functools.partial(attend_back_kernel, n, seqs, heads, size),
        "attend_back",
        2,
        [hbm()] * 14 + [vmem()],
        [
            ((tokens, width), F32, hbm()),
            ((D, 3 * width), BF, hbm()),
            ((width, D), BF, hbm()),
            ((D, units), F32, hbm()),
            ((units, D), F32, hbm()),
            ((seqs, n, rows, width), BF, hbm()),
            ((8, width), F32, vmem()),
        ],
        [
            v((tokens, D), BF),
            v((owned, D), F32),
            v((tokens, D), BF),
            v((tokens, 3 * width), BF),
            v((seqs, heads, SLOT, SLOT), BF),
            v((tokens, width), F32),
            v((tokens, width), BF),
            v((D, 3 * width), BF),
            v((width, D), BF),
            v((SLOT, width), BF),
            v((tokens, 3 * width), BF),
            v((SLOT, SLOT), F32),
            v((SLOT, SLOT), BF),
            v((3, SLOT, width), F32),
            v((SLOT, width), F32),
            v((seqs, nx, SLOT, width), F32),
            v((seqs, nx, SLOT, width), BF),
            v((seqs, nx, SLOT, width), BF),
            v((seqs, nx - 1, SLOT, width), BF),
            v((seqs, nx - 1, SLOT, width), BF),
            v((tokens, width), F32),
            v((D // NB, NB, 3 * width), BF),
            v((width, D), BF),
            v((4, 8, width), F32),
            v((D, units), BF),
            v((units, D), BF),
            dma((14,)),
            dma((seqs,)),
            dma((D // NB,)),
            dma((n - 1,)),
            dma((n - 1,)),
        ]
        + gather_sems(seqs, nx)
        + reduce_sems(seqs, nx)
        + ring_scratch((D, units), size) * 2
        + ring_scratch((units, D), size) * 2,
        20_000_000_000,
    )(*args)


def settle(n, size, seqs, width, units, args):
    v, dma = pltpu.VMEM, pltpu.SemaphoreType.DMA
    tokens = seqs * SLOT
    return call(
        functools.partial(settle_kernel, n, size, seqs),
        "settle",
        3,
        [smem()] + [hbm()] * 4 + [vmem()] * 3,
        [((D, width), F32, hbm())] * 3
        + [((width, D), F32, hbm()), ((8, 2 * width), F32, vmem()), ((2, units), F32, vmem())],
        [
            v((D, 3 * width), BF),
            v((width, D), BF),
            v((tokens, width), BF),
            v((tokens, width), BF),
            v((8, D), F32),
            v((8, 2 * width), F32),
            v((n - 1, 8, width), F32),
            v((size - 1, 8, 2 * width), F32),
            v((size - 1, 2, units), F32),
            dma((4,)),
            dma((n - 1,)),
            dma((n - 1,)),
        ]
        + [dma((size - 1,))] * 4
        + ring_scratch((D, 3 * width), size) * 2
        + ring_scratch((width, D), size) * 2,
        1_000_000_000,
    )(*args)


def on_device(
    n,
    size,
    tokens,
    query_weight,
    query_bias,
    key_weight,
    value_weight,
    value_bias,
    output_weight,
    output_bias,
    attention_gain,
    attention_shift,
    inner_weight,
    inner_bias,
    down_weight,
    down_bias,
    final_gain,
    final_shift,
    head_alpha,
    unit_alpha,
    width_alpha,
    multipliers,
    head_noise,
    unit_noise,
    width_noise,
    lengths,
    teacher,
    upstream,
):
    row_count, width = tokens.shape
    heads = width // HD
    units = inner_weight.shape[1]
    seqs = row_count // SLOT
    rows = SLOT // n
    rank = lax.axis_index("hid")
    local_lengths = lax.dynamic_slice_in_dim(lengths, lax.axis_index("dp") * seqs, seqs)
    head_local = lax.dynamic_slice_in_dim(head_alpha, rank * heads, heads)
    unit_local = lax.dynamic_slice_in_dim(unit_alpha, rank * units, units)
    width_local = lax.dynamic_slice_in_dim(width_alpha, rank * width, width)
    head_gate, head_pull = jax.vjp(lambda part: gate_value(head_noise, part), head_local)
    unit_gate, unit_pull = jax.vjp(lambda part: gate_value(unit_noise, part), unit_local)
    width_gate, width_pull = jax.vjp(lambda part: gate_value(width_noise, part), width_local)
    gate_row = jnp.repeat(head_gate, HD)[None, :]
    vectors = jnp.stack(
        [
            output_bias,
            width_gate,
            attention_gain,
            attention_shift,
            down_bias,
            final_gain,
            final_shift,
            jnp.zeros_like(down_bias),
        ]
    )
    change = (upstream.astype(F32) - teacher.astype(F32)).astype(BF).reshape(seqs, n, rows, width)
    full, qkv, prob, ctx, gat, nrm, pre, rstd, mid, par, change_rows = attend(
        n,
        seqs,
        heads,
        (
            local_lengths,
            tokens,
            change,
            vectors,
            query_weight,
            key_weight,
            value_weight,
            query_bias[None, :],
            value_bias[None, :],
            output_weight,
            gate_row,
        ),
    )
    out_rows, d_low, d_res, dw_inner, dw_down, row_sums, unit_sums = feed(
        n,
        seqs,
        units,
        (
            local_lengths,
            mid,
            nrm,
            pre,
            rstd,
            par,
            change_rows.reshape(seqs * rows, D),
            inner_weight,
            inner_bias[None, :],
            down_weight,
            unit_gate[None, :],
        ),
    )
    tokens_grad, dw_qkv, dw_o, dw_inner, dw_down, output, head_sums = attend_back(
        n,
        seqs,
        heads,
        units,
        size,
        (
            d_low,
            d_res,
            full,
            qkv,
            prob,
            ctx,
            gat,
            query_weight,
            key_weight,
            value_weight,
            output_weight,
            dw_inner,
            dw_down,
            out_rows.reshape(seqs, rows, D),
            gate_row,
        ),
    )
    output = output.reshape(row_count, width)
    dw_q, dw_k, dw_v, dw_o, small, unit_all = settle(
        n,
        size,
        seqs,
        width,
        units,
        (local_lengths, dw_qkv, dw_o, output, teacher, row_sums, unit_sums, head_sums),
    )
    rows_all, head_all = small[:, :width], small[:, width:]
    distill_mse = jnp.sum(rows_all[7]) / (jnp.sum(lengths).astype(F32) * D)
    lag = jax.grad(lagrangian, argnums=(0, 1, 2, 3))(head_alpha, unit_alpha, width_alpha, multipliers)
    head_alpha_grad = head_pull(jnp.sum(head_all[0].reshape(heads, HD), axis=1))[0]
    head_alpha_grad += lax.dynamic_slice_in_dim(lag[0], rank * heads, heads)
    unit_alpha_grad = unit_pull(unit_all[0])[0]
    unit_alpha_grad += lax.dynamic_slice_in_dim(lag[1], rank * units, units)
    width_alpha_grad = width_pull(rows_all[2])[0]
    width_alpha_grad += lax.dynamic_slice_in_dim(lag[2], rank * width, width)
    return (
        output,
        tokens_grad,
        dw_q,
        head_all[1],
        dw_k,
        dw_v,
        head_all[3],
        dw_o,
        rows_all[6],
        rows_all[4],
        rows_all[5],
        dw_inner,
        unit_all[1],
        dw_down,
        rows_all[3],
        rows_all[0],
        rows_all[1],
        head_alpha_grad,
        unit_alpha_grad,
        width_alpha_grad,
        distill_mse,
        multipliers + ASCENT * lag[3],
    )


def solution(mesh):
    tall, wide, vec, rep = P("dp", "hid"), P(None, "hid"), P("hid"), P()
    deep = P("hid", None)
    return jax.shard_map(
        functools.partial(on_device, mesh.shape["hid"], mesh.shape["dp"]),
        mesh=mesh,
        in_specs=(tall, wide, vec, wide, wide, vec, deep, vec, vec, vec, wide, vec, deep)
        + (vec,) * 3
        + (rep,) * 4
        + (vec,) * 3
        + (rep, tall, tall),
        out_specs=(tall, tall, wide, vec, wide, wide, vec, deep, vec, vec, vec, wide, vec, deep)
        + (vec,) * 6
        + (rep, rep),
        check_vma=False,
    )
```

```python
import functools

import jax
import jax.numpy as jnp
from jax import lax
from jax.experimental import pallas as pl
from jax.experimental.pallas import tpu as pltpu
from jax.sharding import PartitionSpec as P

D = 1024
HD = 64
FF = 4096
SLOT = 512

BETA = 2.0 / 3.0
GAMMA = -0.1
ZETA = 1.1
TARGET = 0.7
ASCENT = 1.0
EPS = 1e-12
MASKED = -1000000000.0
ROOT_HALF = 0.7071067811865476
ROOT_TWO_PI = 2.5066282746310002

MESH = pl.DeviceIdType.MESH
VMEM_LIMIT = 66_000_000
BF = jnp.bfloat16
F32 = jnp.float32
NB = 256
RB = 16


def gate_value(noise, alpha):
    logits = (jnp.log(noise) - jnp.log(1.0 - noise) + alpha) / BETA
    stretched = jax.nn.sigmoid(logits) * (ZETA - GAMMA) + GAMMA
    return jnp.clip(stretched, 0.0, 1.0)


def keep_prob(alpha):
    return jax.nn.sigmoid(alpha - BETA * jnp.log(-GAMMA / ZETA))


def lagrangian(head_alpha, unit_alpha, width_alpha, multipliers):
    heads_kept = jnp.sum(keep_prob(head_alpha))
    units_kept = jnp.sum(keep_prob(unit_alpha))
    dims_kept = jnp.sum(keep_prob(width_alpha))
    full_size = 4.0 * D * D + 2.0 * D * FF
    expected = (4.0 * HD * heads_kept * dims_kept + 2.0 * units_kept * dims_kept) / full_size
    gap_value = 1.0 - expected - TARGET
    return multipliers[0] * gap_value + multipliers[1] * gap_value * gap_value


def nn(a, b):
    return jnp.dot(a, b, preferred_element_type=F32)


def nt(a, b):
    return lax.dot_general(a, b, (((1,), (1,)), ((), ())), preferred_element_type=F32)


def tn(a, b):
    return lax.dot_general(a, b, (((0,), (0,)), ((), ())), preferred_element_type=F32)


def fold(values):
    return jnp.sum(values.reshape(values.shape[0] // 8, 8, values.shape[1]), axis=0)


class Group:
    def __init__(self, n):
        self.n = n
        self.nx = n // 2
        self.me = lax.axis_index("hid")
        self.x = lax.div(self.me, 2)
        self.c = lax.rem(self.me, 2)
        self.partner = 2 * self.x + 1 - self.c

    def chip_ahead(self, j):
        return lax.rem(self.x + 1 + j, self.nx)

    def chip_behind(self, j):
        return lax.rem(self.x - 1 - j + self.nx, self.nx)

    def slot(self, h):
        return lax.rem(h, 2) * self.nx + lax.div(h, 2)

    def all_peers(self):
        return [{"hid": lax.rem(self.me + 1 + i, self.n)} for i in range(self.n - 1)]

    def near_peers(self):
        near = [self.partner] + [2 * self.chip_ahead(j) + self.c for j in range(self.nx - 1)]
        return [{"hid": peer} for peer in near]


def remote(src, dst, send_sem, recv_sem, to):
    return pltpu.make_async_remote_copy(
        src_ref=src,
        dst_ref=dst,
        send_sem=send_sem,
        recv_sem=recv_sem,
        device_id=to if isinstance(to, dict) else {"hid": to},
        device_id_type=MESH,
    )


def gather_sems(seqs, nx):
    wide = pltpu.SemaphoreType.DMA((seqs, nx - 1))
    return [wide] * 4 + [pltpu.SemaphoreType.DMA((seqs,))] * 3


def reduce_sems(seqs, nx):
    wide = pltpu.SemaphoreType.DMA((seqs, nx - 1))
    return [wide] * 2 + [pltpu.SemaphoreType.DMA((seqs,))] * 2


class Gather:
    def __init__(self, group, sems, source, region):
        self.g, self.source, self.region = group, source, region
        self.xs, self.xr, self.rs, self.rr, self.ps, self.pr, self.os = sems

    def _own(self, s):
        return pltpu.make_async_copy(self.source(s), self.region(s, self.g.me), self.os.at[s])

    def _cross(self, s, j):
        to = 2 * self.g.chip_ahead(j) + self.g.c
        return remote(
            self.source(s), self.region(s, self.g.me), self.xs.at[s, j], self.xr.at[s, j], to
        )

    def _crossed(self, s, j):
        to = 2 * self.g.chip_ahead(j) + self.g.c
        block = self.region(s, 2 * self.g.chip_behind(j) + self.g.c)
        return remote(self.source(s), block, self.xs.at[s, j], self.xr.at[s, j], to)

    def _pair(self, s):
        return remote(
            self.source(s),
            self.region(s, self.g.me),
            self.ps.at[s],
            self.pr.at[s],
            self.g.partner,
        )

    def _paired(self, s):
        block = self.region(s, self.g.partner)
        return remote(self.source(s), block, self.ps.at[s], self.pr.at[s], self.g.partner)

    def _relay(self, s, j):
        block = self.region(s, 2 * self.g.chip_behind(j) + self.g.c)
        return remote(block, block, self.rs.at[s, j], self.rr.at[s, j], self.g.partner)

    def _relayed(self, s, j):
        block = self.region(s, 2 * self.g.chip_behind(j) + 1 - self.g.c)
        return remote(block, block, self.rs.at[s, j], self.rr.at[s, j], self.g.partner)

    def start(self, s):
        for j in range(self.g.nx - 1):
            self._cross(s, j).start()
        self._pair(s).start()
        self._own(s).start()

    def relay(self, s):
        for j in range(self.g.nx - 1):
            self._crossed(s, j).wait_recv()
            self._relay(s, j).start()

    def wait(self, s):
        self._own(s).wait()
        self._paired(s).wait_recv()
        for j in range(self.g.nx - 1):
            self._relayed(s, j).wait_recv()

    def drain(self, s):
        self._pair(s).wait_send()
        for j in range(self.g.nx - 1):
            self._cross(s, j).wait_send()
            self._relay(s, j).wait_send()


class Reduce:
    def __init__(self, group, sems, psend, precv, own, xsend, xrecv):
        self.g = group
        self.psend, self.precv, self.own, self.xsend, self.xrecv = psend, precv, own, xsend, xrecv
        self.xs, self.xr, self.ps, self.pr = sems

    def _pair(self, s):
        return remote(
            self.psend.at[s], self.precv.at[s], self.ps.at[s], self.pr.at[s], self.g.partner
        )

    def _cross(self, s, j):
        to = 2 * self.g.chip_ahead(j) + self.g.c
        return remote(
            self.xsend.at[s, j], self.xrecv.at[s, j], self.xs.at[s, j], self.xr.at[s, j], to
        )

    def start(self, s):
        self._pair(s).start()

    def cross(self, s):
        self._pair(s).wait()
        rows = self.own.shape[2]
        for j in range(self.g.nx - 1):
            chip = self.g.chip_ahead(j)

            def add(i, carry, chip=chip, j=j):
                at = pl.ds(pl.multiple_of(i * RB, RB), RB)
                total = self.own[s, chip, at, :] + self.precv[s, chip, at, :].astype(F32)
                self.xsend[s, j, at, :] = total.astype(BF)
                return carry

            lax.fori_loop(0, rows // RB, add, 0)
            self._cross(s, j).start()

    def arrive(self, s):
        for j in range(self.g.nx - 1):
            self._cross(s, j).wait()

    def total(self, s, at):
        total = self.own[s, self.g.x, at, :] + self.precv[s, self.g.x, at, :].astype(F32)
        for j in range(self.g.nx - 1):
            total = total + self.xrecv[s, j, at, :].astype(F32)
        return total


class Cycle:
    def __init__(self, size):
        self.size = size
        self.me = lax.axis_index("dp")
        self.length = size // 2
        line, column = lax.div(self.me, 2), lax.rem(self.me, 2)
        self.place = line + column * (size - 1 - 2 * line)

    def device(self, place):
        column = lax.div(place, self.length)
        line = place + column * (self.size - 1 - 2 * place)
        return 2 * line + column

    def beside(self, way):
        return self.device(lax.rem(self.place + way + self.size, self.size))


def split(shape, size):
    tall = max(16, shape[0] // (2 * size))
    across = 2 * size * tall // shape[0]
    return tall, shape[1] // across, across


def ring_scratch(shape, size):
    tall, broad, _ = split(shape, size)
    step = pltpu.SemaphoreType.DMA((size - 1,))
    return [
        pltpu.VMEM((size - 1, tall, broad), BF),
        pltpu.VMEM((2, tall, broad), F32),
        pltpu.SemaphoreType.DMA((2,)),
    ] + [step] * 4 + [pltpu.SemaphoreType.REGULAR]


class Ring:
    def __init__(self, cycle, data, target, way, scratch):
        self.cycle, self.data, self.target, self.way = cycle, data, target, way
        self.size = cycle.size
        self.recv, self.stage, self.stage_sem, self.ss, self.sr, self.gs, self.gr, self.free = scratch
        self.tall, self.broad, self.across = split(data.shape, self.size)
        self.to, self.frm = {"dp": cycle.beside(way)}, {"dp": cycle.beside(-way)}
        self.ticks = 2 * self.size - 1

    def block(self, number):
        place = lax.rem(self.cycle.place + self.way * number + 2 * self.size, self.size)
        index = 2 * place + (0 if self.way > 0 else 1)
        if self.across == 1:
            return pl.multiple_of(index * self.tall, self.tall), 0
        row = lax.div(index, self.across)
        column = lax.rem(index, self.across)
        return (
            pl.multiple_of(row * self.tall, self.tall),
            pl.multiple_of(column * self.broad, self.broad),
        )

    def view(self, number):
        row, column = self.block(number)
        return self.data.at[pl.ds(row, self.tall), pl.ds(column, self.broad)]

    def _add(self, t):
        return remote(self.view(-t), self.recv.at[t], self.ss.at[t], self.sr.at[t], self.to)

    def _pass(self, t):
        block = self.view(1 - t)
        return remote(block, block, self.gs.at[t], self.gr.at[t], self.to)

    def _passed(self, t):
        block = self.view(-t)
        return remote(block, block, self.gs.at[t], self.gr.at[t], self.to)

    def _sum(self, t):
        row, column = self.block(-t)

        def part(i, carry):
            at = pl.ds(pl.multiple_of(row + i * RB, RB), RB)
            cols = pl.ds(column, self.broad)
            arrived = self.recv[t - 1, pl.ds(pl.multiple_of(i * RB, RB), RB), :].astype(F32)
            self.data[at, cols] = (self.data[at, cols].astype(F32) + arrived).astype(BF)
            return carry

        lax.fori_loop(0, self.tall // RB, part, 0)

    def _out(self, number, slot):
        row, column = self.block(number)
        place = self.target.at[pl.ds(row, self.tall), pl.ds(column, self.broad)]
        return pltpu.make_async_copy(self.stage.at[slot], place, self.stage_sem.at[slot])

    def _put(self, number, count):
        slot = lax.rem(count, 2)

        @pl.when(count >= 2)
        def _():
            self._out(number, slot).wait()

        row, column = self.block(number)

        def part(i, carry):
            at = pl.ds(pl.multiple_of(row + i * RB, RB), RB)
            value = self.data[at, pl.ds(column, self.broad)].astype(F32)
            self.stage[slot, pl.ds(pl.multiple_of(i * RB, RB), RB), :] = value
            return carry

        lax.fori_loop(0, self.tall // RB, part, 0)
        self._out(number, slot).start()

    def tick(self, t):
        size = self.size

        @pl.when(t == 0)
        def _():
            self._add(0).start()

        @pl.when((t >= 1) & (t <= size - 1))
        def _():
            self._add(t - 1).wait_recv()
            self._sum(t)

        @pl.when((t >= 1) & (t < size - 1))
        def _():
            self._add(t).start()

        @pl.when((t >= 1) & (t <= size - 1))
        def _():
            self._add(t - 1).wait_send()
            pl.semaphore_signal(self.free, inc=1, device_id=self.frm, device_id_type=MESH)

        @pl.when(t == size - 1)
        def _():
            pl.semaphore_wait(self.free, 1)
            self._pass(0).start()
            self._put(1, 0)

        @pl.when((t > size - 1) & (t < 2 * size - 1))
        def _():
            u = t - size
            self._passed(u).wait_recv()

            @pl.when(t < 2 * size - 2)
            def _():
                pl.semaphore_wait(self.free, 1)
                self._pass(u + 1).start()

            self._put(-u, u + 1)

    def drain(self):
        for slot in range(2):
            self._out(0, slot).wait()

        def step(t, carry):
            self._pass(t).wait_send()
            return carry

        lax.fori_loop(0, self.size - 1, step, 0)


def meet(peers):
    barrier = pltpu.get_barrier_semaphore()
    for peer in peers:
        pl.semaphore_signal(barrier, inc=1, device_id=peer, device_id_type=MESH)
    pl.semaphore_wait(barrier, len(peers))


def mean_of(values):
    return jnp.sum(values, axis=1, keepdims=True) * (1.0 / D)


def attend_kernel(n, seqs, heads, *refs):
    (
        len_ref, tok_ref, change_ref, par_ref, wq_ref, wk_ref, wv_ref, qb_ref, vb_ref, wo_ref, gate_ref,
        full_o, qkv_o, prob_o, ctx_o, gat_o, nrm_o, pre_o, rstd_o, mid_o, par_o, change_o,
        full, wqkv, wo, qkv, prob, ctx, gat, own, psend, precv, xsend, xrecv,
        nrm, pre, rstd, mid, par, chg, score, in_sem, out_sem, vec_send, vec_recv, ch_send, ch_recv, *sems,
    ) = refs
    g = Group(n)
    width = heads * HD
    rows = SLOT // n
    gsems, rsems = sems[:7], sems[7:]
    cols = lambda h: pl.ds(pl.multiple_of(h * width, width), width)
    seq = lambda s: pl.ds(pl.multiple_of(s * SLOT, SLOT), SLOT)
    own_rows = lambda s: pl.ds(pl.multiple_of(s * rows, rows), rows)
    ga = Gather(g, gsems, lambda s: tok_ref.at[seq(s), :], lambda s, h: full.at[seq(s), cols(h)])
    re = Reduce(g, rsems, psend, precv, own, xsend, xrecv)

    def vec_to(i):
        to = lax.rem(g.me + 1 + i, n)
        return remote(par_ref, par.at[:, cols(g.me)], vec_send.at[i], vec_recv.at[i], to)

    def vec_from(i):
        to = lax.rem(g.me + 1 + i, n)
        frm = lax.rem(g.me - 1 - i + n, n)
        return remote(par_ref, par.at[:, cols(frm)], vec_send.at[i], vec_recv.at[i], to)

    def change_to(i):
        to = lax.rem(g.me + 1 + i, n)
        return remote(
            change_ref.at[:, g.slot(to)], chg.at[:, :, cols(g.me)], ch_send.at[i], ch_recv.at[i], to
        )

    def change_from(i):
        to = lax.rem(g.me + 1 + i, n)
        frm = lax.rem(g.me - 1 - i + n, n)
        return remote(
            change_ref.at[:, g.slot(to)], chg.at[:, :, cols(frm)], ch_send.at[i], ch_recv.at[i], to
        )

    loads = [
        pltpu.make_async_copy(wq_ref, wqkv.at[:, pl.ds(0, width)], in_sem.at[0]),
        pltpu.make_async_copy(wk_ref, wqkv.at[:, pl.ds(width, width)], in_sem.at[1]),
        pltpu.make_async_copy(wv_ref, wqkv.at[:, pl.ds(2 * width, width)], in_sem.at[2]),
        pltpu.make_async_copy(wo_ref, wo, in_sem.at[3]),
        pltpu.make_async_copy(par_ref, par.at[:, cols(g.me)], in_sem.at[4]),
        pltpu.make_async_copy(
            change_ref.at[:, g.slot(g.me)], chg.at[:, :, cols(g.me)], in_sem.at[5]
        ),
    ]
    chg_out = pltpu.make_async_copy(chg, change_o, in_sem.at[6])

    def sequence_outs(s):
        return [
            pltpu.make_async_copy(full.at[seq(s), :], full_o.at[seq(s), :], out_sem.at[s, 0]),
            pltpu.make_async_copy(qkv.at[seq(s), :], qkv_o.at[seq(s), :], out_sem.at[s, 1]),
            pltpu.make_async_copy(prob.at[s], prob_o.at[s], out_sem.at[s, 2]),
            pltpu.make_async_copy(ctx.at[seq(s), :], ctx_o.at[seq(s), :], out_sem.at[s, 3]),
            pltpu.make_async_copy(gat.at[seq(s), :], gat_o.at[seq(s), :], out_sem.at[s, 4]),
        ]

    def row_outs(s):
        return [
            pltpu.make_async_copy(nrm.at[own_rows(s), :], nrm_o.at[own_rows(s), :], out_sem.at[s, 5]),
            pltpu.make_async_copy(pre.at[own_rows(s), :], pre_o.at[own_rows(s), :], out_sem.at[s, 6]),
            pltpu.make_async_copy(rstd.at[own_rows(s), :], rstd_o.at[own_rows(s), :], out_sem.at[s, 7]),
            pltpu.make_async_copy(mid.at[own_rows(s), :], mid_o.at[own_rows(s), :], out_sem.at[s, 8]),
        ]

    meet(g.all_peers())

    def begin(s, carry):
        ga.start(s)
        return carry

    for i in range(n - 1):
        vec_to(i).start()
    lax.fori_loop(0, seqs, begin, 0)
    for load in loads:
        load.start()
    for i in range(n - 1):
        change_to(i).start()
    ga.relay(0)
    for load in loads[:5]:
        load.wait()
    for i in range(n - 1):
        vec_from(i).wait()
    par_o[...] = par[...]

    lanes = lax.broadcasted_iota(jnp.int32, (1, width), 1)
    head_lanes = [
        jnp.where((lanes >= h * HD) & (lanes < (h + 1) * HD), 1.0, 0.0).astype(BF) for h in range(heads)
    ]

    def finish(s):
        re.arrive(s)

        def block(i, carry):
            at = pl.ds(pl.multiple_of(i * RB, RB), RB)
            here = pl.ds(pl.multiple_of(s * rows + i * RB, RB), RB)
            token_row = pl.multiple_of(s * SLOT + g.slot(g.me) * rows + i * RB, RB)
            attention_pre = re.total(s, at) + par[0:1, :]
            residual = full[pl.ds(token_row, RB), :].astype(F32) + attention_pre * par[1:2, :]
            centered = residual - mean_of(residual)
            row_rstd = lax.rsqrt(mean_of(centered * centered) + EPS)
            normed = centered * row_rstd
            middle = normed * par[2:3, :] + par[3:4, :]
            nrm[here, :] = normed
            pre[here, :] = attention_pre
            rstd[here, :] = jnp.broadcast_to(row_rstd, (RB, 128))
            mid[here, :] = middle.astype(BF)
            return carry

        lax.fori_loop(0, rows // RB, block, 0)
        for copy in row_outs(s):
            copy.start()

    def sequence(s, carry):
        ga.wait(s)
        here = seq(s)
        projected = nn(full[here, :], wqkv[...])
        qkv[here, 0:width] = (projected[:, 0:width] + qb_ref[...]).astype(BF)
        qkv[here, width : 2 * width] = projected[:, width : 2 * width].astype(BF)
        qkv[here, 2 * width : 3 * width] = (projected[:, 2 * width : 3 * width] + vb_ref[...]).astype(BF)

        @pl.when(s + 1 < seqs)
        def _():
            ga.relay(s + 1)

        @pl.when(s > 0)
        def _():
            re.cross(s - 1)

        length = len_ref[s]
        for h in range(heads):
            score[...] = nt(qkv[here, 0:width] * head_lanes[h], qkv[here, width : 2 * width])

            def softmax(i, carry, h=h):
                at = pl.ds(pl.multiple_of(i * 64, 64), 64)
                places = lax.broadcasted_iota(jnp.int32, (64, SLOT), 1)
                scores = jnp.where(places < length, score[at, :] * (HD**-0.5), MASKED)
                exponent = jnp.exp(scores - jnp.max(scores, axis=1, keepdims=True))
                total = jnp.sum(exponent, axis=1, keepdims=True)
                prob[s, h, at, :] = (exponent * (1.0 / total)).astype(BF)
                return carry

            lax.fori_loop(0, SLOT // 64, softmax, 0)
            term = nn(prob[s, h], qkv[here, 2 * width : 3 * width] * head_lanes[h])
            ctx[here, :] = term if h == 0 else ctx[here, :] + term
        gat[here, :] = (ctx[here, :] * gate_ref[...]).astype(BF)
        for copy in sequence_outs(s):
            copy.start()
        half = SLOT // 2
        there = pl.ds(pl.multiple_of(s * SLOT + (1 - g.c) * half, half), half)
        psend[s] = nn(gat[there, :], wo[...]).astype(BF).reshape(n // 2, rows, D)
        re.start(s)
        mine = pl.ds(pl.multiple_of(s * SLOT + g.c * half, half), half)
        own[s] = nn(gat[mine, :], wo[...]).reshape(n // 2, rows, D)

        @pl.when(s > 0)
        def _():
            finish(s - 1)

        return carry

    lax.fori_loop(0, seqs, sequence, 0)
    re.cross(seqs - 1)
    loads[5].wait()
    for i in range(n - 1):
        change_from(i).wait()
    chg_out.start()
    finish(seqs - 1)
    chg_out.wait()

    def end(s, carry):
        ga.drain(s)
        for copy in sequence_outs(s) + row_outs(s):
            copy.wait()
        return carry

    lax.fori_loop(0, seqs, end, 0)


def feed_kernel(n, seqs, units, *refs):
    (
        len_ref, mid_ref, nrm_ref, pre_ref, rstd_ref, par, change_ref, w1_ref, b1_ref, w2_ref, ugate_ref,
        out_o, dlow_o, dres_o, dw1_o, dw2_o, rowsum_o, unitsum_o,
        midf, dffn, w1, w2, act, inner, slope, own, psend, precv, xsend, xrecv,
        nrm, pre, rstd, change, dtwo, dsend, fout, dlow, dres, wide, grad, sums, unit_sums,
        in_sem, out_sem, grad_sem, *sems,
    ) = refs
    g = Group(n)
    rows = SLOT // n
    half = SLOT // 2
    g1, r1, g2, r2 = sems[:7], sems[7:11], sems[11:18], sems[18:]
    seq = lambda s: pl.ds(pl.multiple_of(s * SLOT, SLOT), SLOT)
    own_rows = lambda s: pl.ds(pl.multiple_of(s * rows, rows), rows)
    spot = lambda s, h: pl.ds(pl.multiple_of(s * SLOT + g.slot(h) * rows, rows), rows)
    gm = Gather(g, g1, lambda s: mid_ref.at[own_rows(s), :], lambda s, h: midf.at[spot(s, h), :])
    gd = Gather(g, g2, lambda s: dsend.at[own_rows(s), :], lambda s, h: dffn.at[spot(s, h), :])
    rf = Reduce(g, r1, psend, precv, own, xsend, xrecv)
    rb = Reduce(g, r2, psend, precv, own, xsend, xrecv)
    loads = [
        pltpu.make_async_copy(w1_ref, w1, in_sem.at[0]),
        pltpu.make_async_copy(w2_ref, w2, in_sem.at[1]),
        pltpu.make_async_copy(nrm_ref, nrm, in_sem.at[2]),
        pltpu.make_async_copy(change_ref, change, in_sem.at[3]),
        pltpu.make_async_copy(pre_ref, pre, in_sem.at[4]),
        pltpu.make_async_copy(rstd_ref, rstd, in_sem.at[5]),
    ]

    meet(g.near_peers())

    def begin(s, carry):
        gm.start(s)
        return carry

    lax.fori_loop(0, seqs, begin, 0)
    for load in loads:
        load.start()
    sums[...] = jnp.zeros_like(sums)
    unit_sums[...] = jnp.zeros_like(unit_sums)
    gm.relay(0)
    for load in loads:
        load.wait()

    def finish_forward(s):
        rf.arrive(s)
        length = len_ref[s]

        def block(i, carry):
            at = pl.ds(pl.multiple_of(i * RB, RB), RB)
            here = pl.ds(pl.multiple_of(s * rows + i * RB, RB), RB)
            ffn_pre = rf.total(s, at) + par[4:5, :]
            middle = nrm[here, :] * par[2:3, :] + par[3:4, :]
            residual = middle + ffn_pre * par[1:2, :]
            centered = residual - mean_of(residual)
            row_rstd = lax.rsqrt(mean_of(centered * centered) + EPS)
            normed = centered * row_rstd
            final = normed * par[5:6, :] + par[6:7, :]
            fout[here, :] = final.astype(BF)
            place = g.slot(g.me) * rows + i * RB + lax.broadcasted_iota(jnp.int32, (RB, 1), 0)
            live = jnp.where(place < length, 1.0, 0.0)
            d_final = live * (change[here, :].astype(F32) + final)
            sums[0] += fold(d_final * normed)
            sums[1] += fold(d_final)
            d_normed = d_final * par[5:6, :]
            d_two = row_rstd * (d_normed - mean_of(d_normed) - normed * mean_of(d_normed * normed))
            sums[2] += fold(d_two * ffn_pre)
            d_ffn = d_two * par[1:2, :]
            sums[3] += fold(d_ffn)
            dtwo[here, :] = d_two
            dsend[here, :] = d_ffn.astype(BF)
            return carry

        lax.fori_loop(0, rows // RB, block, 0)
        gd.start(s)

    def forward(s, carry):
        gm.wait(s)
        here = seq(s)

        def part(b, carry):
            cols = pl.ds(pl.multiple_of(b * NB, NB), NB)
            wide[...] = nn(midf[here, :], w1[:, cols])
            bias = b1_ref[:, cols]
            gate = ugate_ref[:, cols]

            def block(i, carry):
                at = pl.ds(pl.multiple_of(i * 32, 32), 32)
                row = pl.ds(pl.multiple_of(s * SLOT + i * 32, 32), 32)
                v = wide[at, :] + bias
                phi = 0.5 * (1.0 + lax.erf(v * ROOT_HALF))
                activated = v * phi
                act[row, cols] = activated.astype(BF)
                inner[row, cols] = (activated * gate).astype(BF)
                steep = phi + v * jnp.exp(-0.5 * v * v) * (1.0 / ROOT_TWO_PI)
                slope[row, cols] = (gate * steep).astype(BF)
                return carry

            lax.fori_loop(0, SLOT // 32, block, 0)
            return carry

        lax.fori_loop(0, units // NB, part, 0)

        @pl.when(s + 1 < seqs)
        def _():
            gm.relay(s + 1)

        @pl.when(s > 0)
        def _():
            rf.cross(s - 1)

        there = pl.ds(pl.multiple_of(s * SLOT + (1 - g.c) * half, half), half)
        psend[s] = nn(inner[there, :], w2[...]).astype(BF).reshape(n // 2, rows, D)
        rf.start(s)
        mine = pl.ds(pl.multiple_of(s * SLOT + g.c * half, half), half)
        own[s] = nn(inner[mine, :], w2[...]).reshape(n // 2, rows, D)

        @pl.when(s > 1)
        def _():
            finish_forward(s - 2)

        return carry

    lax.fori_loop(0, seqs, forward, 0)
    rf.cross(seqs - 1)
    gd.relay(0)

    def row_outs(s):
        return [
            pltpu.make_async_copy(fout.at[own_rows(s), :], out_o.at[own_rows(s), :], out_sem.at[s, 0]),
            pltpu.make_async_copy(dlow.at[own_rows(s), :], dlow_o.at[own_rows(s), :], out_sem.at[s, 1]),
            pltpu.make_async_copy(dres.at[own_rows(s), :], dres_o.at[own_rows(s), :], out_sem.at[s, 2]),
        ]

    def finish_backward(s):
        rb.arrive(s)

        def block(i, carry):
            at = pl.ds(pl.multiple_of(i * RB, RB), RB)
            here = pl.ds(pl.multiple_of(s * rows + i * RB, RB), RB)
            normed = nrm[here, :]
            d_middle = dtwo[here, :] + rb.total(s, at)
            sums[4] += fold(d_middle * normed)
            sums[5] += fold(d_middle)
            d_normed = d_middle * par[2:3, :]
            d_one = rstd[here, 0:1] * (
                d_normed - mean_of(d_normed) - normed * mean_of(d_normed * normed)
            )
            sums[2] += fold(d_one * pre[here, :])
            d_attn = d_one * par[1:2, :]
            sums[6] += fold(d_attn)
            dres[here, :] = d_one
            dlow[here, :] = d_attn.astype(BF)
            return carry

        lax.fori_loop(0, rows // RB, block, 0)
        for copy in row_outs(s):
            copy.start()

    def backward(s, carry):
        gd.wait(s)
        here = seq(s)

        def part(b, carry):
            cols = pl.ds(pl.multiple_of(b * NB, NB), NB)
            wide[...] = nt(dffn[here, :], w2[cols, :])

            def block(i, sums_here):
                unit_part, bias_part = sums_here
                at = pl.ds(pl.multiple_of(i * 32, 32), 32)
                row = pl.ds(pl.multiple_of(s * SLOT + i * 32, 32), 32)
                d_inner = wide[at, :]
                d_pre = (d_inner * slope[row, cols].astype(F32)).astype(BF)
                unit_part = unit_part + fold(d_inner * act[row, cols].astype(F32))
                bias_part = bias_part + fold(d_pre.astype(F32))
                slope[row, cols] = d_pre
                return (unit_part, bias_part)

            zero = jnp.zeros((8, NB), F32)
            unit_part, bias_part = lax.fori_loop(0, SLOT // 32, block, (zero, zero))
            unit_sums[0, :, cols] += unit_part
            unit_sums[1, :, cols] += bias_part
            return carry

        lax.fori_loop(0, units // NB, part, 0)

        @pl.when(s < 2)
        def _():
            finish_forward(seqs - 2 + s)

        @pl.when(s + 1 < seqs)
        def _():
            gd.relay(s + 1)

        @pl.when(s > 0)
        def _():
            rb.cross(s - 1)

        there = pl.ds(pl.multiple_of(s * SLOT + (1 - g.c) * half, half), half)
        psend[s] = nt(slope[there, :], w1[...]).astype(BF).reshape(n // 2, rows, D)
        rb.start(s)
        mine = pl.ds(pl.multiple_of(s * SLOT + g.c * half, half), half)
        own[s] = nt(slope[mine, :], w1[...]).reshape(n // 2, rows, D)

        @pl.when(s > 1)
        def _():
            finish_backward(s - 2)

        return carry

    lax.fori_loop(0, seqs, backward, 0)
    rb.cross(seqs - 1)

    def grad_out(k, b):
        target = (dw2_o, dw1_o)[k]
        at = pl.ds(pl.multiple_of(b * NB, NB), NB)
        return pltpu.make_async_copy(grad.at[b], target.at[at, :], grad_sem.at[k, b])

    def down_grad(b, carry):
        cols = pl.ds(pl.multiple_of(b * NB, NB), NB)
        grad[b] = tn(inner[:, cols], dffn[...]).astype(BF)
        grad_out(0, b).start()
        return carry

    lax.fori_loop(0, units // NB, down_grad, 0)
    finish_backward(seqs - 2)
    for b in range(units // NB):
        grad_out(0, b).wait()

    def inner_grad(b, carry):
        cols = pl.ds(pl.multiple_of(b * NB, NB), NB)
        grad[b, :, 0:units] = tn(midf[:, cols], slope[...]).astype(BF)
        pltpu.make_async_copy(
            grad.at[b, :, pl.ds(0, units)], dw1_o.at[cols, :], grad_sem.at[1, b]
        ).start()
        return carry

    lax.fori_loop(0, D // NB, inner_grad, 0)
    finish_backward(seqs - 1)
    for k in range(7):
        rowsum_o[k : k + 1, :] = jnp.sum(sums[k], axis=0, keepdims=True)
    rowsum_o[7:8, :] = jnp.zeros((1, D), F32)
    for k in range(2):
        unitsum_o[k : k + 1, :] = jnp.sum(unit_sums[k], axis=0, keepdims=True)
    for b in range(D // NB):
        at = pl.ds(b * NB, NB)
        pltpu.make_async_copy(
            grad.at[b, :, pl.ds(0, units)], dw1_o.at[at, :], grad_sem.at[1, b]
        ).wait()

    def end(s, carry):
        gm.drain(s)
        gd.drain(s)
        for copy in row_outs(s):
            copy.wait()
        return carry

    lax.fori_loop(0, seqs, end, 0)


def attend_back_kernel(n, seqs, heads, size, *refs):
    (
        dlow_ref, dres_ref, full_ref, qkv_ref, prob_ref, ctx_ref, gat_ref,
        wq_ref, wk_ref, wv_ref, wo_ref, dw1_ref, dw2_ref, out_ref, gate_ref,
        tgrad_o, dwqkv_o, dwo_o, dw1_o, dw2_o, output_o, sums_o,
        dattn, dres, full, qkv, prob, ctx, gat, wqkv, wo, dctx, dqkv, dprob, dscore, acc,
        block_f, own, psend, precv, xsend, xrecv, tgrad, grad, gwo, moved, sums, dw1, dw2,
        in_sem, out_sem, grad_sem, move_send, move_recv, *sems,
    ) = refs
    g = Group(n)
    cycle = Cycle(size)
    rings = []
    for k, (data, target) in enumerate(((dw1, dw1_o), (dw2, dw2_o))):
        for way in (1, -1):
            i = 11 + 8 * len(rings)
            rings.append(Ring(cycle, data, target, way, sems[i : i + 8]))
    ticks = rings[0].ticks

    def tick(t, which):
        for ring in rings[2 * which : 2 * which + 2]:
            ring.tick(t)

    def move_to(i):
        to = lax.rem(g.me + 1 + i, n)
        return remote(
            out_ref.at[:, :, cols_of(to)], moved.at[:, g.slot(g.me)], move_send.at[i], move_recv.at[i], to
        )

    def move_from(i):
        to = lax.rem(g.me + 1 + i, n)
        frm = lax.rem(g.me - 1 - i + n, n)
        return remote(
            out_ref.at[:, :, cols_of(to)], moved.at[:, g.slot(frm)], move_send.at[i], move_recv.at[i], to
        )

    width = heads * HD
    rows = SLOT // n
    gsems, rsems = sems[:7], sems[7:11]
    cols_of = lambda h: pl.ds(pl.multiple_of(h * width, width), width)
    seq = lambda s: pl.ds(pl.multiple_of(s * SLOT, SLOT), SLOT)
    own_rows = lambda s: pl.ds(pl.multiple_of(s * rows, rows), rows)
    spot = lambda s, h: pl.ds(pl.multiple_of(s * SLOT + g.slot(h) * rows, rows), rows)
    ga = Gather(g, gsems, lambda s: dlow_ref.at[own_rows(s), :], lambda s, h: dattn.at[spot(s, h), :])
    re = Reduce(g, rsems, psend, precv, own, xsend, xrecv)
    loads = [
        pltpu.make_async_copy(wo_ref, wo, in_sem.at[0]),
        pltpu.make_async_copy(ctx_ref, ctx, in_sem.at[1]),
        pltpu.make_async_copy(qkv_ref, qkv, in_sem.at[2]),
        pltpu.make_async_copy(prob_ref, prob, in_sem.at[3]),
        pltpu.make_async_copy(wq_ref, wqkv.at[:, pl.ds(0, width)], in_sem.at[4]),
        pltpu.make_async_copy(wk_ref, wqkv.at[:, pl.ds(width, width)], in_sem.at[5]),
        pltpu.make_async_copy(wv_ref, wqkv.at[:, pl.ds(2 * width, width)], in_sem.at[6]),
        pltpu.make_async_copy(dres_ref, dres, in_sem.at[7]),
        pltpu.make_async_copy(full_ref, full, in_sem.at[8]),
        pltpu.make_async_copy(gat_ref, gat, in_sem.at[9]),
        pltpu.make_async_copy(
            out_ref.at[:, :, cols_of(g.me)], moved.at[:, g.slot(g.me)], in_sem.at[11]
        ),
    ]
    grads_in = [
        pltpu.make_async_copy(dw1_ref, dw1, in_sem.at[12]),
        pltpu.make_async_copy(dw2_ref, dw2, in_sem.at[13]),
    ]
    meet(g.all_peers() + [{"dp": cycle.beside(1)}, {"dp": cycle.beside(-1)}])
    for load in grads_in:
        load.start()

    def begin(s, carry):
        ga.start(s)
        return carry

    lax.fori_loop(0, seqs, begin, 0)
    for load in loads:
        load.start()
    sums[...] = jnp.zeros_like(sums)
    for load in grads_in:
        load.wait()
    tick(0, 0)
    tick(0, 1)
    ga.relay(0)
    for load in loads[:8]:
        load.wait()
    tick(1, 0)
    tick(1, 1)

    lanes = lax.broadcasted_iota(jnp.int32, (1, width), 1)
    head_lanes = [
        jnp.where((lanes >= h * HD) & (lanes < (h + 1) * HD), 1.0, 0.0).astype(BF) for h in range(heads)
    ]

    def out(s):
        return pltpu.make_async_copy(tgrad.at[seq(s), :], tgrad_o.at[seq(s), :], out_sem.at[s])

    def finish(s):
        re.arrive(s)

        def block(i, carry):
            at = pl.ds(pl.multiple_of(i * 32, 32), 32)
            tgrad[pl.ds(pl.multiple_of(s * SLOT + i * 32, 32), 32), :] = re.total(s, at)
            return carry

        lax.fori_loop(0, SLOT // 32, block, 0)
        out(s).start()

    def token_block(s, h):
        cols = pl.ds(pl.multiple_of(h * width, width), width)
        block_f[...] = nt(dqkv[seq(s), :], wqkv[cols, :])
        mine = pl.ds(pl.multiple_of(g.slot(g.me) * rows, rows), rows)
        block_f[mine, :] += dres[own_rows(s), cols]

    def sequence(s, carry):
        ga.wait(s)
        here = seq(s)
        d_gated = nt(dattn[here, :], wo[...])
        sums[0] += fold(d_gated * ctx[here, :])
        dctx[...] = (d_gated * gate_ref[...]).astype(BF)
        first = 2 + s * (heads + 2) // 2
        tick(first, 0)

        @pl.when(s + 1 < seqs)
        def _():
            ga.relay(s + 1)

        @pl.when(s > 0)
        def _():
            re.cross(s - 1)

        for h in range(heads):
            d_context = dctx[...] * head_lanes[h]
            dprob[...] = nt(d_context, qkv[here, 2 * width : 3 * width])

            def softmax(i, carry, h=h):
                at = pl.ds(pl.multiple_of(i * 64, 64), 64)
                p = prob[s, h, at, :].astype(F32)
                weighted = p * dprob[at, :]
                total = jnp.sum(weighted, axis=1, keepdims=True)
                dscore[at, :] = (weighted - p * total).astype(BF)
                return carry

            lax.fori_loop(0, SLOT // 64, softmax, 0)
            tick(first + (h + 1) // 2, (h + 1) % 2)
            terms = (
                nn(dscore[...], qkv[here, width : 2 * width] * head_lanes[h]),
                tn(dscore[...], qkv[here, 0:width] * head_lanes[h]),
                tn(prob[s, h], d_context),
            )
            for k in range(3):
                acc[k] = terms[k] if h == 0 else acc[k] + terms[k]
        scales = (HD**-0.5, HD**-0.5, 1.0)
        for k in range(3):
            rounded = (acc[k] * scales[k]).astype(BF)
            dqkv[here, k * width : (k + 1) * width] = rounded
            sums[1 + k] += fold(rounded.astype(F32))
        for chip in range(n // 2):
            token_block(s, 2 * chip + 1 - g.c)
            psend[s, chip] = block_f[...].astype(BF)
        re.start(s)
        tick(first + (heads + 1) // 2, 1)
        for chip in range(n // 2):
            token_block(s, 2 * chip + g.c)
            own[s, chip] = block_f[...]

        @pl.when(s > 0)
        def _():
            finish(s - 1)

        return carry

    lax.fori_loop(0, seqs, sequence, 0)
    re.cross(seqs - 1)
    for i in range(n - 1):
        move_to(i).start()
    for load in loads[8:]:
        load.wait()

    def grad_out(b):
        at = pl.ds(pl.multiple_of(b * NB, NB), NB)
        return pltpu.make_async_copy(grad.at[b], dwqkv_o.at[at, :], grad_sem.at[b])

    def token_grad(b, carry):
        cols = pl.ds(pl.multiple_of(b * NB, NB), NB)
        grad[b] = tn(full[:, cols], dqkv[...]).astype(BF)
        grad_out(b).start()
        return carry

    lax.fori_loop(0, D // NB, token_grad, 0)
    gwo[...] = tn(gat[...], dattn[...]).astype(BF)
    gwo_out = pltpu.make_async_copy(gwo, dwo_o, in_sem.at[10])
    gwo_out.start()
    finish(seqs - 1)
    for i in range(n - 1):
        move_from(i).wait()
    moved_out = pltpu.make_async_copy(moved, output_o, in_sem.at[14])
    moved_out.start()
    for k in range(4):
        sums_o[k : k + 1, :] = jnp.sum(sums[k], axis=0, keepdims=True)
    sums_o[4:8, :] = jnp.zeros((4, width), F32)
    gwo_out.wait()

    def rest(t, carry):
        tick(t, 0)
        tick(t, 1)
        return carry

    lax.fori_loop(2 + seqs * (heads + 2) // 2, ticks, rest, 0)
    moved_out.wait()
    for ring in rings:
        ring.drain()

    def end_grad(b, carry):
        grad_out(b).wait()
        return carry

    lax.fori_loop(0, D // NB, end_grad, 0)

    def end(s, carry):
        ga.drain(s)
        out(s).wait()
        return carry

    lax.fori_loop(0, seqs, end, 0)


def settle_kernel(n, size, seqs, *refs):
    (
        len_ref, dwqkv_ref, dwo_ref, output_ref, teacher_ref, row_ref, unit_ref, head_ref,
        dwq_o, dwk_o, dwv_o, dwo_o, small_o, units_o,
        dwq, dwk, dwv, dwo, output, teacher, parts, small, rbuf, sbuf, ubuf,
        in_sem, r_send, r_recv, s_send, s_recv, u_send, u_recv, *sems,
    ) = refs
    g = Group(n)
    cycle = Cycle(size)
    width = head_ref.shape[1]
    cols = lambda h: pl.ds(pl.multiple_of(h * width, width), width)
    rings = []
    for data, target in ((dwq, dwq_o), (dwk, dwk_o), (dwv, dwv_o), (dwo, dwo_o)):
        for way in (1, -1):
            i = 8 * len(rings)
            rings.append(Ring(cycle, data, target, way, sems[i : i + 8]))

    def tick(t):
        for ring in rings:
            ring.tick(t)

    def row_to(i):
        to = lax.rem(g.me + 1 + i, n)
        return remote(parts.at[:, cols(to)], rbuf.at[i], r_send.at[i], r_recv.at[i], to)

    def small_to(i):
        to = {"dp": lax.rem(cycle.me + 1 + i, size)}
        return remote(small, sbuf.at[i], s_send.at[i], s_recv.at[i], to)

    def units_to(i):
        to = {"dp": lax.rem(cycle.me + 1 + i, size)}
        return remote(unit_ref, ubuf.at[i], u_send.at[i], u_recv.at[i], to)

    loads = [
        pltpu.make_async_copy(dwqkv_ref.at[:, pl.ds(0, width)], dwq, in_sem.at[0]),
        pltpu.make_async_copy(dwqkv_ref.at[:, pl.ds(width, width)], dwk, in_sem.at[1]),
        pltpu.make_async_copy(dwqkv_ref.at[:, pl.ds(2 * width, width)], dwv, in_sem.at[2]),
        pltpu.make_async_copy(dwo_ref, dwo, in_sem.at[3]),
        pltpu.make_async_copy(output_ref, output, in_sem.at[4]),
        pltpu.make_async_copy(teacher_ref, teacher, in_sem.at[5]),
    ]
    for load in loads:
        load.start()
    meet(g.all_peers() + [{"dp": lax.rem(cycle.me + 1 + i, size)} for i in range(size - 1)])
    for load in loads[:4]:
        load.wait()
    tick(0)
    for load in loads[4:]:
        load.wait()
    for i in range(size - 1):
        units_to(i).start()

    def sequence(s, total):
        length = len_ref[s]

        def block(i, total):
            at = pl.ds(pl.multiple_of(s * SLOT + i * 32, 32), 32)
            place = i * 32 + lax.broadcasted_iota(jnp.int32, (32, 1), 0)
            differ = output[at, :].astype(F32) - teacher[at, :].astype(F32)
            return total + fold(jnp.where(place < length, differ * differ, 0.0))

        return lax.fori_loop(0, SLOT // 32, block, total)

    squares = lax.fori_loop(0, seqs, sequence, jnp.zeros((8, width), F32))
    parts[...] = row_ref[...]
    for h in range(n):
        parts[7:8, h * width : (h + 1) * width] = jnp.sum(squares, axis=0, keepdims=True)
    for i in range(n - 1):
        row_to(i).start()
    tick(1)
    total = parts[:, cols(g.me)]
    for i in range(n - 1):
        row_to(i).wait()
        total = total + rbuf[i]
    small[:, 0:width] = total
    small[:, width : 2 * width] = head_ref[...]
    for i in range(size - 1):
        small_to(i).start()

    def rest(t, carry):
        tick(t)
        return carry

    lax.fori_loop(2, rings[0].ticks, rest, 0)
    small_sum = small[...]
    unit_sum = unit_ref[...]
    for i in range(size - 1):
        small_to(i).wait()
        units_to(i).wait()
        small_sum = small_sum + sbuf[i]
        unit_sum = unit_sum + ubuf[i]
    small_o[...] = small_sum
    units_o[...] = unit_sum
    for ring in rings:
        ring.drain()


def hbm():
    return pl.BlockSpec(memory_space=pl.ANY)


def vmem():
    return pl.BlockSpec(memory_space=pltpu.VMEM)


def smem():
    return pl.BlockSpec(memory_space=pltpu.SMEM)


def call(kernel, name, ident, ins, outs, scratch, flops):
    return pl.pallas_call(
        kernel,
        name=name,
        out_shape=[jax.ShapeDtypeStruct(shape, dtype) for shape, dtype, _ in outs],
        in_specs=ins,
        out_specs=[spec for _, _, spec in outs],
        scratch_shapes=scratch,
        compiler_params=pltpu.CompilerParams(
            collective_id=ident, has_side_effects=True, vmem_limit_bytes=VMEM_LIMIT
        ),
        cost_estimate=pl.CostEstimate(flops=flops, bytes_accessed=30_000_000, transcendentals=0),
    )


def attend(n, seqs, heads, args):
    width, rows, nx, half = heads * HD, SLOT // n, n // 2, SLOT // 2
    tokens, owned = seqs * SLOT, seqs * rows
    v, dma = pltpu.VMEM, pltpu.SemaphoreType.DMA
    return call(
        functools.partial(attend_kernel, n, seqs, heads),
        "attend",
        0,
        [smem(), hbm(), hbm(), vmem(), hbm(), hbm(), hbm(), vmem(), vmem(), hbm(), vmem()],
        [
            ((tokens, D), BF, hbm()),
            ((tokens, 3 * width), BF, hbm()),
            ((seqs, heads, SLOT, SLOT), BF, hbm()),
            ((tokens, width), F32, hbm()),
            ((tokens, width), BF, hbm()),
            ((owned, D), F32, hbm()),
            ((owned, D), F32, hbm()),
            ((owned, 128), F32, hbm()),
            ((owned, D), BF, hbm()),
            ((8, D), F32, vmem()),
            ((seqs, rows, D), BF, hbm()),
        ],
        [
            v((tokens, D), BF),
            v((D, 3 * width), BF),
            v((width, D), BF),
            v((tokens, 3 * width), BF),
            v((seqs, heads, SLOT, SLOT), BF),
            v((tokens, width), F32),
            v((tokens, width), BF),
            v((seqs, nx, rows, D), F32),
            v((seqs, nx, rows, D), BF),
            v((seqs, nx, rows, D), BF),
            v((seqs, nx - 1, rows, D), BF),
            v((seqs, nx - 1, rows, D), BF),
            v((owned, D), F32),
            v((owned, D), F32),
            v((owned, 128), F32),
            v((owned, D), BF),
            v((8, D), F32),
            v((seqs, rows, D), BF),
            v((SLOT, SLOT), F32),
            dma((7,)),
            dma((seqs, 9)),
            dma((n - 1,)),
            dma((n - 1,)),
            dma((n - 1,)),
            dma((n - 1,)),
        ]
        + gather_sems(seqs, nx)
        + reduce_sems(seqs, nx),
        10_000_000_000,
    )(*args)


def feed(n, seqs, units, args):
    rows, nx = SLOT // n, n // 2
    tokens, owned = seqs * SLOT, seqs * rows
    v, dma = pltpu.VMEM, pltpu.SemaphoreType.DMA
    return call(
        functools.partial(feed_kernel, n, seqs, units),
        "feed",
        1,
        [smem(), hbm(), hbm(), hbm(), hbm(), vmem(), hbm(), hbm(), vmem(), hbm(), vmem()],
        [
            ((owned, D), BF, hbm()),
            ((owned, D), BF, hbm()),
            ((owned, D), F32, hbm()),
            ((D, units), BF, hbm()),
            ((units, D), BF, hbm()),
            ((8, D), F32, vmem()),
            ((2, units), F32, vmem()),
        ],
        [
            v((tokens, D), BF),
            v((tokens, D), BF),
            v((D, units), BF),
            v((units, D), BF),
            v((tokens, units), BF),
            v((tokens, units), BF),
            v((tokens, units), BF),
            v((seqs, nx, rows, D), F32),
            v((seqs, nx, rows, D), BF),
            v((seqs, nx, rows, D), BF),
            v((seqs, nx - 1, rows, D), BF),
            v((seqs, nx - 1, rows, D), BF),
            v((owned, D), F32),
            v((owned, D), F32),
            v((owned, 128), F32),
            v((owned, D), BF),
            v((owned, D), F32),
            v((owned, D), BF),
            v((owned, D), BF),
            v((owned, D), BF),
            v((owned, D), F32),
            v((SLOT, NB), F32),
            v((D // NB, NB, D), BF),
            v((7, 8, D), F32),
            v((2, 8, units), F32),
            dma((6,)),
            dma((seqs, 3)),
            dma((2, D // NB)),
        ]
        + (gather_sems(seqs, nx) + reduce_sems(seqs, nx)) * 2,
        30_000_000_000,
    )(*args)


def attend_back(n, seqs, heads, units, size, args):
    width, rows, nx = heads * HD, SLOT // n, n // 2
    tokens, owned = seqs * SLOT, seqs * rows
    v, dma = pltpu.VMEM, pltpu.SemaphoreType.DMA
    return call(
        functools.partial(attend_back_kernel, n, seqs, heads, size),
        "attend_back",
        2,
        [hbm()] * 14 + [vmem()],
        [
            ((tokens, width), F32, hbm()),
            ((D, 3 * width), BF, hbm()),
            ((width, D), BF, hbm()),
            ((D, units), F32, hbm()),
            ((units, D), F32, hbm()),
            ((seqs, n, rows, width), BF, hbm()),
            ((8, width), F32, vmem()),
        ],
        [
            v((tokens, D), BF),
            v((owned, D), F32),
            v((tokens, D), BF),
            v((tokens, 3 * width), BF),
            v((seqs, heads, SLOT, SLOT), BF),
            v((tokens, width), F32),
            v((tokens, width), BF),
            v((D, 3 * width), BF),
            v((width, D), BF),
            v((SLOT, width), BF),
            v((tokens, 3 * width), BF),
            v((SLOT, SLOT), F32),
            v((SLOT, SLOT), BF),
            v((3, SLOT, width), F32),
            v((SLOT, width), F32),
            v((seqs, nx, SLOT, width), F32),
            v((seqs, nx, SLOT, width), BF),
            v((seqs, nx, SLOT, width), BF),
            v((seqs, nx - 1, SLOT, width), BF),
            v((seqs, nx - 1, SLOT, width), BF),
            v((tokens, width), F32),
            v((D // NB, NB, 3 * width), BF),
            v((width, D), BF),
            v((seqs, n, rows, width), BF),
            v((4, 8, width), F32),
            v((D, units), BF),
            v((units, D), BF),
            dma((15,)),
            dma((seqs,)),
            dma((D // NB,)),
            dma((n - 1,)),
            dma((n - 1,)),
        ]
        + gather_sems(seqs, nx)
        + reduce_sems(seqs, nx)
        + ring_scratch((D, units), size) * 2
        + ring_scratch((units, D), size) * 2,
        20_000_000_000,
    )(*args)


def settle(n, size, seqs, width, units, args):
    v, dma = pltpu.VMEM, pltpu.SemaphoreType.DMA
    tokens = seqs * SLOT
    return call(
        functools.partial(settle_kernel, n, size, seqs),
        "settle",
        3,
        [smem()] + [hbm()] * 4 + [vmem()] * 3,
        [((D, width), F32, hbm())] * 3
        + [((width, D), F32, hbm()), ((8, 2 * width), F32, vmem()), ((2, units), F32, vmem())],
        [
            v((D, width), BF),
            v((D, width), BF),
            v((D, width), BF),
            v((width, D), BF),
            v((tokens, width), BF),
            v((tokens, width), BF),
            v((8, D), F32),
            v((8, 2 * width), F32),
            v((n - 1, 8, width), F32),
            v((size - 1, 8, 2 * width), F32),
            v((size - 1, 2, units), F32),
            dma((6,)),
            dma((n - 1,)),
            dma((n - 1,)),
        ]
        + [dma((size - 1,))] * 4
        + ring_scratch((D, width), size) * 6
        + ring_scratch((width, D), size) * 2,
        1_000_000_000,
    )(*args)


def on_device(
    n,
    size,
    tokens,
    query_weight,
    query_bias,
    key_weight,
    value_weight,
    value_bias,
    output_weight,
    output_bias,
    attention_gain,
    attention_shift,
    inner_weight,
    inner_bias,
    down_weight,
    down_bias,
    final_gain,
    final_shift,
    head_alpha,
    unit_alpha,
    width_alpha,
    multipliers,
    head_noise,
    unit_noise,
    width_noise,
    lengths,
    teacher,
    upstream,
):
    row_count, width = tokens.shape
    heads = width // HD
    units = inner_weight.shape[1]
    seqs = row_count // SLOT
    rows = SLOT // n
    rank = lax.axis_index("hid")
    local_lengths = lax.dynamic_slice_in_dim(lengths, lax.axis_index("dp") * seqs, seqs)
    head_local = lax.dynamic_slice_in_dim(head_alpha, rank * heads, heads)
    unit_local = lax.dynamic_slice_in_dim(unit_alpha, rank * units, units)
    width_local = lax.dynamic_slice_in_dim(width_alpha, rank * width, width)
    head_gate, head_pull = jax.vjp(lambda part: gate_value(head_noise, part), head_local)
    unit_gate, unit_pull = jax.vjp(lambda part: gate_value(unit_noise, part), unit_local)
    width_gate, width_pull = jax.vjp(lambda part: gate_value(width_noise, part), width_local)
    gate_row = jnp.repeat(head_gate, HD)[None, :]
    vectors = jnp.stack(
        [
            output_bias,
            width_gate,
            attention_gain,
            attention_shift,
            down_bias,
            final_gain,
            final_shift,
            jnp.zeros_like(down_bias),
        ]
    )
    change = (upstream.astype(F32) - teacher.astype(F32)).astype(BF).reshape(seqs, n, rows, width)
    full, qkv, prob, ctx, gat, nrm, pre, rstd, mid, par, change_rows = attend(
        n,
        seqs,
        heads,
        (
            local_lengths,
            tokens,
            change,
            vectors,
            query_weight,
            key_weight,
            value_weight,
            query_bias[None, :],
            value_bias[None, :],
            output_weight,
            gate_row,
        ),
    )
    out_rows, d_low, d_res, dw_inner, dw_down, row_sums, unit_sums = feed(
        n,
        seqs,
        units,
        (
            local_lengths,
            mid,
            nrm,
            pre,
            rstd,
            par,
            change_rows.reshape(seqs * rows, D),
            inner_weight,
            inner_bias[None, :],
            down_weight,
            unit_gate[None, :],
        ),
    )
    tokens_grad, dw_qkv, dw_o, dw_inner, dw_down, output, head_sums = attend_back(
        n,
        seqs,
        heads,
        units,
        size,
        (
            d_low,
            d_res,
            full,
            qkv,
            prob,
            ctx,
            gat,
            query_weight,
            key_weight,
            value_weight,
            output_weight,
            dw_inner,
            dw_down,
            out_rows.reshape(seqs, rows, D),
            gate_row,
        ),
    )
    output = output.reshape(row_count, width)
    dw_q, dw_k, dw_v, dw_o, small, unit_all = settle(
        n,
        size,
        seqs,
        width,
        units,
        (local_lengths, dw_qkv, dw_o, output, teacher, row_sums, unit_sums, head_sums),
    )
    rows_all, head_all = small[:, :width], small[:, width:]
    distill_mse = jnp.sum(rows_all[7]) / (jnp.sum(lengths).astype(F32) * D)
    lag = jax.grad(lagrangian, argnums=(0, 1, 2, 3))(head_alpha, unit_alpha, width_alpha, multipliers)
    head_alpha_grad = head_pull(jnp.sum(head_all[0].reshape(heads, HD), axis=1))[0]
    head_alpha_grad += lax.dynamic_slice_in_dim(lag[0], rank * heads, heads)
    unit_alpha_grad = unit_pull(unit_all[0])[0]
    unit_alpha_grad += lax.dynamic_slice_in_dim(lag[1], rank * units, units)
    width_alpha_grad = width_pull(rows_all[2])[0]
    width_alpha_grad += lax.dynamic_slice_in_dim(lag[2], rank * width, width)
    return (
        output,
        tokens_grad,
        dw_q,
        head_all[1],
        dw_k,
        dw_v,
        head_all[3],
        dw_o,
        rows_all[6],
        rows_all[4],
        rows_all[5],
        dw_inner,
        unit_all[1],
        dw_down,
        rows_all[3],
        rows_all[0],
        rows_all[1],
        head_alpha_grad,
        unit_alpha_grad,
        width_alpha_grad,
        distill_mse,
        multipliers + ASCENT * lag[3],
    )


def solution(mesh):
    tall, wide, vec, rep = P("dp", "hid"), P(None, "hid"), P("hid"), P()
    deep = P("hid", None)
    return jax.shard_map(
        functools.partial(on_device, mesh.shape["hid"], mesh.shape["dp"]),
        mesh=mesh,
        in_specs=(tall, wide, vec, wide, wide, vec, deep, vec, vec, vec, wide, vec, deep)
        + (vec,) * 3
        + (rep,) * 4
        + (vec,) * 3
        + (rep, tall, tall),
        out_specs=(tall, tall, wide, vec, wide, wide, vec, deep, vec, vec, vec, wide, vec, deep)
        + (vec,) * 6
        + (rep, rep),
        check_vma=False,
    )
```

```python
import functools
import math

import jax
import jax.numpy as jnp
from jax import lax
from jax.experimental import pallas as pl
from jax.experimental.pallas import tpu as pltpu
from jax.sharding import PartitionSpec as P

D = 1024
HD = 64
FF = 4096
SLOT = 512

BETA = 2.0 / 3.0
GAMMA = -0.1
ZETA = 1.1
TARGET = 0.7
ASCENT = 1.0
EPS = 1e-12
MASKED = -1000000000.0
ROOT_HALF = 0.7071067811865476
ROOT_TWO_PI = 2.5066282746310002

MESH = pl.DeviceIdType.MESH
VMEM_LIMIT = 66_000_000
BF = jnp.bfloat16
F32 = jnp.float32
NB = 256
RB = 16


def gate_value(noise, alpha):
    logits = (jnp.log(noise) - jnp.log(1.0 - noise) + alpha) / BETA
    stretched = jax.nn.sigmoid(logits) * (ZETA - GAMMA) + GAMMA
    return jnp.clip(stretched, 0.0, 1.0)


def gate_slope(noise, alpha):
    s = jax.nn.sigmoid((jnp.log(noise) - jnp.log(1.0 - noise) + alpha) / BETA)
    stretched = s * (ZETA - GAMMA) + GAMMA
    free = (stretched > 0.0) & (stretched < 1.0)
    return jnp.where(free, (ZETA - GAMMA) / BETA * s * (1.0 - s), 0.0)


def keep_prob(alpha):
    return jax.nn.sigmoid(alpha - BETA * math.log(-GAMMA / ZETA))


def lane_of(row, place):
    lanes = lax.broadcasted_iota(jnp.int32, row.shape, 1)
    return jnp.sum(jnp.where(lanes == place, row, 0.0), axis=1, keepdims=True)


def head_row(noise_ref, alpha_ref, rank, heads):
    lanes = lax.broadcasted_iota(jnp.int32, (1, heads * HD), 1)
    noise = jnp.full((1, heads * HD), 0.5, F32)
    alpha = jnp.zeros((1, heads * HD), F32)
    for h in range(heads):
        here = (lanes >= h * HD) & (lanes < (h + 1) * HD)
        noise = jnp.where(here, lane_of(noise_ref[...], h), noise)
        alpha = jnp.where(here, lane_of(alpha_ref[...], rank * heads + h), alpha)
    return noise, alpha


def part_of(ref, rank, width):
    return ref[:, pl.ds(pl.multiple_of(rank * width, width), width)]


def nn(a, b):
    return jnp.dot(a, b, preferred_element_type=F32)


def nt(a, b):
    return lax.dot_general(a, b, (((1,), (1,)), ((), ())), preferred_element_type=F32)


def tn(a, b):
    return lax.dot_general(a, b, (((0,), (0,)), ((), ())), preferred_element_type=F32)


def fold(values):
    return jnp.sum(values.reshape(values.shape[0] // 8, 8, values.shape[1]), axis=0)


class Group:
    def __init__(self, n):
        self.n = n
        self.nx = n // 2
        self.me = lax.axis_index("hid")
        self.x = lax.div(self.me, 2)
        self.c = lax.rem(self.me, 2)
        self.partner = 2 * self.x + 1 - self.c

    def chip_ahead(self, j):
        return lax.rem(self.x + 1 + j, self.nx)

    def chip_behind(self, j):
        return lax.rem(self.x - 1 - j + self.nx, self.nx)

    def slot(self, h):
        return lax.rem(h, 2) * self.nx + lax.div(h, 2)

    def all_peers(self):
        return [{"hid": lax.rem(self.me + 1 + i, self.n)} for i in range(self.n - 1)]

    def near_peers(self):
        near = [self.partner] + [2 * self.chip_ahead(j) + self.c for j in range(self.nx - 1)]
        return [{"hid": peer} for peer in near]


def remote(src, dst, send_sem, recv_sem, to):
    return pltpu.make_async_remote_copy(
        src_ref=src,
        dst_ref=dst,
        send_sem=send_sem,
        recv_sem=recv_sem,
        device_id=to if isinstance(to, dict) else {"hid": to},
        device_id_type=MESH,
    )


def gather_sems(seqs, nx):
    wide = pltpu.SemaphoreType.DMA((seqs, nx - 1))
    return [wide] * 4 + [pltpu.SemaphoreType.DMA((seqs,))] * 3


def reduce_sems(seqs, nx):
    wide = pltpu.SemaphoreType.DMA((seqs, nx - 1))
    return [wide] * 2 + [pltpu.SemaphoreType.DMA((seqs,))] * 2


class Gather:
    def __init__(self, group, sems, source, region):
        self.g, self.source, self.region = group, source, region
        self.xs, self.xr, self.rs, self.rr, self.ps, self.pr, self.os = sems

    def _own(self, s):
        return pltpu.make_async_copy(self.source(s), self.region(s, self.g.me), self.os.at[s])

    def _cross(self, s, j):
        to = 2 * self.g.chip_ahead(j) + self.g.c
        return remote(
            self.source(s), self.region(s, self.g.me), self.xs.at[s, j], self.xr.at[s, j], to
        )

    def _crossed(self, s, j):
        to = 2 * self.g.chip_ahead(j) + self.g.c
        block = self.region(s, 2 * self.g.chip_behind(j) + self.g.c)
        return remote(self.source(s), block, self.xs.at[s, j], self.xr.at[s, j], to)

    def _pair(self, s):
        return remote(
            self.source(s),
            self.region(s, self.g.me),
            self.ps.at[s],
            self.pr.at[s],
            self.g.partner,
        )

    def _paired(self, s):
        block = self.region(s, self.g.partner)
        return remote(self.source(s), block, self.ps.at[s], self.pr.at[s], self.g.partner)

    def _relay(self, s, j):
        block = self.region(s, 2 * self.g.chip_behind(j) + self.g.c)
        return remote(block, block, self.rs.at[s, j], self.rr.at[s, j], self.g.partner)

    def _relayed(self, s, j):
        block = self.region(s, 2 * self.g.chip_behind(j) + 1 - self.g.c)
        return remote(block, block, self.rs.at[s, j], self.rr.at[s, j], self.g.partner)

    def start(self, s):
        for j in range(self.g.nx - 1):
            self._cross(s, j).start()
        self._pair(s).start()
        self._own(s).start()

    def relay(self, s):
        for j in range(self.g.nx - 1):
            self._crossed(s, j).wait_recv()
            self._relay(s, j).start()

    def wait(self, s):
        self._own(s).wait()
        self._paired(s).wait_recv()
        for j in range(self.g.nx - 1):
            self._relayed(s, j).wait_recv()

    def drain(self, s):
        self._pair(s).wait_send()
        for j in range(self.g.nx - 1):
            self._cross(s, j).wait_send()
            self._relay(s, j).wait_send()


class Reduce:
    def __init__(self, group, sems, psend, precv, own, xsend, xrecv):
        self.g = group
        self.psend, self.precv, self.own, self.xsend, self.xrecv = psend, precv, own, xsend, xrecv
        self.xs, self.xr, self.ps, self.pr = sems

    def _pair(self, s):
        return remote(
            self.psend.at[s], self.precv.at[s], self.ps.at[s], self.pr.at[s], self.g.partner
        )

    def _cross(self, s, j):
        to = 2 * self.g.chip_ahead(j) + self.g.c
        return remote(
            self.xsend.at[s, j], self.xrecv.at[s, j], self.xs.at[s, j], self.xr.at[s, j], to
        )

    def start(self, s):
        self._pair(s).start()

    def cross(self, s):
        self._pair(s).wait()
        rows = self.own.shape[2]
        for j in range(self.g.nx - 1):
            chip = self.g.chip_ahead(j)

            def add(i, carry, chip=chip, j=j):
                at = pl.ds(pl.multiple_of(i * RB, RB), RB)
                total = self.own[s, chip, at, :] + self.precv[s, chip, at, :].astype(F32)
                self.xsend[s, j, at, :] = total.astype(BF)
                return carry

            lax.fori_loop(0, rows // RB, add, 0)
            self._cross(s, j).start()

    def arrive(self, s):
        for j in range(self.g.nx - 1):
            self._cross(s, j).wait()

    def total(self, s, at):
        total = self.own[s, self.g.x, at, :] + self.precv[s, self.g.x, at, :].astype(F32)
        for j in range(self.g.nx - 1):
            total = total + self.xrecv[s, j, at, :].astype(F32)
        return total


class Cycle:
    def __init__(self, size):
        self.size = size
        self.me = lax.axis_index("dp")
        self.length = size // 2
        line, column = lax.div(self.me, 2), lax.rem(self.me, 2)
        self.place = line + column * (size - 1 - 2 * line)

    def device(self, place):
        column = lax.div(place, self.length)
        line = place + column * (self.size - 1 - 2 * place)
        return 2 * line + column

    def beside(self, way):
        return self.device(lax.rem(self.place + way + self.size, self.size))


def split(shape, size):
    tall = max(16, shape[0] // (2 * size))
    across = 2 * size * tall // shape[0]
    return tall, shape[1] // across, across


def ring_scratch(shape, size):
    tall, broad, _ = split(shape, size)
    step = pltpu.SemaphoreType.DMA((size - 1,))
    return [
        pltpu.VMEM((size - 1, tall, broad), BF),
        pltpu.SemaphoreType.DMA((size,)),
    ] + [step] * 4 + [pltpu.SemaphoreType.REGULAR]


class Ring:
    def __init__(self, cycle, data, target, way, scratch):
        self.cycle, self.data, self.target, self.way = cycle, data, target, way
        self.size = cycle.size
        self.recv, self.out_sem, self.ss, self.sr, self.gs, self.gr, self.free = scratch
        self.tall, self.broad, self.across = split(data.shape, self.size)
        self.to, self.frm = {"dp": cycle.beside(way)}, {"dp": cycle.beside(-way)}
        self.ticks = 2 * self.size - 1

    def block(self, number):
        place = lax.rem(self.cycle.place + self.way * number + 2 * self.size, self.size)
        index = 2 * place + (0 if self.way > 0 else 1)
        if self.across == 1:
            return pl.multiple_of(index * self.tall, self.tall), 0
        row = lax.div(index, self.across)
        column = lax.rem(index, self.across)
        return (
            pl.multiple_of(row * self.tall, self.tall),
            pl.multiple_of(column * self.broad, self.broad),
        )

    def view(self, number):
        row, column = self.block(number)
        return self.data.at[pl.ds(row, self.tall), pl.ds(column, self.broad)]

    def _add(self, t):
        return remote(self.view(-t), self.recv.at[t], self.ss.at[t], self.sr.at[t], self.to)

    def _pass(self, t):
        block = self.view(1 - t)
        return remote(block, block, self.gs.at[t], self.gr.at[t], self.to)

    def _passed(self, t):
        block = self.view(-t)
        return remote(block, block, self.gs.at[t], self.gr.at[t], self.to)

    def _sum(self, t):
        row, column = self.block(-t)

        def part(i, carry):
            at = pl.ds(pl.multiple_of(row + i * RB, RB), RB)
            cols = pl.ds(column, self.broad)
            arrived = self.recv[t - 1, pl.ds(pl.multiple_of(i * RB, RB), RB), :].astype(F32)
            self.data[at, cols] = (self.data[at, cols].astype(F32) + arrived).astype(BF)
            return carry

        lax.fori_loop(0, self.tall // RB, part, 0)

    def _out(self, number, count):
        row, column = self.block(number)
        place = self.target.at[pl.ds(row, self.tall), pl.ds(column, self.broad)]
        return pltpu.make_async_copy(self.view(number), place, self.out_sem.at[count])

    def tick(self, t):
        size = self.size

        @pl.when(t == 0)
        def _():
            self._add(0).start()

        @pl.when((t >= 1) & (t <= size - 1))
        def _():
            self._add(t - 1).wait_recv()
            self._sum(t)

        @pl.when((t >= 1) & (t < size - 1))
        def _():
            self._add(t).start()

        @pl.when((t >= 1) & (t <= size - 1))
        def _():
            self._add(t - 1).wait_send()
            pl.semaphore_signal(self.free, inc=1, device_id=self.frm, device_id_type=MESH)

        @pl.when(t == size - 1)
        def _():
            pl.semaphore_wait(self.free, 1)
            self._pass(0).start()
            self._out(1, 0).start()

        @pl.when((t > size - 1) & (t < 2 * size - 1))
        def _():
            u = t - size
            self._passed(u).wait_recv()

            @pl.when(t < 2 * size - 2)
            def _():
                pl.semaphore_wait(self.free, 1)
                self._pass(u + 1).start()

            self._out(-u, u + 1).start()

    def drain(self):
        self._out(1, 0).wait()

        def step(t, carry):
            self._pass(t).wait_send()
            self._out(-t, t + 1).wait()
            return carry

        lax.fori_loop(0, self.size - 1, step, 0)


def meet(peers):
    barrier = pltpu.get_barrier_semaphore()
    for peer in peers:
        pl.semaphore_signal(barrier, inc=1, device_id=peer, device_id_type=MESH)
    pl.semaphore_wait(barrier, len(peers))


def mean_of(values):
    return jnp.sum(values, axis=1, keepdims=True) * (1.0 / D)


def attend_kernel(n, seqs, heads, *refs):
    (
        len_ref, tok_ref, up_ref, tea_ref, ob_ref, ag_ref, as_ref, db_ref, fg_ref, fs_ref,
        wn_ref, wa_ref, hn_ref, ha_ref, wq_ref, wk_ref, wv_ref, qb_ref, vb_ref, wo_ref,
        full_o, qkv_o, prob_o, ctx_o, gat_o, nrm_o, pre_o, rstd_o, mid_o, par_o, change_o, gate_o,
        full, wqkv, wo, qkv, prob, ctx, gat, own, psend, precv, xsend, xrecv,
        nrm, pre, rstd, mid, par, chg, up, tea, change, vec, score, in_sem, out_sem, vec_send, vec_recv, ch_send, ch_recv, *sems,
    ) = refs
    g = Group(n)
    width = heads * HD
    rows = SLOT // n
    gsems, rsems = sems[:7], sems[7:]
    cols = lambda h: pl.ds(pl.multiple_of(h * width, width), width)
    seq = lambda s: pl.ds(pl.multiple_of(s * SLOT, SLOT), SLOT)
    own_rows = lambda s: pl.ds(pl.multiple_of(s * rows, rows), rows)
    ga = Gather(g, gsems, lambda s: tok_ref.at[seq(s), :], lambda s, h: full.at[seq(s), cols(h)])
    re = Reduce(g, rsems, psend, precv, own, xsend, xrecv)

    def vec_to(i):
        to = lax.rem(g.me + 1 + i, n)
        return remote(vec, par.at[:, cols(g.me)], vec_send.at[i], vec_recv.at[i], to)

    def vec_from(i):
        to = lax.rem(g.me + 1 + i, n)
        frm = lax.rem(g.me - 1 - i + n, n)
        return remote(vec, par.at[:, cols(frm)], vec_send.at[i], vec_recv.at[i], to)

    def change_to(i):
        to = lax.rem(g.me + 1 + i, n)
        return remote(
            change.at[:, g.slot(to)], chg.at[:, :, cols(g.me)], ch_send.at[i], ch_recv.at[i], to
        )

    def change_from(i):
        to = lax.rem(g.me + 1 + i, n)
        frm = lax.rem(g.me - 1 - i + n, n)
        return remote(
            change.at[:, g.slot(to)], chg.at[:, :, cols(frm)], ch_send.at[i], ch_recv.at[i], to
        )

    loads = [
        pltpu.make_async_copy(wq_ref, wqkv.at[:, pl.ds(0, width)], in_sem.at[0]),
        pltpu.make_async_copy(wk_ref, wqkv.at[:, pl.ds(width, width)], in_sem.at[1]),
        pltpu.make_async_copy(wv_ref, wqkv.at[:, pl.ds(2 * width, width)], in_sem.at[2]),
        pltpu.make_async_copy(wo_ref, wo, in_sem.at[3]),
        pltpu.make_async_copy(up_ref, up, in_sem.at[4]),
        pltpu.make_async_copy(tea_ref, tea, in_sem.at[5]),
    ]
    par_own = pltpu.make_async_copy(vec, par.at[:, cols(g.me)], in_sem.at[7])
    change_own = pltpu.make_async_copy(
        change.at[:, g.slot(g.me)], chg.at[:, :, cols(g.me)], in_sem.at[8]
    )
    chg_out = pltpu.make_async_copy(chg, change_o, in_sem.at[6])

    def sequence_outs(s):
        return [
            pltpu.make_async_copy(full.at[seq(s), :], full_o.at[seq(s), :], out_sem.at[s, 0]),
            pltpu.make_async_copy(qkv.at[seq(s), :], qkv_o.at[seq(s), :], out_sem.at[s, 1]),
            pltpu.make_async_copy(prob.at[s], prob_o.at[s], out_sem.at[s, 2]),
            pltpu.make_async_copy(ctx.at[seq(s), :], ctx_o.at[seq(s), :], out_sem.at[s, 3]),
            pltpu.make_async_copy(gat.at[seq(s), :], gat_o.at[seq(s), :], out_sem.at[s, 4]),
        ]

    def row_outs(s):
        return [
            pltpu.make_async_copy(nrm.at[own_rows(s), :], nrm_o.at[own_rows(s), :], out_sem.at[s, 5]),
            pltpu.make_async_copy(pre.at[own_rows(s), :], pre_o.at[own_rows(s), :], out_sem.at[s, 6]),
            pltpu.make_async_copy(rstd.at[own_rows(s), :], rstd_o.at[own_rows(s), :], out_sem.at[s, 7]),
            pltpu.make_async_copy(mid.at[own_rows(s), :], mid_o.at[own_rows(s), :], out_sem.at[s, 8]),
        ]

    for load in loads:
        load.start()
    for row, ref in ((0, ob_ref), (2, ag_ref), (3, as_ref), (4, db_ref), (5, fg_ref), (6, fs_ref)):
        vec[row : row + 1, :] = ref[...]
    vec[1:2, :] = gate_value(wn_ref[...], part_of(wa_ref, g.me, width))
    vec[7:8, :] = jnp.zeros((1, width), F32)
    meet(g.all_peers())

    def begin(s, carry):
        ga.start(s)
        return carry

    for i in range(n - 1):
        vec_to(i).start()
    lax.fori_loop(0, seqs, begin, 0)
    par_own.start()
    gate_row = gate_value(*head_row(hn_ref, ha_ref, g.me, heads))
    gate_o[...] = gate_row
    for load in loads:
        load.wait()

    def differ(i, carry):
        at = pl.ds(pl.multiple_of(i * 32, 32), 32)
        value = (up[at, :].astype(F32) - tea[at, :].astype(F32)).astype(BF)
        each = SLOT // n // 32
        s, q = lax.div(i, SLOT // 32), lax.rem(i, SLOT // 32)
        change[s, lax.div(q, each), pl.ds(pl.multiple_of(lax.rem(q, each) * 32, 32), 32), :] = value
        return carry

    lax.fori_loop(0, seqs * SLOT // 32, differ, 0)
    change_own.start()
    for i in range(n - 1):
        change_to(i).start()
    ga.relay(0)
    par_own.wait()
    for i in range(n - 1):
        vec_from(i).wait()
    par_o[...] = par[...]

    lanes = lax.broadcasted_iota(jnp.int32, (1, width), 1)
    head_lanes = [
        jnp.where((lanes >= h * HD) & (lanes < (h + 1) * HD), 1.0, 0.0).astype(BF) for h in range(heads)
    ]

    def finish(s):
        re.arrive(s)

        def block(i, carry):
            at = pl.ds(pl.multiple_of(i * RB, RB), RB)
            here = pl.ds(pl.multiple_of(s * rows + i * RB, RB), RB)
            token_row = pl.multiple_of(s * SLOT + g.slot(g.me) * rows + i * RB, RB)
            attention_pre = re.total(s, at) + par[0:1, :]
            residual = full[pl.ds(token_row, RB), :].astype(F32) + attention_pre * par[1:2, :]
            centered = residual - mean_of(residual)
            row_rstd = lax.rsqrt(mean_of(centered * centered) + EPS)
            normed = centered * row_rstd
            middle = normed * par[2:3, :] + par[3:4, :]
            nrm[here, :] = normed
            pre[here, :] = attention_pre
            rstd[here, :] = jnp.broadcast_to(row_rstd, (RB, 128))
            mid[here, :] = middle.astype(BF)
            return carry

        lax.fori_loop(0, rows // RB, block, 0)
        for copy in row_outs(s):
            copy.start()

    def sequence(s, carry):
        ga.wait(s)
        here = seq(s)
        projected = nn(full[here, :], wqkv[...])
        qkv[here, 0:width] = (projected[:, 0:width] + qb_ref[...]).astype(BF)
        qkv[here, width : 2 * width] = projected[:, width : 2 * width].astype(BF)
        qkv[here, 2 * width : 3 * width] = (projected[:, 2 * width : 3 * width] + vb_ref[...]).astype(BF)

        @pl.when(s + 1 < seqs)
        def _():
            ga.relay(s + 1)

        @pl.when(s > 0)
        def _():
            re.cross(s - 1)

        length = len_ref[lax.axis_index("dp") * seqs + s]
        for h in range(heads):
            score[...] = nt(qkv[here, 0:width] * head_lanes[h], qkv[here, width : 2 * width])

            def softmax(i, carry, h=h):
                at = pl.ds(pl.multiple_of(i * 64, 64), 64)
                places = lax.broadcasted_iota(jnp.int32, (64, SLOT), 1)
                scores = jnp.where(places < length, score[at, :] * (HD**-0.5), MASKED)
                exponent = jnp.exp(scores - jnp.max(scores, axis=1, keepdims=True))
                total = jnp.sum(exponent, axis=1, keepdims=True)
                prob[s, h, at, :] = (exponent * (1.0 / total)).astype(BF)
                return carry

            lax.fori_loop(0, SLOT // 64, softmax, 0)
            term = nn(prob[s, h], qkv[here, 2 * width : 3 * width] * head_lanes[h])
            ctx[here, :] = term if h == 0 else ctx[here, :] + term
        gat[here, :] = (ctx[here, :] * gate_row).astype(BF)
        for copy in sequence_outs(s):
            copy.start()
        half = SLOT // 2
        there = pl.ds(pl.multiple_of(s * SLOT + (1 - g.c) * half, half), half)
        psend[s] = nn(gat[there, :], wo[...]).astype(BF).reshape(n // 2, rows, D)
        re.start(s)
        mine = pl.ds(pl.multiple_of(s * SLOT + g.c * half, half), half)
        own[s] = nn(gat[mine, :], wo[...]).reshape(n // 2, rows, D)

        @pl.when(s > 0)
        def _():
            finish(s - 1)

        return carry

    lax.fori_loop(0, seqs, sequence, 0)
    re.cross(seqs - 1)
    change_own.wait()
    for i in range(n - 1):
        change_from(i).wait()
    chg_out.start()
    finish(seqs - 1)
    chg_out.wait()

    def end(s, carry):
        ga.drain(s)
        for copy in sequence_outs(s) + row_outs(s):
            copy.wait()
        return carry

    lax.fori_loop(0, seqs, end, 0)


def feed_kernel(n, seqs, units, *refs):
    (
        len_ref, mid_ref, nrm_ref, pre_ref, rstd_ref, par, change_ref, w1_ref, b1_ref, w2_ref, un_ref, ua_ref,
        out_o, dlow_o, dres_o, dw1_o, dw2_o, rowsum_o, unitsum_o,
        midf, dffn, w1, w2, act, inner, slope, own, psend, precv, xsend, xrecv,
        nrm, pre, rstd, change, dtwo, dsend, fout, dlow, dres, wide, grad, sums, unit_sums, ugate_ref,
        in_sem, out_sem, grad_sem, *sems,
    ) = refs
    g = Group(n)
    rows = SLOT // n
    half = SLOT // 2
    g1, r1, g2, r2 = sems[:7], sems[7:11], sems[11:18], sems[18:]
    seq = lambda s: pl.ds(pl.multiple_of(s * SLOT, SLOT), SLOT)
    own_rows = lambda s: pl.ds(pl.multiple_of(s * rows, rows), rows)
    spot = lambda s, h: pl.ds(pl.multiple_of(s * SLOT + g.slot(h) * rows, rows), rows)
    gm = Gather(g, g1, lambda s: mid_ref.at[own_rows(s), :], lambda s, h: midf.at[spot(s, h), :])
    gd = Gather(g, g2, lambda s: dsend.at[own_rows(s), :], lambda s, h: dffn.at[spot(s, h), :])
    rf = Reduce(g, r1, psend, precv, own, xsend, xrecv)
    rb = Reduce(g, r2, psend, precv, own, xsend, xrecv)
    loads = [
        pltpu.make_async_copy(w1_ref, w1, in_sem.at[0]),
        pltpu.make_async_copy(w2_ref, w2, in_sem.at[1]),
        pltpu.make_async_copy(nrm_ref, nrm, in_sem.at[2]),
        pltpu.make_async_copy(change_ref, change, in_sem.at[3]),
        pltpu.make_async_copy(pre_ref, pre, in_sem.at[4]),
        pltpu.make_async_copy(rstd_ref, rstd, in_sem.at[5]),
    ]

    meet(g.near_peers())

    def begin(s, carry):
        gm.start(s)
        return carry

    lax.fori_loop(0, seqs, begin, 0)
    for load in loads:
        load.start()
    sums[...] = jnp.zeros_like(sums)
    unit_sums[...] = jnp.zeros_like(unit_sums)
    ugate_ref[...] = gate_value(un_ref[...], part_of(ua_ref, g.me, units))
    gm.relay(0)
    for load in loads:
        load.wait()

    def finish_forward(s):
        rf.arrive(s)
        length = len_ref[lax.axis_index("dp") * seqs + s]

        def block(i, carry):
            at = pl.ds(pl.multiple_of(i * RB, RB), RB)
            here = pl.ds(pl.multiple_of(s * rows + i * RB, RB), RB)
            ffn_pre = rf.total(s, at) + par[4:5, :]
            middle = nrm[here, :] * par[2:3, :] + par[3:4, :]
            residual = middle + ffn_pre * par[1:2, :]
            centered = residual - mean_of(residual)
            row_rstd = lax.rsqrt(mean_of(centered * centered) + EPS)
            normed = centered * row_rstd
            final = normed * par[5:6, :] + par[6:7, :]
            fout[here, :] = final.astype(BF)
            place = g.slot(g.me) * rows + i * RB + lax.broadcasted_iota(jnp.int32, (RB, 1), 0)
            live = jnp.where(place < length, 1.0, 0.0)
            d_final = live * (change[here, :].astype(F32) + final)
            sums[0] += fold(d_final * normed)
            sums[1] += fold(d_final)
            d_normed = d_final * par[5:6, :]
            d_two = row_rstd * (d_normed - mean_of(d_normed) - normed * mean_of(d_normed * normed))
            sums[2] += fold(d_two * ffn_pre)
            d_ffn = d_two * par[1:2, :]
            sums[3] += fold(d_ffn)
            dtwo[here, :] = d_two
            dsend[here, :] = d_ffn.astype(BF)
            return carry

        lax.fori_loop(0, rows // RB, block, 0)
        gd.start(s)

    def forward(s, carry):
        gm.wait(s)
        here = seq(s)

        def part(b, carry):
            cols = pl.ds(pl.multiple_of(b * NB, NB), NB)
            wide[...] = nn(midf[here, :], w1[:, cols])
            bias = b1_ref[:, cols]
            gate = ugate_ref[:, cols]

            def block(i, carry):
                at = pl.ds(pl.multiple_of(i * 32, 32), 32)
                row = pl.ds(pl.multiple_of(s * SLOT + i * 32, 32), 32)
                v = wide[at, :] + bias
                phi = 0.5 * (1.0 + lax.erf(v * ROOT_HALF))
                activated = v * phi
                act[row, cols] = activated.astype(BF)
                inner[row, cols] = (activated * gate).astype(BF)
                steep = phi + v * jnp.exp(-0.5 * v * v) * (1.0 / ROOT_TWO_PI)
                slope[row, cols] = (gate * steep).astype(BF)
                return carry

            lax.fori_loop(0, SLOT // 32, block, 0)
            return carry

        lax.fori_loop(0, units // NB, part, 0)

        @pl.when(s + 1 < seqs)
        def _():
            gm.relay(s + 1)

        @pl.when(s > 0)
        def _():
            rf.cross(s - 1)

        there = pl.ds(pl.multiple_of(s * SLOT + (1 - g.c) * half, half), half)
        psend[s] = nn(inner[there, :], w2[...]).astype(BF).reshape(n // 2, rows, D)
        rf.start(s)
        mine = pl.ds(pl.multiple_of(s * SLOT + g.c * half, half), half)
        own[s] = nn(inner[mine, :], w2[...]).reshape(n // 2, rows, D)

        @pl.when(s > 1)
        def _():
            finish_forward(s - 2)

        return carry

    lax.fori_loop(0, seqs, forward, 0)
    rf.cross(seqs - 1)
    gd.relay(0)

    def row_outs(s):
        return [
            pltpu.make_async_copy(fout.at[own_rows(s), :], out_o.at[own_rows(s), :], out_sem.at[s, 0]),
            pltpu.make_async_copy(dlow.at[own_rows(s), :], dlow_o.at[own_rows(s), :], out_sem.at[s, 1]),
            pltpu.make_async_copy(dres.at[own_rows(s), :], dres_o.at[own_rows(s), :], out_sem.at[s, 2]),
        ]

    def finish_backward(s):
        rb.arrive(s)

        def block(i, carry):
            at = pl.ds(pl.multiple_of(i * RB, RB), RB)
            here = pl.ds(pl.multiple_of(s * rows + i * RB, RB), RB)
            normed = nrm[here, :]
            d_middle = dtwo[here, :] + rb.total(s, at)
            sums[4] += fold(d_middle * normed)
            sums[5] += fold(d_middle)
            d_normed = d_middle * par[2:3, :]
            d_one = rstd[here, 0:1] * (
                d_normed - mean_of(d_normed) - normed * mean_of(d_normed * normed)
            )
            sums[2] += fold(d_one * pre[here, :])
            d_attn = d_one * par[1:2, :]
            sums[6] += fold(d_attn)
            dres[here, :] = d_one
            dlow[here, :] = d_attn.astype(BF)
            return carry

        lax.fori_loop(0, rows // RB, block, 0)
        for copy in row_outs(s):
            copy.start()

    def backward(s, carry):
        gd.wait(s)
        here = seq(s)

        def part(b, carry):
            cols = pl.ds(pl.multiple_of(b * NB, NB), NB)
            wide[...] = nt(dffn[here, :], w2[cols, :])

            def block(i, sums_here):
                unit_part, bias_part = sums_here
                at = pl.ds(pl.multiple_of(i * 32, 32), 32)
                row = pl.ds(pl.multiple_of(s * SLOT + i * 32, 32), 32)
                d_inner = wide[at, :]
                d_pre = (d_inner * slope[row, cols].astype(F32)).astype(BF)
                unit_part = unit_part + fold(d_inner * act[row, cols].astype(F32))
                bias_part = bias_part + fold(d_pre.astype(F32))
                slope[row, cols] = d_pre
                return (unit_part, bias_part)

            zero = jnp.zeros((8, NB), F32)
            unit_part, bias_part = lax.fori_loop(0, SLOT // 32, block, (zero, zero))
            unit_sums[0, :, cols] += unit_part
            unit_sums[1, :, cols] += bias_part
            return carry

        lax.fori_loop(0, units // NB, part, 0)

        @pl.when(s < 2)
        def _():
            finish_forward(seqs - 2 + s)

        @pl.when(s + 1 < seqs)
        def _():
            gd.relay(s + 1)

        @pl.when(s > 0)
        def _():
            rb.cross(s - 1)

        there = pl.ds(pl.multiple_of(s * SLOT + (1 - g.c) * half, half), half)
        psend[s] = nt(slope[there, :], w1[...]).astype(BF).reshape(n // 2, rows, D)
        rb.start(s)
        mine = pl.ds(pl.multiple_of(s * SLOT + g.c * half, half), half)
        own[s] = nt(slope[mine, :], w1[...]).reshape(n // 2, rows, D)

        @pl.when(s > 1)
        def _():
            finish_backward(s - 2)

        return carry

    lax.fori_loop(0, seqs, backward, 0)
    rb.cross(seqs - 1)

    def grad_out(k, b):
        target = (dw2_o, dw1_o)[k]
        at = pl.ds(pl.multiple_of(b * NB, NB), NB)
        return pltpu.make_async_copy(grad.at[b], target.at[at, :], grad_sem.at[k, b])

    def down_grad(b, carry):
        cols = pl.ds(pl.multiple_of(b * NB, NB), NB)
        grad[b] = tn(inner[:, cols], dffn[...]).astype(BF)
        grad_out(0, b).start()
        return carry

    lax.fori_loop(0, units // NB, down_grad, 0)
    finish_backward(seqs - 2)
    for b in range(units // NB):
        grad_out(0, b).wait()

    def inner_grad(b, carry):
        cols = pl.ds(pl.multiple_of(b * NB, NB), NB)
        grad[b, :, 0:units] = tn(midf[:, cols], slope[...]).astype(BF)
        pltpu.make_async_copy(
            grad.at[b, :, pl.ds(0, units)], dw1_o.at[cols, :], grad_sem.at[1, b]
        ).start()
        return carry

    lax.fori_loop(0, D // NB, inner_grad, 0)
    finish_backward(seqs - 1)
    for k in range(7):
        rowsum_o[k : k + 1, :] = jnp.sum(sums[k], axis=0, keepdims=True)
    rowsum_o[7:8, :] = jnp.zeros((1, D), F32)
    for k in range(2):
        unitsum_o[k : k + 1, :] = jnp.sum(unit_sums[k], axis=0, keepdims=True)
    for b in range(D // NB):
        at = pl.ds(b * NB, NB)
        pltpu.make_async_copy(
            grad.at[b, :, pl.ds(0, units)], dw1_o.at[at, :], grad_sem.at[1, b]
        ).wait()

    def end(s, carry):
        gm.drain(s)
        gd.drain(s)
        for copy in row_outs(s):
            copy.wait()
        return carry

    lax.fori_loop(0, seqs, end, 0)


def attend_back_kernel(n, seqs, heads, size, *refs):
    (
        dlow_ref, dres_ref, full_ref, qkv_ref, prob_ref, ctx_ref, gat_ref,
        wq_ref, wk_ref, wv_ref, wo_ref, dw1_ref, dw2_ref, out_ref, gate_ref,
        tgrad_o, dwqkv_o, dwo_o, dw1_o, dw2_o, output_o, sums_o,
        dattn, dres, full, qkv, prob, ctx, gat, wqkv, wo, dctx, dqkv, dprob, dscore, acc,
        block_f, own, psend, precv, xsend, xrecv, tgrad, grad, gwo, moved, sums, dw1, dw2,
        in_sem, out_sem, grad_sem, move_send, move_recv, *sems,
    ) = refs
    g = Group(n)
    cycle = Cycle(size)
    rings = []
    for k, (data, target) in enumerate(((dw1, dw1_o), (dw2, dw2_o))):
        for way in (1, -1):
            i = 11 + 7 * len(rings)
            rings.append(Ring(cycle, data, target, way, sems[i : i + 7]))
    ticks = rings[0].ticks

    def tick(t, which):
        for ring in rings[2 * which : 2 * which + 2]:
            ring.tick(t)

    def move_to(i):
        to = lax.rem(g.me + 1 + i, n)
        return remote(
            out_ref.at[:, :, cols_of(to)], moved.at[:, g.slot(g.me)], move_send.at[i], move_recv.at[i], to
        )

    def move_from(i):
        to = lax.rem(g.me + 1 + i, n)
        frm = lax.rem(g.me - 1 - i + n, n)
        return remote(
            out_ref.at[:, :, cols_of(to)], moved.at[:, g.slot(frm)], move_send.at[i], move_recv.at[i], to
        )

    width = heads * HD
    rows = SLOT // n
    gsems, rsems = sems[:7], sems[7:11]
    cols_of = lambda h: pl.ds(pl.multiple_of(h * width, width), width)
    seq = lambda s: pl.ds(pl.multiple_of(s * SLOT, SLOT), SLOT)
    own_rows = lambda s: pl.ds(pl.multiple_of(s * rows, rows), rows)
    spot = lambda s, h: pl.ds(pl.multiple_of(s * SLOT + g.slot(h) * rows, rows), rows)
    ga = Gather(g, gsems, lambda s: dlow_ref.at[own_rows(s), :], lambda s, h: dattn.at[spot(s, h), :])
    re = Reduce(g, rsems, psend, precv, own, xsend, xrecv)
    loads = [
        pltpu.make_async_copy(wo_ref, wo, in_sem.at[0]),
        pltpu.make_async_copy(ctx_ref, ctx, in_sem.at[1]),
        pltpu.make_async_copy(qkv_ref, qkv, in_sem.at[2]),
        pltpu.make_async_copy(prob_ref, prob, in_sem.at[3]),
        pltpu.make_async_copy(wq_ref, wqkv.at[:, pl.ds(0, width)], in_sem.at[4]),
        pltpu.make_async_copy(wk_ref, wqkv.at[:, pl.ds(width, width)], in_sem.at[5]),
        pltpu.make_async_copy(wv_ref, wqkv.at[:, pl.ds(2 * width, width)], in_sem.at[6]),
        pltpu.make_async_copy(dres_ref, dres, in_sem.at[7]),
        pltpu.make_async_copy(full_ref, full, in_sem.at[8]),
        pltpu.make_async_copy(gat_ref, gat, in_sem.at[9]),
        pltpu.make_async_copy(
            out_ref.at[:, :, cols_of(g.me)], moved.at[:, g.slot(g.me)], in_sem.at[11]
        ),
    ]
    grads_in = [
        pltpu.make_async_copy(dw1_ref, dw1, in_sem.at[12]),
        pltpu.make_async_copy(dw2_ref, dw2, in_sem.at[13]),
    ]
    meet(g.all_peers() + [{"dp": cycle.beside(1)}, {"dp": cycle.beside(-1)}])
    for load in grads_in:
        load.start()

    def begin(s, carry):
        ga.start(s)
        return carry

    lax.fori_loop(0, seqs, begin, 0)
    for load in loads:
        load.start()
    sums[...] = jnp.zeros_like(sums)
    for load in grads_in:
        load.wait()
    tick(0, 0)
    tick(0, 1)
    ga.relay(0)
    for load in loads[:8]:
        load.wait()
    tick(1, 0)
    tick(1, 1)

    lanes = lax.broadcasted_iota(jnp.int32, (1, width), 1)
    head_lanes = [
        jnp.where((lanes >= h * HD) & (lanes < (h + 1) * HD), 1.0, 0.0).astype(BF) for h in range(heads)
    ]

    def out(s):
        return pltpu.make_async_copy(tgrad.at[seq(s), :], tgrad_o.at[seq(s), :], out_sem.at[s])

    def finish(s):
        re.arrive(s)

        def block(i, carry):
            at = pl.ds(pl.multiple_of(i * 32, 32), 32)
            tgrad[pl.ds(pl.multiple_of(s * SLOT + i * 32, 32), 32), :] = re.total(s, at)
            return carry

        lax.fori_loop(0, SLOT // 32, block, 0)
        out(s).start()

    def token_block(s, h):
        cols = pl.ds(pl.multiple_of(h * width, width), width)
        block_f[...] = nt(dqkv[seq(s), :], wqkv[cols, :])
        mine = pl.ds(pl.multiple_of(g.slot(g.me) * rows, rows), rows)
        block_f[mine, :] += dres[own_rows(s), cols]

    def sequence(s, carry):
        ga.wait(s)
        here = seq(s)
        d_gated = nt(dattn[here, :], wo[...])
        sums[0] += fold(d_gated * ctx[here, :])
        dctx[...] = (d_gated * gate_ref[...]).astype(BF)
        first = 2 + s * (heads + 2) // 2
        tick(first, 0)

        @pl.when(s + 1 < seqs)
        def _():
            ga.relay(s + 1)

        @pl.when(s > 0)
        def _():
            re.cross(s - 1)

        for h in range(heads):
            d_context = dctx[...] * head_lanes[h]
            dprob[...] = nt(d_context, qkv[here, 2 * width : 3 * width])

            def softmax(i, carry, h=h):
                at = pl.ds(pl.multiple_of(i * 64, 64), 64)
                p = prob[s, h, at, :].astype(F32)
                weighted = p * dprob[at, :]
                total = jnp.sum(weighted, axis=1, keepdims=True)
                dscore[at, :] = (weighted - p * total).astype(BF)
                return carry

            lax.fori_loop(0, SLOT // 64, softmax, 0)
            tick(first + (h + 1) // 2, (h + 1) % 2)
            terms = (
                nn(dscore[...], qkv[here, width : 2 * width] * head_lanes[h]),
                tn(dscore[...], qkv[here, 0:width] * head_lanes[h]),
                tn(prob[s, h], d_context),
            )
            for k in range(3):
                acc[k] = terms[k] if h == 0 else acc[k] + terms[k]
        scales = (HD**-0.5, HD**-0.5, 1.0)
        for k in range(3):
            rounded = (acc[k] * scales[k]).astype(BF)
            dqkv[here, k * width : (k + 1) * width] = rounded
            sums[1 + k] += fold(rounded.astype(F32))
        for chip in range(n // 2):
            token_block(s, 2 * chip + 1 - g.c)
            psend[s, chip] = block_f[...].astype(BF)
        re.start(s)
        tick(first + (heads + 1) // 2, 1)
        for chip in range(n // 2):
            token_block(s, 2 * chip + g.c)
            own[s, chip] = block_f[...]

        @pl.when(s > 0)
        def _():
            finish(s - 1)

        return carry

    lax.fori_loop(0, seqs, sequence, 0)
    re.cross(seqs - 1)
    for i in range(n - 1):
        move_to(i).start()
    for load in loads[8:]:
        load.wait()

    def grad_out(b):
        at = pl.ds(pl.multiple_of(b * NB, NB), NB)
        return pltpu.make_async_copy(grad.at[b], dwqkv_o.at[at, :], grad_sem.at[b])

    def token_grad(b, carry):
        cols = pl.ds(pl.multiple_of(b * NB, NB), NB)
        grad[b] = tn(full[:, cols], dqkv[...]).astype(BF)
        grad_out(b).start()
        return carry

    lax.fori_loop(0, D // NB, token_grad, 0)
    gwo[...] = tn(gat[...], dattn[...]).astype(BF)
    gwo_out = pltpu.make_async_copy(gwo, dwo_o, in_sem.at[10])
    gwo_out.start()
    finish(seqs - 1)
    for i in range(n - 1):
        move_from(i).wait()
    moved_out = pltpu.make_async_copy(moved, output_o, in_sem.at[14])
    moved_out.start()
    for k in range(4):
        sums_o[k : k + 1, :] = jnp.sum(sums[k], axis=0, keepdims=True)
    sums_o[4:8, :] = jnp.zeros((4, width), F32)
    gwo_out.wait()

    def rest(t, carry):
        tick(t, 0)
        tick(t, 1)
        return carry

    lax.fori_loop(2 + seqs * (heads + 2) // 2, ticks, rest, 0)
    moved_out.wait()
    for ring in rings:
        ring.drain()

    def end_grad(b, carry):
        grad_out(b).wait()
        return carry

    lax.fori_loop(0, D // NB, end_grad, 0)

    def end(s, carry):
        ga.drain(s)
        out(s).wait()
        return carry

    lax.fori_loop(0, seqs, end, 0)


def settle_kernel(n, size, seqs, *refs):
    (
        len_ref, dwqkv_ref, dwo_ref, output_ref, teacher_ref, row_ref, unit_ref, head_ref,
        dwq_o, dwk_o, dwv_o, dwo_o, small_o, units_o,
        dwq, dwk, dwv, dwo, output, teacher, parts, small, rbuf, sbuf, ubuf,
        in_sem, r_send, r_recv, s_send, s_recv, u_send, u_recv, *sems,
    ) = refs
    g = Group(n)
    cycle = Cycle(size)
    width = head_ref.shape[1]
    cols = lambda h: pl.ds(pl.multiple_of(h * width, width), width)
    rings = []
    for data, target in ((dwq, dwq_o), (dwk, dwk_o), (dwv, dwv_o), (dwo, dwo_o)):
        for way in (1, -1):
            i = 7 * len(rings)
            rings.append(Ring(cycle, data, target, way, sems[i : i + 7]))

    def tick(t):
        for ring in rings:
            ring.tick(t)

    def row_to(i):
        to = lax.rem(g.me + 1 + i, n)
        return remote(parts.at[:, cols(to)], rbuf.at[i], r_send.at[i], r_recv.at[i], to)

    def small_to(i):
        to = {"dp": lax.rem(cycle.me + 1 + i, size)}
        return remote(small, sbuf.at[i], s_send.at[i], s_recv.at[i], to)

    def units_to(i):
        to = {"dp": lax.rem(cycle.me + 1 + i, size)}
        return remote(unit_ref, ubuf.at[i], u_send.at[i], u_recv.at[i], to)

    loads = [
        pltpu.make_async_copy(dwqkv_ref.at[:, pl.ds(0, width)], dwq, in_sem.at[0]),
        pltpu.make_async_copy(dwqkv_ref.at[:, pl.ds(width, width)], dwk, in_sem.at[1]),
        pltpu.make_async_copy(dwqkv_ref.at[:, pl.ds(2 * width, width)], dwv, in_sem.at[2]),
        pltpu.make_async_copy(dwo_ref, dwo, in_sem.at[3]),
        pltpu.make_async_copy(output_ref, output, in_sem.at[4]),
        pltpu.make_async_copy(teacher_ref, teacher, in_sem.at[5]),
    ]
    for load in loads:
        load.start()
    meet(g.all_peers() + [{"dp": lax.rem(cycle.me + 1 + i, size)} for i in range(size - 1)])
    for load in loads[:4]:
        load.wait()
    tick(0)
    for load in loads[4:]:
        load.wait()
    for i in range(size - 1):
        units_to(i).start()

    def sequence(s, total):
        length = len_ref[cycle.me * seqs + s]

        def block(i, total):
            at = pl.ds(pl.multiple_of(s * SLOT + i * 32, 32), 32)
            place = i * 32 + lax.broadcasted_iota(jnp.int32, (32, 1), 0)
            differ = output[at, :].astype(F32) - teacher[at, :].astype(F32)
            return total + fold(jnp.where(place < length, differ * differ, 0.0))

        return lax.fori_loop(0, SLOT // 32, block, total)

    squares = lax.fori_loop(0, seqs, sequence, jnp.zeros((8, width), F32))
    parts[...] = row_ref[...]
    for h in range(n):
        parts[7:8, h * width : (h + 1) * width] = jnp.sum(squares, axis=0, keepdims=True)
    for i in range(n - 1):
        row_to(i).start()
    tick(1)
    total = parts[:, cols(g.me)]
    for i in range(n - 1):
        row_to(i).wait()
        total = total + rbuf[i]
    small[:, 0:width] = total
    small[:, width : 2 * width] = head_ref[...]
    for i in range(size - 1):
        small_to(i).start()

    def rest(t, carry):
        tick(t)
        return carry

    lax.fori_loop(2, rings[0].ticks, rest, 0)
    small_sum = small[...]
    unit_sum = unit_ref[...]
    for i in range(size - 1):
        small_to(i).wait()
        units_to(i).wait()
        small_sum = small_sum + sbuf[i]
        unit_sum = unit_sum + ubuf[i]
    small_o[...] = small_sum
    units_o[...] = unit_sum
    for ring in rings:
        ring.drain()


def complete_kernel(n, heads, units, *refs):
    (
        dw1_ref, dw2_ref, dwq_ref, dwk_ref, dwv_ref, dwo_ref, tgrad_ref, output_ref,
        small_ref, unit_ref, ha_ref, ua_ref, wa_ref, mult_ref, hn_ref, un_ref, wn_ref, len_ref,
        dw1_o, dw2_o, dwq_o, dwk_o, dwv_o, dwo_o, tgrad_o, output_o,
        qb_o, vb_o, ob_o, ag_o, as_o, db_o, fg_o, fs_o, b1_o, ha_o, ua_o, wa_o, mse_o, mult_o,
        dw1, dw2, dwq, dwk, dwv, dwo, tgrad, output, fw1, fw2, fwq, fwk, fwv, fwo, in_sem, out_sem,
    ) = refs
    width = heads * HD
    rank = lax.axis_index("hid")
    wide = (
        (dw1_ref, dw1, fw1, dw1_o), (dw2_ref, dw2, fw2, dw2_o), (dwq_ref, dwq, fwq, dwq_o),
        (dwk_ref, dwk, fwk, dwk_o), (dwv_ref, dwv, fwv, dwv_o), (dwo_ref, dwo, fwo, dwo_o),
        (tgrad_ref, tgrad, tgrad, tgrad_o), (output_ref, output, output, output_o),
    )
    parts = 4

    def piece(ref, p):
        rows = ref.shape[0] // parts
        return ref.at[pl.ds(pl.multiple_of(p * rows, rows), rows), :]

    def load(k, p):
        return pltpu.make_async_copy(piece(wide[k][0], p), piece(wide[k][1], p), in_sem.at[k, p])

    def store(k, p):
        return pltpu.make_async_copy(piece(wide[k][2], p), piece(wide[k][3], p), out_sem.at[k, p])

    for k in range(len(wide)):
        for p in range(parts):
            load(k, p).start()

    head_all = small_ref[:, width : 2 * width]
    for ref, row in ((ob_o, 6), (ag_o, 4), (as_o, 5), (db_o, 3), (fg_o, 0), (fs_o, 1)):
        ref[...] = small_ref[row : row + 1, 0:width]
    qb_o[...] = head_all[1:2, :]
    vb_o[...] = head_all[3:4, :]
    b1_o[...] = unit_ref[1:2, :]
    keeps = [keep_prob(ref[...]) for ref in (ha_ref, ua_ref, wa_ref)]
    heads_kept, units_kept, dims_kept = [jnp.sum(k, axis=1, keepdims=True) for k in keeps]
    full_size = 4.0 * D * D + 2.0 * D * FF
    gap = 1.0 - (4.0 * HD * heads_kept * dims_kept + 2.0 * units_kept * dims_kept) / full_size - TARGET
    pull = -(lane_of(mult_ref[...], 0) + 2.0 * lane_of(mult_ref[...], 1) * gap) / full_size
    slot = lax.broadcasted_iota(jnp.int32, (1, 2), 1)
    mult_o[...] = mult_ref[...] + ASCENT * jnp.where(slot == 0, gap, gap * gap)

    def pulled(alpha, factor):
        k = keep_prob(alpha)
        return pull * factor * k * (1.0 - k)

    unit_alpha = part_of(ua_ref, rank, units)
    ua_o[...] = unit_ref[0:1, :] * gate_slope(un_ref[...], unit_alpha) + pulled(unit_alpha, 2.0 * dims_kept)
    width_alpha = part_of(wa_ref, rank, width)
    wa_o[...] = small_ref[2:3, 0:width] * gate_slope(wn_ref[...], width_alpha) + pulled(
        width_alpha, 4.0 * HD * heads_kept + 2.0 * units_kept
    )
    noise_row, alpha_row = head_row(hn_ref, ha_ref, rank, heads)
    lanes = lax.broadcasted_iota(jnp.int32, (1, width), 1)
    per_lane = head_all[0:1, :] * gate_slope(noise_row, alpha_row)
    head_pulled = pulled(alpha_row, 4.0 * HD * dims_kept) * (1.0 / HD)
    for h in range(heads):
        here = (lanes >= h * HD) & (lanes < (h + 1) * HD)
        ha_o[:, h : h + 1] = jnp.sum(jnp.where(here, per_lane + head_pulled, 0.0), axis=1, keepdims=True)
    live = jnp.sum(len_ref[...].astype(F32), axis=1, keepdims=True)
    mse_o[...] = jnp.sum(small_ref[7:8, 0:width], axis=1, keepdims=True) / (live * D)

    for k, (_, low, high, _) in enumerate(wide):
        rows = low.shape[0] // parts
        for p in range(parts):
            load(k, p).wait()
            if low is not high:

                step = min(64, rows)

                def widen(i, carry, low=low, high=high, first=p * rows, step=step):
                    at = pl.ds(pl.multiple_of(first + i * step, step), step)
                    high[at, :] = low[at, :].astype(F32)
                    return carry

                lax.fori_loop(0, rows // step, widen, 0)
            store(k, p).start()
    for k in range(len(wide)):
        for p in range(parts):
            store(k, p).wait()


def hbm():
    return pl.BlockSpec(memory_space=pl.ANY)


def vmem():
    return pl.BlockSpec(memory_space=pltpu.VMEM)


def smem():
    return pl.BlockSpec(memory_space=pltpu.SMEM)


def call(kernel, name, ident, ins, outs, scratch, flops):
    return pl.pallas_call(
        kernel,
        name=name,
        out_shape=[jax.ShapeDtypeStruct(shape, dtype) for shape, dtype, _ in outs],
        in_specs=ins,
        out_specs=[spec for _, _, spec in outs],
        scratch_shapes=scratch,
        compiler_params=pltpu.CompilerParams(
            collective_id=ident, has_side_effects=True, vmem_limit_bytes=VMEM_LIMIT
        ),
        cost_estimate=pl.CostEstimate(flops=flops, bytes_accessed=30_000_000, transcendentals=0),
    )


def attend(n, seqs, heads, args):
    width, rows, nx, half = heads * HD, SLOT // n, n // 2, SLOT // 2
    tokens, owned = seqs * SLOT, seqs * rows
    v, dma = pltpu.VMEM, pltpu.SemaphoreType.DMA
    return call(
        functools.partial(attend_kernel, n, seqs, heads),
        "attend",
        0,
        [smem()] + [hbm()] * 3 + [vmem()] * 10 + [hbm()] * 3 + [vmem()] * 2 + [hbm()],
        [
            ((tokens, D), BF, hbm()),
            ((tokens, 3 * width), BF, hbm()),
            ((seqs, heads, SLOT, SLOT), BF, hbm()),
            ((tokens, width), F32, hbm()),
            ((tokens, width), BF, hbm()),
            ((owned, D), F32, hbm()),
            ((owned, D), F32, hbm()),
            ((owned, 128), F32, hbm()),
            ((owned, D), BF, hbm()),
            ((8, D), F32, vmem()),
            ((seqs, rows, D), BF, hbm()),
            ((1, width), F32, vmem()),
        ],
        [
            v((tokens, D), BF),
            v((D, 3 * width), BF),
            v((width, D), BF),
            v((tokens, 3 * width), BF),
            v((seqs, heads, SLOT, SLOT), BF),
            v((tokens, width), F32),
            v((tokens, width), BF),
            v((seqs, nx, rows, D), F32),
            v((seqs, nx, rows, D), BF),
            v((seqs, nx, rows, D), BF),
            v((seqs, nx - 1, rows, D), BF),
            v((seqs, nx - 1, rows, D), BF),
            v((owned, D), F32),
            v((owned, D), F32),
            v((owned, 128), F32),
            v((owned, D), BF),
            v((8, D), F32),
            v((seqs, rows, D), BF),
            v((tokens, width), BF),
            v((tokens, width), BF),
            v((seqs, n, rows, width), BF),
            v((8, width), F32),
            v((SLOT, SLOT), F32),
            dma((9,)),
            dma((seqs, 9)),
            dma((n - 1,)),
            dma((n - 1,)),
            dma((n - 1,)),
            dma((n - 1,)),
        ]
        + gather_sems(seqs, nx)
        + reduce_sems(seqs, nx),
        10_000_000_000,
    )(*args)


def feed(n, seqs, units, args):
    rows, nx = SLOT // n, n // 2
    tokens, owned = seqs * SLOT, seqs * rows
    v, dma = pltpu.VMEM, pltpu.SemaphoreType.DMA
    return call(
        functools.partial(feed_kernel, n, seqs, units),
        "feed",
        1,
        [smem(), hbm(), hbm(), hbm(), hbm(), vmem(), hbm(), hbm(), vmem(), hbm(), vmem(), vmem()],
        [
            ((owned, D), BF, hbm()),
            ((owned, D), BF, hbm()),
            ((owned, D), F32, hbm()),
            ((D, units), BF, hbm()),
            ((units, D), BF, hbm()),
            ((8, D), F32, vmem()),
            ((2, units), F32, vmem()),
        ],
        [
            v((tokens, D), BF),
            v((tokens, D), BF),
            v((D, units), BF),
            v((units, D), BF),
            v((tokens, units), BF),
            v((tokens, units), BF),
            v((tokens, units), BF),
            v((seqs, nx, rows, D), F32),
            v((seqs, nx, rows, D), BF),
            v((seqs, nx, rows, D), BF),
            v((seqs, nx - 1, rows, D), BF),
            v((seqs, nx - 1, rows, D), BF),
            v((owned, D), F32),
            v((owned, D), F32),
            v((owned, 128), F32),
            v((owned, D), BF),
            v((owned, D), F32),
            v((owned, D), BF),
            v((owned, D), BF),
            v((owned, D), BF),
            v((owned, D), F32),
            v((SLOT, NB), F32),
            v((D // NB, NB, D), BF),
            v((7, 8, D), F32),
            v((2, 8, units), F32),
            v((1, units), F32),
            dma((6,)),
            dma((seqs, 3)),
            dma((2, D // NB)),
        ]
        + (gather_sems(seqs, nx) + reduce_sems(seqs, nx)) * 2,
        30_000_000_000,
    )(*args)


def attend_back(n, seqs, heads, units, size, args):
    width, rows, nx = heads * HD, SLOT // n, n // 2
    tokens, owned = seqs * SLOT, seqs * rows
    v, dma = pltpu.VMEM, pltpu.SemaphoreType.DMA
    return call(
        functools.partial(attend_back_kernel, n, seqs, heads, size),
        "attend_back",
        2,
        [hbm()] * 14 + [vmem()],
        [
            ((tokens, width), F32, hbm()),
            ((D, 3 * width), BF, hbm()),
            ((width, D), BF, hbm()),
            ((D, units), BF, hbm()),
            ((units, D), BF, hbm()),
            ((seqs, n, rows, width), BF, hbm()),
            ((8, width), F32, vmem()),
        ],
        [
            v((tokens, D), BF),
            v((owned, D), F32),
            v((tokens, D), BF),
            v((tokens, 3 * width), BF),
            v((seqs, heads, SLOT, SLOT), BF),
            v((tokens, width), F32),
            v((tokens, width), BF),
            v((D, 3 * width), BF),
            v((width, D), BF),
            v((SLOT, width), BF),
            v((tokens, 3 * width), BF),
            v((SLOT, SLOT), F32),
            v((SLOT, SLOT), BF),
            v((3, SLOT, width), F32),
            v((SLOT, width), F32),
            v((seqs, nx, SLOT, width), F32),
            v((seqs, nx, SLOT, width), BF),
            v((seqs, nx, SLOT, width), BF),
            v((seqs, nx - 1, SLOT, width), BF),
            v((seqs, nx - 1, SLOT, width), BF),
            v((tokens, width), F32),
            v((D // NB, NB, 3 * width), BF),
            v((width, D), BF),
            v((seqs, n, rows, width), BF),
            v((4, 8, width), F32),
            v((D, units), BF),
            v((units, D), BF),
            dma((15,)),
            dma((seqs,)),
            dma((D // NB,)),
            dma((n - 1,)),
            dma((n - 1,)),
        ]
        + gather_sems(seqs, nx)
        + reduce_sems(seqs, nx)
        + ring_scratch((D, units), size) * 2
        + ring_scratch((units, D), size) * 2,
        20_000_000_000,
    )(*args)


def settle(n, size, seqs, width, units, args):
    v, dma = pltpu.VMEM, pltpu.SemaphoreType.DMA
    tokens = seqs * SLOT
    return call(
        functools.partial(settle_kernel, n, size, seqs),
        "settle",
        3,
        [smem()] + [hbm()] * 4 + [vmem()] * 3,
        [((D, width), BF, hbm())] * 3
        + [((width, D), BF, hbm()), ((8, 2 * width), F32, vmem()), ((2, units), F32, vmem())],
        [
            v((D, width), BF),
            v((D, width), BF),
            v((D, width), BF),
            v((width, D), BF),
            v((tokens, width), BF),
            v((tokens, width), BF),
            v((8, D), F32),
            v((8, 2 * width), F32),
            v((n - 1, 8, width), F32),
            v((size - 1, 8, 2 * width), F32),
            v((size - 1, 2, units), F32),
            dma((6,)),
            dma((n - 1,)),
            dma((n - 1,)),
        ]
        + [dma((size - 1,))] * 4
        + ring_scratch((D, width), size) * 6
        + ring_scratch((width, D), size) * 2,
        1_000_000_000,
    )(*args)


def complete(n, heads, units, tokens, args):
    v, dma, width = pltpu.VMEM, pltpu.SemaphoreType.DMA, heads * HD
    shapes = [(D, units), (units, D), (D, width), (D, width), (D, width), (width, D)]
    rows = [(width,)] * 8 + [(units,), (heads,), (units,), (width,), (1,), (2,)]
    return pl.pallas_call(
        functools.partial(complete_kernel, n, heads, units),
        name="complete",
        out_shape=[jax.ShapeDtypeStruct(shape, F32) for shape in shapes]
        + [jax.ShapeDtypeStruct((tokens, width), F32), jax.ShapeDtypeStruct((tokens, width), BF)]
        + [jax.ShapeDtypeStruct((1, count), F32) for (count,) in rows],
        in_specs=[hbm()] * 8 + [vmem()] * 10,
        out_specs=[hbm()] * 8 + [vmem()] * len(rows),
        scratch_shapes=[v(shape, BF) for shape in shapes]
        + [v((tokens, width), F32), v((tokens, width), BF)]
        + [v(shape, F32) for shape in shapes]
        + [dma((8, 4))] * 2,
        compiler_params=pltpu.CompilerParams(vmem_limit_bytes=VMEM_LIMIT),
        cost_estimate=pl.CostEstimate(flops=10_000_000, bytes_accessed=24_000_000, transcendentals=0),
    )(*args)


def on_device(
    n,
    size,
    tokens,
    query_weight,
    query_bias,
    key_weight,
    value_weight,
    value_bias,
    output_weight,
    output_bias,
    attention_gain,
    attention_shift,
    inner_weight,
    inner_bias,
    down_weight,
    down_bias,
    final_gain,
    final_shift,
    head_alpha,
    unit_alpha,
    width_alpha,
    multipliers,
    head_noise,
    unit_noise,
    width_noise,
    lengths,
    teacher,
    upstream,
):
    row_count, width = tokens.shape
    heads = width // HD
    units = inner_weight.shape[1]
    seqs = row_count // SLOT
    rows = SLOT // n
    flat = lambda vector: vector.reshape(1, vector.shape[0])
    head_alpha, unit_alpha, width_alpha = flat(head_alpha), flat(unit_alpha), flat(width_alpha)
    head_noise, unit_noise, width_noise = flat(head_noise), flat(unit_noise), flat(width_noise)
    full, qkv, prob, ctx, gat, nrm, pre, rstd, mid, par, change_rows, gate_row = attend(
        n,
        seqs,
        heads,
        (
            lengths,
            tokens,
            upstream,
            teacher,
            flat(output_bias),
            flat(attention_gain),
            flat(attention_shift),
            flat(down_bias),
            flat(final_gain),
            flat(final_shift),
            width_noise,
            width_alpha,
            head_noise,
            head_alpha,
            query_weight,
            key_weight,
            value_weight,
            flat(query_bias),
            flat(value_bias),
            output_weight,
        ),
    )
    out_rows, d_low, d_res, dw_inner, dw_down, row_sums, unit_sums = feed(
        n,
        seqs,
        units,
        (
            lengths,
            mid,
            nrm,
            pre,
            rstd,
            par,
            change_rows.reshape(seqs * rows, D),
            inner_weight,
            flat(inner_bias),
            down_weight,
            unit_noise,
            unit_alpha,
        ),
    )
    tokens_grad, dw_qkv, dw_o, dw_inner, dw_down, output, head_sums = attend_back(
        n,
        seqs,
        heads,
        units,
        size,
        (
            d_low,
            d_res,
            full,
            qkv,
            prob,
            ctx,
            gat,
            query_weight,
            key_weight,
            value_weight,
            output_weight,
            dw_inner,
            dw_down,
            out_rows.reshape(seqs, rows, D),
            gate_row,
        ),
    )
    output = output.reshape(row_count, width)
    dw_q, dw_k, dw_v, dw_o, small, unit_all = settle(
        n,
        size,
        seqs,
        width,
        units,
        (lengths, dw_qkv, dw_o, output, teacher, row_sums, unit_sums, head_sums),
    )
    dw_inner, dw_down, dw_q, dw_k, dw_v, dw_o, tokens_grad, output, *vectors = complete(
        n,
        heads,
        units,
        row_count,
        (
            dw_inner,
            dw_down,
            dw_q,
            dw_k,
            dw_v,
            dw_o,
            tokens_grad,
            output,
            small,
            unit_all,
            head_alpha,
            unit_alpha,
            width_alpha,
            flat(multipliers),
            head_noise,
            unit_noise,
            width_noise,
            flat(lengths),
        ),
    )
    qb, vb, ob, ag, shift, db, fg, fs, b1, ha, ua, wa, mse, mult = [v.reshape(v.shape[1]) for v in vectors]
    return (
        output,
        tokens_grad,
        dw_q,
        qb,
        dw_k,
        dw_v,
        vb,
        dw_o,
        ob,
        ag,
        shift,
        dw_inner,
        b1,
        dw_down,
        db,
        fg,
        fs,
        ha,
        ua,
        wa,
        mse.reshape(()),
        mult,
    )


def solution(mesh):
    tall, wide, vec, rep = P("dp", "hid"), P(None, "hid"), P("hid"), P()
    deep = P("hid", None)
    return jax.shard_map(
        functools.partial(on_device, mesh.shape["hid"], mesh.shape["dp"]),
        mesh=mesh,
        in_specs=(tall, wide, vec, wide, wide, vec, deep, vec, vec, vec, wide, vec, deep)
        + (vec,) * 3
        + (rep,) * 4
        + (vec,) * 3
        + (rep, tall, tall),
        out_specs=(tall, tall, wide, vec, wide, wide, vec, deep, vec, vec, vec, wide, vec, deep)
        + (vec,) * 6
        + (rep, rep),
        check_vma=False,
    )
```

```python
import functools
import math

import jax
import jax.numpy as jnp
from jax import lax
from jax.experimental import pallas as pl
from jax.experimental.pallas import tpu as pltpu
from jax.sharding import PartitionSpec as P

D = 1024
HD = 64
FF = 4096
SLOT = 512

BETA = 2.0 / 3.0
GAMMA = -0.1
ZETA = 1.1
TARGET = 0.7
ASCENT = 1.0
EPS = 1e-12
MASKED = -1000000000.0
ROOT_HALF = 0.7071067811865476
ROOT_TWO_PI = 2.5066282746310002

MESH = pl.DeviceIdType.MESH
VMEM_LIMIT = 66_000_000
BF = jnp.bfloat16
F32 = jnp.float32
NB = 256
RB = 16


def gate_value(noise, alpha):
    logits = (jnp.log(noise) - jnp.log(1.0 - noise) + alpha) / BETA
    stretched = jax.nn.sigmoid(logits) * (ZETA - GAMMA) + GAMMA
    return jnp.clip(stretched, 0.0, 1.0)


def gate_slope(noise, alpha):
    s = jax.nn.sigmoid((jnp.log(noise) - jnp.log(1.0 - noise) + alpha) / BETA)
    stretched = s * (ZETA - GAMMA) + GAMMA
    free = (stretched > 0.0) & (stretched < 1.0)
    return jnp.where(free, (ZETA - GAMMA) / BETA * s * (1.0 - s), 0.0)


def keep_prob(alpha):
    return jax.nn.sigmoid(alpha - BETA * math.log(-GAMMA / ZETA))


def lane_of(row, place):
    lanes = lax.broadcasted_iota(jnp.int32, row.shape, 1)
    return jnp.sum(jnp.where(lanes == place, row, 0.0), axis=1, keepdims=True)


def head_row(noise_ref, alpha_ref, rank, heads):
    lanes = lax.broadcasted_iota(jnp.int32, (1, heads * HD), 1)
    noise = jnp.full((1, heads * HD), 0.5, F32)
    alpha = jnp.zeros((1, heads * HD), F32)
    for h in range(heads):
        here = (lanes >= h * HD) & (lanes < (h + 1) * HD)
        noise = jnp.where(here, lane_of(noise_ref[...], h), noise)
        alpha = jnp.where(here, lane_of(alpha_ref[...], rank * heads + h), alpha)
    return noise, alpha


def part_of(ref, rank, width):
    return ref[:, pl.ds(pl.multiple_of(rank * width, width), width)]


def nn(a, b):
    return jnp.dot(a, b, preferred_element_type=F32)


def nt(a, b):
    return lax.dot_general(a, b, (((1,), (1,)), ((), ())), preferred_element_type=F32)


def tn(a, b):
    return lax.dot_general(a, b, (((0,), (0,)), ((), ())), preferred_element_type=F32)


def fold(values):
    return jnp.sum(values.reshape(values.shape[0] // 8, 8, values.shape[1]), axis=0)


class Group:
    def __init__(self, n):
        self.n = n
        self.nx = n // 2
        self.me = lax.axis_index("hid")
        self.x = lax.div(self.me, 2)
        self.c = lax.rem(self.me, 2)
        self.partner = 2 * self.x + 1 - self.c

    def chip_ahead(self, j):
        return lax.rem(self.x + 1 + j, self.nx)

    def chip_behind(self, j):
        return lax.rem(self.x - 1 - j + self.nx, self.nx)

    def slot(self, h):
        return lax.rem(h, 2) * self.nx + lax.div(h, 2)

    def all_peers(self):
        return [{"hid": lax.rem(self.me + 1 + i, self.n)} for i in range(self.n - 1)]

    def near_peers(self):
        near = [self.partner] + [2 * self.chip_ahead(j) + self.c for j in range(self.nx - 1)]
        return [{"hid": peer} for peer in near]


def remote(src, dst, send_sem, recv_sem, to):
    return pltpu.make_async_remote_copy(
        src_ref=src,
        dst_ref=dst,
        send_sem=send_sem,
        recv_sem=recv_sem,
        device_id=to if isinstance(to, dict) else {"hid": to},
        device_id_type=MESH,
    )


def gather_sems(seqs, nx):
    wide = pltpu.SemaphoreType.DMA((seqs, nx - 1))
    return [wide] * 4 + [pltpu.SemaphoreType.DMA((seqs,))] * 3


def reduce_sems(seqs, nx):
    wide = pltpu.SemaphoreType.DMA((seqs, nx - 1))
    return [wide] * 2 + [pltpu.SemaphoreType.DMA((seqs,))] * 2


class Gather:
    def __init__(self, group, sems, source, region):
        self.g, self.source, self.region = group, source, region
        self.xs, self.xr, self.rs, self.rr, self.ps, self.pr, self.os = sems

    def _own(self, s):
        return pltpu.make_async_copy(self.source(s), self.region(s, self.g.me), self.os.at[s])

    def _cross(self, s, j):
        to = 2 * self.g.chip_ahead(j) + self.g.c
        return remote(
            self.source(s), self.region(s, self.g.me), self.xs.at[s, j], self.xr.at[s, j], to
        )

    def _crossed(self, s, j):
        to = 2 * self.g.chip_ahead(j) + self.g.c
        block = self.region(s, 2 * self.g.chip_behind(j) + self.g.c)
        return remote(self.source(s), block, self.xs.at[s, j], self.xr.at[s, j], to)

    def _pair(self, s):
        return remote(
            self.source(s),
            self.region(s, self.g.me),
            self.ps.at[s],
            self.pr.at[s],
            self.g.partner,
        )

    def _paired(self, s):
        block = self.region(s, self.g.partner)
        return remote(self.source(s), block, self.ps.at[s], self.pr.at[s], self.g.partner)

    def _relay(self, s, j):
        block = self.region(s, 2 * self.g.chip_behind(j) + self.g.c)
        return remote(block, block, self.rs.at[s, j], self.rr.at[s, j], self.g.partner)

    def _relayed(self, s, j):
        block = self.region(s, 2 * self.g.chip_behind(j) + 1 - self.g.c)
        return remote(block, block, self.rs.at[s, j], self.rr.at[s, j], self.g.partner)

    def start(self, s):
        for j in range(self.g.nx - 1):
            self._cross(s, j).start()
        self._pair(s).start()
        self._own(s).start()

    def relay(self, s):
        for j in range(self.g.nx - 1):
            self._crossed(s, j).wait_recv()
            self._relay(s, j).start()

    def wait(self, s):
        self._own(s).wait()
        self._paired(s).wait_recv()
        for j in range(self.g.nx - 1):
            self._relayed(s, j).wait_recv()

    def drain(self, s):
        self._pair(s).wait_send()
        for j in range(self.g.nx - 1):
            self._cross(s, j).wait_send()
            self._relay(s, j).wait_send()


class Reduce:
    def __init__(self, group, sems, psend, precv, own, xsend, xrecv):
        self.g = group
        self.psend, self.precv, self.own, self.xsend, self.xrecv = psend, precv, own, xsend, xrecv
        self.xs, self.xr, self.ps, self.pr = sems

    def _pair(self, s):
        return remote(
            self.psend.at[s], self.precv.at[s], self.ps.at[s], self.pr.at[s], self.g.partner
        )

    def _cross(self, s, j):
        to = 2 * self.g.chip_ahead(j) + self.g.c
        return remote(
            self.xsend.at[s, j], self.xrecv.at[s, j], self.xs.at[s, j], self.xr.at[s, j], to
        )

    def start(self, s):
        self._pair(s).start()

    def cross(self, s):
        self._pair(s).wait()
        rows = self.own.shape[2]
        for j in range(self.g.nx - 1):
            chip = self.g.chip_ahead(j)

            def add(i, carry, chip=chip, j=j):
                at = pl.ds(pl.multiple_of(i * RB, RB), RB)
                total = self.own[s, chip, at, :] + self.precv[s, chip, at, :].astype(F32)
                self.xsend[s, j, at, :] = total.astype(BF)
                return carry

            lax.fori_loop(0, rows // RB, add, 0)
            self._cross(s, j).start()

    def arrive(self, s):
        for j in range(self.g.nx - 1):
            self._cross(s, j).wait()

    def total(self, s, at):
        total = self.own[s, self.g.x, at, :] + self.precv[s, self.g.x, at, :].astype(F32)
        for j in range(self.g.nx - 1):
            total = total + self.xrecv[s, j, at, :].astype(F32)
        return total


class Cycle:
    def __init__(self, size):
        self.size = size
        self.me = lax.axis_index("dp")
        self.length = size // 2
        line, column = lax.div(self.me, 2), lax.rem(self.me, 2)
        self.place = line + column * (size - 1 - 2 * line)

    def device(self, place):
        column = lax.div(place, self.length)
        line = place + column * (self.size - 1 - 2 * place)
        return 2 * line + column

    def beside(self, way):
        return self.device(lax.rem(self.place + way + self.size, self.size))


def split(shape, size):
    tall = max(16, shape[0] // (2 * size))
    across = 2 * size * tall // shape[0]
    return tall, shape[1] // across, across


def ring_scratch(shape, size):
    tall, broad, _ = split(shape, size)
    step = pltpu.SemaphoreType.DMA((size - 1,))
    return [
        pltpu.VMEM((size - 1, tall, broad), BF),
        pltpu.SemaphoreType.DMA((size,)),
    ] + [step] * 4 + [pltpu.SemaphoreType.REGULAR]


class Ring:
    def __init__(self, cycle, data, target, way, scratch):
        self.cycle, self.data, self.target, self.way = cycle, data, target, way
        self.size = cycle.size
        self.recv, self.out_sem, self.ss, self.sr, self.gs, self.gr, self.free = scratch
        self.tall, self.broad, self.across = split(data.shape, self.size)
        self.to, self.frm = {"dp": cycle.beside(way)}, {"dp": cycle.beside(-way)}
        self.ticks = 2 * self.size - 1

    def block(self, number):
        place = lax.rem(self.cycle.place + self.way * number + 2 * self.size, self.size)
        index = 2 * place + (0 if self.way > 0 else 1)
        if self.across == 1:
            return pl.multiple_of(index * self.tall, self.tall), 0
        row = lax.div(index, self.across)
        column = lax.rem(index, self.across)
        return (
            pl.multiple_of(row * self.tall, self.tall),
            pl.multiple_of(column * self.broad, self.broad),
        )

    def view(self, number):
        row, column = self.block(number)
        return self.data.at[pl.ds(row, self.tall), pl.ds(column, self.broad)]

    def _add(self, t):
        return remote(self.view(-t), self.recv.at[t], self.ss.at[t], self.sr.at[t], self.to)

    def _pass(self, t):
        block = self.view(1 - t)
        return remote(block, block, self.gs.at[t], self.gr.at[t], self.to)

    def _passed(self, t):
        block = self.view(-t)
        return remote(block, block, self.gs.at[t], self.gr.at[t], self.to)

    def _sum(self, t):
        row, column = self.block(-t)

        def part(i, carry):
            at = pl.ds(pl.multiple_of(row + i * RB, RB), RB)
            cols = pl.ds(column, self.broad)
            arrived = self.recv[t - 1, pl.ds(pl.multiple_of(i * RB, RB), RB), :].astype(F32)
            self.data[at, cols] = (self.data[at, cols].astype(F32) + arrived).astype(BF)
            return carry

        lax.fori_loop(0, self.tall // RB, part, 0)

    def _out(self, number, count):
        row, column = self.block(number)
        place = self.target.at[pl.ds(row, self.tall), pl.ds(column, self.broad)]
        return pltpu.make_async_copy(self.view(number), place, self.out_sem.at[count])

    def tick(self, t):
        size = self.size

        @pl.when(t == 0)
        def _():
            self._add(0).start()

        @pl.when((t >= 1) & (t <= size - 1))
        def _():
            self._add(t - 1).wait_recv()
            self._sum(t)

        @pl.when((t >= 1) & (t < size - 1))
        def _():
            self._add(t).start()

        @pl.when((t >= 1) & (t <= size - 1))
        def _():
            self._add(t - 1).wait_send()
            pl.semaphore_signal(self.free, inc=1, device_id=self.frm, device_id_type=MESH)

        @pl.when(t == size - 1)
        def _():
            pl.semaphore_wait(self.free, 1)
            self._pass(0).start()
            self._out(1, 0).start()

        @pl.when((t > size - 1) & (t < 2 * size - 1))
        def _():
            u = t - size
            self._passed(u).wait_recv()

            @pl.when(t < 2 * size - 2)
            def _():
                pl.semaphore_wait(self.free, 1)
                self._pass(u + 1).start()

            self._out(-u, u + 1).start()

    def drain(self):
        self._out(1, 0).wait()

        def step(t, carry):
            self._pass(t).wait_send()
            self._out(-t, t + 1).wait()
            return carry

        lax.fori_loop(0, self.size - 1, step, 0)


def meet(peers):
    barrier = pltpu.get_barrier_semaphore()
    for peer in peers:
        pl.semaphore_signal(barrier, inc=1, device_id=peer, device_id_type=MESH)
    pl.semaphore_wait(barrier, len(peers))


def mean_of(values):
    return jnp.sum(values, axis=1, keepdims=True) * (1.0 / D)


def attend_kernel(n, seqs, heads, *refs):
    (
        len_ref, tok_ref, up_ref, tea_ref, ob_ref, ag_ref, as_ref, db_ref, fg_ref, fs_ref,
        wn_ref, wa_ref, hn_ref, ha_ref, wq_ref, wk_ref, wv_ref, qb_ref, vb_ref, wo_ref,
        full_o, qkv_o, prob_o, ctx_o, gat_o, nrm_o, pre_o, rstd_o, mid_o, par_o, change_o, gate_o,
        full, wqkv, wo, qkv, prob, ctx, gat, own, psend, precv, xsend, xrecv,
        nrm, pre, rstd, mid, par, chg, up, tea, change, vec, score, in_sem, out_sem, vec_send, vec_recv, ch_send, ch_recv, *sems,
    ) = refs
    g = Group(n)
    width = heads * HD
    rows = SLOT // n
    gsems, rsems = sems[:7], sems[7:]
    cols = lambda h: pl.ds(pl.multiple_of(h * width, width), width)
    seq = lambda s: pl.ds(pl.multiple_of(s * SLOT, SLOT), SLOT)
    own_rows = lambda s: pl.ds(pl.multiple_of(s * rows, rows), rows)
    ga = Gather(g, gsems, lambda s: tok_ref.at[seq(s), :], lambda s, h: full.at[seq(s), cols(h)])
    re = Reduce(g, rsems, psend, precv, own, xsend, xrecv)

    def vec_to(i):
        to = lax.rem(g.me + 1 + i, n)
        return remote(vec, par.at[:, cols(g.me)], vec_send.at[i], vec_recv.at[i], to)

    def vec_from(i):
        to = lax.rem(g.me + 1 + i, n)
        frm = lax.rem(g.me - 1 - i + n, n)
        return remote(vec, par.at[:, cols(frm)], vec_send.at[i], vec_recv.at[i], to)

    def change_to(i):
        to = lax.rem(g.me + 1 + i, n)
        return remote(
            change.at[:, g.slot(to)], chg.at[:, :, cols(g.me)], ch_send.at[i], ch_recv.at[i], to
        )

    def change_from(i):
        to = lax.rem(g.me + 1 + i, n)
        frm = lax.rem(g.me - 1 - i + n, n)
        return remote(
            change.at[:, g.slot(to)], chg.at[:, :, cols(frm)], ch_send.at[i], ch_recv.at[i], to
        )

    loads = [
        pltpu.make_async_copy(wq_ref, wqkv.at[:, pl.ds(0, width)], in_sem.at[0]),
        pltpu.make_async_copy(wk_ref, wqkv.at[:, pl.ds(width, width)], in_sem.at[1]),
        pltpu.make_async_copy(wv_ref, wqkv.at[:, pl.ds(2 * width, width)], in_sem.at[2]),
        pltpu.make_async_copy(wo_ref, wo, in_sem.at[3]),
        pltpu.make_async_copy(up_ref, up, in_sem.at[4]),
        pltpu.make_async_copy(tea_ref, tea, in_sem.at[5]),
    ]
    par_own = pltpu.make_async_copy(vec, par.at[:, cols(g.me)], in_sem.at[7])
    change_own = pltpu.make_async_copy(
        change.at[:, g.slot(g.me)], chg.at[:, :, cols(g.me)], in_sem.at[8]
    )
    chg_out = pltpu.make_async_copy(chg, change_o, in_sem.at[6])

    def sequence_outs(s):
        return [
            pltpu.make_async_copy(full.at[seq(s), :], full_o.at[seq(s), :], out_sem.at[s, 0]),
            pltpu.make_async_copy(qkv.at[seq(s), :], qkv_o.at[seq(s), :], out_sem.at[s, 1]),
            pltpu.make_async_copy(prob.at[s], prob_o.at[s], out_sem.at[s, 2]),
            pltpu.make_async_copy(ctx.at[seq(s), :], ctx_o.at[seq(s), :], out_sem.at[s, 3]),
            pltpu.make_async_copy(gat.at[seq(s), :], gat_o.at[seq(s), :], out_sem.at[s, 4]),
        ]

    def row_outs(s):
        return [
            pltpu.make_async_copy(nrm.at[own_rows(s), :], nrm_o.at[own_rows(s), :], out_sem.at[s, 5]),
            pltpu.make_async_copy(pre.at[own_rows(s), :], pre_o.at[own_rows(s), :], out_sem.at[s, 6]),
            pltpu.make_async_copy(rstd.at[own_rows(s), :], rstd_o.at[own_rows(s), :], out_sem.at[s, 7]),
            pltpu.make_async_copy(mid.at[own_rows(s), :], mid_o.at[own_rows(s), :], out_sem.at[s, 8]),
        ]

    for load in loads:
        load.start()
    for row, ref in ((0, ob_ref), (2, ag_ref), (3, as_ref), (4, db_ref), (5, fg_ref), (6, fs_ref)):
        vec[row : row + 1, :] = ref[...]
    vec[1:2, :] = gate_value(wn_ref[...], part_of(wa_ref, g.me, width))
    vec[7:8, :] = jnp.zeros((1, width), F32)
    meet(g.all_peers())

    def begin(s, carry):
        ga.start(s)
        return carry

    for i in range(n - 1):
        vec_to(i).start()
    lax.fori_loop(0, seqs, begin, 0)
    par_own.start()
    gate_row = gate_value(*head_row(hn_ref, ha_ref, g.me, heads))
    gate_o[...] = gate_row
    for load in loads:
        load.wait()

    def differ(i, carry):
        at = pl.ds(pl.multiple_of(i * 32, 32), 32)
        value = (up[at, :].astype(F32) - tea[at, :].astype(F32)).astype(BF)
        each = SLOT // n // 32
        s, q = lax.div(i, SLOT // 32), lax.rem(i, SLOT // 32)
        change[s, lax.div(q, each), pl.ds(pl.multiple_of(lax.rem(q, each) * 32, 32), 32), :] = value
        return carry

    lax.fori_loop(0, seqs * SLOT // 32, differ, 0)
    change_own.start()
    ga.relay(0)
    par_own.wait()
    for i in range(n - 1):
        vec_from(i).wait()
    par_o[...] = par[...]

    lanes = lax.broadcasted_iota(jnp.int32, (1, width), 1)
    head_lanes = [
        jnp.where((lanes >= h * HD) & (lanes < (h + 1) * HD), 1.0, 0.0).astype(BF) for h in range(heads)
    ]

    scaled_lanes = [lane * HD**-0.5 for lane in head_lanes]

    def finish(s):
        re.arrive(s)

        def block(i, carry):
            at = pl.ds(pl.multiple_of(i * RB, RB), RB)
            here = pl.ds(pl.multiple_of(s * rows + i * RB, RB), RB)
            token_row = pl.multiple_of(s * SLOT + g.slot(g.me) * rows + i * RB, RB)
            attention_pre = re.total(s, at) + par[0:1, :]
            residual = full[pl.ds(token_row, RB), :].astype(F32) + attention_pre * par[1:2, :]
            centered = residual - mean_of(residual)
            row_rstd = lax.rsqrt(mean_of(centered * centered) + EPS)
            normed = centered * row_rstd
            middle = normed * par[2:3, :] + par[3:4, :]
            nrm[here, :] = normed
            pre[here, :] = attention_pre
            rstd[here, :] = jnp.broadcast_to(row_rstd, (RB, 128))
            mid[here, :] = middle.astype(BF)
            return carry

        lax.fori_loop(0, rows // RB, block, 0)
        for copy in row_outs(s):
            copy.start()

    def sequence(s, carry):
        ga.wait(s)
        here = seq(s)
        projected = nn(full[here, :], wqkv[...])
        qkv[here, 0:width] = (projected[:, 0:width] + qb_ref[...]).astype(BF)
        qkv[here, width : 2 * width] = projected[:, width : 2 * width].astype(BF)
        qkv[here, 2 * width : 3 * width] = (projected[:, 2 * width : 3 * width] + vb_ref[...]).astype(BF)

        @pl.when(s + 1 < seqs)
        def _():
            ga.relay(s + 1)

        @pl.when(s > 0)
        def _():
            re.cross(s - 1)

        @pl.when(s == seqs - 2)
        def _():
            for i in range(n - 1):
                change_to(i).start()

        length = len_ref[lax.axis_index("dp") * seqs + s]
        bias = jnp.where(lax.broadcasted_iota(jnp.int32, (1, SLOT), 1) < length, 0.0, MASKED)
        for h in range(heads):
            score[...] = nt(qkv[here, 0:width] * scaled_lanes[h], qkv[here, width : 2 * width])

            def softmax(i, carry, h=h):
                at = pl.ds(pl.multiple_of(i * 64, 64), 64)
                scores = score[at, :] + bias
                exponent = jnp.exp(scores - jnp.max(scores, axis=1, keepdims=True))
                total = jnp.sum(exponent, axis=1, keepdims=True)
                prob[s, h, at, :] = (exponent * (1.0 / total)).astype(BF)
                return carry

            lax.fori_loop(0, SLOT // 64, softmax, 0, unroll=True)
            term = nn(prob[s, h], qkv[here, 2 * width : 3 * width] * head_lanes[h])
            ctx[here, :] = term if h == 0 else ctx[here, :] + term
        gat[here, :] = (ctx[here, :] * gate_row).astype(BF)
        for copy in sequence_outs(s):
            copy.start()
        half = SLOT // 2
        there = pl.ds(pl.multiple_of(s * SLOT + (1 - g.c) * half, half), half)
        psend[s] = nn(gat[there, :], wo[...]).astype(BF).reshape(n // 2, rows, D)
        re.start(s)
        mine = pl.ds(pl.multiple_of(s * SLOT + g.c * half, half), half)
        own[s] = nn(gat[mine, :], wo[...]).reshape(n // 2, rows, D)

        @pl.when(s > 0)
        def _():
            finish(s - 1)

        return carry

    lax.fori_loop(0, seqs, sequence, 0)
    re.cross(seqs - 1)
    change_own.wait()
    for i in range(n - 1):
        change_from(i).wait()
    chg_out.start()
    finish(seqs - 1)
    chg_out.wait()

    def end(s, carry):
        ga.drain(s)
        for copy in sequence_outs(s) + row_outs(s):
            copy.wait()
        return carry

    lax.fori_loop(0, seqs, end, 0)


def feed_kernel(n, seqs, units, *refs):
    (
        len_ref, mid_ref, nrm_ref, pre_ref, rstd_ref, par, change_ref, w1_ref, b1_ref, w2_ref, un_ref, ua_ref,
        out_o, dlow_o, dres_o, dw1_o, dw2_o, rowsum_o, unitsum_o,
        midf, dffn, w1, w2, act, inner, slope, own, psend, precv, xsend, xrecv,
        nrm, pre, rstd, change, dtwo, dsend, fout, dlow, dres, wide, grad, sums, unit_sums, ugate_ref,
        in_sem, out_sem, grad_sem, *sems,
    ) = refs
    g = Group(n)
    rows = SLOT // n
    half = SLOT // 2
    g1, r1, g2, r2 = sems[:7], sems[7:11], sems[11:18], sems[18:]
    seq = lambda s: pl.ds(pl.multiple_of(s * SLOT, SLOT), SLOT)
    own_rows = lambda s: pl.ds(pl.multiple_of(s * rows, rows), rows)
    spot = lambda s, h: pl.ds(pl.multiple_of(s * SLOT + g.slot(h) * rows, rows), rows)
    gm = Gather(g, g1, lambda s: mid_ref.at[own_rows(s), :], lambda s, h: midf.at[spot(s, h), :])
    gd = Gather(g, g2, lambda s: dsend.at[own_rows(s), :], lambda s, h: dffn.at[spot(s, h), :])
    rf = Reduce(g, r1, psend, precv, own, xsend, xrecv)
    rb = Reduce(g, r2, psend, precv, own, xsend, xrecv)
    loads = [
        pltpu.make_async_copy(w1_ref, w1, in_sem.at[0]),
        pltpu.make_async_copy(w2_ref, w2, in_sem.at[1]),
        pltpu.make_async_copy(nrm_ref, nrm, in_sem.at[2]),
        pltpu.make_async_copy(change_ref, change, in_sem.at[3]),
        pltpu.make_async_copy(pre_ref, pre, in_sem.at[4]),
        pltpu.make_async_copy(rstd_ref, rstd, in_sem.at[5]),
    ]

    meet(g.near_peers())

    def begin(s, carry):
        gm.start(s)
        return carry

    lax.fori_loop(0, seqs, begin, 0)
    for load in loads:
        load.start()
    sums[...] = jnp.zeros_like(sums)
    unit_sums[...] = jnp.zeros_like(unit_sums)
    ugate_ref[...] = gate_value(un_ref[...], part_of(ua_ref, g.me, units))
    gm.relay(0)
    for load in loads:
        load.wait()

    def finish_forward(s):
        rf.arrive(s)
        length = len_ref[lax.axis_index("dp") * seqs + s]

        def block(i, carry):
            at = pl.ds(pl.multiple_of(i * RB, RB), RB)
            here = pl.ds(pl.multiple_of(s * rows + i * RB, RB), RB)
            ffn_pre = rf.total(s, at) + par[4:5, :]
            middle = nrm[here, :] * par[2:3, :] + par[3:4, :]
            residual = middle + ffn_pre * par[1:2, :]
            centered = residual - mean_of(residual)
            row_rstd = lax.rsqrt(mean_of(centered * centered) + EPS)
            normed = centered * row_rstd
            final = normed * par[5:6, :] + par[6:7, :]
            fout[here, :] = final.astype(BF)
            place = g.slot(g.me) * rows + i * RB + lax.broadcasted_iota(jnp.int32, (RB, 1), 0)
            live = jnp.where(place < length, 1.0, 0.0)
            d_final = live * (change[here, :].astype(F32) + final)
            sums[0] += fold(d_final * normed)
            sums[1] += fold(d_final)
            d_normed = d_final * par[5:6, :]
            d_two = row_rstd * (d_normed - mean_of(d_normed) - normed * mean_of(d_normed * normed))
            sums[2] += fold(d_two * ffn_pre)
            d_ffn = d_two * par[1:2, :]
            sums[3] += fold(d_ffn)
            dtwo[here, :] = d_two
            dsend[here, :] = d_ffn.astype(BF)
            return carry

        lax.fori_loop(0, rows // RB, block, 0)
        gd.start(s)

    def forward(s, carry):
        gm.wait(s)
        here = seq(s)

        def part(b, carry):
            cols = pl.ds(pl.multiple_of(b * NB, NB), NB)
            wide[...] = nn(midf[here, :], w1[:, cols])
            bias = b1_ref[:, cols]
            gate = ugate_ref[:, cols]

            def block(i, carry):
                at = pl.ds(pl.multiple_of(i * 32, 32), 32)
                row = pl.ds(pl.multiple_of(s * SLOT + i * 32, 32), 32)
                v = wide[at, :] + bias
                phi = 0.5 * (1.0 + lax.erf(v * ROOT_HALF))
                activated = v * phi
                act[row, cols] = activated.astype(BF)
                inner[row, cols] = (activated * gate).astype(BF)
                steep = phi + v * jnp.exp(-0.5 * v * v) * (1.0 / ROOT_TWO_PI)
                slope[row, cols] = (gate * steep).astype(BF)
                return carry

            lax.fori_loop(0, SLOT // 32, block, 0)
            return carry

        lax.fori_loop(0, units // NB, part, 0)

        @pl.when(s + 1 < seqs)
        def _():
            gm.relay(s + 1)

        @pl.when(s > 0)
        def _():
            rf.cross(s - 1)

        there = pl.ds(pl.multiple_of(s * SLOT + (1 - g.c) * half, half), half)
        psend[s] = nn(inner[there, :], w2[...]).astype(BF).reshape(n // 2, rows, D)
        rf.start(s)
        mine = pl.ds(pl.multiple_of(s * SLOT + g.c * half, half), half)
        own[s] = nn(inner[mine, :], w2[...]).reshape(n // 2, rows, D)

        @pl.when(s > 1)
        def _():
            finish_forward(s - 2)

        return carry

    lax.fori_loop(0, seqs, forward, 0)
    rf.cross(seqs - 1)
    gd.relay(0)

    def row_outs(s):
        return [
            pltpu.make_async_copy(fout.at[own_rows(s), :], out_o.at[own_rows(s), :], out_sem.at[s, 0]),
            pltpu.make_async_copy(dlow.at[own_rows(s), :], dlow_o.at[own_rows(s), :], out_sem.at[s, 1]),
            pltpu.make_async_copy(dres.at[own_rows(s), :], dres_o.at[own_rows(s), :], out_sem.at[s, 2]),
        ]

    def finish_backward(s):
        rb.arrive(s)

        def block(i, carry):
            at = pl.ds(pl.multiple_of(i * RB, RB), RB)
            here = pl.ds(pl.multiple_of(s * rows + i * RB, RB), RB)
            normed = nrm[here, :]
            d_middle = dtwo[here, :] + rb.total(s, at)
            sums[4] += fold(d_middle * normed)
            sums[5] += fold(d_middle)
            d_normed = d_middle * par[2:3, :]
            d_one = rstd[here, 0:1] * (
                d_normed - mean_of(d_normed) - normed * mean_of(d_normed * normed)
            )
            sums[2] += fold(d_one * pre[here, :])
            d_attn = d_one * par[1:2, :]
            sums[6] += fold(d_attn)
            dres[here, :] = d_one
            dlow[here, :] = d_attn.astype(BF)
            return carry

        lax.fori_loop(0, rows // RB, block, 0)
        for copy in row_outs(s):
            copy.start()

    def backward(s, carry):
        gd.wait(s)
        here = seq(s)

        def part(b, carry):
            cols = pl.ds(pl.multiple_of(b * NB, NB), NB)
            wide[...] = nt(dffn[here, :], w2[cols, :])

            def block(i, sums_here):
                unit_part, bias_part = sums_here
                at = pl.ds(pl.multiple_of(i * 32, 32), 32)
                row = pl.ds(pl.multiple_of(s * SLOT + i * 32, 32), 32)
                d_inner = wide[at, :]
                d_pre = (d_inner * slope[row, cols].astype(F32)).astype(BF)
                unit_part = unit_part + fold(d_inner * act[row, cols].astype(F32))
                bias_part = bias_part + fold(d_pre.astype(F32))
                slope[row, cols] = d_pre
                return (unit_part, bias_part)

            zero = jnp.zeros((8, NB), F32)
            unit_part, bias_part = lax.fori_loop(0, SLOT // 32, block, (zero, zero))
            unit_sums[0, :, cols] += unit_part
            unit_sums[1, :, cols] += bias_part
            return carry

        lax.fori_loop(0, units // NB, part, 0)

        @pl.when(s < 2)
        def _():
            finish_forward(seqs - 2 + s)

        @pl.when(s + 1 < seqs)
        def _():
            gd.relay(s + 1)

        @pl.when(s > 0)
        def _():
            rb.cross(s - 1)

        there = pl.ds(pl.multiple_of(s * SLOT + (1 - g.c) * half, half), half)
        psend[s] = nt(slope[there, :], w1[...]).astype(BF).reshape(n // 2, rows, D)
        rb.start(s)
        mine = pl.ds(pl.multiple_of(s * SLOT + g.c * half, half), half)
        own[s] = nt(slope[mine, :], w1[...]).reshape(n // 2, rows, D)

        @pl.when(s > 1)
        def _():
            finish_backward(s - 2)

        return carry

    lax.fori_loop(0, seqs, backward, 0)
    rb.cross(seqs - 1)

    def grad_out(k, b):
        target = (dw2_o, dw1_o)[k]
        at = pl.ds(pl.multiple_of(b * NB, NB), NB)
        return pltpu.make_async_copy(grad.at[b], target.at[at, :], grad_sem.at[k, b])

    def down_grad(b, carry):
        cols = pl.ds(pl.multiple_of(b * NB, NB), NB)
        grad[b] = tn(inner[:, cols], dffn[...]).astype(BF)
        grad_out(0, b).start()
        return carry

    lax.fori_loop(0, units // NB, down_grad, 0)
    finish_backward(seqs - 2)
    for b in range(units // NB):
        grad_out(0, b).wait()

    def inner_grad(b, carry):
        cols = pl.ds(pl.multiple_of(b * NB, NB), NB)
        grad[b, :, 0:units] = tn(midf[:, cols], slope[...]).astype(BF)
        pltpu.make_async_copy(
            grad.at[b, :, pl.ds(0, units)], dw1_o.at[cols, :], grad_sem.at[1, b]
        ).start()
        return carry

    lax.fori_loop(0, D // NB, inner_grad, 0)
    finish_backward(seqs - 1)
    for k in range(7):
        rowsum_o[k : k + 1, :] = jnp.sum(sums[k], axis=0, keepdims=True)
    rowsum_o[7:8, :] = jnp.zeros((1, D), F32)
    for k in range(2):
        unitsum_o[k : k + 1, :] = jnp.sum(unit_sums[k], axis=0, keepdims=True)
    for b in range(D // NB):
        at = pl.ds(b * NB, NB)
        pltpu.make_async_copy(
            grad.at[b, :, pl.ds(0, units)], dw1_o.at[at, :], grad_sem.at[1, b]
        ).wait()

    def end(s, carry):
        gm.drain(s)
        gd.drain(s)
        for copy in row_outs(s):
            copy.wait()
        return carry

    lax.fori_loop(0, seqs, end, 0)


def attend_back_kernel(n, seqs, heads, size, *refs):
    (
        dlow_ref, dres_ref, full_ref, qkv_ref, prob_ref, ctx_ref, gat_ref,
        wq_ref, wk_ref, wv_ref, wo_ref, dw1_ref, dw2_ref, out_ref, gate_ref,
        tgrad_o, dwqkv_o, dwo_o, dw1_o, dw2_o, output_o, sums_o,
        dattn, dres, full, qkv, prob, ctx, gat, wqkv, wo, dctx, dqkv, dprob, dscore, acc,
        block_f, own, psend, precv, xsend, xrecv, tgrad, grad, gwo, moved, sums, dw1, dw2,
        in_sem, out_sem, grad_sem, move_send, move_recv, *sems,
    ) = refs
    g = Group(n)
    cycle = Cycle(size)
    rings = []
    for k, (data, target) in enumerate(((dw1, dw1_o), (dw2, dw2_o))):
        for way in (1, -1):
            i = 11 + 7 * len(rings)
            rings.append(Ring(cycle, data, target, way, sems[i : i + 7]))
    ticks = rings[0].ticks

    def tick(t, which):
        for ring in rings[2 * which : 2 * which + 2]:
            ring.tick(t)

    def move_to(i):
        to = lax.rem(g.me + 1 + i, n)
        return remote(
            out_ref.at[:, :, cols_of(to)], moved.at[:, g.slot(g.me)], move_send.at[i], move_recv.at[i], to
        )

    def move_from(i):
        to = lax.rem(g.me + 1 + i, n)
        frm = lax.rem(g.me - 1 - i + n, n)
        return remote(
            out_ref.at[:, :, cols_of(to)], moved.at[:, g.slot(frm)], move_send.at[i], move_recv.at[i], to
        )

    width = heads * HD
    rows = SLOT // n
    gsems, rsems = sems[:7], sems[7:11]
    cols_of = lambda h: pl.ds(pl.multiple_of(h * width, width), width)
    seq = lambda s: pl.ds(pl.multiple_of(s * SLOT, SLOT), SLOT)
    own_rows = lambda s: pl.ds(pl.multiple_of(s * rows, rows), rows)
    spot = lambda s, h: pl.ds(pl.multiple_of(s * SLOT + g.slot(h) * rows, rows), rows)
    ga = Gather(g, gsems, lambda s: dlow_ref.at[own_rows(s), :], lambda s, h: dattn.at[spot(s, h), :])
    re = Reduce(g, rsems, psend, precv, own, xsend, xrecv)
    loads = [
        pltpu.make_async_copy(wo_ref, wo, in_sem.at[0]),
        pltpu.make_async_copy(ctx_ref, ctx, in_sem.at[1]),
        pltpu.make_async_copy(qkv_ref, qkv, in_sem.at[2]),
        pltpu.make_async_copy(prob_ref, prob, in_sem.at[3]),
        pltpu.make_async_copy(wq_ref, wqkv.at[:, pl.ds(0, width)], in_sem.at[4]),
        pltpu.make_async_copy(wk_ref, wqkv.at[:, pl.ds(width, width)], in_sem.at[5]),
        pltpu.make_async_copy(wv_ref, wqkv.at[:, pl.ds(2 * width, width)], in_sem.at[6]),
        pltpu.make_async_copy(dres_ref, dres, in_sem.at[7]),
        pltpu.make_async_copy(full_ref, full, in_sem.at[8]),
        pltpu.make_async_copy(gat_ref, gat, in_sem.at[9]),
        pltpu.make_async_copy(
            out_ref.at[:, :, cols_of(g.me)], moved.at[:, g.slot(g.me)], in_sem.at[11]
        ),
    ]
    grads_in = [
        pltpu.make_async_copy(dw1_ref, dw1, in_sem.at[12]),
        pltpu.make_async_copy(dw2_ref, dw2, in_sem.at[13]),
    ]
    meet(g.all_peers() + [{"dp": cycle.beside(1)}, {"dp": cycle.beside(-1)}])
    for load in grads_in:
        load.start()

    def begin(s, carry):
        ga.start(s)
        return carry

    lax.fori_loop(0, seqs, begin, 0)
    for load in loads:
        load.start()
    sums[...] = jnp.zeros_like(sums)
    for load in grads_in:
        load.wait()
    tick(0, 0)
    tick(0, 1)
    ga.relay(0)
    for load in loads[:8]:
        load.wait()
    tick(1, 0)
    tick(1, 1)

    lanes = lax.broadcasted_iota(jnp.int32, (1, width), 1)
    head_lanes = [
        jnp.where((lanes >= h * HD) & (lanes < (h + 1) * HD), 1.0, 0.0).astype(BF) for h in range(heads)
    ]

    def out(s):
        return pltpu.make_async_copy(tgrad.at[seq(s), :], tgrad_o.at[seq(s), :], out_sem.at[s])

    def finish(s):
        re.arrive(s)

        def block(i, carry):
            at = pl.ds(pl.multiple_of(i * 32, 32), 32)
            tgrad[pl.ds(pl.multiple_of(s * SLOT + i * 32, 32), 32), :] = re.total(s, at)
            return carry

        lax.fori_loop(0, SLOT // 32, block, 0)
        out(s).start()

    def token_block(s, h):
        cols = pl.ds(pl.multiple_of(h * width, width), width)
        block_f[...] = nt(dqkv[seq(s), :], wqkv[cols, :])
        mine = pl.ds(pl.multiple_of(g.slot(g.me) * rows, rows), rows)
        block_f[mine, :] += dres[own_rows(s), cols]

    def sequence(s, carry):
        ga.wait(s)
        here = seq(s)
        d_gated = nt(dattn[here, :], wo[...])
        sums[0] += fold(d_gated * ctx[here, :])
        dctx[...] = (d_gated * gate_ref[...]).astype(BF)
        first = 2 + s * (heads + 2) // 2
        tick(first, 0)

        @pl.when(s + 1 < seqs)
        def _():
            ga.relay(s + 1)

        @pl.when(s > 0)
        def _():
            re.cross(s - 1)

        for h in range(heads):
            d_context = dctx[...] * head_lanes[h]
            dprob[...] = nt(d_context, qkv[here, 2 * width : 3 * width])

            def softmax(i, carry, h=h):
                at = pl.ds(pl.multiple_of(i * 64, 64), 64)
                p = prob[s, h, at, :].astype(F32)
                weighted = p * dprob[at, :]
                total = jnp.sum(weighted, axis=1, keepdims=True)
                dscore[at, :] = (weighted - p * total).astype(BF)
                return carry

            lax.fori_loop(0, SLOT // 64, softmax, 0, unroll=True)
            tick(first + (h + 1) // 2, (h + 1) % 2)
            terms = (
                nn(dscore[...], qkv[here, width : 2 * width] * head_lanes[h]),
                tn(dscore[...], qkv[here, 0:width] * head_lanes[h]),
                tn(prob[s, h], d_context),
            )
            for k in range(3):
                acc[k] = terms[k] if h == 0 else acc[k] + terms[k]
        scales = (HD**-0.5, HD**-0.5, 1.0)
        for k in range(3):
            rounded = (acc[k] * scales[k]).astype(BF)
            dqkv[here, k * width : (k + 1) * width] = rounded
            sums[1 + k] += fold(rounded.astype(F32))
        for chip in range(n // 2):
            token_block(s, 2 * chip + 1 - g.c)
            psend[s, chip] = block_f[...].astype(BF)
        re.start(s)
        tick(first + (heads + 1) // 2, 1)
        for chip in range(n // 2):
            token_block(s, 2 * chip + g.c)
            own[s, chip] = block_f[...]

        @pl.when(s > 0)
        def _():
            finish(s - 1)

        return carry

    lax.fori_loop(0, seqs, sequence, 0)
    re.cross(seqs - 1)
    for i in range(n - 1):
        move_to(i).start()
    for load in loads[8:]:
        load.wait()

    def grad_out(b):
        at = pl.ds(pl.multiple_of(b * NB, NB), NB)
        return pltpu.make_async_copy(grad.at[b], dwqkv_o.at[at, :], grad_sem.at[b])

    def token_grad(b, carry):
        cols = pl.ds(pl.multiple_of(b * NB, NB), NB)
        grad[b] = tn(full[:, cols], dqkv[...]).astype(BF)
        grad_out(b).start()
        return carry

    lax.fori_loop(0, D // NB, token_grad, 0)
    gwo[...] = tn(gat[...], dattn[...]).astype(BF)
    gwo_out = pltpu.make_async_copy(gwo, dwo_o, in_sem.at[10])
    gwo_out.start()
    finish(seqs - 1)
    for i in range(n - 1):
        move_from(i).wait()
    moved_out = pltpu.make_async_copy(moved, output_o, in_sem.at[14])
    moved_out.start()
    for k in range(4):
        sums_o[k : k + 1, :] = jnp.sum(sums[k], axis=0, keepdims=True)
    sums_o[4:8, :] = jnp.zeros((4, width), F32)
    gwo_out.wait()

    def rest(t, carry):
        tick(t, 0)
        tick(t, 1)
        return carry

    lax.fori_loop(2 + seqs * (heads + 2) // 2, ticks, rest, 0)
    moved_out.wait()
    for ring in rings:
        ring.drain()

    def end_grad(b, carry):
        grad_out(b).wait()
        return carry

    lax.fori_loop(0, D // NB, end_grad, 0)

    def end(s, carry):
        ga.drain(s)
        out(s).wait()
        return carry

    lax.fori_loop(0, seqs, end, 0)


def settle_kernel(n, size, seqs, *refs):
    (
        len_ref, dwqkv_ref, dwo_ref, output_ref, teacher_ref, row_ref, unit_ref, head_ref,
        dwq_o, dwk_o, dwv_o, dwo_o, small_o, units_o,
        dwq, dwk, dwv, dwo, output, teacher, parts, small, rbuf, sbuf, ubuf,
        in_sem, r_send, r_recv, s_send, s_recv, u_send, u_recv, *sems,
    ) = refs
    g = Group(n)
    cycle = Cycle(size)
    width = head_ref.shape[1]
    cols = lambda h: pl.ds(pl.multiple_of(h * width, width), width)
    rings = []
    for data, target in ((dwq, dwq_o), (dwk, dwk_o), (dwv, dwv_o), (dwo, dwo_o)):
        for way in (1, -1):
            i = 7 * len(rings)
            rings.append(Ring(cycle, data, target, way, sems[i : i + 7]))

    def tick(t):
        for ring in rings:
            ring.tick(t)

    def row_to(i):
        to = lax.rem(g.me + 1 + i, n)
        return remote(parts.at[:, cols(to)], rbuf.at[i], r_send.at[i], r_recv.at[i], to)

    def small_to(i):
        to = {"dp": lax.rem(cycle.me + 1 + i, size)}
        return remote(small, sbuf.at[i], s_send.at[i], s_recv.at[i], to)

    def units_to(i):
        to = {"dp": lax.rem(cycle.me + 1 + i, size)}
        return remote(unit_ref, ubuf.at[i], u_send.at[i], u_recv.at[i], to)

    loads = [
        pltpu.make_async_copy(dwqkv_ref.at[:, pl.ds(0, width)], dwq, in_sem.at[0]),
        pltpu.make_async_copy(dwqkv_ref.at[:, pl.ds(width, width)], dwk, in_sem.at[1]),
        pltpu.make_async_copy(dwqkv_ref.at[:, pl.ds(2 * width, width)], dwv, in_sem.at[2]),
        pltpu.make_async_copy(dwo_ref, dwo, in_sem.at[3]),
        pltpu.make_async_copy(output_ref, output, in_sem.at[4]),
        pltpu.make_async_copy(teacher_ref, teacher, in_sem.at[5]),
    ]
    for load in loads:
        load.start()
    meet(g.all_peers() + [{"dp": lax.rem(cycle.me + 1 + i, size)} for i in range(size - 1)])
    for load in loads[:4]:
        load.wait()
    tick(0)
    for load in loads[4:]:
        load.wait()
    for i in range(size - 1):
        units_to(i).start()

    def sequence(s, total):
        length = len_ref[cycle.me * seqs + s]

        def block(i, total):
            at = pl.ds(pl.multiple_of(s * SLOT + i * 32, 32), 32)
            place = i * 32 + lax.broadcasted_iota(jnp.int32, (32, 1), 0)
            differ = output[at, :].astype(F32) - teacher[at, :].astype(F32)
            return total + fold(jnp.where(place < length, differ * differ, 0.0))

        return lax.fori_loop(0, SLOT // 32, block, total)

    squares = lax.fori_loop(0, seqs, sequence, jnp.zeros((8, width), F32))
    parts[...] = row_ref[...]
    for h in range(n):
        parts[7:8, h * width : (h + 1) * width] = jnp.sum(squares, axis=0, keepdims=True)
    for i in range(n - 1):
        row_to(i).start()
    tick(1)
    total = parts[:, cols(g.me)]
    for i in range(n - 1):
        row_to(i).wait()
        total = total + rbuf[i]
    small[:, 0:width] = total
    small[:, width : 2 * width] = head_ref[...]
    for i in range(size - 1):
        small_to(i).start()

    def rest(t, carry):
        tick(t)
        return carry

    lax.fori_loop(2, rings[0].ticks, rest, 0)
    small_sum = small[...]
    unit_sum = unit_ref[...]
    for i in range(size - 1):
        small_to(i).wait()
        units_to(i).wait()
        small_sum = small_sum + sbuf[i]
        unit_sum = unit_sum + ubuf[i]
    small_o[...] = small_sum
    units_o[...] = unit_sum
    for ring in rings:
        ring.drain()


def complete_kernel(n, heads, units, *refs):
    (
        dw1_ref, dw2_ref, dwq_ref, dwk_ref, dwv_ref, dwo_ref, tgrad_ref, output_ref,
        small_ref, unit_ref, ha_ref, ua_ref, wa_ref, mult_ref, hn_ref, un_ref, wn_ref, len_ref,
        dw1_o, dw2_o, dwq_o, dwk_o, dwv_o, dwo_o, tgrad_o, output_o,
        qb_o, vb_o, ob_o, ag_o, as_o, db_o, fg_o, fs_o, b1_o, ha_o, ua_o, wa_o, mse_o, mult_o,
        dw1, dw2, dwq, dwk, dwv, dwo, tgrad, output, fw1, fw2, fwq, fwk, fwv, fwo, in_sem, out_sem,
    ) = refs
    width = heads * HD
    rank = lax.axis_index("hid")
    wide = (
        (dw1_ref, dw1, fw1, dw1_o), (dw2_ref, dw2, fw2, dw2_o), (dwq_ref, dwq, fwq, dwq_o),
        (dwk_ref, dwk, fwk, dwk_o), (dwv_ref, dwv, fwv, dwv_o), (dwo_ref, dwo, fwo, dwo_o),
        (tgrad_ref, tgrad, tgrad, tgrad_o), (output_ref, output, output, output_o),
    )
    parts = 4

    def piece(ref, p):
        rows = ref.shape[0] // parts
        return ref.at[pl.ds(pl.multiple_of(p * rows, rows), rows), :]

    def load(k, p):
        return pltpu.make_async_copy(piece(wide[k][0], p), piece(wide[k][1], p), in_sem.at[k, p])

    def store(k, p):
        return pltpu.make_async_copy(piece(wide[k][2], p), piece(wide[k][3], p), out_sem.at[k, p])

    for k in range(len(wide)):
        for p in range(parts):
            load(k, p).start()

    head_all = small_ref[:, width : 2 * width]
    for ref, row in ((ob_o, 6), (ag_o, 4), (as_o, 5), (db_o, 3), (fg_o, 0), (fs_o, 1)):
        ref[...] = small_ref[row : row + 1, 0:width]
    qb_o[...] = head_all[1:2, :]
    vb_o[...] = head_all[3:4, :]
    b1_o[...] = unit_ref[1:2, :]
    keeps = [keep_prob(ref[...]) for ref in (ha_ref, ua_ref, wa_ref)]
    heads_kept, units_kept, dims_kept = [jnp.sum(k, axis=1, keepdims=True) for k in keeps]
    full_size = 4.0 * D * D + 2.0 * D * FF
    gap = 1.0 - (4.0 * HD * heads_kept * dims_kept + 2.0 * units_kept * dims_kept) / full_size - TARGET
    pull = -(lane_of(mult_ref[...], 0) + 2.0 * lane_of(mult_ref[...], 1) * gap) / full_size
    slot = lax.broadcasted_iota(jnp.int32, (1, 2), 1)
    mult_o[...] = mult_ref[...] + ASCENT * jnp.where(slot == 0, gap, gap * gap)

    def pulled(alpha, factor):
        k = keep_prob(alpha)
        return pull * factor * k * (1.0 - k)

    unit_alpha = part_of(ua_ref, rank, units)
    ua_o[...] = unit_ref[0:1, :] * gate_slope(un_ref[...], unit_alpha) + pulled(unit_alpha, 2.0 * dims_kept)
    width_alpha = part_of(wa_ref, rank, width)
    wa_o[...] = small_ref[2:3, 0:width] * gate_slope(wn_ref[...], width_alpha) + pulled(
        width_alpha, 4.0 * HD * heads_kept + 2.0 * units_kept
    )
    noise_row, alpha_row = head_row(hn_ref, ha_ref, rank, heads)
    lanes = lax.broadcasted_iota(jnp.int32, (1, width), 1)
    per_lane = head_all[0:1, :] * gate_slope(noise_row, alpha_row)
    head_pulled = pulled(alpha_row, 4.0 * HD * dims_kept) * (1.0 / HD)
    for h in range(heads):
        here = (lanes >= h * HD) & (lanes < (h + 1) * HD)
        ha_o[:, h : h + 1] = jnp.sum(jnp.where(here, per_lane + head_pulled, 0.0), axis=1, keepdims=True)
    live = jnp.sum(len_ref[...].astype(F32), axis=1, keepdims=True)
    mse_o[...] = jnp.sum(small_ref[7:8, 0:width], axis=1, keepdims=True) / (live * D)

    for k, (_, low, high, _) in enumerate(wide):
        rows = low.shape[0] // parts
        for p in range(parts):
            load(k, p).wait()
            if low is not high:

                step = min(64, rows)

                def widen(i, carry, low=low, high=high, first=p * rows, step=step):
                    at = pl.ds(pl.multiple_of(first + i * step, step), step)
                    high[at, :] = low[at, :].astype(F32)
                    return carry

                lax.fori_loop(0, rows // step, widen, 0)
            store(k, p).start()
    for k in range(len(wide)):
        for p in range(parts):
            store(k, p).wait()


def hbm():
    return pl.BlockSpec(memory_space=pl.ANY)


def vmem():
    return pl.BlockSpec(memory_space=pltpu.VMEM)


def smem():
    return pl.BlockSpec(memory_space=pltpu.SMEM)


def call(kernel, name, ident, ins, outs, scratch, flops):
    return pl.pallas_call(
        kernel,
        name=name,
        out_shape=[jax.ShapeDtypeStruct(shape, dtype) for shape, dtype, _ in outs],
        in_specs=ins,
        out_specs=[spec for _, _, spec in outs],
        scratch_shapes=scratch,
        compiler_params=pltpu.CompilerParams(
            collective_id=ident, has_side_effects=True, vmem_limit_bytes=VMEM_LIMIT
        ),
        cost_estimate=pl.CostEstimate(flops=flops, bytes_accessed=30_000_000, transcendentals=0),
    )


def attend(n, seqs, heads, args):
    width, rows, nx, half = heads * HD, SLOT // n, n // 2, SLOT // 2
    tokens, owned = seqs * SLOT, seqs * rows
    v, dma = pltpu.VMEM, pltpu.SemaphoreType.DMA
    return call(
        functools.partial(attend_kernel, n, seqs, heads),
        "attend",
        0,
        [smem()] + [hbm()] * 3 + [vmem()] * 10 + [hbm()] * 3 + [vmem()] * 2 + [hbm()],
        [
            ((tokens, D), BF, hbm()),
            ((tokens, 3 * width), BF, hbm()),
            ((seqs, heads, SLOT, SLOT), BF, hbm()),
            ((tokens, width), F32, hbm()),
            ((tokens, width), BF, hbm()),
            ((owned, D), F32, hbm()),
            ((owned, D), F32, hbm()),
            ((owned, 128), F32, hbm()),
            ((owned, D), BF, hbm()),
            ((8, D), F32, vmem()),
            ((seqs, rows, D), BF, hbm()),
            ((1, width), F32, vmem()),
        ],
        [
            v((tokens, D), BF),
            v((D, 3 * width), BF),
            v((width, D), BF),
            v((tokens, 3 * width), BF),
            v((seqs, heads, SLOT, SLOT), BF),
            v((tokens, width), F32),
            v((tokens, width), BF),
            v((seqs, nx, rows, D), F32),
            v((seqs, nx, rows, D), BF),
            v((seqs, nx, rows, D), BF),
            v((seqs, nx - 1, rows, D), BF),
            v((seqs, nx - 1, rows, D), BF),
            v((owned, D), F32),
            v((owned, D), F32),
            v((owned, 128), F32),
            v((owned, D), BF),
            v((8, D), F32),
            v((seqs, rows, D), BF),
            v((tokens, width), BF),
            v((tokens, width), BF),
            v((seqs, n, rows, width), BF),
            v((8, width), F32),
            v((SLOT, SLOT), F32),
            dma((9,)),
            dma((seqs, 9)),
            dma((n - 1,)),
            dma((n - 1,)),
            dma((n - 1,)),
            dma((n - 1,)),
        ]
        + gather_sems(seqs, nx)
        + reduce_sems(seqs, nx),
        10_000_000_000,
    )(*args)


def feed(n, seqs, units, args):
    rows, nx = SLOT // n, n // 2
    tokens, owned = seqs * SLOT, seqs * rows
    v, dma = pltpu.VMEM, pltpu.SemaphoreType.DMA
    return call(
        functools.partial(feed_kernel, n, seqs, units),
        "feed",
        1,
        [smem(), hbm(), hbm(), hbm(), hbm(), vmem(), hbm(), hbm(), vmem(), hbm(), vmem(), vmem()],
        [
            ((owned, D), BF, hbm()),
            ((owned, D), BF, hbm()),
            ((owned, D), F32, hbm()),
            ((D, units), BF, hbm()),
            ((units, D), BF, hbm()),
            ((8, D), F32, vmem()),
            ((2, units), F32, vmem()),
        ],
        [
            v((tokens, D), BF),
            v((tokens, D), BF),
            v((D, units), BF),
            v((units, D), BF),
            v((tokens, units), BF),
            v((tokens, units), BF),
            v((tokens, units), BF),
            v((seqs, nx, rows, D), F32),
            v((seqs, nx, rows, D), BF),
            v((seqs, nx, rows, D), BF),
            v((seqs, nx - 1, rows, D), BF),
            v((seqs, nx - 1, rows, D), BF),
            v((owned, D), F32),
            v((owned, D), F32),
            v((owned, 128), F32),
            v((owned, D), BF),
            v((owned, D), F32),
            v((owned, D), BF),
            v((owned, D), BF),
            v((owned, D), BF),
            v((owned, D), F32),
            v((SLOT, NB), F32),
            v((D // NB, NB, D), BF),
            v((7, 8, D), F32),
            v((2, 8, units), F32),
            v((1, units), F32),
            dma((6,)),
            dma((seqs, 3)),
            dma((2, D // NB)),
        ]
        + (gather_sems(seqs, nx) + reduce_sems(seqs, nx)) * 2,
        30_000_000_000,
    )(*args)


def attend_back(n, seqs, heads, units, size, args):
    width, rows, nx = heads * HD, SLOT // n, n // 2
    tokens, owned = seqs * SLOT, seqs * rows
    v, dma = pltpu.VMEM, pltpu.SemaphoreType.DMA
    return call(
        functools.partial(attend_back_kernel, n, seqs, heads, size),
        "attend_back",
        2,
        [hbm()] * 14 + [vmem()],
        [
            ((tokens, width), F32, hbm()),
            ((D, 3 * width), BF, hbm()),
            ((width, D), BF, hbm()),
            ((D, units), BF, hbm()),
            ((units, D), BF, hbm()),
            ((seqs, n, rows, width), BF, hbm()),
            ((8, width), F32, vmem()),
        ],
        [
            v((tokens, D), BF),
            v((owned, D), F32),
            v((tokens, D), BF),
            v((tokens, 3 * width), BF),
            v((seqs, heads, SLOT, SLOT), BF),
            v((tokens, width), F32),
            v((tokens, width), BF),
            v((D, 3 * width), BF),
            v((width, D), BF),
            v((SLOT, width), BF),
            v((tokens, 3 * width), BF),
            v((SLOT, SLOT), F32),
            v((SLOT, SLOT), BF),
            v((3, SLOT, width), F32),
            v((SLOT, width), F32),
            v((seqs, nx, SLOT, width), F32),
            v((seqs, nx, SLOT, width), BF),
            v((seqs, nx, SLOT, width), BF),
            v((seqs, nx - 1, SLOT, width), BF),
            v((seqs, nx - 1, SLOT, width), BF),
            v((tokens, width), F32),
            v((D // NB, NB, 3 * width), BF),
            v((width, D), BF),
            v((seqs, n, rows, width), BF),
            v((4, 8, width), F32),
            v((D, units), BF),
            v((units, D), BF),
            dma((15,)),
            dma((seqs,)),
            dma((D // NB,)),
            dma((n - 1,)),
            dma((n - 1,)),
        ]
        + gather_sems(seqs, nx)
        + reduce_sems(seqs, nx)
        + ring_scratch((D, units), size) * 2
        + ring_scratch((units, D), size) * 2,
        20_000_000_000,
    )(*args)


def settle(n, size, seqs, width, units, args):
    v, dma = pltpu.VMEM, pltpu.SemaphoreType.DMA
    tokens = seqs * SLOT
    return call(
        functools.partial(settle_kernel, n, size, seqs),
        "settle",
        3,
        [smem()] + [hbm()] * 4 + [vmem()] * 3,
        [((D, width), BF, hbm())] * 3
        + [((width, D), BF, hbm()), ((8, 2 * width), F32, vmem()), ((2, units), F32, vmem())],
        [
            v((D, width), BF),
            v((D, width), BF),
            v((D, width), BF),
            v((width, D), BF),
            v((tokens, width), BF),
            v((tokens, width), BF),
            v((8, D), F32),
            v((8, 2 * width), F32),
            v((n - 1, 8, width), F32),
            v((size - 1, 8, 2 * width), F32),
            v((size - 1, 2, units), F32),
            dma((6,)),
            dma((n - 1,)),
            dma((n - 1,)),
        ]
        + [dma((size - 1,))] * 4
        + ring_scratch((D, width), size) * 6
        + ring_scratch((width, D), size) * 2,
        1_000_000_000,
    )(*args)


def complete(n, heads, units, tokens, args):
    v, dma, width = pltpu.VMEM, pltpu.SemaphoreType.DMA, heads * HD
    shapes = [(D, units), (units, D), (D, width), (D, width), (D, width), (width, D)]
    rows = [(width,)] * 8 + [(units,), (heads,), (units,), (width,), (1,), (2,)]
    return pl.pallas_call(
        functools.partial(complete_kernel, n, heads, units),
        name="complete",
        out_shape=[jax.ShapeDtypeStruct(shape, F32) for shape in shapes]
        + [jax.ShapeDtypeStruct((tokens, width), F32), jax.ShapeDtypeStruct((tokens, width), BF)]
        + [jax.ShapeDtypeStruct((1, count), F32) for (count,) in rows],
        in_specs=[hbm()] * 8 + [vmem()] * 10,
        out_specs=[hbm()] * 8 + [vmem()] * len(rows),
        scratch_shapes=[v(shape, BF) for shape in shapes]
        + [v((tokens, width), F32), v((tokens, width), BF)]
        + [v(shape, F32) for shape in shapes]
        + [dma((8, 4))] * 2,
        compiler_params=pltpu.CompilerParams(vmem_limit_bytes=VMEM_LIMIT),
        cost_estimate=pl.CostEstimate(flops=10_000_000, bytes_accessed=24_000_000, transcendentals=0),
    )(*args)


def on_device(
    n,
    size,
    tokens,
    query_weight,
    query_bias,
    key_weight,
    value_weight,
    value_bias,
    output_weight,
    output_bias,
    attention_gain,
    attention_shift,
    inner_weight,
    inner_bias,
    down_weight,
    down_bias,
    final_gain,
    final_shift,
    head_alpha,
    unit_alpha,
    width_alpha,
    multipliers,
    head_noise,
    unit_noise,
    width_noise,
    lengths,
    teacher,
    upstream,
):
    row_count, width = tokens.shape
    heads = width // HD
    units = inner_weight.shape[1]
    seqs = row_count // SLOT
    rows = SLOT // n
    flat = lambda vector: vector.reshape(1, vector.shape[0])
    head_alpha, unit_alpha, width_alpha = flat(head_alpha), flat(unit_alpha), flat(width_alpha)
    head_noise, unit_noise, width_noise = flat(head_noise), flat(unit_noise), flat(width_noise)
    full, qkv, prob, ctx, gat, nrm, pre, rstd, mid, par, change_rows, gate_row = attend(
        n,
        seqs,
        heads,
        (
            lengths,
            tokens,
            upstream,
            teacher,
            flat(output_bias),
            flat(attention_gain),
            flat(attention_shift),
            flat(down_bias),
            flat(final_gain),
            flat(final_shift),
            width_noise,
            width_alpha,
            head_noise,
            head_alpha,
            query_weight,
            key_weight,
            value_weight,
            flat(query_bias),
            flat(value_bias),
            output_weight,
        ),
    )
    out_rows, d_low, d_res, dw_inner, dw_down, row_sums, unit_sums = feed(
        n,
        seqs,
        units,
        (
            lengths,
            mid,
            nrm,
            pre,
            rstd,
            par,
            change_rows.reshape(seqs * rows, D),
            inner_weight,
            flat(inner_bias),
            down_weight,
            unit_noise,
            unit_alpha,
        ),
    )
    tokens_grad, dw_qkv, dw_o, dw_inner, dw_down, output, head_sums = attend_back(
        n,
        seqs,
        heads,
        units,
        size,
        (
            d_low,
            d_res,
            full,
            qkv,
            prob,
            ctx,
            gat,
            query_weight,
            key_weight,
            value_weight,
            output_weight,
            dw_inner,
            dw_down,
            out_rows.reshape(seqs, rows, D),
            gate_row,
        ),
    )
    output = output.reshape(row_count, width)
    dw_q, dw_k, dw_v, dw_o, small, unit_all = settle(
        n,
        size,
        seqs,
        width,
        units,
        (lengths, dw_qkv, dw_o, output, teacher, row_sums, unit_sums, head_sums),
    )
    dw_inner, dw_down, dw_q, dw_k, dw_v, dw_o, tokens_grad, output, *vectors = complete(
        n,
        heads,
        units,
        row_count,
        (
            dw_inner,
            dw_down,
            dw_q,
            dw_k,
            dw_v,
            dw_o,
            tokens_grad,
            output,
            small,
            unit_all,
            head_alpha,
            unit_alpha,
            width_alpha,
            flat(multipliers),
            head_noise,
            unit_noise,
            width_noise,
            flat(lengths),
        ),
    )
    qb, vb, ob, ag, shift, db, fg, fs, b1, ha, ua, wa, mse, mult = [v.reshape(v.shape[1]) for v in vectors]
    return (
        output,
        tokens_grad,
        dw_q,
        qb,
        dw_k,
        dw_v,
        vb,
        dw_o,
        ob,
        ag,
        shift,
        dw_inner,
        b1,
        dw_down,
        db,
        fg,
        fs,
        ha,
        ua,
        wa,
        mse.reshape(()),
        mult,
    )


def solution(mesh):
    tall, wide, vec, rep = P("dp", "hid"), P(None, "hid"), P("hid"), P()
    deep = P("hid", None)
    return jax.shard_map(
        functools.partial(on_device, mesh.shape["hid"], mesh.shape["dp"]),
        mesh=mesh,
        in_specs=(tall, wide, vec, wide, wide, vec, deep, vec, vec, vec, wide, vec, deep)
        + (vec,) * 3
        + (rep,) * 4
        + (vec,) * 3
        + (rep, tall, tall),
        out_specs=(tall, tall, wide, vec, wide, wide, vec, deep, vec, vec, vec, wide, vec, deep)
        + (vec,) * 6
        + (rep, rep),
        check_vma=False,
    )
```

```python
import functools
import math

import jax
import jax.numpy as jnp
from jax import lax
from jax.experimental import pallas as pl
from jax.experimental.pallas import tpu as pltpu
from jax.sharding import PartitionSpec as P

D = 1024
HD = 64
FF = 4096
SLOT = 512

BETA = 2.0 / 3.0
GAMMA = -0.1
ZETA = 1.1
TARGET = 0.7
ASCENT = 1.0
EPS = 1e-12
MASKED = -1000000000.0
ROOT_HALF = 0.7071067811865476
ROOT_TWO_PI = 2.5066282746310002

MESH = pl.DeviceIdType.MESH
VMEM_LIMIT = 66_000_000
BF = jnp.bfloat16
F32 = jnp.float32
NB = 256
RB = 16


def gate_value(noise, alpha):
    logits = (jnp.log(noise) - jnp.log(1.0 - noise) + alpha) / BETA
    stretched = jax.nn.sigmoid(logits) * (ZETA - GAMMA) + GAMMA
    return jnp.clip(stretched, 0.0, 1.0)


def gate_slope(noise, alpha):
    s = jax.nn.sigmoid((jnp.log(noise) - jnp.log(1.0 - noise) + alpha) / BETA)
    stretched = s * (ZETA - GAMMA) + GAMMA
    free = (stretched > 0.0) & (stretched < 1.0)
    return jnp.where(free, (ZETA - GAMMA) / BETA * s * (1.0 - s), 0.0)


def keep_prob(alpha):
    return jax.nn.sigmoid(alpha - BETA * math.log(-GAMMA / ZETA))


def lane_of(row, place):
    lanes = lax.broadcasted_iota(jnp.int32, row.shape, 1)
    return jnp.sum(jnp.where(lanes == place, row, 0.0), axis=1, keepdims=True)


def head_row(noise_ref, alpha_ref, rank, heads):
    lanes = lax.broadcasted_iota(jnp.int32, (1, heads * HD), 1)
    noise = jnp.full((1, heads * HD), 0.5, F32)
    alpha = jnp.zeros((1, heads * HD), F32)
    for h in range(heads):
        here = (lanes >= h * HD) & (lanes < (h + 1) * HD)
        noise = jnp.where(here, lane_of(noise_ref[...], h), noise)
        alpha = jnp.where(here, lane_of(alpha_ref[...], rank * heads + h), alpha)
    return noise, alpha


def part_of(ref, rank, width):
    return ref[:, pl.ds(pl.multiple_of(rank * width, width), width)]


def nn(a, b):
    return jnp.dot(a, b, preferred_element_type=F32)


def nt(a, b):
    return lax.dot_general(a, b, (((1,), (1,)), ((), ())), preferred_element_type=F32)


def tn(a, b):
    return lax.dot_general(a, b, (((0,), (0,)), ((), ())), preferred_element_type=F32)


def fold(values):
    return jnp.sum(values.reshape(values.shape[0] // 8, 8, values.shape[1]), axis=0)


class Group:
    def __init__(self, n):
        self.n = n
        self.nx = n // 2
        self.me = lax.axis_index("hid")
        self.x = lax.div(self.me, 2)
        self.c = lax.rem(self.me, 2)
        self.partner = 2 * self.x + 1 - self.c

    def chip_ahead(self, j):
        return lax.rem(self.x + 1 + j, self.nx)

    def chip_behind(self, j):
        return lax.rem(self.x - 1 - j + self.nx, self.nx)

    def slot(self, h):
        return lax.rem(h, 2) * self.nx + lax.div(h, 2)

    def all_peers(self):
        return [{"hid": lax.rem(self.me + 1 + i, self.n)} for i in range(self.n - 1)]

    def near_peers(self):
        near = [self.partner] + [2 * self.chip_ahead(j) + self.c for j in range(self.nx - 1)]
        return [{"hid": peer} for peer in near]


def remote(src, dst, send_sem, recv_sem, to):
    return pltpu.make_async_remote_copy(
        src_ref=src,
        dst_ref=dst,
        send_sem=send_sem,
        recv_sem=recv_sem,
        device_id=to if isinstance(to, dict) else {"hid": to},
        device_id_type=MESH,
    )


def gather_sems(seqs, nx):
    wide = pltpu.SemaphoreType.DMA((seqs, nx - 1))
    return [wide] * 4 + [pltpu.SemaphoreType.DMA((seqs,))] * 3


def reduce_sems(seqs, nx):
    wide = pltpu.SemaphoreType.DMA((seqs, nx - 1))
    return [wide] * 2 + [pltpu.SemaphoreType.DMA((seqs,))] * 2


class Gather:
    def __init__(self, group, sems, source, region):
        self.g, self.source, self.region = group, source, region
        self.xs, self.xr, self.rs, self.rr, self.ps, self.pr, self.os = sems

    def _own(self, s):
        return pltpu.make_async_copy(self.source(s), self.region(s, self.g.me), self.os.at[s])

    def _cross(self, s, j):
        to = 2 * self.g.chip_ahead(j) + self.g.c
        return remote(
            self.source(s), self.region(s, self.g.me), self.xs.at[s, j], self.xr.at[s, j], to
        )

    def _crossed(self, s, j):
        to = 2 * self.g.chip_ahead(j) + self.g.c
        block = self.region(s, 2 * self.g.chip_behind(j) + self.g.c)
        return remote(self.source(s), block, self.xs.at[s, j], self.xr.at[s, j], to)

    def _pair(self, s):
        return remote(
            self.source(s),
            self.region(s, self.g.me),
            self.ps.at[s],
            self.pr.at[s],
            self.g.partner,
        )

    def _paired(self, s):
        block = self.region(s, self.g.partner)
        return remote(self.source(s), block, self.ps.at[s], self.pr.at[s], self.g.partner)

    def _relay(self, s, j):
        block = self.region(s, 2 * self.g.chip_behind(j) + self.g.c)
        return remote(block, block, self.rs.at[s, j], self.rr.at[s, j], self.g.partner)

    def _relayed(self, s, j):
        block = self.region(s, 2 * self.g.chip_behind(j) + 1 - self.g.c)
        return remote(block, block, self.rs.at[s, j], self.rr.at[s, j], self.g.partner)

    def start(self, s):
        for j in range(self.g.nx - 1):
            self._cross(s, j).start()
        self._pair(s).start()
        self._own(s).start()

    def relay(self, s):
        for j in range(self.g.nx - 1):
            self._crossed(s, j).wait_recv()
            self._relay(s, j).start()

    def wait(self, s):
        self._own(s).wait()
        self._paired(s).wait_recv()
        for j in range(self.g.nx - 1):
            self._relayed(s, j).wait_recv()

    def drain(self, s):
        self._pair(s).wait_send()
        for j in range(self.g.nx - 1):
            self._cross(s, j).wait_send()
            self._relay(s, j).wait_send()


class Reduce:
    def __init__(self, group, sems, psend, precv, own, xsend, xrecv):
        self.g = group
        self.psend, self.precv, self.own, self.xsend, self.xrecv = psend, precv, own, xsend, xrecv
        self.xs, self.xr, self.ps, self.pr = sems

    def _pair(self, s):
        return remote(
            self.psend.at[s], self.precv.at[s], self.ps.at[s], self.pr.at[s], self.g.partner
        )

    def _cross(self, s, j):
        to = 2 * self.g.chip_ahead(j) + self.g.c
        return remote(
            self.xsend.at[s, j], self.xrecv.at[s, j], self.xs.at[s, j], self.xr.at[s, j], to
        )

    def start(self, s):
        self._pair(s).start()

    def cross(self, s):
        self._pair(s).wait()
        rows = self.own.shape[2]
        for j in range(self.g.nx - 1):
            chip = self.g.chip_ahead(j)

            def add(i, carry, chip=chip, j=j):
                at = pl.ds(pl.multiple_of(i * RB, RB), RB)
                total = self.own[s, chip, at, :] + self.precv[s, chip, at, :].astype(F32)
                self.xsend[s, j, at, :] = total.astype(BF)
                return carry

            lax.fori_loop(0, rows // RB, add, 0)
            self._cross(s, j).start()

    def arrive(self, s):
        for j in range(self.g.nx - 1):
            self._cross(s, j).wait()

    def total(self, s, at):
        total = self.own[s, self.g.x, at, :] + self.precv[s, self.g.x, at, :].astype(F32)
        for j in range(self.g.nx - 1):
            total = total + self.xrecv[s, j, at, :].astype(F32)
        return total


class Cycle:
    def __init__(self, size):
        self.size = size
        self.me = lax.axis_index("dp")
        self.length = size // 2
        line, column = lax.div(self.me, 2), lax.rem(self.me, 2)
        self.place = line + column * (size - 1 - 2 * line)

    def device(self, place):
        column = lax.div(place, self.length)
        line = place + column * (self.size - 1 - 2 * place)
        return 2 * line + column

    def beside(self, way):
        return self.device(lax.rem(self.place + way + self.size, self.size))


def split(shape, size):
    tall = max(16, shape[0] // (2 * size))
    across = 2 * size * tall // shape[0]
    return tall, shape[1] // across, across


def ring_scratch(shape, size):
    tall, broad, _ = split(shape, size)
    step = pltpu.SemaphoreType.DMA((size - 1,))
    return [
        pltpu.VMEM((size - 1, tall, broad), BF),
        pltpu.SemaphoreType.DMA((size,)),
    ] + [step] * 4 + [pltpu.SemaphoreType.REGULAR]


class Ring:
    def __init__(self, cycle, data, target, way, scratch):
        self.cycle, self.data, self.target, self.way = cycle, data, target, way
        self.size = cycle.size
        self.recv, self.out_sem, self.ss, self.sr, self.gs, self.gr, self.free = scratch
        self.tall, self.broad, self.across = split(data.shape, self.size)
        self.to, self.frm = {"dp": cycle.beside(way)}, {"dp": cycle.beside(-way)}
        self.ticks = 2 * self.size - 1

    def block(self, number):
        place = lax.rem(self.cycle.place + self.way * number + 2 * self.size, self.size)
        index = 2 * place + (0 if self.way > 0 else 1)
        if self.across == 1:
            return pl.multiple_of(index * self.tall, self.tall), 0
        row = lax.div(index, self.across)
        column = lax.rem(index, self.across)
        return (
            pl.multiple_of(row * self.tall, self.tall),
            pl.multiple_of(column * self.broad, self.broad),
        )

    def view(self, number):
        row, column = self.block(number)
        return self.data.at[pl.ds(row, self.tall), pl.ds(column, self.broad)]

    def _add(self, t):
        return remote(self.view(-t), self.recv.at[t], self.ss.at[t], self.sr.at[t], self.to)

    def _pass(self, t):
        block = self.view(1 - t)
        return remote(block, block, self.gs.at[t], self.gr.at[t], self.to)

    def _passed(self, t):
        block = self.view(-t)
        return remote(block, block, self.gs.at[t], self.gr.at[t], self.to)

    def _sum(self, t):
        row, column = self.block(-t)

        def part(i, carry):
            at = pl.ds(pl.multiple_of(row + i * RB, RB), RB)
            cols = pl.ds(column, self.broad)
            arrived = self.recv[t - 1, pl.ds(pl.multiple_of(i * RB, RB), RB), :].astype(F32)
            self.data[at, cols] = (self.data[at, cols].astype(F32) + arrived).astype(BF)
            return carry

        lax.fori_loop(0, self.tall // RB, part, 0)

    def _out(self, number, count):
        row, column = self.block(number)
        place = self.target.at[pl.ds(row, self.tall), pl.ds(column, self.broad)]
        return pltpu.make_async_copy(self.view(number), place, self.out_sem.at[count])

    def tick(self, t):
        size = self.size

        @pl.when(t == 0)
        def _():
            self._add(0).start()

        @pl.when((t >= 1) & (t <= size - 1))
        def _():
            self._add(t - 1).wait_recv()
            self._sum(t)

        @pl.when((t >= 1) & (t < size - 1))
        def _():
            self._add(t).start()

        @pl.when((t >= 1) & (t <= size - 1))
        def _():
            self._add(t - 1).wait_send()
            pl.semaphore_signal(self.free, inc=1, device_id=self.frm, device_id_type=MESH)

        @pl.when(t == size - 1)
        def _():
            pl.semaphore_wait(self.free, 1)
            self._pass(0).start()
            self._out(1, 0).start()

        @pl.when((t > size - 1) & (t < 2 * size - 1))
        def _():
            u = t - size
            self._passed(u).wait_recv()

            @pl.when(t < 2 * size - 2)
            def _():
                pl.semaphore_wait(self.free, 1)
                self._pass(u + 1).start()

            self._out(-u, u + 1).start()

    def drain(self):
        self._out(1, 0).wait()

        def step(t, carry):
            self._pass(t).wait_send()
            self._out(-t, t + 1).wait()
            return carry

        lax.fori_loop(0, self.size - 1, step, 0)


def meet(peers):
    barrier = pltpu.get_barrier_semaphore()
    for peer in peers:
        pl.semaphore_signal(barrier, inc=1, device_id=peer, device_id_type=MESH)
    pl.semaphore_wait(barrier, len(peers))


def mean_of(values):
    return jnp.sum(values, axis=1, keepdims=True) * (1.0 / D)


def attend_kernel(n, seqs, heads, *refs):
    (
        len_ref, tok_ref, up_ref, tea_ref, ob_ref, ag_ref, as_ref, db_ref, fg_ref, fs_ref,
        wn_ref, wa_ref, hn_ref, ha_ref, wq_ref, wk_ref, wv_ref, qb_ref, vb_ref, wo_ref,
        full_o, qkv_o, prob_o, ctx_o, gat_o, nrm_o, pre_o, rstd_o, mid_o, par_o, change_o, gate_o,
        full, wqkv, wo, qkv, prob, ctx, gat, own, psend, precv, xsend, xrecv,
        nrm, pre, rstd, mid, par, chg, up, tea, change, vec, score, in_sem, out_sem, vec_send, vec_recv, ch_send, ch_recv, *sems,
    ) = refs
    g = Group(n)
    width = heads * HD
    rows = SLOT // n
    gsems, rsems = sems[:7], sems[7:]
    cols = lambda h: pl.ds(pl.multiple_of(h * width, width), width)
    seq = lambda s: pl.ds(pl.multiple_of(s * SLOT, SLOT), SLOT)
    own_rows = lambda s: pl.ds(pl.multiple_of(s * rows, rows), rows)
    ga = Gather(g, gsems, lambda s: tok_ref.at[seq(s), :], lambda s, h: full.at[seq(s), cols(h)])
    re = Reduce(g, rsems, psend, precv, own, xsend, xrecv)

    def vec_to(i):
        to = lax.rem(g.me + 1 + i, n)
        return remote(vec, par.at[:, cols(g.me)], vec_send.at[i], vec_recv.at[i], to)

    def vec_from(i):
        to = lax.rem(g.me + 1 + i, n)
        frm = lax.rem(g.me - 1 - i + n, n)
        return remote(vec, par.at[:, cols(frm)], vec_send.at[i], vec_recv.at[i], to)

    def change_to(i):
        to = lax.rem(g.me + 1 + i, n)
        return remote(
            change.at[:, g.slot(to)], chg.at[:, :, cols(g.me)], ch_send.at[i], ch_recv.at[i], to
        )

    def change_from(i):
        to = lax.rem(g.me + 1 + i, n)
        frm = lax.rem(g.me - 1 - i + n, n)
        return remote(
            change.at[:, g.slot(to)], chg.at[:, :, cols(frm)], ch_send.at[i], ch_recv.at[i], to
        )

    loads = [
        pltpu.make_async_copy(wq_ref, wqkv.at[:, pl.ds(0, width)], in_sem.at[0]),
        pltpu.make_async_copy(wk_ref, wqkv.at[:, pl.ds(width, width)], in_sem.at[1]),
        pltpu.make_async_copy(wv_ref, wqkv.at[:, pl.ds(2 * width, width)], in_sem.at[2]),
        pltpu.make_async_copy(wo_ref, wo, in_sem.at[3]),
        pltpu.make_async_copy(up_ref, up, in_sem.at[4]),
        pltpu.make_async_copy(tea_ref, tea, in_sem.at[5]),
    ]
    par_own = pltpu.make_async_copy(vec, par.at[:, cols(g.me)], in_sem.at[7])
    change_own = pltpu.make_async_copy(
        change.at[:, g.slot(g.me)], chg.at[:, :, cols(g.me)], in_sem.at[8]
    )
    chg_out = pltpu.make_async_copy(chg, change_o, in_sem.at[6])

    def sequence_outs(s):
        return [
            pltpu.make_async_copy(full.at[seq(s), :], full_o.at[seq(s), :], out_sem.at[s, 0]),
            pltpu.make_async_copy(qkv.at[seq(s), :], qkv_o.at[seq(s), :], out_sem.at[s, 1]),
            pltpu.make_async_copy(prob.at[s], prob_o.at[s], out_sem.at[s, 2]),
            pltpu.make_async_copy(ctx.at[seq(s), :], ctx_o.at[seq(s), :], out_sem.at[s, 3]),
            pltpu.make_async_copy(gat.at[seq(s), :], gat_o.at[seq(s), :], out_sem.at[s, 4]),
        ]

    def row_outs(s):
        return [
            pltpu.make_async_copy(nrm.at[own_rows(s), :], nrm_o.at[own_rows(s), :], out_sem.at[s, 5]),
            pltpu.make_async_copy(pre.at[own_rows(s), :], pre_o.at[own_rows(s), :], out_sem.at[s, 6]),
            pltpu.make_async_copy(rstd.at[own_rows(s), :], rstd_o.at[own_rows(s), :], out_sem.at[s, 7]),
            pltpu.make_async_copy(mid.at[own_rows(s), :], mid_o.at[own_rows(s), :], out_sem.at[s, 8]),
        ]

    for load in loads:
        load.start()
    for row, ref in ((0, ob_ref), (2, ag_ref), (3, as_ref), (4, db_ref), (5, fg_ref), (6, fs_ref)):
        vec[row : row + 1, :] = ref[...]
    vec[1:2, :] = gate_value(wn_ref[...], part_of(wa_ref, g.me, width))
    vec[7:8, :] = jnp.zeros((1, width), F32)
    meet(g.all_peers())

    def begin(s, carry):
        ga.start(s)
        return carry

    for i in range(n - 1):
        vec_to(i).start()
    lax.fori_loop(0, seqs, begin, 0)
    par_own.start()
    gate_row = gate_value(*head_row(hn_ref, ha_ref, g.me, heads))
    gate_o[...] = gate_row
    for load in loads:
        load.wait()

    def differ(i, carry):
        at = pl.ds(pl.multiple_of(i * 32, 32), 32)
        value = (up[at, :].astype(F32) - tea[at, :].astype(F32)).astype(BF)
        each = SLOT // n // 32
        s, q = lax.div(i, SLOT // 32), lax.rem(i, SLOT // 32)
        change[s, lax.div(q, each), pl.ds(pl.multiple_of(lax.rem(q, each) * 32, 32), 32), :] = value
        return carry

    lax.fori_loop(0, seqs * SLOT // 32, differ, 0)
    change_own.start()
    ga.relay(0)
    par_own.wait()
    for i in range(n - 1):
        vec_from(i).wait()
    par_o[...] = par[...]

    lanes = lax.broadcasted_iota(jnp.int32, (1, width), 1)
    head_lanes = [
        jnp.where((lanes >= h * HD) & (lanes < (h + 1) * HD), 1.0, 0.0).astype(BF) for h in range(heads)
    ]

    scaled_lanes = [lane * HD**-0.5 for lane in head_lanes]

    def finish(s):
        re.arrive(s)

        def block(i, carry):
            at = pl.ds(pl.multiple_of(i * RB, RB), RB)
            here = pl.ds(pl.multiple_of(s * rows + i * RB, RB), RB)
            token_row = pl.multiple_of(s * SLOT + g.slot(g.me) * rows + i * RB, RB)
            attention_pre = re.total(s, at) + par[0:1, :]
            residual = full[pl.ds(token_row, RB), :].astype(F32) + attention_pre * par[1:2, :]
            centered = residual - mean_of(residual)
            row_rstd = lax.rsqrt(mean_of(centered * centered) + EPS)
            normed = centered * row_rstd
            middle = normed * par[2:3, :] + par[3:4, :]
            nrm[here, :] = normed
            pre[here, :] = attention_pre
            rstd[here, :] = jnp.broadcast_to(row_rstd, (RB, 128))
            mid[here, :] = middle.astype(BF)
            return carry

        lax.fori_loop(0, rows // RB, block, 0)
        for copy in row_outs(s):
            copy.start()

    def sequence(s, carry):
        ga.wait(s)
        here = seq(s)
        projected = nn(full[here, :], wqkv[...])
        qkv[here, 0:width] = (projected[:, 0:width] + qb_ref[...]).astype(BF)
        qkv[here, width : 2 * width] = projected[:, width : 2 * width].astype(BF)
        qkv[here, 2 * width : 3 * width] = (projected[:, 2 * width : 3 * width] + vb_ref[...]).astype(BF)

        @pl.when(s + 1 < seqs)
        def _():
            ga.relay(s + 1)

        @pl.when(s > 0)
        def _():
            re.cross(s - 1)

        @pl.when(s == seqs - 2)
        def _():
            for i in range(n - 1):
                change_to(i).start()

        length = len_ref[lax.axis_index("dp") * seqs + s]
        bias = jnp.where(lax.broadcasted_iota(jnp.int32, (1, SLOT), 1) < length, 0.0, MASKED)
        for h in range(heads):
            score[...] = nt(qkv[here, 0:width] * scaled_lanes[h], qkv[here, width : 2 * width])

            def softmax(i, carry, h=h):
                at = pl.ds(pl.multiple_of(i * 64, 64), 64)
                scores = score[at, :] + bias
                exponent = jnp.exp(scores - jnp.max(scores, axis=1, keepdims=True))
                total = jnp.sum(exponent, axis=1, keepdims=True)
                prob[s, h, at, :] = (exponent * (1.0 / total)).astype(BF)
                return carry

            lax.fori_loop(0, SLOT // 64, softmax, 0, unroll=True)
            term = nn(prob[s, h], qkv[here, 2 * width : 3 * width] * head_lanes[h])
            ctx[here, :] = term if h == 0 else ctx[here, :] + term
        gat[here, :] = (ctx[here, :] * gate_row).astype(BF)
        for copy in sequence_outs(s):
            copy.start()
        half = SLOT // 2
        there = pl.ds(pl.multiple_of(s * SLOT + (1 - g.c) * half, half), half)
        psend[s] = nn(gat[there, :], wo[...]).astype(BF).reshape(n // 2, rows, D)
        re.start(s)
        mine = pl.ds(pl.multiple_of(s * SLOT + g.c * half, half), half)
        own[s] = nn(gat[mine, :], wo[...]).reshape(n // 2, rows, D)

        @pl.when(s > 0)
        def _():
            finish(s - 1)

        return carry

    lax.fori_loop(0, seqs, sequence, 0)
    re.cross(seqs - 1)
    change_own.wait()
    for i in range(n - 1):
        change_from(i).wait()
    chg_out.start()
    finish(seqs - 1)
    chg_out.wait()

    def end(s, carry):
        ga.drain(s)
        for copy in sequence_outs(s) + row_outs(s):
            copy.wait()
        return carry

    lax.fori_loop(0, seqs, end, 0)


def feed_kernel(n, seqs, units, *refs):
    (
        len_ref, mid_ref, nrm_ref, pre_ref, rstd_ref, par, change_ref, w1_ref, b1_ref, w2_ref, un_ref, ua_ref,
        out_o, dlow_o, dres_o, dw1_o, dw2_o, rowsum_o, unitsum_o,
        midf, dffn, w1, w2, act, inner, slope, own, psend, precv, xsend, xrecv,
        nrm, pre, rstd, change, dtwo, dsend, fout, dlow, dres, wide, grad, sums, unit_sums, ugate_ref,
        in_sem, out_sem, grad_sem, *sems,
    ) = refs
    g = Group(n)
    rows = SLOT // n
    half = SLOT // 2
    g1, r1, g2, r2 = sems[:7], sems[7:11], sems[11:18], sems[18:]
    seq = lambda s: pl.ds(pl.multiple_of(s * SLOT, SLOT), SLOT)
    own_rows = lambda s: pl.ds(pl.multiple_of(s * rows, rows), rows)
    spot = lambda s, h: pl.ds(pl.multiple_of(s * SLOT + g.slot(h) * rows, rows), rows)
    gm = Gather(g, g1, lambda s: mid_ref.at[own_rows(s), :], lambda s, h: midf.at[spot(s, h), :])
    gd = Gather(g, g2, lambda s: dsend.at[own_rows(s), :], lambda s, h: dffn.at[spot(s, h), :])
    rf = Reduce(g, r1, psend, precv, own, xsend, xrecv)
    rb = Reduce(g, r2, psend, precv, own, xsend, xrecv)
    loads = [
        pltpu.make_async_copy(w1_ref, w1, in_sem.at[0]),
        pltpu.make_async_copy(w2_ref, w2, in_sem.at[1]),
        pltpu.make_async_copy(nrm_ref, nrm, in_sem.at[2]),
        pltpu.make_async_copy(change_ref, change, in_sem.at[3]),
        pltpu.make_async_copy(pre_ref, pre, in_sem.at[4]),
        pltpu.make_async_copy(rstd_ref, rstd, in_sem.at[5]),
    ]

    meet(g.near_peers())

    def begin(s, carry):
        gm.start(s)
        return carry

    lax.fori_loop(0, seqs, begin, 0)
    for load in loads:
        load.start()
    sums[...] = jnp.zeros_like(sums)
    unit_sums[...] = jnp.zeros_like(unit_sums)
    ugate_ref[...] = gate_value(un_ref[...], part_of(ua_ref, g.me, units))
    gm.relay(0)
    for load in loads:
        load.wait()

    def finish_forward(s):
        rf.arrive(s)
        length = len_ref[lax.axis_index("dp") * seqs + s]

        def block(i, carry):
            at = pl.ds(pl.multiple_of(i * RB, RB), RB)
            here = pl.ds(pl.multiple_of(s * rows + i * RB, RB), RB)
            ffn_pre = rf.total(s, at) + par[4:5, :]
            middle = nrm[here, :] * par[2:3, :] + par[3:4, :]
            residual = middle + ffn_pre * par[1:2, :]
            centered = residual - mean_of(residual)
            row_rstd = lax.rsqrt(mean_of(centered * centered) + EPS)
            normed = centered * row_rstd
            final = normed * par[5:6, :] + par[6:7, :]
            fout[here, :] = final.astype(BF)
            place = g.slot(g.me) * rows + i * RB + lax.broadcasted_iota(jnp.int32, (RB, 1), 0)
            live = jnp.where(place < length, 1.0, 0.0)
            d_final = live * (change[here, :].astype(F32) + final)
            sums[0] += fold(d_final * normed)
            sums[1] += fold(d_final)
            d_normed = d_final * par[5:6, :]
            d_two = row_rstd * (d_normed - mean_of(d_normed) - normed * mean_of(d_normed * normed))
            sums[2] += fold(d_two * ffn_pre)
            d_ffn = d_two * par[1:2, :]
            sums[3] += fold(d_ffn)
            dtwo[here, :] = d_two
            dsend[here, :] = d_ffn.astype(BF)
            return carry

        lax.fori_loop(0, rows // RB, block, 0)
        gd.start(s)

    def forward(s, carry):
        gm.wait(s)
        here = seq(s)

        def part(b, carry):
            cols = pl.ds(pl.multiple_of(b * NB, NB), NB)
            wide[...] = nn(midf[here, :], w1[:, cols])
            bias = b1_ref[:, cols]
            gate = ugate_ref[:, cols]

            def block(i, carry):
                at = pl.ds(pl.multiple_of(i * 32, 32), 32)
                row = pl.ds(pl.multiple_of(s * SLOT + i * 32, 32), 32)
                v = wide[at, :] + bias
                phi = 0.5 * (1.0 + lax.erf(v * ROOT_HALF))
                activated = v * phi
                act[row, cols] = activated.astype(BF)
                inner[row, cols] = (activated * gate).astype(BF)
                steep = phi + v * jnp.exp(-0.5 * v * v) * (1.0 / ROOT_TWO_PI)
                slope[row, cols] = (gate * steep).astype(BF)
                return carry

            lax.fori_loop(0, SLOT // 32, block, 0)
            return carry

        lax.fori_loop(0, units // NB, part, 0)

        @pl.when(s + 1 < seqs)
        def _():
            gm.relay(s + 1)

        @pl.when(s > 0)
        def _():
            rf.cross(s - 1)

        there = pl.ds(pl.multiple_of(s * SLOT + (1 - g.c) * half, half), half)
        psend[s] = nn(inner[there, :], w2[...]).astype(BF).reshape(n // 2, rows, D)
        rf.start(s)
        mine = pl.ds(pl.multiple_of(s * SLOT + g.c * half, half), half)
        own[s] = nn(inner[mine, :], w2[...]).reshape(n // 2, rows, D)

        @pl.when(s > 1)
        def _():
            finish_forward(s - 2)

        return carry

    lax.fori_loop(0, seqs, forward, 0)
    rf.cross(seqs - 1)
    gd.relay(0)

    def row_outs(s):
        return [
            pltpu.make_async_copy(fout.at[own_rows(s), :], out_o.at[own_rows(s), :], out_sem.at[s, 0]),
            pltpu.make_async_copy(dlow.at[own_rows(s), :], dlow_o.at[own_rows(s), :], out_sem.at[s, 1]),
            pltpu.make_async_copy(dres.at[own_rows(s), :], dres_o.at[own_rows(s), :], out_sem.at[s, 2]),
        ]

    def finish_backward(s):
        rb.arrive(s)

        def block(i, carry):
            at = pl.ds(pl.multiple_of(i * RB, RB), RB)
            here = pl.ds(pl.multiple_of(s * rows + i * RB, RB), RB)
            normed = nrm[here, :]
            d_middle = dtwo[here, :] + rb.total(s, at)
            sums[4] += fold(d_middle * normed)
            sums[5] += fold(d_middle)
            d_normed = d_middle * par[2:3, :]
            d_one = rstd[here, 0:1] * (
                d_normed - mean_of(d_normed) - normed * mean_of(d_normed * normed)
            )
            sums[2] += fold(d_one * pre[here, :])
            d_attn = d_one * par[1:2, :]
            sums[6] += fold(d_attn)
            dres[here, :] = d_one
            dlow[here, :] = d_attn.astype(BF)
            return carry

        lax.fori_loop(0, rows // RB, block, 0)
        for copy in row_outs(s):
            copy.start()

    def backward(s, carry):
        gd.wait(s)
        here = seq(s)

        def part(b, carry):
            cols = pl.ds(pl.multiple_of(b * NB, NB), NB)
            wide[...] = nt(dffn[here, :], w2[cols, :])

            def block(i, sums_here):
                unit_part, bias_part = sums_here
                at = pl.ds(pl.multiple_of(i * 32, 32), 32)
                row = pl.ds(pl.multiple_of(s * SLOT + i * 32, 32), 32)
                d_inner = wide[at, :]
                d_pre = (d_inner * slope[row, cols].astype(F32)).astype(BF)
                unit_part = unit_part + fold(d_inner * act[row, cols].astype(F32))
                bias_part = bias_part + fold(d_pre.astype(F32))
                slope[row, cols] = d_pre
                return (unit_part, bias_part)

            zero = jnp.zeros((8, NB), F32)
            unit_part, bias_part = lax.fori_loop(0, SLOT // 32, block, (zero, zero))
            unit_sums[0, :, cols] += unit_part
            unit_sums[1, :, cols] += bias_part
            return carry

        lax.fori_loop(0, units // NB, part, 0)

        @pl.when(s < 2)
        def _():
            finish_forward(seqs - 2 + s)

        @pl.when(s + 1 < seqs)
        def _():
            gd.relay(s + 1)

        @pl.when(s > 0)
        def _():
            rb.cross(s - 1)

        there = pl.ds(pl.multiple_of(s * SLOT + (1 - g.c) * half, half), half)
        psend[s] = nt(slope[there, :], w1[...]).astype(BF).reshape(n // 2, rows, D)
        rb.start(s)
        mine = pl.ds(pl.multiple_of(s * SLOT + g.c * half, half), half)
        own[s] = nt(slope[mine, :], w1[...]).reshape(n // 2, rows, D)

        @pl.when(s > 1)
        def _():
            finish_backward(s - 2)

        return carry

    lax.fori_loop(0, seqs, backward, 0)
    rb.cross(seqs - 1)

    def grad_out(k, b):
        target = (dw2_o, dw1_o)[k]
        at = pl.ds(pl.multiple_of(b * NB, NB), NB)
        return pltpu.make_async_copy(grad.at[b], target.at[at, :], grad_sem.at[k, b])

    def down_grad(b, carry):
        cols = pl.ds(pl.multiple_of(b * NB, NB), NB)
        grad[b] = tn(inner[:, cols], dffn[...]).astype(BF)
        grad_out(0, b).start()
        return carry

    lax.fori_loop(0, units // NB, down_grad, 0)
    finish_backward(seqs - 2)
    for b in range(units // NB):
        grad_out(0, b).wait()

    def inner_grad(b, carry):
        cols = pl.ds(pl.multiple_of(b * NB, NB), NB)
        grad[b, :, 0:units] = tn(midf[:, cols], slope[...]).astype(BF)
        pltpu.make_async_copy(
            grad.at[b, :, pl.ds(0, units)], dw1_o.at[cols, :], grad_sem.at[1, b]
        ).start()
        return carry

    lax.fori_loop(0, D // NB, inner_grad, 0)
    finish_backward(seqs - 1)
    for k in range(7):
        rowsum_o[k : k + 1, :] = jnp.sum(sums[k], axis=0, keepdims=True)
    rowsum_o[7:8, :] = jnp.zeros((1, D), F32)
    for k in range(2):
        unitsum_o[k : k + 1, :] = jnp.sum(unit_sums[k], axis=0, keepdims=True)
    for b in range(D // NB):
        at = pl.ds(b * NB, NB)
        pltpu.make_async_copy(
            grad.at[b, :, pl.ds(0, units)], dw1_o.at[at, :], grad_sem.at[1, b]
        ).wait()

    def end(s, carry):
        gm.drain(s)
        gd.drain(s)
        for copy in row_outs(s):
            copy.wait()
        return carry

    lax.fori_loop(0, seqs, end, 0)


def attend_back_kernel(n, seqs, heads, size, *refs):
    (
        len_ref, dlow_ref, dres_ref, full_ref, qkv_ref, prob_ref, ctx_ref, gat_ref,
        wq_ref, wk_ref, wv_ref, wo_ref, dw1_ref, dw2_ref, out_ref, teacher_ref, gate_ref, row_ref, unit_ref,
        tgrad_o, dwq_o, dwk_o, dwv_o, dwo_o, dw1_o, dw2_o, output_o, small_o, units_o,
        dattn, dres, full, qkv, prob, ctx, gat, wqkv, wo, dctx, dqkv, dprob, dscore, acc,
        block_f, own, psend, precv, xsend, xrecv, tgrad, moved, sums, dw1, dw2,
        dwq, dwk, dwv, dwo, teacher, parts, small, rbuf, sbuf, ubuf,
        in_sem, out_sem, move_send, move_recv, r_send, r_recv, s_send, s_recv, u_send, u_recv, *sems,
    ) = refs
    g = Group(n)
    cycle = Cycle(size)
    rings = []
    grads = ((dw1, dw1_o), (dw2, dw2_o), (dwq, dwq_o), (dwk, dwk_o), (dwv, dwv_o), (dwo, dwo_o))
    for data, target in grads:
        for way in (1, -1):
            i = 11 + 7 * len(rings)
            rings.append(Ring(cycle, data, target, way, sems[i : i + 7]))
    ticks = rings[0].ticks

    def tick(t, which):
        for ring in rings[2 * which : 2 * which + 2]:
            ring.tick(t)

    def row_to(i):
        to = lax.rem(g.me + 1 + i, n)
        return remote(parts.at[:, cols_of(to)], rbuf.at[i], r_send.at[i], r_recv.at[i], to)

    def small_to(i):
        to = {"dp": lax.rem(cycle.me + 1 + i, size)}
        return remote(small, sbuf.at[i], s_send.at[i], s_recv.at[i], to)

    def units_to(i):
        to = {"dp": lax.rem(cycle.me + 1 + i, size)}
        return remote(unit_ref, ubuf.at[i], u_send.at[i], u_recv.at[i], to)

    def move_to(i):
        to = lax.rem(g.me + 1 + i, n)
        return remote(
            out_ref.at[:, :, cols_of(to)], moved.at[:, g.slot(g.me)], move_send.at[i], move_recv.at[i], to
        )

    def move_from(i):
        to = lax.rem(g.me + 1 + i, n)
        frm = lax.rem(g.me - 1 - i + n, n)
        return remote(
            out_ref.at[:, :, cols_of(to)], moved.at[:, g.slot(frm)], move_send.at[i], move_recv.at[i], to
        )

    width = heads * HD
    rows = SLOT // n
    gsems, rsems = sems[:7], sems[7:11]
    cols_of = lambda h: pl.ds(pl.multiple_of(h * width, width), width)
    seq = lambda s: pl.ds(pl.multiple_of(s * SLOT, SLOT), SLOT)
    own_rows = lambda s: pl.ds(pl.multiple_of(s * rows, rows), rows)
    spot = lambda s, h: pl.ds(pl.multiple_of(s * SLOT + g.slot(h) * rows, rows), rows)
    ga = Gather(g, gsems, lambda s: dlow_ref.at[own_rows(s), :], lambda s, h: dattn.at[spot(s, h), :])
    re = Reduce(g, rsems, psend, precv, own, xsend, xrecv)
    loads = [
        pltpu.make_async_copy(wo_ref, wo, in_sem.at[0]),
        pltpu.make_async_copy(ctx_ref, ctx, in_sem.at[1]),
        pltpu.make_async_copy(qkv_ref, qkv, in_sem.at[2]),
        pltpu.make_async_copy(prob_ref, prob, in_sem.at[3]),
        pltpu.make_async_copy(wq_ref, wqkv.at[:, pl.ds(0, width)], in_sem.at[4]),
        pltpu.make_async_copy(wk_ref, wqkv.at[:, pl.ds(width, width)], in_sem.at[5]),
        pltpu.make_async_copy(wv_ref, wqkv.at[:, pl.ds(2 * width, width)], in_sem.at[6]),
        pltpu.make_async_copy(dres_ref, dres, in_sem.at[7]),
        pltpu.make_async_copy(full_ref, full, in_sem.at[8]),
        pltpu.make_async_copy(gat_ref, gat, in_sem.at[9]),
        pltpu.make_async_copy(
            out_ref.at[:, :, cols_of(g.me)], moved.at[:, g.slot(g.me)], in_sem.at[11]
        ),
        pltpu.make_async_copy(teacher_ref, teacher, in_sem.at[10]),
    ]
    grads_in = [
        pltpu.make_async_copy(dw1_ref, dw1, in_sem.at[12]),
        pltpu.make_async_copy(dw2_ref, dw2, in_sem.at[13]),
    ]
    for load in grads_in:
        load.start()
    meet(g.all_peers() + [{"dp": lax.rem(cycle.me + 1 + i, size)} for i in range(size - 1)])

    def begin(s, carry):
        ga.start(s)
        return carry

    lax.fori_loop(0, seqs, begin, 0)
    for load in loads:
        load.start()
    sums[...] = jnp.zeros_like(sums)
    for load in grads_in:
        load.wait()
    tick(0, 0)
    tick(0, 1)
    ga.relay(0)
    for load in loads[:8]:
        load.wait()
    tick(1, 0)
    tick(1, 1)

    lanes = lax.broadcasted_iota(jnp.int32, (1, width), 1)
    head_lanes = [
        jnp.where((lanes >= h * HD) & (lanes < (h + 1) * HD), 1.0, 0.0).astype(BF) for h in range(heads)
    ]

    def out(s):
        return pltpu.make_async_copy(tgrad.at[seq(s), :], tgrad_o.at[seq(s), :], out_sem.at[s])

    def finish(s):
        re.arrive(s)

        def block(i, carry):
            at = pl.ds(pl.multiple_of(i * 32, 32), 32)
            tgrad[pl.ds(pl.multiple_of(s * SLOT + i * 32, 32), 32), :] = re.total(s, at)
            return carry

        lax.fori_loop(0, SLOT // 32, block, 0)
        out(s).start()

    def token_block(s, h):
        cols = pl.ds(pl.multiple_of(h * width, width), width)
        block_f[...] = nt(dqkv[seq(s), :], wqkv[cols, :])
        mine = pl.ds(pl.multiple_of(g.slot(g.me) * rows, rows), rows)
        block_f[mine, :] += dres[own_rows(s), cols]

    def sequence(s, carry):
        ga.wait(s)
        here = seq(s)
        d_gated = nt(dattn[here, :], wo[...])
        sums[0] += fold(d_gated * ctx[here, :])
        dctx[...] = (d_gated * gate_ref[...]).astype(BF)
        first = 2 + s * (heads + 2) // 2
        tick(first, 0)

        @pl.when(s + 1 < seqs)
        def _():
            ga.relay(s + 1)

        @pl.when(s > 0)
        def _():
            re.cross(s - 1)

        @pl.when(s == 1)
        def _():
            for i in range(n - 1):
                move_to(i).start()
            for i in range(size - 1):
                units_to(i).start()

        for h in range(heads):
            d_context = dctx[...] * head_lanes[h]
            dprob[...] = nt(d_context, qkv[here, 2 * width : 3 * width])

            def softmax(i, carry, h=h):
                at = pl.ds(pl.multiple_of(i * 64, 64), 64)
                p = prob[s, h, at, :].astype(F32)
                weighted = p * dprob[at, :]
                total = jnp.sum(weighted, axis=1, keepdims=True)
                dscore[at, :] = (weighted - p * total).astype(BF)
                return carry

            lax.fori_loop(0, SLOT // 64, softmax, 0, unroll=True)
            tick(first + (h + 1) // 2, (h + 1) % 2)
            terms = (
                nn(dscore[...], qkv[here, width : 2 * width] * head_lanes[h]),
                tn(dscore[...], qkv[here, 0:width] * head_lanes[h]),
                tn(prob[s, h], d_context),
            )
            for k in range(3):
                acc[k] = terms[k] if h == 0 else acc[k] + terms[k]
        scales = (HD**-0.5, HD**-0.5, 1.0)
        for k in range(3):
            rounded = (acc[k] * scales[k]).astype(BF)
            dqkv[here, k * width : (k + 1) * width] = rounded
            sums[1 + k] += fold(rounded.astype(F32))
        for chip in range(n // 2):
            token_block(s, 2 * chip + 1 - g.c)
            psend[s, chip] = block_f[...].astype(BF)
        re.start(s)
        tick(first + (heads + 1) // 2, 1)
        for chip in range(n // 2):
            token_block(s, 2 * chip + g.c)
            own[s, chip] = block_f[...]

        @pl.when(s > 0)
        def _():
            finish(s - 1)

        return carry

    lax.fori_loop(0, seqs, sequence, 0)
    re.cross(seqs - 1)
    for load in loads[8:]:
        load.wait()

    def rest(t, carry):
        tick(t, 0)
        tick(t, 1)
        return carry

    lax.fori_loop(2 + seqs * (heads + 2) // 2, ticks, rest, 0)

    def token_grad(b, carry):
        cols = pl.ds(pl.multiple_of(b * NB, NB), NB)
        term = tn(full[:, cols], dqkv[...])
        for k, grad in enumerate((dwq, dwk, dwv)):
            grad[cols, :] = term[:, k * width : (k + 1) * width].astype(BF)
        return carry

    lax.fori_loop(0, D // NB, token_grad, 0)
    for which in range(2, 5):
        tick(0, which)
    dwo[...] = tn(gat[...], dattn[...]).astype(BF)
    tick(0, 5)
    for i in range(n - 1):
        move_from(i).wait()
    moved_out = pltpu.make_async_copy(moved, output_o, in_sem.at[14])
    moved_out.start()

    def squares(s, total):
        length = len_ref[cycle.me * seqs + s]

        def block(i, total):
            each = rows // 32
            at = pl.ds(pl.multiple_of(lax.rem(i, each) * 32, 32), 32)
            value = moved[s, lax.div(i, each), at, :].astype(F32)
            place = i * 32 + lax.broadcasted_iota(jnp.int32, (32, 1), 0)
            differ = value - teacher[pl.ds(pl.multiple_of(s * SLOT + i * 32, 32), 32), :].astype(F32)
            return total + fold(jnp.where(place < length, differ * differ, 0.0))

        return lax.fori_loop(0, SLOT // 32, block, total)

    square_sum = lax.fori_loop(0, seqs, squares, jnp.zeros((8, width), F32))
    parts[...] = row_ref[...]
    for h in range(n):
        parts[7:8, h * width : (h + 1) * width] = jnp.sum(square_sum, axis=0, keepdims=True)
    for i in range(n - 1):
        row_to(i).start()
    for which in range(2, 6):
        tick(1, which)
    finish(seqs - 1)
    total = parts[:, cols_of(g.me)]
    for i in range(n - 1):
        row_to(i).wait()
        total = total + rbuf[i]
    small[:, 0:width] = total
    for k in range(4):
        small[k : k + 1, width : 2 * width] = jnp.sum(sums[k], axis=0, keepdims=True)
    small[4:8, width : 2 * width] = jnp.zeros((4, width), F32)
    for i in range(size - 1):
        small_to(i).start()

    def last(t, carry):
        for which in range(2, 6):
            tick(t, which)
        return carry

    lax.fori_loop(2, ticks, last, 0)
    small_sum = small[...]
    unit_sum = unit_ref[...]
    for i in range(size - 1):
        small_to(i).wait()
        units_to(i).wait()
        small_sum = small_sum + sbuf[i]
        unit_sum = unit_sum + ubuf[i]
    small_o[...] = small_sum
    units_o[...] = unit_sum
    moved_out.wait()
    for ring in rings:
        ring.drain()

    def end(s, carry):
        ga.drain(s)
        out(s).wait()
        return carry

    lax.fori_loop(0, seqs, end, 0)


def complete_kernel(n, heads, units, *refs):
    (
        dw1_ref, dw2_ref, dwq_ref, dwk_ref, dwv_ref, dwo_ref, tgrad_ref, output_ref,
        small_ref, unit_ref, ha_ref, ua_ref, wa_ref, mult_ref, hn_ref, un_ref, wn_ref, len_ref,
        dw1_o, dw2_o, dwq_o, dwk_o, dwv_o, dwo_o, tgrad_o, output_o,
        qb_o, vb_o, ob_o, ag_o, as_o, db_o, fg_o, fs_o, b1_o, ha_o, ua_o, wa_o, mse_o, mult_o,
        dw1, dw2, dwq, dwk, dwv, dwo, tgrad, output, fw1, fw2, fwq, fwk, fwv, fwo, in_sem, out_sem,
    ) = refs
    width = heads * HD
    rank = lax.axis_index("hid")
    wide = (
        (dw1_ref, dw1, fw1, dw1_o), (dw2_ref, dw2, fw2, dw2_o), (dwq_ref, dwq, fwq, dwq_o),
        (dwk_ref, dwk, fwk, dwk_o), (dwv_ref, dwv, fwv, dwv_o), (dwo_ref, dwo, fwo, dwo_o),
        (tgrad_ref, tgrad, tgrad, tgrad_o), (output_ref, output, output, output_o),
    )
    parts = 4

    def piece(ref, p):
        rows = ref.shape[0] // parts
        return ref.at[pl.ds(pl.multiple_of(p * rows, rows), rows), :]

    def load(k, p):
        return pltpu.make_async_copy(piece(wide[k][0], p), piece(wide[k][1], p), in_sem.at[k, p])

    def store(k, p):
        return pltpu.make_async_copy(piece(wide[k][2], p), piece(wide[k][3], p), out_sem.at[k, p])

    for k in range(len(wide)):
        for p in range(parts):
            load(k, p).start()

    head_all = small_ref[:, width : 2 * width]
    for ref, row in ((ob_o, 6), (ag_o, 4), (as_o, 5), (db_o, 3), (fg_o, 0), (fs_o, 1)):
        ref[...] = small_ref[row : row + 1, 0:width]
    qb_o[...] = head_all[1:2, :]
    vb_o[...] = head_all[3:4, :]
    b1_o[...] = unit_ref[1:2, :]
    keeps = [keep_prob(ref[...]) for ref in (ha_ref, ua_ref, wa_ref)]
    heads_kept, units_kept, dims_kept = [jnp.sum(k, axis=1, keepdims=True) for k in keeps]
    full_size = 4.0 * D * D + 2.0 * D * FF
    gap = 1.0 - (4.0 * HD * heads_kept * dims_kept + 2.0 * units_kept * dims_kept) / full_size - TARGET
    pull = -(lane_of(mult_ref[...], 0) + 2.0 * lane_of(mult_ref[...], 1) * gap) / full_size
    slot = lax.broadcasted_iota(jnp.int32, (1, 2), 1)
    mult_o[...] = mult_ref[...] + ASCENT * jnp.where(slot == 0, gap, gap * gap)

    def pulled(alpha, factor):
        k = keep_prob(alpha)
        return pull * factor * k * (1.0 - k)

    unit_alpha = part_of(ua_ref, rank, units)
    ua_o[...] = unit_ref[0:1, :] * gate_slope(un_ref[...], unit_alpha) + pulled(unit_alpha, 2.0 * dims_kept)
    width_alpha = part_of(wa_ref, rank, width)
    wa_o[...] = small_ref[2:3, 0:width] * gate_slope(wn_ref[...], width_alpha) + pulled(
        width_alpha, 4.0 * HD * heads_kept + 2.0 * units_kept
    )
    noise_row, alpha_row = head_row(hn_ref, ha_ref, rank, heads)
    lanes = lax.broadcasted_iota(jnp.int32, (1, width), 1)
    per_lane = head_all[0:1, :] * gate_slope(noise_row, alpha_row)
    head_pulled = pulled(alpha_row, 4.0 * HD * dims_kept) * (1.0 / HD)
    for h in range(heads):
        here = (lanes >= h * HD) & (lanes < (h + 1) * HD)
        ha_o[:, h : h + 1] = jnp.sum(jnp.where(here, per_lane + head_pulled, 0.0), axis=1, keepdims=True)
    live = jnp.sum(len_ref[...].astype(F32), axis=1, keepdims=True)
    mse_o[...] = jnp.sum(small_ref[7:8, 0:width], axis=1, keepdims=True) / (live * D)

    for k, (_, low, high, _) in enumerate(wide):
        rows = low.shape[0] // parts
        for p in range(parts):
            load(k, p).wait()
            if low is not high:

                step = min(64, rows)

                def widen(i, carry, low=low, high=high, first=p * rows, step=step):
                    at = pl.ds(pl.multiple_of(first + i * step, step), step)
                    high[at, :] = low[at, :].astype(F32)
                    return carry

                lax.fori_loop(0, rows // step, widen, 0)
            store(k, p).start()
    for k in range(len(wide)):
        for p in range(parts):
            store(k, p).wait()


def hbm():
    return pl.BlockSpec(memory_space=pl.ANY)


def vmem():
    return pl.BlockSpec(memory_space=pltpu.VMEM)


def smem():
    return pl.BlockSpec(memory_space=pltpu.SMEM)


def call(kernel, name, ident, ins, outs, scratch, flops):
    return pl.pallas_call(
        kernel,
        name=name,
        out_shape=[jax.ShapeDtypeStruct(shape, dtype) for shape, dtype, _ in outs],
        in_specs=ins,
        out_specs=[spec for _, _, spec in outs],
        scratch_shapes=scratch,
        compiler_params=pltpu.CompilerParams(
            collective_id=ident, has_side_effects=True, vmem_limit_bytes=VMEM_LIMIT
        ),
        cost_estimate=pl.CostEstimate(flops=flops, bytes_accessed=30_000_000, transcendentals=0),
    )


def attend(n, seqs, heads, args):
    width, rows, nx, half = heads * HD, SLOT // n, n // 2, SLOT // 2
    tokens, owned = seqs * SLOT, seqs * rows
    v, dma = pltpu.VMEM, pltpu.SemaphoreType.DMA
    return call(
        functools.partial(attend_kernel, n, seqs, heads),
        "attend",
        0,
        [smem()] + [hbm()] * 3 + [vmem()] * 10 + [hbm()] * 3 + [vmem()] * 2 + [hbm()],
        [
            ((tokens, D), BF, hbm()),
            ((tokens, 3 * width), BF, hbm()),
            ((seqs, heads, SLOT, SLOT), BF, hbm()),
            ((tokens, width), F32, hbm()),
            ((tokens, width), BF, hbm()),
            ((owned, D), F32, hbm()),
            ((owned, D), F32, hbm()),
            ((owned, 128), F32, hbm()),
            ((owned, D), BF, hbm()),
            ((8, D), F32, vmem()),
            ((seqs, rows, D), BF, hbm()),
            ((1, width), F32, vmem()),
        ],
        [
            v((tokens, D), BF),
            v((D, 3 * width), BF),
            v((width, D), BF),
            v((tokens, 3 * width), BF),
            v((seqs, heads, SLOT, SLOT), BF),
            v((tokens, width), F32),
            v((tokens, width), BF),
            v((seqs, nx, rows, D), F32),
            v((seqs, nx, rows, D), BF),
            v((seqs, nx, rows, D), BF),
            v((seqs, nx - 1, rows, D), BF),
            v((seqs, nx - 1, rows, D), BF),
            v((owned, D), F32),
            v((owned, D), F32),
            v((owned, 128), F32),
            v((owned, D), BF),
            v((8, D), F32),
            v((seqs, rows, D), BF),
            v((tokens, width), BF),
            v((tokens, width), BF),
            v((seqs, n, rows, width), BF),
            v((8, width), F32),
            v((SLOT, SLOT), F32),
            dma((9,)),
            dma((seqs, 9)),
            dma((n - 1,)),
            dma((n - 1,)),
            dma((n - 1,)),
            dma((n - 1,)),
        ]
        + gather_sems(seqs, nx)
        + reduce_sems(seqs, nx),
        10_000_000_000,
    )(*args)


def feed(n, seqs, units, args):
    rows, nx = SLOT // n, n // 2
    tokens, owned = seqs * SLOT, seqs * rows
    v, dma = pltpu.VMEM, pltpu.SemaphoreType.DMA
    return call(
        functools.partial(feed_kernel, n, seqs, units),
        "feed",
        1,
        [smem(), hbm(), hbm(), hbm(), hbm(), vmem(), hbm(), hbm(), vmem(), hbm(), vmem(), vmem()],
        [
            ((owned, D), BF, hbm()),
            ((owned, D), BF, hbm()),
            ((owned, D), F32, hbm()),
            ((D, units), BF, hbm()),
            ((units, D), BF, hbm()),
            ((8, D), F32, vmem()),
            ((2, units), F32, vmem()),
        ],
        [
            v((tokens, D), BF),
            v((tokens, D), BF),
            v((D, units), BF),
            v((units, D), BF),
            v((tokens, units), BF),
            v((tokens, units), BF),
            v((tokens, units), BF),
            v((seqs, nx, rows, D), F32),
            v((seqs, nx, rows, D), BF),
            v((seqs, nx, rows, D), BF),
            v((seqs, nx - 1, rows, D), BF),
            v((seqs, nx - 1, rows, D), BF),
            v((owned, D), F32),
            v((owned, D), F32),
            v((owned, 128), F32),
            v((owned, D), BF),
            v((owned, D), F32),
            v((owned, D), BF),
            v((owned, D), BF),
            v((owned, D), BF),
            v((owned, D), F32),
            v((SLOT, NB), F32),
            v((D // NB, NB, D), BF),
            v((7, 8, D), F32),
            v((2, 8, units), F32),
            v((1, units), F32),
            dma((6,)),
            dma((seqs, 3)),
            dma((2, D // NB)),
        ]
        + (gather_sems(seqs, nx) + reduce_sems(seqs, nx)) * 2,
        30_000_000_000,
    )(*args)


def attend_back(n, seqs, heads, units, size, args):
    width, rows, nx = heads * HD, SLOT // n, n // 2
    tokens, owned = seqs * SLOT, seqs * rows
    v, dma = pltpu.VMEM, pltpu.SemaphoreType.DMA
    return call(
        functools.partial(attend_back_kernel, n, seqs, heads, size),
        "attend_back",
        2,
        [smem()] + [hbm()] * 15 + [vmem()] * 3,
        [
            ((tokens, width), F32, hbm()),
            ((D, width), BF, hbm()),
            ((D, width), BF, hbm()),
            ((D, width), BF, hbm()),
            ((width, D), BF, hbm()),
            ((D, units), BF, hbm()),
            ((units, D), BF, hbm()),
            ((seqs, n, rows, width), BF, hbm()),
            ((8, 2 * width), F32, vmem()),
            ((2, units), F32, vmem()),
        ],
        [
            v((tokens, D), BF),
            v((owned, D), F32),
            v((tokens, D), BF),
            v((tokens, 3 * width), BF),
            v((seqs, heads, SLOT, SLOT), BF),
            v((tokens, width), F32),
            v((tokens, width), BF),
            v((D, 3 * width), BF),
            v((width, D), BF),
            v((SLOT, width), BF),
            v((tokens, 3 * width), BF),
            v((SLOT, SLOT), F32),
            v((SLOT, SLOT), BF),
            v((3, SLOT, width), F32),
            v((SLOT, width), F32),
            v((seqs, nx, SLOT, width), F32),
            v((seqs, nx, SLOT, width), BF),
            v((seqs, nx, SLOT, width), BF),
            v((seqs, nx - 1, SLOT, width), BF),
            v((seqs, nx - 1, SLOT, width), BF),
            v((tokens, width), F32),
            v((seqs, n, rows, width), BF),
            v((4, 8, width), F32),
            v((D, units), BF),
            v((units, D), BF),
            v((D, width), BF),
            v((D, width), BF),
            v((D, width), BF),
            v((width, D), BF),
            v((tokens, width), BF),
            v((8, D), F32),
            v((8, 2 * width), F32),
            v((n - 1, 8, width), F32),
            v((size - 1, 8, 2 * width), F32),
            v((size - 1, 2, units), F32),
            dma((15,)),
            dma((seqs,)),
            dma((n - 1,)),
            dma((n - 1,)),
            dma((n - 1,)),
            dma((n - 1,)),
        ]
        + [dma((size - 1,))] * 4
        + gather_sems(seqs, nx)
        + reduce_sems(seqs, nx)
        + ring_scratch((D, units), size) * 2
        + ring_scratch((units, D), size) * 2
        + ring_scratch((D, width), size) * 6
        + ring_scratch((width, D), size) * 2,
        20_000_000_000,
    )(*args)


def complete(n, heads, units, tokens, args):
    v, dma, width = pltpu.VMEM, pltpu.SemaphoreType.DMA, heads * HD
    shapes = [(D, units), (units, D), (D, width), (D, width), (D, width), (width, D)]
    rows = [(width,)] * 8 + [(units,), (heads,), (units,), (width,), (1,), (2,)]
    return pl.pallas_call(
        functools.partial(complete_kernel, n, heads, units),
        name="complete",
        out_shape=[jax.ShapeDtypeStruct(shape, F32) for shape in shapes]
        + [jax.ShapeDtypeStruct((tokens, width), F32), jax.ShapeDtypeStruct((tokens, width), BF)]
        + [jax.ShapeDtypeStruct((1, count), F32) for (count,) in rows],
        in_specs=[hbm()] * 8 + [vmem()] * 10,
        out_specs=[hbm()] * 8 + [vmem()] * len(rows),
        scratch_shapes=[v(shape, BF) for shape in shapes]
        + [v((tokens, width), F32), v((tokens, width), BF)]
        + [v(shape, F32) for shape in shapes]
        + [dma((8, 4))] * 2,
        compiler_params=pltpu.CompilerParams(vmem_limit_bytes=VMEM_LIMIT),
        cost_estimate=pl.CostEstimate(flops=10_000_000, bytes_accessed=24_000_000, transcendentals=0),
    )(*args)


def on_device(
    n,
    size,
    tokens,
    query_weight,
    query_bias,
    key_weight,
    value_weight,
    value_bias,
    output_weight,
    output_bias,
    attention_gain,
    attention_shift,
    inner_weight,
    inner_bias,
    down_weight,
    down_bias,
    final_gain,
    final_shift,
    head_alpha,
    unit_alpha,
    width_alpha,
    multipliers,
    head_noise,
    unit_noise,
    width_noise,
    lengths,
    teacher,
    upstream,
):
    row_count, width = tokens.shape
    heads = width // HD
    units = inner_weight.shape[1]
    seqs = row_count // SLOT
    rows = SLOT // n
    flat = lambda vector: vector.reshape(1, vector.shape[0])
    head_alpha, unit_alpha, width_alpha = flat(head_alpha), flat(unit_alpha), flat(width_alpha)
    head_noise, unit_noise, width_noise = flat(head_noise), flat(unit_noise), flat(width_noise)
    full, qkv, prob, ctx, gat, nrm, pre, rstd, mid, par, change_rows, gate_row = attend(
        n,
        seqs,
        heads,
        (
            lengths,
            tokens,
            upstream,
            teacher,
            flat(output_bias),
            flat(attention_gain),
            flat(attention_shift),
            flat(down_bias),
            flat(final_gain),
            flat(final_shift),
            width_noise,
            width_alpha,
            head_noise,
            head_alpha,
            query_weight,
            key_weight,
            value_weight,
            flat(query_bias),
            flat(value_bias),
            output_weight,
        ),
    )
    out_rows, d_low, d_res, dw_inner, dw_down, row_sums, unit_sums = feed(
        n,
        seqs,
        units,
        (
            lengths,
            mid,
            nrm,
            pre,
            rstd,
            par,
            change_rows.reshape(seqs * rows, D),
            inner_weight,
            flat(inner_bias),
            down_weight,
            unit_noise,
            unit_alpha,
        ),
    )
    tokens_grad, dw_q, dw_k, dw_v, dw_o, dw_inner, dw_down, output, small, unit_all = attend_back(
        n,
        seqs,
        heads,
        units,
        size,
        (
            lengths,
            d_low,
            d_res,
            full,
            qkv,
            prob,
            ctx,
            gat,
            query_weight,
            key_weight,
            value_weight,
            output_weight,
            dw_inner,
            dw_down,
            out_rows.reshape(seqs, rows, D),
            teacher,
            gate_row,
            row_sums,
            unit_sums,
        ),
    )
    output = output.reshape(row_count, width)
    dw_inner, dw_down, dw_q, dw_k, dw_v, dw_o, tokens_grad, output, *vectors = complete(
        n,
        heads,
        units,
        row_count,
        (
            dw_inner,
            dw_down,
            dw_q,
            dw_k,
            dw_v,
            dw_o,
            tokens_grad,
            output,
            small,
            unit_all,
            head_alpha,
            unit_alpha,
            width_alpha,
            flat(multipliers),
            head_noise,
            unit_noise,
            width_noise,
            flat(lengths),
        ),
    )
    qb, vb, ob, ag, shift, db, fg, fs, b1, ha, ua, wa, mse, mult = [v.reshape(v.shape[1]) for v in vectors]
    return (
        output,
        tokens_grad,
        dw_q,
        qb,
        dw_k,
        dw_v,
        vb,
        dw_o,
        ob,
        ag,
        shift,
        dw_inner,
        b1,
        dw_down,
        db,
        fg,
        fs,
        ha,
        ua,
        wa,
        mse.reshape(()),
        mult,
    )


def solution(mesh):
    tall, wide, vec, rep = P("dp", "hid"), P(None, "hid"), P("hid"), P()
    deep = P("hid", None)
    return jax.shard_map(
        functools.partial(on_device, mesh.shape["hid"], mesh.shape["dp"]),
        mesh=mesh,
        in_specs=(tall, wide, vec, wide, wide, vec, deep, vec, vec, vec, wide, vec, deep)
        + (vec,) * 3
        + (rep,) * 4
        + (vec,) * 3
        + (rep, tall, tall),
        out_specs=(tall, tall, wide, vec, wide, wide, vec, deep, vec, vec, vec, wide, vec, deep)
        + (vec,) * 6
        + (rep, rep),
        check_vma=False,
    )
```

```python
import functools
import math

import jax
import jax.numpy as jnp
from jax import lax
from jax.experimental import pallas as pl
from jax.experimental.pallas import tpu as pltpu
from jax.sharding import PartitionSpec as P

D = 1024
HD = 64
FF = 4096
SLOT = 512

BETA = 2.0 / 3.0
GAMMA = -0.1
ZETA = 1.1
TARGET = 0.7
ASCENT = 1.0
EPS = 1e-12
MASKED = -1000000000.0
ROOT_HALF = 0.7071067811865476
ROOT_TWO_PI = 2.5066282746310002

MESH = pl.DeviceIdType.MESH
VMEM_LIMIT = 66_000_000
BF = jnp.bfloat16
F32 = jnp.float32
NB = 256
RB = 16


def gate_value(noise, alpha):
    logits = (jnp.log(noise) - jnp.log(1.0 - noise) + alpha) / BETA
    stretched = jax.nn.sigmoid(logits) * (ZETA - GAMMA) + GAMMA
    return jnp.clip(stretched, 0.0, 1.0)


def gate_slope(noise, alpha):
    s = jax.nn.sigmoid((jnp.log(noise) - jnp.log(1.0 - noise) + alpha) / BETA)
    stretched = s * (ZETA - GAMMA) + GAMMA
    free = (stretched > 0.0) & (stretched < 1.0)
    return jnp.where(free, (ZETA - GAMMA) / BETA * s * (1.0 - s), 0.0)


def keep_prob(alpha):
    return jax.nn.sigmoid(alpha - BETA * math.log(-GAMMA / ZETA))


def lane_of(row, place):
    lanes = lax.broadcasted_iota(jnp.int32, row.shape, 1)
    return jnp.sum(jnp.where(lanes == place, row, 0.0), axis=1, keepdims=True)


def head_row(noise_ref, alpha_ref, rank, heads):
    lanes = lax.broadcasted_iota(jnp.int32, (1, heads * HD), 1)
    noise = jnp.full((1, heads * HD), 0.5, F32)
    alpha = jnp.zeros((1, heads * HD), F32)
    for h in range(heads):
        here = (lanes >= h * HD) & (lanes < (h + 1) * HD)
        noise = jnp.where(here, lane_of(noise_ref[...], h), noise)
        alpha = jnp.where(here, lane_of(alpha_ref[...], rank * heads + h), alpha)
    return noise, alpha


def part_of(ref, rank, width):
    return ref[:, pl.ds(pl.multiple_of(rank * width, width), width)]


def nn(a, b):
    return jnp.dot(a, b, preferred_element_type=F32)


def nt(a, b):
    return lax.dot_general(a, b, (((1,), (1,)), ((), ())), preferred_element_type=F32)


def tn(a, b):
    return lax.dot_general(a, b, (((0,), (0,)), ((), ())), preferred_element_type=F32)


def fold(values):
    return jnp.sum(values.reshape(values.shape[0] // 8, 8, values.shape[1]), axis=0)


class Group:
    def __init__(self, n):
        self.n = n
        self.nx = n // 2
        self.me = lax.axis_index("hid")
        self.x = lax.div(self.me, 2)
        self.c = lax.rem(self.me, 2)
        self.partner = 2 * self.x + 1 - self.c

    def chip_ahead(self, j):
        return lax.rem(self.x + 1 + j, self.nx)

    def chip_behind(self, j):
        return lax.rem(self.x - 1 - j + self.nx, self.nx)

    def slot(self, h):
        return lax.rem(h, 2) * self.nx + lax.div(h, 2)

    def all_peers(self):
        return [{"hid": lax.rem(self.me + 1 + i, self.n)} for i in range(self.n - 1)]

    def near_peers(self):
        near = [self.partner] + [2 * self.chip_ahead(j) + self.c for j in range(self.nx - 1)]
        return [{"hid": peer} for peer in near]


def remote(src, dst, send_sem, recv_sem, to):
    return pltpu.make_async_remote_copy(
        src_ref=src,
        dst_ref=dst,
        send_sem=send_sem,
        recv_sem=recv_sem,
        device_id=to if isinstance(to, dict) else {"hid": to},
        device_id_type=MESH,
    )


def gather_sems(seqs, nx):
    wide = pltpu.SemaphoreType.DMA((seqs, nx - 1))
    return [wide] * 4 + [pltpu.SemaphoreType.DMA((seqs,))] * 3


def reduce_sems(seqs, nx):
    wide = pltpu.SemaphoreType.DMA((seqs, nx - 1))
    return [wide] * 2 + [pltpu.SemaphoreType.DMA((seqs,))] * 2


class Gather:
    def __init__(self, group, sems, source, region):
        self.g, self.source, self.region = group, source, region
        self.xs, self.xr, self.rs, self.rr, self.ps, self.pr, self.os = sems

    def _own(self, s):
        return pltpu.make_async_copy(self.source(s), self.region(s, self.g.me), self.os.at[s])

    def _cross(self, s, j):
        to = 2 * self.g.chip_ahead(j) + self.g.c
        return remote(
            self.source(s), self.region(s, self.g.me), self.xs.at[s, j], self.xr.at[s, j], to
        )

    def _crossed(self, s, j):
        to = 2 * self.g.chip_ahead(j) + self.g.c
        block = self.region(s, 2 * self.g.chip_behind(j) + self.g.c)
        return remote(self.source(s), block, self.xs.at[s, j], self.xr.at[s, j], to)

    def _pair(self, s):
        return remote(
            self.source(s),
            self.region(s, self.g.me),
            self.ps.at[s],
            self.pr.at[s],
            self.g.partner,
        )

    def _paired(self, s):
        block = self.region(s, self.g.partner)
        return remote(self.source(s), block, self.ps.at[s], self.pr.at[s], self.g.partner)

    def _relay(self, s, j):
        block = self.region(s, 2 * self.g.chip_behind(j) + self.g.c)
        return remote(block, block, self.rs.at[s, j], self.rr.at[s, j], self.g.partner)

    def _relayed(self, s, j):
        block = self.region(s, 2 * self.g.chip_behind(j) + 1 - self.g.c)
        return remote(block, block, self.rs.at[s, j], self.rr.at[s, j], self.g.partner)

    def start(self, s):
        for j in range(self.g.nx - 1):
            self._cross(s, j).start()
        self._pair(s).start()
        self._own(s).start()

    def relay(self, s):
        for j in range(self.g.nx - 1):
            self._crossed(s, j).wait_recv()
            self._relay(s, j).start()

    def wait(self, s):
        self._own(s).wait()
        self._paired(s).wait_recv()
        for j in range(self.g.nx - 1):
            self._relayed(s, j).wait_recv()

    def drain(self, s):
        self._pair(s).wait_send()
        for j in range(self.g.nx - 1):
            self._cross(s, j).wait_send()
            self._relay(s, j).wait_send()


class Reduce:
    def __init__(self, group, sems, psend, precv, own, xsend, xrecv):
        self.g = group
        self.psend, self.precv, self.own, self.xsend, self.xrecv = psend, precv, own, xsend, xrecv
        self.xs, self.xr, self.ps, self.pr = sems

    def _pair(self, s):
        return remote(
            self.psend.at[s], self.precv.at[s], self.ps.at[s], self.pr.at[s], self.g.partner
        )

    def _cross(self, s, j):
        to = 2 * self.g.chip_ahead(j) + self.g.c
        return remote(
            self.xsend.at[s, j], self.xrecv.at[s, j], self.xs.at[s, j], self.xr.at[s, j], to
        )

    def start(self, s):
        self._pair(s).start()

    def cross(self, s):
        self._pair(s).wait()
        rows = self.own.shape[2]
        for j in range(self.g.nx - 1):
            chip = self.g.chip_ahead(j)

            def add(i, carry, chip=chip, j=j):
                at = pl.ds(pl.multiple_of(i * RB, RB), RB)
                total = self.own[s, chip, at, :] + self.precv[s, chip, at, :].astype(F32)
                self.xsend[s, j, at, :] = total.astype(BF)
                return carry

            lax.fori_loop(0, rows // RB, add, 0)
            self._cross(s, j).start()

    def arrive(self, s):
        for j in range(self.g.nx - 1):
            self._cross(s, j).wait()

    def total(self, s, at):
        total = self.own[s, self.g.x, at, :] + self.precv[s, self.g.x, at, :].astype(F32)
        for j in range(self.g.nx - 1):
            total = total + self.xrecv[s, j, at, :].astype(F32)
        return total


class Cycle:
    def __init__(self, size):
        self.size = size
        self.me = lax.axis_index("dp")
        self.length = size // 2
        line, column = lax.div(self.me, 2), lax.rem(self.me, 2)
        self.place = line + column * (size - 1 - 2 * line)

    def device(self, place):
        column = lax.div(place, self.length)
        line = place + column * (self.size - 1 - 2 * place)
        return 2 * line + column

    def beside(self, way):
        return self.device(lax.rem(self.place + way + self.size, self.size))


def split(shape, size):
    tall = max(16, shape[0] // (2 * size))
    across = 2 * size * tall // shape[0]
    return tall, shape[1] // across, across


def ring_scratch(shape, size):
    tall, broad, _ = split(shape, size)
    step = pltpu.SemaphoreType.DMA((size - 1,))
    return [
        pltpu.VMEM((size - 1, tall, broad), BF),
        pltpu.SemaphoreType.DMA((size,)),
    ] + [step] * 4 + [pltpu.SemaphoreType.REGULAR]


class Ring:
    def __init__(self, cycle, data, target, way, scratch):
        self.cycle, self.data, self.target, self.way = cycle, data, target, way
        self.size = cycle.size
        self.recv, self.out_sem, self.ss, self.sr, self.gs, self.gr, self.free = scratch
        self.tall, self.broad, self.across = split(data.shape, self.size)
        self.to, self.frm = {"dp": cycle.beside(way)}, {"dp": cycle.beside(-way)}
        self.ticks = 2 * self.size - 1

    def block(self, number):
        place = lax.rem(self.cycle.place + self.way * number + 2 * self.size, self.size)
        index = 2 * place + (0 if self.way > 0 else 1)
        if self.across == 1:
            return pl.multiple_of(index * self.tall, self.tall), 0
        row = lax.div(index, self.across)
        column = lax.rem(index, self.across)
        return (
            pl.multiple_of(row * self.tall, self.tall),
            pl.multiple_of(column * self.broad, self.broad),
        )

    def view(self, number):
        row, column = self.block(number)
        return self.data.at[pl.ds(row, self.tall), pl.ds(column, self.broad)]

    def _add(self, t):
        return remote(self.view(-t), self.recv.at[t], self.ss.at[t], self.sr.at[t], self.to)

    def _pass(self, t):
        block = self.view(1 - t)
        return remote(block, block, self.gs.at[t], self.gr.at[t], self.to)

    def _passed(self, t):
        block = self.view(-t)
        return remote(block, block, self.gs.at[t], self.gr.at[t], self.to)

    def _sum(self, t):
        row, column = self.block(-t)

        def part(i, carry):
            at = pl.ds(pl.multiple_of(row + i * RB, RB), RB)
            cols = pl.ds(column, self.broad)
            arrived = self.recv[t - 1, pl.ds(pl.multiple_of(i * RB, RB), RB), :].astype(F32)
            self.data[at, cols] = (self.data[at, cols].astype(F32) + arrived).astype(BF)
            return carry

        lax.fori_loop(0, self.tall // RB, part, 0)

    def _out(self, number, count):
        row, column = self.block(number)
        place = self.target.at[pl.ds(row, self.tall), pl.ds(column, self.broad)]
        return pltpu.make_async_copy(self.view(number), place, self.out_sem.at[count])

    def tick(self, t):
        size = self.size

        @pl.when(t == 0)
        def _():
            self._add(0).start()

        @pl.when((t >= 1) & (t <= size - 1))
        def _():
            self._add(t - 1).wait_recv()
            self._sum(t)

        @pl.when((t >= 1) & (t < size - 1))
        def _():
            self._add(t).start()

        @pl.when((t >= 1) & (t <= size - 1))
        def _():
            self._add(t - 1).wait_send()
            pl.semaphore_signal(self.free, inc=1, device_id=self.frm, device_id_type=MESH)

        @pl.when(t == size - 1)
        def _():
            pl.semaphore_wait(self.free, 1)
            self._pass(0).start()
            self._out(1, 0).start()

        @pl.when((t > size - 1) & (t < 2 * size - 1))
        def _():
            u = t - size
            self._passed(u).wait_recv()

            @pl.when(t < 2 * size - 2)
            def _():
                pl.semaphore_wait(self.free, 1)
                self._pass(u + 1).start()

            self._out(-u, u + 1).start()

    def drain(self):
        self._out(1, 0).wait()

        def step(t, carry):
            self._pass(t).wait_send()
            self._out(-t, t + 1).wait()
            return carry

        lax.fori_loop(0, self.size - 1, step, 0)


def meet(peers):
    barrier = pltpu.get_barrier_semaphore()
    for peer in peers:
        pl.semaphore_signal(barrier, inc=1, device_id=peer, device_id_type=MESH)
    pl.semaphore_wait(barrier, len(peers))


def mean_of(values):
    return jnp.sum(values, axis=1, keepdims=True) * (1.0 / D)


def attend_kernel(n, seqs, heads, *refs):
    (
        len_ref, tok_ref, up_ref, tea_ref, ob_ref, ag_ref, as_ref, db_ref, fg_ref, fs_ref,
        wn_ref, wa_ref, hn_ref, ha_ref, wq_ref, wk_ref, wv_ref, qb_ref, vb_ref, wo_ref,
        full_o, qkv_o, prob_o, ctx_o, gat_o, nrm_o, pre_o, rstd_o, mid_o, par_o, change_o, gate_o,
        full, wqkv, wo, qkv, prob, ctx, gat, own, psend, precv, xsend, xrecv,
        nrm, pre, rstd, mid, par, chg, up, tea, change, vec, score, in_sem, out_sem, vec_send, vec_recv, ch_send, ch_recv, *sems,
    ) = refs
    g = Group(n)
    width = heads * HD
    rows = SLOT // n
    gsems, rsems = sems[:7], sems[7:]
    cols = lambda h: pl.ds(pl.multiple_of(h * width, width), width)
    seq = lambda s: pl.ds(pl.multiple_of(s * SLOT, SLOT), SLOT)
    own_rows = lambda s: pl.ds(pl.multiple_of(s * rows, rows), rows)
    ga = Gather(g, gsems, lambda s: tok_ref.at[seq(s), :], lambda s, h: full.at[seq(s), cols(h)])
    re = Reduce(g, rsems, psend, precv, own, xsend, xrecv)

    def vec_to(i):
        to = lax.rem(g.me + 1 + i, n)
        return remote(vec, par.at[:, cols(g.me)], vec_send.at[i], vec_recv.at[i], to)

    def vec_from(i):
        to = lax.rem(g.me + 1 + i, n)
        frm = lax.rem(g.me - 1 - i + n, n)
        return remote(vec, par.at[:, cols(frm)], vec_send.at[i], vec_recv.at[i], to)

    def change_to(i):
        to = lax.rem(g.me + 1 + i, n)
        return remote(
            change.at[:, g.slot(to)], chg.at[:, :, cols(g.me)], ch_send.at[i], ch_recv.at[i], to
        )

    def change_from(i):
        to = lax.rem(g.me + 1 + i, n)
        frm = lax.rem(g.me - 1 - i + n, n)
        return remote(
            change.at[:, g.slot(to)], chg.at[:, :, cols(frm)], ch_send.at[i], ch_recv.at[i], to
        )

    loads = [
        pltpu.make_async_copy(wq_ref, wqkv.at[:, pl.ds(0, width)], in_sem.at[0]),
        pltpu.make_async_copy(wk_ref, wqkv.at[:, pl.ds(width, width)], in_sem.at[1]),
        pltpu.make_async_copy(wv_ref, wqkv.at[:, pl.ds(2 * width, width)], in_sem.at[2]),
        pltpu.make_async_copy(wo_ref, wo, in_sem.at[3]),
        pltpu.make_async_copy(up_ref, up, in_sem.at[4]),
        pltpu.make_async_copy(tea_ref, tea, in_sem.at[5]),
    ]
    par_own = pltpu.make_async_copy(vec, par.at[:, cols(g.me)], in_sem.at[7])
    change_own = pltpu.make_async_copy(
        change.at[:, g.slot(g.me)], chg.at[:, :, cols(g.me)], in_sem.at[8]
    )
    chg_out = pltpu.make_async_copy(chg, change_o, in_sem.at[6])

    def sequence_outs(s):
        return [
            pltpu.make_async_copy(full.at[seq(s), :], full_o.at[seq(s), :], out_sem.at[s, 0]),
            pltpu.make_async_copy(qkv.at[seq(s), :], qkv_o.at[seq(s), :], out_sem.at[s, 1]),
            pltpu.make_async_copy(prob.at[s], prob_o.at[s], out_sem.at[s, 2]),
            pltpu.make_async_copy(ctx.at[seq(s), :], ctx_o.at[seq(s), :], out_sem.at[s, 3]),
            pltpu.make_async_copy(gat.at[seq(s), :], gat_o.at[seq(s), :], out_sem.at[s, 4]),
        ]

    def row_outs(s):
        return [
            pltpu.make_async_copy(nrm.at[own_rows(s), :], nrm_o.at[own_rows(s), :], out_sem.at[s, 5]),
            pltpu.make_async_copy(pre.at[own_rows(s), :], pre_o.at[own_rows(s), :], out_sem.at[s, 6]),
            pltpu.make_async_copy(rstd.at[own_rows(s), :], rstd_o.at[own_rows(s), :], out_sem.at[s, 7]),
            pltpu.make_async_copy(mid.at[own_rows(s), :], mid_o.at[own_rows(s), :], out_sem.at[s, 8]),
        ]

    for load in loads:
        load.start()
    for row, ref in ((0, ob_ref), (2, ag_ref), (3, as_ref), (4, db_ref), (5, fg_ref), (6, fs_ref)):
        vec[row : row + 1, :] = ref[...]
    vec[1:2, :] = gate_value(wn_ref[...], part_of(wa_ref, g.me, width))
    vec[7:8, :] = jnp.zeros((1, width), F32)
    meet(g.all_peers())

    def begin(s, carry):
        ga.start(s)
        return carry

    for i in range(n - 1):
        vec_to(i).start()
    lax.fori_loop(0, seqs, begin, 0)
    par_own.start()
    gate_row = gate_value(*head_row(hn_ref, ha_ref, g.me, heads))
    gate_o[...] = gate_row
    for load in loads:
        load.wait()

    def differ(i, carry):
        at = pl.ds(pl.multiple_of(i * 32, 32), 32)
        value = (up[at, :].astype(F32) - tea[at, :].astype(F32)).astype(BF)
        each = SLOT // n // 32
        s, q = lax.div(i, SLOT // 32), lax.rem(i, SLOT // 32)
        change[s, lax.div(q, each), pl.ds(pl.multiple_of(lax.rem(q, each) * 32, 32), 32), :] = value
        return carry

    lax.fori_loop(0, seqs * SLOT // 32, differ, 0)
    change_own.start()
    ga.relay(0)
    par_own.wait()
    for i in range(n - 1):
        vec_from(i).wait()
    par_o[...] = par[...]

    lanes = lax.broadcasted_iota(jnp.int32, (1, width), 1)
    head_lanes = [
        jnp.where((lanes >= h * HD) & (lanes < (h + 1) * HD), 1.0, 0.0).astype(BF) for h in range(heads)
    ]

    scaled_lanes = [lane * HD**-0.5 for lane in head_lanes]

    def finish(s):
        re.arrive(s)

        def block(i, carry):
            at = pl.ds(pl.multiple_of(i * RB, RB), RB)
            here = pl.ds(pl.multiple_of(s * rows + i * RB, RB), RB)
            token_row = pl.multiple_of(s * SLOT + g.slot(g.me) * rows + i * RB, RB)
            attention_pre = re.total(s, at) + par[0:1, :]
            residual = full[pl.ds(token_row, RB), :].astype(F32) + attention_pre * par[1:2, :]
            centered = residual - mean_of(residual)
            row_rstd = lax.rsqrt(mean_of(centered * centered) + EPS)
            normed = centered * row_rstd
            middle = normed * par[2:3, :] + par[3:4, :]
            nrm[here, :] = normed
            pre[here, :] = attention_pre
            rstd[here, :] = jnp.broadcast_to(row_rstd, (RB, 128))
            mid[here, :] = middle.astype(BF)
            return carry

        lax.fori_loop(0, rows // RB, block, 0)
        for copy in row_outs(s):
            copy.start()

    def sequence(s, carry):
        ga.wait(s)
        here = seq(s)
        projected = nn(full[here, :], wqkv[...])
        qkv[here, 0:width] = (projected[:, 0:width] + qb_ref[...]).astype(BF)
        qkv[here, width : 2 * width] = projected[:, width : 2 * width].astype(BF)
        qkv[here, 2 * width : 3 * width] = (projected[:, 2 * width : 3 * width] + vb_ref[...]).astype(BF)

        @pl.when(s + 1 < seqs)
        def _():
            ga.relay(s + 1)

        @pl.when(s > 0)
        def _():
            re.cross(s - 1)

        @pl.when(s == seqs - 2)
        def _():
            for i in range(n - 1):
                change_to(i).start()

        length = len_ref[lax.axis_index("dp") * seqs + s]
        bias = jnp.where(lax.broadcasted_iota(jnp.int32, (1, SLOT), 1) < length, 0.0, MASKED)
        for h in range(heads):
            score[...] = nt(qkv[here, 0:width] * scaled_lanes[h], qkv[here, width : 2 * width])

            def softmax(i, carry, h=h):
                at = pl.ds(pl.multiple_of(i * 64, 64), 64)
                scores = score[at, :] + bias
                exponent = jnp.exp(scores - jnp.max(scores, axis=1, keepdims=True))
                total = jnp.sum(exponent, axis=1, keepdims=True)
                prob[s, h, at, :] = (exponent * (1.0 / total)).astype(BF)
                return carry

            lax.fori_loop(0, SLOT // 64, softmax, 0, unroll=True)
            term = nn(prob[s, h], qkv[here, 2 * width : 3 * width] * head_lanes[h])
            ctx[here, :] = term if h == 0 else ctx[here, :] + term
        gat[here, :] = (ctx[here, :] * gate_row).astype(BF)
        for copy in sequence_outs(s):
            copy.start()
        half = SLOT // 2
        there = pl.ds(pl.multiple_of(s * SLOT + (1 - g.c) * half, half), half)
        psend[s] = nn(gat[there, :], wo[...]).astype(BF).reshape(n // 2, rows, D)
        re.start(s)
        mine = pl.ds(pl.multiple_of(s * SLOT + g.c * half, half), half)
        own[s] = nn(gat[mine, :], wo[...]).reshape(n // 2, rows, D)

        @pl.when(s > 0)
        def _():
            finish(s - 1)

        return carry

    lax.fori_loop(0, seqs, sequence, 0)
    re.cross(seqs - 1)
    change_own.wait()
    for i in range(n - 1):
        change_from(i).wait()
    chg_out.start()
    finish(seqs - 1)
    chg_out.wait()

    def end(s, carry):
        ga.drain(s)
        for copy in sequence_outs(s) + row_outs(s):
            copy.wait()
        return carry

    lax.fori_loop(0, seqs, end, 0)


def feed_kernel(n, seqs, units, *refs):
    (
        len_ref, mid_ref, nrm_ref, pre_ref, rstd_ref, par, change_ref, w1_ref, b1_ref, w2_ref, un_ref, ua_ref,
        out_o, dlow_o, dres_o, dw1_o, dw2_o, rowsum_o, unitsum_o,
        midf, dffn, w1, w2, act, inner, slope, own, psend, precv, xsend, xrecv,
        nrm, pre, rstd, change, dtwo, dsend, fout, dlow, dres, wide, grad, sums, unit_sums, ugate_ref,
        in_sem, out_sem, grad_sem, *sems,
    ) = refs
    g = Group(n)
    rows = SLOT // n
    half = SLOT // 2
    g1, r1, g2, r2 = sems[:7], sems[7:11], sems[11:18], sems[18:]
    seq = lambda s: pl.ds(pl.multiple_of(s * SLOT, SLOT), SLOT)
    own_rows = lambda s: pl.ds(pl.multiple_of(s * rows, rows), rows)
    spot = lambda s, h: pl.ds(pl.multiple_of(s * SLOT + g.slot(h) * rows, rows), rows)
    gm = Gather(g, g1, lambda s: mid_ref.at[own_rows(s), :], lambda s, h: midf.at[spot(s, h), :])
    gd = Gather(g, g2, lambda s: dsend.at[own_rows(s), :], lambda s, h: dffn.at[spot(s, h), :])
    rf = Reduce(g, r1, psend, precv, own, xsend, xrecv)
    rb = Reduce(g, r2, psend, precv, own, xsend, xrecv)
    loads = [
        pltpu.make_async_copy(w1_ref, w1, in_sem.at[0]),
        pltpu.make_async_copy(w2_ref, w2, in_sem.at[1]),
        pltpu.make_async_copy(nrm_ref, nrm, in_sem.at[2]),
        pltpu.make_async_copy(change_ref, change, in_sem.at[3]),
        pltpu.make_async_copy(pre_ref, pre, in_sem.at[4]),
        pltpu.make_async_copy(rstd_ref, rstd, in_sem.at[5]),
    ]

    meet(g.near_peers())

    def begin(s, carry):
        gm.start(s)
        return carry

    lax.fori_loop(0, seqs, begin, 0)
    for load in loads:
        load.start()
    sums[...] = jnp.zeros_like(sums)
    unit_sums[...] = jnp.zeros_like(unit_sums)
    ugate_ref[...] = gate_value(un_ref[...], part_of(ua_ref, g.me, units))
    gm.relay(0)
    for load in loads:
        load.wait()

    def finish_forward(s):
        rf.arrive(s)
        length = len_ref[lax.axis_index("dp") * seqs + s]

        def block(i, carry):
            at = pl.ds(pl.multiple_of(i * RB, RB), RB)
            here = pl.ds(pl.multiple_of(s * rows + i * RB, RB), RB)
            ffn_pre = rf.total(s, at) + par[4:5, :]
            middle = nrm[here, :] * par[2:3, :] + par[3:4, :]
            residual = middle + ffn_pre * par[1:2, :]
            centered = residual - mean_of(residual)
            row_rstd = lax.rsqrt(mean_of(centered * centered) + EPS)
            normed = centered * row_rstd
            final = normed * par[5:6, :] + par[6:7, :]
            fout[here, :] = final.astype(BF)
            place = g.slot(g.me) * rows + i * RB + lax.broadcasted_iota(jnp.int32, (RB, 1), 0)
            live = jnp.where(place < length, 1.0, 0.0)
            d_final = live * (change[here, :].astype(F32) + final)
            sums[0] += fold(d_final * normed)
            sums[1] += fold(d_final)
            d_normed = d_final * par[5:6, :]
            d_two = row_rstd * (d_normed - mean_of(d_normed) - normed * mean_of(d_normed * normed))
            sums[2] += fold(d_two * ffn_pre)
            d_ffn = d_two * par[1:2, :]
            sums[3] += fold(d_ffn)
            dtwo[here, :] = d_two
            dsend[here, :] = d_ffn.astype(BF)
            return carry

        lax.fori_loop(0, rows // RB, block, 0)
        gd.start(s)

    def forward(s, carry):
        gm.wait(s)
        here = seq(s)

        def part(b, carry):
            cols = pl.ds(pl.multiple_of(b * NB, NB), NB)
            wide[...] = nn(midf[here, :], w1[:, cols])
            bias = b1_ref[:, cols]
            gate = ugate_ref[:, cols]

            def block(i, carry):
                at = pl.ds(pl.multiple_of(i * 32, 32), 32)
                row = pl.ds(pl.multiple_of(s * SLOT + i * 32, 32), 32)
                v = wide[at, :] + bias
                phi = 0.5 * (1.0 + lax.erf(v * ROOT_HALF))
                activated = v * phi
                act[row, cols] = activated.astype(BF)
                inner[row, cols] = (activated * gate).astype(BF)
                steep = phi + v * jnp.exp(-0.5 * v * v) * (1.0 / ROOT_TWO_PI)
                slope[row, cols] = (gate * steep).astype(BF)
                return carry

            lax.fori_loop(0, SLOT // 32, block, 0)
            return carry

        lax.fori_loop(0, units // NB, part, 0)

        @pl.when(s + 1 < seqs)
        def _():
            gm.relay(s + 1)

        @pl.when(s > 0)
        def _():
            rf.cross(s - 1)

        there = pl.ds(pl.multiple_of(s * SLOT + (1 - g.c) * half, half), half)
        psend[s] = nn(inner[there, :], w2[...]).astype(BF).reshape(n // 2, rows, D)
        rf.start(s)
        mine = pl.ds(pl.multiple_of(s * SLOT + g.c * half, half), half)
        own[s] = nn(inner[mine, :], w2[...]).reshape(n // 2, rows, D)

        @pl.when(s > 1)
        def _():
            finish_forward(s - 2)

        return carry

    lax.fori_loop(0, seqs, forward, 0)
    rf.cross(seqs - 1)
    gd.relay(0)

    def row_outs(s):
        return [
            pltpu.make_async_copy(fout.at[own_rows(s), :], out_o.at[own_rows(s), :], out_sem.at[s, 0]),
            pltpu.make_async_copy(dlow.at[own_rows(s), :], dlow_o.at[own_rows(s), :], out_sem.at[s, 1]),
            pltpu.make_async_copy(dres.at[own_rows(s), :], dres_o.at[own_rows(s), :], out_sem.at[s, 2]),
        ]

    def finish_backward(s):
        rb.arrive(s)

        def block(i, carry):
            at = pl.ds(pl.multiple_of(i * RB, RB), RB)
            here = pl.ds(pl.multiple_of(s * rows + i * RB, RB), RB)
            normed = nrm[here, :]
            d_middle = dtwo[here, :] + rb.total(s, at)
            sums[4] += fold(d_middle * normed)
            sums[5] += fold(d_middle)
            d_normed = d_middle * par[2:3, :]
            d_one = rstd[here, 0:1] * (
                d_normed - mean_of(d_normed) - normed * mean_of(d_normed * normed)
            )
            sums[2] += fold(d_one * pre[here, :])
            d_attn = d_one * par[1:2, :]
            sums[6] += fold(d_attn)
            dres[here, :] = d_one
            dlow[here, :] = d_attn.astype(BF)
            return carry

        lax.fori_loop(0, rows // RB, block, 0)
        for copy in row_outs(s):
            copy.start()

    def backward(s, carry):
        gd.wait(s)
        here = seq(s)

        def part(b, carry):
            cols = pl.ds(pl.multiple_of(b * NB, NB), NB)
            wide[...] = nt(dffn[here, :], w2[cols, :])

            def block(i, sums_here):
                unit_part, bias_part = sums_here
                at = pl.ds(pl.multiple_of(i * 32, 32), 32)
                row = pl.ds(pl.multiple_of(s * SLOT + i * 32, 32), 32)
                d_inner = wide[at, :]
                d_pre = (d_inner * slope[row, cols].astype(F32)).astype(BF)
                unit_part = unit_part + fold(d_inner * act[row, cols].astype(F32))
                bias_part = bias_part + fold(d_pre.astype(F32))
                slope[row, cols] = d_pre
                return (unit_part, bias_part)

            zero = jnp.zeros((8, NB), F32)
            unit_part, bias_part = lax.fori_loop(0, SLOT // 32, block, (zero, zero))
            unit_sums[0, :, cols] += unit_part
            unit_sums[1, :, cols] += bias_part
            return carry

        lax.fori_loop(0, units // NB, part, 0)

        @pl.when(s < 2)
        def _():
            finish_forward(seqs - 2 + s)

        @pl.when(s + 1 < seqs)
        def _():
            gd.relay(s + 1)

        @pl.when(s > 0)
        def _():
            rb.cross(s - 1)

        there = pl.ds(pl.multiple_of(s * SLOT + (1 - g.c) * half, half), half)
        psend[s] = nt(slope[there, :], w1[...]).astype(BF).reshape(n // 2, rows, D)
        rb.start(s)
        mine = pl.ds(pl.multiple_of(s * SLOT + g.c * half, half), half)
        own[s] = nt(slope[mine, :], w1[...]).reshape(n // 2, rows, D)

        @pl.when(s > 1)
        def _():
            finish_backward(s - 2)

        return carry

    lax.fori_loop(0, seqs, backward, 0)
    rb.cross(seqs - 1)

    def grad_out(k, b):
        target = (dw2_o, dw1_o)[k]
        at = pl.ds(pl.multiple_of(b * NB, NB), NB)
        return pltpu.make_async_copy(grad.at[b], target.at[at, :], grad_sem.at[k, b])

    def down_grad(b, carry):
        cols = pl.ds(pl.multiple_of(b * NB, NB), NB)
        grad[b] = tn(inner[:, cols], dffn[...]).astype(BF)
        grad_out(0, b).start()
        return carry

    lax.fori_loop(0, units // NB, down_grad, 0)
    finish_backward(seqs - 2)
    for b in range(units // NB):
        grad_out(0, b).wait()

    def inner_grad(b, carry):
        cols = pl.ds(pl.multiple_of(b * NB, NB), NB)
        grad[b, :, 0:units] = tn(midf[:, cols], slope[...]).astype(BF)
        pltpu.make_async_copy(
            grad.at[b, :, pl.ds(0, units)], dw1_o.at[cols, :], grad_sem.at[1, b]
        ).start()
        return carry

    lax.fori_loop(0, D // NB, inner_grad, 0)
    finish_backward(seqs - 1)
    for k in range(7):
        rowsum_o[k : k + 1, :] = jnp.sum(sums[k], axis=0, keepdims=True)
    rowsum_o[7:8, :] = jnp.zeros((1, D), F32)
    for k in range(2):
        unitsum_o[k : k + 1, :] = jnp.sum(unit_sums[k], axis=0, keepdims=True)
    for b in range(D // NB):
        at = pl.ds(b * NB, NB)
        pltpu.make_async_copy(
            grad.at[b, :, pl.ds(0, units)], dw1_o.at[at, :], grad_sem.at[1, b]
        ).wait()

    def end(s, carry):
        gm.drain(s)
        gd.drain(s)
        for copy in row_outs(s):
            copy.wait()
        return carry

    lax.fori_loop(0, seqs, end, 0)


def attend_back_kernel(n, seqs, heads, size, *refs):
    (
        len_ref, dlow_ref, dres_ref, full_ref, qkv_ref, prob_ref, ctx_ref, gat_ref,
        wq_ref, wk_ref, wv_ref, wo_ref, dw1_ref, dw2_ref, out_ref, teacher_ref, gate_ref, row_ref, unit_ref,
        tgrad_o, dwq_o, dwk_o, dwv_o, dwo_o, dw1_o, dw2_o, output_o, small_o, units_o,
        dattn, dres, full, qkv, prob, ctx, gat, wqkv, wo, dctx, dqkv, dprob, dscore, acc,
        block_f, own, psend, precv, xsend, xrecv, tgrad, moved, sums, dw1, dw2,
        dwq, dwk, dwv, dwo, teacher, parts, small, rbuf, sbuf, ubuf,
        in_sem, out_sem, move_send, move_recv, r_send, r_recv, s_send, s_recv, u_send, u_recv, *sems,
    ) = refs
    g = Group(n)
    cycle = Cycle(size)
    rings = []
    grads = ((dw1, dw1_o), (dw2, dw2_o), (dwq, dwq_o), (dwk, dwk_o), (dwv, dwv_o), (dwo, dwo_o))
    for data, target in grads:
        for way in (1, -1):
            i = 11 + 7 * len(rings)
            rings.append(Ring(cycle, data, target, way, sems[i : i + 7]))
    ticks = rings[0].ticks

    def tick(t, which):
        for ring in rings[2 * which : 2 * which + 2]:
            ring.tick(t)

    def slot_tick(s, place):
        served = [0, heads // 2, heads // 2 + 1, heads + 1]
        if place in served:
            k = served.index(place)
            tick(2 + s * 2 + k // 2, k % 2)

    def row_to(i):
        to = lax.rem(g.me + 1 + i, n)
        return remote(parts.at[:, cols_of(to)], rbuf.at[i], r_send.at[i], r_recv.at[i], to)

    def small_to(i):
        to = {"dp": lax.rem(cycle.me + 1 + i, size)}
        return remote(small, sbuf.at[i], s_send.at[i], s_recv.at[i], to)

    def units_to(i):
        to = {"dp": lax.rem(cycle.me + 1 + i, size)}
        return remote(unit_ref, ubuf.at[i], u_send.at[i], u_recv.at[i], to)

    def move_to(i):
        to = lax.rem(g.me + 1 + i, n)
        return remote(
            out_ref.at[:, :, cols_of(to)], moved.at[:, g.slot(g.me)], move_send.at[i], move_recv.at[i], to
        )

    def move_from(i):
        to = lax.rem(g.me + 1 + i, n)
        frm = lax.rem(g.me - 1 - i + n, n)
        return remote(
            out_ref.at[:, :, cols_of(to)], moved.at[:, g.slot(frm)], move_send.at[i], move_recv.at[i], to
        )

    width = heads * HD
    rows = SLOT // n
    gsems, rsems = sems[:7], sems[7:11]
    cols_of = lambda h: pl.ds(pl.multiple_of(h * width, width), width)
    seq = lambda s: pl.ds(pl.multiple_of(s * SLOT, SLOT), SLOT)
    own_rows = lambda s: pl.ds(pl.multiple_of(s * rows, rows), rows)
    spot = lambda s, h: pl.ds(pl.multiple_of(s * SLOT + g.slot(h) * rows, rows), rows)
    ga = Gather(g, gsems, lambda s: dlow_ref.at[own_rows(s), :], lambda s, h: dattn.at[spot(s, h), :])
    re = Reduce(g, rsems, psend, precv, own, xsend, xrecv)
    loads = [
        pltpu.make_async_copy(wo_ref, wo, in_sem.at[0]),
        pltpu.make_async_copy(ctx_ref, ctx, in_sem.at[1]),
        pltpu.make_async_copy(qkv_ref, qkv, in_sem.at[2]),
        pltpu.make_async_copy(prob_ref, prob, in_sem.at[3]),
        pltpu.make_async_copy(wq_ref, wqkv.at[:, pl.ds(0, width)], in_sem.at[4]),
        pltpu.make_async_copy(wk_ref, wqkv.at[:, pl.ds(width, width)], in_sem.at[5]),
        pltpu.make_async_copy(wv_ref, wqkv.at[:, pl.ds(2 * width, width)], in_sem.at[6]),
        pltpu.make_async_copy(dres_ref, dres, in_sem.at[7]),
        pltpu.make_async_copy(full_ref, full, in_sem.at[8]),
        pltpu.make_async_copy(gat_ref, gat, in_sem.at[9]),
        pltpu.make_async_copy(
            out_ref.at[:, :, cols_of(g.me)], moved.at[:, g.slot(g.me)], in_sem.at[11]
        ),
        pltpu.make_async_copy(teacher_ref, teacher, in_sem.at[10]),
    ]
    grads_in = [
        pltpu.make_async_copy(dw1_ref, dw1, in_sem.at[12]),
        pltpu.make_async_copy(dw2_ref, dw2, in_sem.at[13]),
    ]
    for load in grads_in:
        load.start()
    meet(g.all_peers() + [{"dp": lax.rem(cycle.me + 1 + i, size)} for i in range(size - 1)])

    def begin(s, carry):
        ga.start(s)
        return carry

    lax.fori_loop(0, seqs, begin, 0)
    for load in loads:
        load.start()
    sums[...] = jnp.zeros_like(sums)
    for load in grads_in:
        load.wait()
    for t in range(2):
        tick(t, 0)
        tick(t, 1)
    ga.relay(0)
    for load in loads[:8]:
        load.wait()

    lanes = lax.broadcasted_iota(jnp.int32, (1, width), 1)
    head_lanes = [
        jnp.where((lanes >= h * HD) & (lanes < (h + 1) * HD), 1.0, 0.0).astype(BF) for h in range(heads)
    ]

    def out(s):
        return pltpu.make_async_copy(tgrad.at[seq(s), :], tgrad_o.at[seq(s), :], out_sem.at[s])

    def finish(s):
        re.arrive(s)

        def block(i, carry):
            at = pl.ds(pl.multiple_of(i * 32, 32), 32)
            tgrad[pl.ds(pl.multiple_of(s * SLOT + i * 32, 32), 32), :] = re.total(s, at)
            return carry

        lax.fori_loop(0, SLOT // 32, block, 0)
        out(s).start()

    def token_block(s, h):
        cols = pl.ds(pl.multiple_of(h * width, width), width)
        block_f[...] = nt(dqkv[seq(s), :], wqkv[cols, :])
        mine = pl.ds(pl.multiple_of(g.slot(g.me) * rows, rows), rows)
        block_f[mine, :] += dres[own_rows(s), cols]

    def sequence(s, carry):
        ga.wait(s)
        here = seq(s)
        d_gated = nt(dattn[here, :], wo[...])
        sums[0] += fold(d_gated * ctx[here, :])
        dctx[...] = (d_gated * gate_ref[...]).astype(BF)
        slot_tick(s, 0)

        @pl.when(s + 1 < seqs)
        def _():
            ga.relay(s + 1)

        @pl.when(s > 0)
        def _():
            re.cross(s - 1)

        @pl.when(s == 1)
        def _():
            for i in range(n - 1):
                move_to(i).start()
            for i in range(size - 1):
                units_to(i).start()

        for h in range(heads):
            d_context = dctx[...] * head_lanes[h]
            dprob[...] = nt(d_context, qkv[here, 2 * width : 3 * width])

            def softmax(i, carry, h=h):
                at = pl.ds(pl.multiple_of(i * 64, 64), 64)
                p = prob[s, h, at, :].astype(F32)
                weighted = p * dprob[at, :]
                total = jnp.sum(weighted, axis=1, keepdims=True)
                dscore[at, :] = (weighted - p * total).astype(BF)
                return carry

            lax.fori_loop(0, SLOT // 64, softmax, 0, unroll=True)
            slot_tick(s, h + 1)
            terms = (
                nn(dscore[...], qkv[here, width : 2 * width] * head_lanes[h]),
                tn(dscore[...], qkv[here, 0:width] * head_lanes[h]),
                tn(prob[s, h], d_context),
            )
            for k in range(3):
                acc[k] = terms[k] if h == 0 else acc[k] + terms[k]
        scales = (HD**-0.5, HD**-0.5, 1.0)
        for k in range(3):
            rounded = (acc[k] * scales[k]).astype(BF)
            dqkv[here, k * width : (k + 1) * width] = rounded
            sums[1 + k] += fold(rounded.astype(F32))
        for chip in range(n // 2):
            token_block(s, 2 * chip + 1 - g.c)
            psend[s, chip] = block_f[...].astype(BF)
        re.start(s)
        slot_tick(s, heads + 1)
        for chip in range(n // 2):
            token_block(s, 2 * chip + g.c)
            own[s, chip] = block_f[...]

        @pl.when(s > 0)
        def _():
            finish(s - 1)

        return carry

    lax.fori_loop(0, seqs, sequence, 0)
    re.cross(seqs - 1)
    for load in loads[8:]:
        load.wait()

    def rest(t, carry):
        tick(t, 0)
        tick(t, 1)
        return carry

    def token_grad(b, carry):
        cols = pl.ds(pl.multiple_of(b * NB, NB), NB)
        term = tn(full[:, cols], dqkv[...])
        for k, grad in enumerate((dwq, dwk, dwv)):
            grad[cols, :] = term[:, k * width : (k + 1) * width].astype(BF)
        tick(2 + 2 * seqs + b, 0)
        tick(2 + 2 * seqs + b, 1)
        return carry

    lax.fori_loop(0, D // NB, token_grad, 0)
    for which in range(2, 5):
        tick(0, which)
    dwo[...] = tn(gat[...], dattn[...]).astype(BF)
    tick(0, 5)
    lax.fori_loop(2 + 2 * seqs + D // NB, ticks, rest, 0)
    for i in range(n - 1):
        move_from(i).wait()
    moved_out = pltpu.make_async_copy(moved, output_o, in_sem.at[14])
    moved_out.start()

    def squares(s, total):
        length = len_ref[cycle.me * seqs + s]

        def block(i, total):
            each = rows // 32
            at = pl.ds(pl.multiple_of(lax.rem(i, each) * 32, 32), 32)
            value = moved[s, lax.div(i, each), at, :].astype(F32)
            place = i * 32 + lax.broadcasted_iota(jnp.int32, (32, 1), 0)
            differ = value - teacher[pl.ds(pl.multiple_of(s * SLOT + i * 32, 32), 32), :].astype(F32)
            return total + fold(jnp.where(place < length, differ * differ, 0.0))

        return lax.fori_loop(0, SLOT // 32, block, total)

    square_sum = lax.fori_loop(0, seqs, squares, jnp.zeros((8, width), F32))
    parts[...] = row_ref[...]
    for h in range(n):
        parts[7:8, h * width : (h + 1) * width] = jnp.sum(square_sum, axis=0, keepdims=True)
    for i in range(n - 1):
        row_to(i).start()
    for which in range(2, 6):
        tick(1, which)
    finish(seqs - 1)
    total = parts[:, cols_of(g.me)]
    for i in range(n - 1):
        row_to(i).wait()
        total = total + rbuf[i]
    small[:, 0:width] = total
    for k in range(4):
        small[k : k + 1, width : 2 * width] = jnp.sum(sums[k], axis=0, keepdims=True)
    small[4:8, width : 2 * width] = jnp.zeros((4, width), F32)
    for i in range(size - 1):
        small_to(i).start()

    def last(t, carry):
        for which in range(2, 6):
            tick(t, which)
        return carry

    lax.fori_loop(2, ticks, last, 0)
    small_sum = small[...]
    unit_sum = unit_ref[...]
    for i in range(size - 1):
        small_to(i).wait()
        units_to(i).wait()
        small_sum = small_sum + sbuf[i]
        unit_sum = unit_sum + ubuf[i]
    small_o[...] = small_sum
    units_o[...] = unit_sum
    moved_out.wait()
    for ring in rings:
        ring.drain()

    def end(s, carry):
        ga.drain(s)
        out(s).wait()
        return carry

    lax.fori_loop(0, seqs, end, 0)


def complete_kernel(n, heads, units, *refs):
    (
        dw1_ref, dw2_ref, dwq_ref, dwk_ref, dwv_ref, dwo_ref, tgrad_ref, output_ref,
        small_ref, unit_ref, ha_ref, ua_ref, wa_ref, mult_ref, hn_ref, un_ref, wn_ref, len_ref,
        dw1_o, dw2_o, dwq_o, dwk_o, dwv_o, dwo_o, tgrad_o, output_o,
        qb_o, vb_o, ob_o, ag_o, as_o, db_o, fg_o, fs_o, b1_o, ha_o, ua_o, wa_o, mse_o, mult_o,
        dw1, dw2, dwq, dwk, dwv, dwo, tgrad, output, fw1, fw2, fwq, fwk, fwv, fwo, in_sem, out_sem,
    ) = refs
    width = heads * HD
    rank = lax.axis_index("hid")
    wide = (
        (dw1_ref, dw1, fw1, dw1_o), (dw2_ref, dw2, fw2, dw2_o), (dwq_ref, dwq, fwq, dwq_o),
        (dwk_ref, dwk, fwk, dwk_o), (dwv_ref, dwv, fwv, dwv_o), (dwo_ref, dwo, fwo, dwo_o),
        (tgrad_ref, tgrad, tgrad, tgrad_o), (output_ref, output, output, output_o),
    )
    parts = 4

    def piece(ref, p):
        rows = ref.shape[0] // parts
        return ref.at[pl.ds(pl.multiple_of(p * rows, rows), rows), :]

    def load(k, p):
        return pltpu.make_async_copy(piece(wide[k][0], p), piece(wide[k][1], p), in_sem.at[k, p])

    def store(k, p):
        return pltpu.make_async_copy(piece(wide[k][2], p), piece(wide[k][3], p), out_sem.at[k, p])

    for k in range(len(wide)):
        for p in range(parts):
            load(k, p).start()

    head_all = small_ref[:, width : 2 * width]
    for ref, row in ((ob_o, 6), (ag_o, 4), (as_o, 5), (db_o, 3), (fg_o, 0), (fs_o, 1)):
        ref[...] = small_ref[row : row + 1, 0:width]
    qb_o[...] = head_all[1:2, :]
    vb_o[...] = head_all[3:4, :]
    b1_o[...] = unit_ref[1:2, :]
    keeps = [keep_prob(ref[...]) for ref in (ha_ref, ua_ref, wa_ref)]
    heads_kept, units_kept, dims_kept = [jnp.sum(k, axis=1, keepdims=True) for k in keeps]
    full_size = 4.0 * D * D + 2.0 * D * FF
    gap = 1.0 - (4.0 * HD * heads_kept * dims_kept + 2.0 * units_kept * dims_kept) / full_size - TARGET
    pull = -(lane_of(mult_ref[...], 0) + 2.0 * lane_of(mult_ref[...], 1) * gap) / full_size
    slot = lax.broadcasted_iota(jnp.int32, (1, 2), 1)
    mult_o[...] = mult_ref[...] + ASCENT * jnp.where(slot == 0, gap, gap * gap)

    def pulled(alpha, factor):
        k = keep_prob(alpha)
        return pull * factor * k * (1.0 - k)

    unit_alpha = part_of(ua_ref, rank, units)
    ua_o[...] = unit_ref[0:1, :] * gate_slope(un_ref[...], unit_alpha) + pulled(unit_alpha, 2.0 * dims_kept)
    width_alpha = part_of(wa_ref, rank, width)
    wa_o[...] = small_ref[2:3, 0:width] * gate_slope(wn_ref[...], width_alpha) + pulled(
        width_alpha, 4.0 * HD * heads_kept + 2.0 * units_kept
    )
    noise_row, alpha_row = head_row(hn_ref, ha_ref, rank, heads)
    lanes = lax.broadcasted_iota(jnp.int32, (1, width), 1)
    per_lane = head_all[0:1, :] * gate_slope(noise_row, alpha_row)
    head_pulled = pulled(alpha_row, 4.0 * HD * dims_kept) * (1.0 / HD)
    for h in range(heads):
        here = (lanes >= h * HD) & (lanes < (h + 1) * HD)
        ha_o[:, h : h + 1] = jnp.sum(jnp.where(here, per_lane + head_pulled, 0.0), axis=1, keepdims=True)
    live = jnp.sum(len_ref[...].astype(F32), axis=1, keepdims=True)
    mse_o[...] = jnp.sum(small_ref[7:8, 0:width], axis=1, keepdims=True) / (live * D)

    for k, (_, low, high, _) in enumerate(wide):
        rows = low.shape[0] // parts
        for p in range(parts):
            load(k, p).wait()
            if low is not high:

                step = min(64, rows)

                def widen(i, carry, low=low, high=high, first=p * rows, step=step):
                    at = pl.ds(pl.multiple_of(first + i * step, step), step)
                    high[at, :] = low[at, :].astype(F32)
                    return carry

                lax.fori_loop(0, rows // step, widen, 0)
            store(k, p).start()
    for k in range(len(wide)):
        for p in range(parts):
            store(k, p).wait()


def hbm():
    return pl.BlockSpec(memory_space=pl.ANY)


def vmem():
    return pl.BlockSpec(memory_space=pltpu.VMEM)


def smem():
    return pl.BlockSpec(memory_space=pltpu.SMEM)


def call(kernel, name, ident, ins, outs, scratch, flops):
    return pl.pallas_call(
        kernel,
        name=name,
        out_shape=[jax.ShapeDtypeStruct(shape, dtype) for shape, dtype, _ in outs],
        in_specs=ins,
        out_specs=[spec for _, _, spec in outs],
        scratch_shapes=scratch,
        compiler_params=pltpu.CompilerParams(
            collective_id=ident, has_side_effects=True, vmem_limit_bytes=VMEM_LIMIT
        ),
        cost_estimate=pl.CostEstimate(flops=flops, bytes_accessed=30_000_000, transcendentals=0),
    )


def attend(n, seqs, heads, args):
    width, rows, nx, half = heads * HD, SLOT // n, n // 2, SLOT // 2
    tokens, owned = seqs * SLOT, seqs * rows
    v, dma = pltpu.VMEM, pltpu.SemaphoreType.DMA
    return call(
        functools.partial(attend_kernel, n, seqs, heads),
        "attend",
        0,
        [smem()] + [hbm()] * 3 + [vmem()] * 10 + [hbm()] * 3 + [vmem()] * 2 + [hbm()],
        [
            ((tokens, D), BF, hbm()),
            ((tokens, 3 * width), BF, hbm()),
            ((seqs, heads, SLOT, SLOT), BF, hbm()),
            ((tokens, width), F32, hbm()),
            ((tokens, width), BF, hbm()),
            ((owned, D), F32, hbm()),
            ((owned, D), F32, hbm()),
            ((owned, 128), F32, hbm()),
            ((owned, D), BF, hbm()),
            ((8, D), F32, vmem()),
            ((seqs, rows, D), BF, hbm()),
            ((1, width), F32, vmem()),
        ],
        [
            v((tokens, D), BF),
            v((D, 3 * width), BF),
            v((width, D), BF),
            v((tokens, 3 * width), BF),
            v((seqs, heads, SLOT, SLOT), BF),
            v((tokens, width), F32),
            v((tokens, width), BF),
            v((seqs, nx, rows, D), F32),
            v((seqs, nx, rows, D), BF),
            v((seqs, nx, rows, D), BF),
            v((seqs, nx - 1, rows, D), BF),
            v((seqs, nx - 1, rows, D), BF),
            v((owned, D), F32),
            v((owned, D), F32),
            v((owned, 128), F32),
            v((owned, D), BF),
            v((8, D), F32),
            v((seqs, rows, D), BF),
            v((tokens, width), BF),
            v((tokens, width), BF),
            v((seqs, n, rows, width), BF),
            v((8, width), F32),
            v((SLOT, SLOT), F32),
            dma((9,)),
            dma((seqs, 9)),
            dma((n - 1,)),
            dma((n - 1,)),
            dma((n - 1,)),
            dma((n - 1,)),
        ]
        + gather_sems(seqs, nx)
        + reduce_sems(seqs, nx),
        10_000_000_000,
    )(*args)


def feed(n, seqs, units, args):
    rows, nx = SLOT // n, n // 2
    tokens, owned = seqs * SLOT, seqs * rows
    v, dma = pltpu.VMEM, pltpu.SemaphoreType.DMA
    return call(
        functools.partial(feed_kernel, n, seqs, units),
        "feed",
        1,
        [smem(), hbm(), hbm(), hbm(), hbm(), vmem(), hbm(), hbm(), vmem(), hbm(), vmem(), vmem()],
        [
            ((owned, D), BF, hbm()),
            ((owned, D), BF, hbm()),
            ((owned, D), F32, hbm()),
            ((D, units), BF, hbm()),
            ((units, D), BF, hbm()),
            ((8, D), F32, vmem()),
            ((2, units), F32, vmem()),
        ],
        [
            v((tokens, D), BF),
            v((tokens, D), BF),
            v((D, units), BF),
            v((units, D), BF),
            v((tokens, units), BF),
            v((tokens, units), BF),
            v((tokens, units), BF),
            v((seqs, nx, rows, D), F32),
            v((seqs, nx, rows, D), BF),
            v((seqs, nx, rows, D), BF),
            v((seqs, nx - 1, rows, D), BF),
            v((seqs, nx - 1, rows, D), BF),
            v((owned, D), F32),
            v((owned, D), F32),
            v((owned, 128), F32),
            v((owned, D), BF),
            v((owned, D), F32),
            v((owned, D), BF),
            v((owned, D), BF),
            v((owned, D), BF),
            v((owned, D), F32),
            v((SLOT, NB), F32),
            v((D // NB, NB, D), BF),
            v((7, 8, D), F32),
            v((2, 8, units), F32),
            v((1, units), F32),
            dma((6,)),
            dma((seqs, 3)),
            dma((2, D // NB)),
        ]
        + (gather_sems(seqs, nx) + reduce_sems(seqs, nx)) * 2,
        30_000_000_000,
    )(*args)


def attend_back(n, seqs, heads, units, size, args):
    width, rows, nx = heads * HD, SLOT // n, n // 2
    tokens, owned = seqs * SLOT, seqs * rows
    v, dma = pltpu.VMEM, pltpu.SemaphoreType.DMA
    return call(
        functools.partial(attend_back_kernel, n, seqs, heads, size),
        "attend_back",
        2,
        [smem()] + [hbm()] * 15 + [vmem()] * 3,
        [
            ((tokens, width), F32, hbm()),
            ((D, width), BF, hbm()),
            ((D, width), BF, hbm()),
            ((D, width), BF, hbm()),
            ((width, D), BF, hbm()),
            ((D, units), BF, hbm()),
            ((units, D), BF, hbm()),
            ((seqs, n, rows, width), BF, hbm()),
            ((8, 2 * width), F32, vmem()),
            ((2, units), F32, vmem()),
        ],
        [
            v((tokens, D), BF),
            v((owned, D), F32),
            v((tokens, D), BF),
            v((tokens, 3 * width), BF),
            v((seqs, heads, SLOT, SLOT), BF),
            v((tokens, width), F32),
            v((tokens, width), BF),
            v((D, 3 * width), BF),
            v((width, D), BF),
            v((SLOT, width), BF),
            v((tokens, 3 * width), BF),
            v((SLOT, SLOT), F32),
            v((SLOT, SLOT), BF),
            v((3, SLOT, width), F32),
            v((SLOT, width), F32),
            v((seqs, nx, SLOT, width), F32),
            v((seqs, nx, SLOT, width), BF),
            v((seqs, nx, SLOT, width), BF),
            v((seqs, nx - 1, SLOT, width), BF),
            v((seqs, nx - 1, SLOT, width), BF),
            v((tokens, width), F32),
            v((seqs, n, rows, width), BF),
            v((4, 8, width), F32),
            v((D, units), BF),
            v((units, D), BF),
            v((D, width), BF),
            v((D, width), BF),
            v((D, width), BF),
            v((width, D), BF),
            v((tokens, width), BF),
            v((8, D), F32),
            v((8, 2 * width), F32),
            v((n - 1, 8, width), F32),
            v((size - 1, 8, 2 * width), F32),
            v((size - 1, 2, units), F32),
            dma((15,)),
            dma((seqs,)),
            dma((n - 1,)),
            dma((n - 1,)),
            dma((n - 1,)),
            dma((n - 1,)),
        ]
        + [dma((size - 1,))] * 4
        + gather_sems(seqs, nx)
        + reduce_sems(seqs, nx)
        + ring_scratch((D, units), size) * 2
        + ring_scratch((units, D), size) * 2
        + ring_scratch((D, width), size) * 6
        + ring_scratch((width, D), size) * 2,
        20_000_000_000,
    )(*args)


def complete(n, heads, units, tokens, args):
    v, dma, width = pltpu.VMEM, pltpu.SemaphoreType.DMA, heads * HD
    shapes = [(D, units), (units, D), (D, width), (D, width), (D, width), (width, D)]
    rows = [(width,)] * 8 + [(units,), (heads,), (units,), (width,), (1,), (2,)]
    return pl.pallas_call(
        functools.partial(complete_kernel, n, heads, units),
        name="complete",
        out_shape=[jax.ShapeDtypeStruct(shape, F32) for shape in shapes]
        + [jax.ShapeDtypeStruct((tokens, width), F32), jax.ShapeDtypeStruct((tokens, width), BF)]
        + [jax.ShapeDtypeStruct((1, count), F32) for (count,) in rows],
        in_specs=[hbm()] * 8 + [vmem()] * 10,
        out_specs=[hbm()] * 8 + [vmem()] * len(rows),
        scratch_shapes=[v(shape, BF) for shape in shapes]
        + [v((tokens, width), F32), v((tokens, width), BF)]
        + [v(shape, F32) for shape in shapes]
        + [dma((8, 4))] * 2,
        compiler_params=pltpu.CompilerParams(vmem_limit_bytes=VMEM_LIMIT),
        cost_estimate=pl.CostEstimate(flops=10_000_000, bytes_accessed=24_000_000, transcendentals=0),
    )(*args)


def on_device(
    n,
    size,
    tokens,
    query_weight,
    query_bias,
    key_weight,
    value_weight,
    value_bias,
    output_weight,
    output_bias,
    attention_gain,
    attention_shift,
    inner_weight,
    inner_bias,
    down_weight,
    down_bias,
    final_gain,
    final_shift,
    head_alpha,
    unit_alpha,
    width_alpha,
    multipliers,
    head_noise,
    unit_noise,
    width_noise,
    lengths,
    teacher,
    upstream,
):
    row_count, width = tokens.shape
    heads = width // HD
    units = inner_weight.shape[1]
    seqs = row_count // SLOT
    rows = SLOT // n
    flat = lambda vector: vector.reshape(1, vector.shape[0])
    head_alpha, unit_alpha, width_alpha = flat(head_alpha), flat(unit_alpha), flat(width_alpha)
    head_noise, unit_noise, width_noise = flat(head_noise), flat(unit_noise), flat(width_noise)
    full, qkv, prob, ctx, gat, nrm, pre, rstd, mid, par, change_rows, gate_row = attend(
        n,
        seqs,
        heads,
        (
            lengths,
            tokens,
            upstream,
            teacher,
            flat(output_bias),
            flat(attention_gain),
            flat(attention_shift),
            flat(down_bias),
            flat(final_gain),
            flat(final_shift),
            width_noise,
            width_alpha,
            head_noise,
            head_alpha,
            query_weight,
            key_weight,
            value_weight,
            flat(query_bias),
            flat(value_bias),
            output_weight,
        ),
    )
    out_rows, d_low, d_res, dw_inner, dw_down, row_sums, unit_sums = feed(
        n,
        seqs,
        units,
        (
            lengths,
            mid,
            nrm,
            pre,
            rstd,
            par,
            change_rows.reshape(seqs * rows, D),
            inner_weight,
            flat(inner_bias),
            down_weight,
            unit_noise,
            unit_alpha,
        ),
    )
    tokens_grad, dw_q, dw_k, dw_v, dw_o, dw_inner, dw_down, output, small, unit_all = attend_back(
        n,
        seqs,
        heads,
        units,
        size,
        (
            lengths,
            d_low,
            d_res,
            full,
            qkv,
            prob,
            ctx,
            gat,
            query_weight,
            key_weight,
            value_weight,
            output_weight,
            dw_inner,
            dw_down,
            out_rows.reshape(seqs, rows, D),
            teacher,
            gate_row,
            row_sums,
            unit_sums,
        ),
    )
    output = output.reshape(row_count, width)
    dw_inner, dw_down, dw_q, dw_k, dw_v, dw_o, tokens_grad, output, *vectors = complete(
        n,
        heads,
        units,
        row_count,
        (
            dw_inner,
            dw_down,
            dw_q,
            dw_k,
            dw_v,
            dw_o,
            tokens_grad,
            output,
            small,
            unit_all,
            head_alpha,
            unit_alpha,
            width_alpha,
            flat(multipliers),
            head_noise,
            unit_noise,
            width_noise,
            flat(lengths),
        ),
    )
    qb, vb, ob, ag, shift, db, fg, fs, b1, ha, ua, wa, mse, mult = [v.reshape(v.shape[1]) for v in vectors]
    return (
        output,
        tokens_grad,
        dw_q,
        qb,
        dw_k,
        dw_v,
        vb,
        dw_o,
        ob,
        ag,
        shift,
        dw_inner,
        b1,
        dw_down,
        db,
        fg,
        fs,
        ha,
        ua,
        wa,
        mse.reshape(()),
        mult,
    )


def solution(mesh):
    tall, wide, vec, rep = P("dp", "hid"), P(None, "hid"), P("hid"), P()
    deep = P("hid", None)
    return jax.shard_map(
        functools.partial(on_device, mesh.shape["hid"], mesh.shape["dp"]),
        mesh=mesh,
        in_specs=(tall, wide, vec, wide, wide, vec, deep, vec, vec, vec, wide, vec, deep)
        + (vec,) * 3
        + (rep,) * 4
        + (vec,) * 3
        + (rep, tall, tall),
        out_specs=(tall, tall, wide, vec, wide, wide, vec, deep, vec, vec, vec, wide, vec, deep)
        + (vec,) * 6
        + (rep, rep),
        check_vma=False,
    )
```

```python
import functools
import math

import jax
import jax.numpy as jnp
from jax import lax
from jax.experimental import pallas as pl
from jax.experimental.pallas import tpu as pltpu
from jax.sharding import PartitionSpec as P

D = 1024
HD = 64
FF = 4096
SLOT = 512

BETA = 2.0 / 3.0
GAMMA = -0.1
ZETA = 1.1
TARGET = 0.7
ASCENT = 1.0
EPS = 1e-12
MASKED = -1000000000.0
ROOT_HALF = 0.7071067811865476
ROOT_TWO_PI = 2.5066282746310002

MESH = pl.DeviceIdType.MESH
VMEM_LIMIT = 66_000_000
BF = jnp.bfloat16
F32 = jnp.float32
NB = 256
RB = 16


def gate_value(noise, alpha):
    logits = (jnp.log(noise) - jnp.log(1.0 - noise) + alpha) / BETA
    stretched = jax.nn.sigmoid(logits) * (ZETA - GAMMA) + GAMMA
    return jnp.clip(stretched, 0.0, 1.0)


def gate_slope(noise, alpha):
    s = jax.nn.sigmoid((jnp.log(noise) - jnp.log(1.0 - noise) + alpha) / BETA)
    stretched = s * (ZETA - GAMMA) + GAMMA
    free = (stretched > 0.0) & (stretched < 1.0)
    return jnp.where(free, (ZETA - GAMMA) / BETA * s * (1.0 - s), 0.0)


def keep_prob(alpha):
    return jax.nn.sigmoid(alpha - BETA * math.log(-GAMMA / ZETA))


def lane_of(row, place):
    lanes = lax.broadcasted_iota(jnp.int32, row.shape, 1)
    return jnp.sum(jnp.where(lanes == place, row, 0.0), axis=1, keepdims=True)


def head_row(noise_ref, alpha_ref, rank, heads):
    lanes = lax.broadcasted_iota(jnp.int32, (1, heads * HD), 1)
    noise = jnp.full((1, heads * HD), 0.5, F32)
    alpha = jnp.zeros((1, heads * HD), F32)
    for h in range(heads):
        here = (lanes >= h * HD) & (lanes < (h + 1) * HD)
        noise = jnp.where(here, lane_of(noise_ref[...], h), noise)
        alpha = jnp.where(here, lane_of(alpha_ref[...], rank * heads + h), alpha)
    return noise, alpha


def part_of(ref, rank, width):
    return ref[:, pl.ds(pl.multiple_of(rank * width, width), width)]


def nn(a, b):
    return jnp.dot(a, b, preferred_element_type=F32)


def nt(a, b):
    return lax.dot_general(a, b, (((1,), (1,)), ((), ())), preferred_element_type=F32)


def tn(a, b):
    return lax.dot_general(a, b, (((0,), (0,)), ((), ())), preferred_element_type=F32)


def fold(values):
    return jnp.sum(values.reshape(values.shape[0] // 8, 8, values.shape[1]), axis=0)


class Group:
    def __init__(self, n):
        self.n = n
        self.nx = n // 2
        self.me = lax.axis_index("hid")
        self.x = lax.div(self.me, 2)
        self.c = lax.rem(self.me, 2)
        self.partner = 2 * self.x + 1 - self.c

    def chip_ahead(self, j):
        return lax.rem(self.x + 1 + j, self.nx)

    def chip_behind(self, j):
        return lax.rem(self.x - 1 - j + self.nx, self.nx)

    def slot(self, h):
        return lax.rem(h, 2) * self.nx + lax.div(h, 2)

    def all_peers(self):
        return [{"hid": lax.rem(self.me + 1 + i, self.n)} for i in range(self.n - 1)]

    def near_peers(self):
        near = [self.partner] + [2 * self.chip_ahead(j) + self.c for j in range(self.nx - 1)]
        return [{"hid": peer} for peer in near]


def remote(src, dst, send_sem, recv_sem, to):
    return pltpu.make_async_remote_copy(
        src_ref=src,
        dst_ref=dst,
        send_sem=send_sem,
        recv_sem=recv_sem,
        device_id=to if isinstance(to, dict) else {"hid": to},
        device_id_type=MESH,
    )


def gather_sems(seqs, nx):
    wide = pltpu.SemaphoreType.DMA((seqs, nx - 1))
    return [wide] * 4 + [pltpu.SemaphoreType.DMA((seqs,))] * 3


def reduce_sems(seqs, nx):
    wide = pltpu.SemaphoreType.DMA((seqs, nx - 1))
    return [wide] * 2 + [pltpu.SemaphoreType.DMA((seqs,))] * 2


class Gather:
    def __init__(self, group, sems, source, region):
        self.g, self.source, self.region = group, source, region
        self.xs, self.xr, self.rs, self.rr, self.ps, self.pr, self.os = sems

    def _own(self, s):
        return pltpu.make_async_copy(self.source(s), self.region(s, self.g.me), self.os.at[s])

    def _cross(self, s, j):
        to = 2 * self.g.chip_ahead(j) + self.g.c
        return remote(
            self.source(s), self.region(s, self.g.me), self.xs.at[s, j], self.xr.at[s, j], to
        )

    def _crossed(self, s, j):
        to = 2 * self.g.chip_ahead(j) + self.g.c
        block = self.region(s, 2 * self.g.chip_behind(j) + self.g.c)
        return remote(self.source(s), block, self.xs.at[s, j], self.xr.at[s, j], to)

    def _pair(self, s):
        return remote(
            self.source(s),
            self.region(s, self.g.me),
            self.ps.at[s],
            self.pr.at[s],
            self.g.partner,
        )

    def _paired(self, s):
        block = self.region(s, self.g.partner)
        return remote(self.source(s), block, self.ps.at[s], self.pr.at[s], self.g.partner)

    def _relay(self, s, j):
        block = self.region(s, 2 * self.g.chip_behind(j) + self.g.c)
        return remote(block, block, self.rs.at[s, j], self.rr.at[s, j], self.g.partner)

    def _relayed(self, s, j):
        block = self.region(s, 2 * self.g.chip_behind(j) + 1 - self.g.c)
        return remote(block, block, self.rs.at[s, j], self.rr.at[s, j], self.g.partner)

    def start(self, s):
        for j in range(self.g.nx - 1):
            self._cross(s, j).start()
        self._pair(s).start()
        self._own(s).start()

    def relay(self, s):
        for j in range(self.g.nx - 1):
            self._crossed(s, j).wait_recv()
            self._relay(s, j).start()

    def wait(self, s):
        self._own(s).wait()
        self._paired(s).wait_recv()
        for j in range(self.g.nx - 1):
            self._relayed(s, j).wait_recv()

    def drain(self, s):
        self._pair(s).wait_send()
        for j in range(self.g.nx - 1):
            self._cross(s, j).wait_send()
            self._relay(s, j).wait_send()


class Reduce:
    def __init__(self, group, sems, psend, precv, own, xsend, xrecv):
        self.g = group
        self.psend, self.precv, self.own, self.xsend, self.xrecv = psend, precv, own, xsend, xrecv
        self.xs, self.xr, self.ps, self.pr = sems

    def _pair(self, s):
        return remote(
            self.psend.at[s], self.precv.at[s], self.ps.at[s], self.pr.at[s], self.g.partner
        )

    def _cross(self, s, j):
        to = 2 * self.g.chip_ahead(j) + self.g.c
        return remote(
            self.xsend.at[s, j], self.xrecv.at[s, j], self.xs.at[s, j], self.xr.at[s, j], to
        )

    def start(self, s):
        self._pair(s).start()

    def cross(self, s):
        self._pair(s).wait()
        rows = self.own.shape[2]
        for j in range(self.g.nx - 1):
            chip = self.g.chip_ahead(j)

            def add(i, carry, chip=chip, j=j):
                at = pl.ds(pl.multiple_of(i * RB, RB), RB)
                total = self.own[s, chip, at, :] + self.precv[s, chip, at, :].astype(F32)
                self.xsend[s, j, at, :] = total.astype(BF)
                return carry

            lax.fori_loop(0, rows // RB, add, 0, unroll=4)
            self._cross(s, j).start()

    def arrive(self, s):
        for j in range(self.g.nx - 1):
            self._cross(s, j).wait()

    def total(self, s, at):
        total = self.own[s, self.g.x, at, :] + self.precv[s, self.g.x, at, :].astype(F32)
        for j in range(self.g.nx - 1):
            total = total + self.xrecv[s, j, at, :].astype(F32)
        return total


class Cycle:
    def __init__(self, size):
        self.size = size
        self.me = lax.axis_index("dp")
        self.length = size // 2
        line, column = lax.div(self.me, 2), lax.rem(self.me, 2)
        self.place = line + column * (size - 1 - 2 * line)

    def device(self, place):
        column = lax.div(place, self.length)
        line = place + column * (self.size - 1 - 2 * place)
        return 2 * line + column

    def beside(self, way):
        return self.device(lax.rem(self.place + way + self.size, self.size))


def split(shape, size):
    tall = max(16, shape[0] // (2 * size))
    across = 2 * size * tall // shape[0]
    return tall, shape[1] // across, across


def ring_scratch(shape, size):
    tall, broad, _ = split(shape, size)
    step = pltpu.SemaphoreType.DMA((size - 1,))
    return [
        pltpu.VMEM((size - 1, tall, broad), BF),
        pltpu.SemaphoreType.DMA((size,)),
    ] + [step] * 4 + [pltpu.SemaphoreType.REGULAR]


class Ring:
    def __init__(self, cycle, data, target, way, scratch):
        self.cycle, self.data, self.target, self.way = cycle, data, target, way
        self.size = cycle.size
        self.recv, self.out_sem, self.ss, self.sr, self.gs, self.gr, self.free = scratch
        self.tall, self.broad, self.across = split(data.shape, self.size)
        self.to, self.frm = {"dp": cycle.beside(way)}, {"dp": cycle.beside(-way)}
        self.ticks = 2 * self.size - 1

    def block(self, number):
        place = lax.rem(self.cycle.place + self.way * number + 2 * self.size, self.size)
        index = 2 * place + (0 if self.way > 0 else 1)
        if self.across == 1:
            return pl.multiple_of(index * self.tall, self.tall), 0
        row = lax.div(index, self.across)
        column = lax.rem(index, self.across)
        return (
            pl.multiple_of(row * self.tall, self.tall),
            pl.multiple_of(column * self.broad, self.broad),
        )

    def view(self, number):
        row, column = self.block(number)
        return self.data.at[pl.ds(row, self.tall), pl.ds(column, self.broad)]

    def _add(self, t):
        return remote(self.view(-t), self.recv.at[t], self.ss.at[t], self.sr.at[t], self.to)

    def _pass(self, t):
        block = self.view(1 - t)
        return remote(block, block, self.gs.at[t], self.gr.at[t], self.to)

    def _passed(self, t):
        block = self.view(-t)
        return remote(block, block, self.gs.at[t], self.gr.at[t], self.to)

    def _sum(self, t):
        row, column = self.block(-t)

        def part(i, carry):
            at = pl.ds(pl.multiple_of(row + i * RB, RB), RB)
            cols = pl.ds(column, self.broad)
            arrived = self.recv[t - 1, pl.ds(pl.multiple_of(i * RB, RB), RB), :].astype(F32)
            self.data[at, cols] = (self.data[at, cols].astype(F32) + arrived).astype(BF)
            return carry

        lax.fori_loop(0, self.tall // RB, part, 0, unroll=True)

    def _out(self, number, count):
        row, column = self.block(number)
        place = self.target.at[pl.ds(row, self.tall), pl.ds(column, self.broad)]
        return pltpu.make_async_copy(self.view(number), place, self.out_sem.at[count])

    def tick(self, t):
        size = self.size

        @pl.when(t == 0)
        def _():
            self._add(0).start()

        @pl.when((t >= 1) & (t <= size - 1))
        def _():
            self._add(t - 1).wait_recv()
            self._sum(t)

        @pl.when((t >= 1) & (t < size - 1))
        def _():
            self._add(t).start()

        @pl.when((t >= 1) & (t <= size - 1))
        def _():
            self._add(t - 1).wait_send()
            pl.semaphore_signal(self.free, inc=1, device_id=self.frm, device_id_type=MESH)

        @pl.when(t == size - 1)
        def _():
            pl.semaphore_wait(self.free, 1)
            self._pass(0).start()
            self._out(1, 0).start()

        @pl.when((t > size - 1) & (t < 2 * size - 1))
        def _():
            u = t - size
            self._passed(u).wait_recv()

            @pl.when(t < 2 * size - 2)
            def _():
                pl.semaphore_wait(self.free, 1)
                self._pass(u + 1).start()

            self._out(-u, u + 1).start()

    def drain(self):
        self._out(1, 0).wait()

        def step(t, carry):
            self._pass(t).wait_send()
            self._out(-t, t + 1).wait()
            return carry

        lax.fori_loop(0, self.size - 1, step, 0)


def meet(peers):
    barrier = pltpu.get_barrier_semaphore()
    for peer in peers:
        pl.semaphore_signal(barrier, inc=1, device_id=peer, device_id_type=MESH)
    pl.semaphore_wait(barrier, len(peers))


def mean_of(values):
    return jnp.sum(values, axis=1, keepdims=True) * (1.0 / D)


def attend_kernel(n, seqs, heads, *refs):
    (
        len_ref, tok_ref, up_ref, tea_ref, ob_ref, ag_ref, as_ref, db_ref, fg_ref, fs_ref,
        wn_ref, wa_ref, hn_ref, ha_ref, wq_ref, wk_ref, wv_ref, qb_ref, vb_ref, wo_ref,
        full_o, qkv_o, prob_o, ctx_o, gat_o, nrm_o, pre_o, rstd_o, mid_o, par_o, change_o, gate_o,
        full, wqkv, wo, qkv, prob, ctx, gat, own, psend, precv, xsend, xrecv,
        nrm, pre, rstd, mid, par, chg, up, tea, change, vec, score, in_sem, out_sem, vec_send, vec_recv, ch_send, ch_recv, *sems,
    ) = refs
    g = Group(n)
    width = heads * HD
    rows = SLOT // n
    gsems, rsems = sems[:7], sems[7:]
    cols = lambda h: pl.ds(pl.multiple_of(h * width, width), width)
    seq = lambda s: pl.ds(pl.multiple_of(s * SLOT, SLOT), SLOT)
    own_rows = lambda s: pl.ds(pl.multiple_of(s * rows, rows), rows)
    ga = Gather(g, gsems, lambda s: tok_ref.at[seq(s), :], lambda s, h: full.at[seq(s), cols(h)])
    re = Reduce(g, rsems, psend, precv, own, xsend, xrecv)

    def vec_to(i):
        to = lax.rem(g.me + 1 + i, n)
        return remote(vec, par.at[:, cols(g.me)], vec_send.at[i], vec_recv.at[i], to)

    def vec_from(i):
        to = lax.rem(g.me + 1 + i, n)
        frm = lax.rem(g.me - 1 - i + n, n)
        return remote(vec, par.at[:, cols(frm)], vec_send.at[i], vec_recv.at[i], to)

    def change_to(i):
        to = lax.rem(g.me + 1 + i, n)
        return remote(
            change.at[:, g.slot(to)], chg.at[:, :, cols(g.me)], ch_send.at[i], ch_recv.at[i], to
        )

    def change_from(i):
        to = lax.rem(g.me + 1 + i, n)
        frm = lax.rem(g.me - 1 - i + n, n)
        return remote(
            change.at[:, g.slot(to)], chg.at[:, :, cols(frm)], ch_send.at[i], ch_recv.at[i], to
        )

    loads = [
        pltpu.make_async_copy(wq_ref, wqkv.at[:, pl.ds(0, width)], in_sem.at[0]),
        pltpu.make_async_copy(wk_ref, wqkv.at[:, pl.ds(width, width)], in_sem.at[1]),
        pltpu.make_async_copy(wv_ref, wqkv.at[:, pl.ds(2 * width, width)], in_sem.at[2]),
        pltpu.make_async_copy(wo_ref, wo, in_sem.at[3]),
        pltpu.make_async_copy(up_ref, up, in_sem.at[4]),
        pltpu.make_async_copy(tea_ref, tea, in_sem.at[5]),
    ]
    par_own = pltpu.make_async_copy(vec, par.at[:, cols(g.me)], in_sem.at[7])
    change_own = pltpu.make_async_copy(
        change.at[:, g.slot(g.me)], chg.at[:, :, cols(g.me)], in_sem.at[8]
    )
    chg_out = pltpu.make_async_copy(chg, change_o, in_sem.at[6])

    def sequence_outs(s):
        return [
            pltpu.make_async_copy(full.at[seq(s), :], full_o.at[seq(s), :], out_sem.at[s, 0]),
            pltpu.make_async_copy(qkv.at[seq(s), :], qkv_o.at[seq(s), :], out_sem.at[s, 1]),
            pltpu.make_async_copy(prob.at[s], prob_o.at[s], out_sem.at[s, 2]),
            pltpu.make_async_copy(ctx.at[seq(s), :], ctx_o.at[seq(s), :], out_sem.at[s, 3]),
            pltpu.make_async_copy(gat.at[seq(s), :], gat_o.at[seq(s), :], out_sem.at[s, 4]),
        ]

    def row_outs(s):
        return [
            pltpu.make_async_copy(nrm.at[own_rows(s), :], nrm_o.at[own_rows(s), :], out_sem.at[s, 5]),
            pltpu.make_async_copy(pre.at[own_rows(s), :], pre_o.at[own_rows(s), :], out_sem.at[s, 6]),
            pltpu.make_async_copy(rstd.at[own_rows(s), :], rstd_o.at[own_rows(s), :], out_sem.at[s, 7]),
            pltpu.make_async_copy(mid.at[own_rows(s), :], mid_o.at[own_rows(s), :], out_sem.at[s, 8]),
        ]

    for load in loads:
        load.start()
    for row, ref in ((0, ob_ref), (2, ag_ref), (3, as_ref), (4, db_ref), (5, fg_ref), (6, fs_ref)):
        vec[row : row + 1, :] = ref[...]
    vec[1:2, :] = gate_value(wn_ref[...], part_of(wa_ref, g.me, width))
    vec[7:8, :] = jnp.zeros((1, width), F32)
    meet(g.all_peers())

    def begin(s, carry):
        ga.start(s)
        return carry

    for i in range(n - 1):
        vec_to(i).start()
    lax.fori_loop(0, seqs, begin, 0)
    par_own.start()
    gate_row = gate_value(*head_row(hn_ref, ha_ref, g.me, heads))
    gate_o[...] = gate_row
    for load in loads:
        load.wait()

    def differ(i, carry):
        at = pl.ds(pl.multiple_of(i * 32, 32), 32)
        value = (up[at, :].astype(F32) - tea[at, :].astype(F32)).astype(BF)
        each = SLOT // n // 32
        s, q = lax.div(i, SLOT // 32), lax.rem(i, SLOT // 32)
        change[s, lax.div(q, each), pl.ds(pl.multiple_of(lax.rem(q, each) * 32, 32), 32), :] = value
        return carry

    lax.fori_loop(0, seqs * SLOT // 32, differ, 0)
    change_own.start()
    ga.relay(0)
    par_own.wait()
    for i in range(n - 1):
        vec_from(i).wait()
    par_o[...] = par[...]

    lanes = lax.broadcasted_iota(jnp.int32, (1, width), 1)
    head_lanes = [
        jnp.where((lanes >= h * HD) & (lanes < (h + 1) * HD), 1.0, 0.0).astype(BF) for h in range(heads)
    ]

    scaled_lanes = [lane * HD**-0.5 for lane in head_lanes]

    def finish(s):
        re.arrive(s)

        def block(i, carry):
            at = pl.ds(pl.multiple_of(i * RB, RB), RB)
            here = pl.ds(pl.multiple_of(s * rows + i * RB, RB), RB)
            token_row = pl.multiple_of(s * SLOT + g.slot(g.me) * rows + i * RB, RB)
            attention_pre = re.total(s, at) + par[0:1, :]
            residual = full[pl.ds(token_row, RB), :].astype(F32) + attention_pre * par[1:2, :]
            centered = residual - mean_of(residual)
            row_rstd = lax.rsqrt(mean_of(centered * centered) + EPS)
            normed = centered * row_rstd
            middle = normed * par[2:3, :] + par[3:4, :]
            nrm[here, :] = normed
            pre[here, :] = attention_pre
            rstd[here, :] = jnp.broadcast_to(row_rstd, (RB, 128))
            mid[here, :] = middle.astype(BF)
            return carry

        lax.fori_loop(0, rows // RB, block, 0, unroll=4)
        for copy in row_outs(s):
            copy.start()

    def sequence(s, carry):
        ga.wait(s)
        here = seq(s)
        projected = nn(full[here, :], wqkv[...])
        qkv[here, 0:width] = (projected[:, 0:width] + qb_ref[...]).astype(BF)
        qkv[here, width : 2 * width] = projected[:, width : 2 * width].astype(BF)
        qkv[here, 2 * width : 3 * width] = (projected[:, 2 * width : 3 * width] + vb_ref[...]).astype(BF)

        @pl.when(s + 1 < seqs)
        def _():
            ga.relay(s + 1)

        @pl.when(s > 0)
        def _():
            re.cross(s - 1)

        @pl.when(s == seqs - 2)
        def _():
            for i in range(n - 1):
                change_to(i).start()

        length = len_ref[lax.axis_index("dp") * seqs + s]
        bias = jnp.where(lax.broadcasted_iota(jnp.int32, (1, SLOT), 1) < length, 0.0, MASKED)
        for h in range(heads):
            score[...] = nt(qkv[here, 0:width] * scaled_lanes[h], qkv[here, width : 2 * width])

            def softmax(i, carry, h=h):
                at = pl.ds(pl.multiple_of(i * 64, 64), 64)
                scores = score[at, :] + bias
                exponent = jnp.exp(scores - jnp.max(scores, axis=1, keepdims=True))
                total = jnp.sum(exponent, axis=1, keepdims=True)
                prob[s, h, at, :] = (exponent * (1.0 / total)).astype(BF)
                return carry

            lax.fori_loop(0, SLOT // 64, softmax, 0, unroll=True)
            term = nn(prob[s, h], qkv[here, 2 * width : 3 * width] * head_lanes[h])
            ctx[here, :] = term if h == 0 else ctx[here, :] + term
        gat[here, :] = (ctx[here, :] * gate_row).astype(BF)
        for copy in sequence_outs(s):
            copy.start()
        half = SLOT // 2
        there = pl.ds(pl.multiple_of(s * SLOT + (1 - g.c) * half, half), half)
        psend[s] = nn(gat[there, :], wo[...]).astype(BF).reshape(n // 2, rows, D)
        re.start(s)
        mine = pl.ds(pl.multiple_of(s * SLOT + g.c * half, half), half)
        own[s] = nn(gat[mine, :], wo[...]).reshape(n // 2, rows, D)

        @pl.when(s > 0)
        def _():
            finish(s - 1)

        return carry

    lax.fori_loop(0, seqs, sequence, 0)
    re.cross(seqs - 1)
    change_own.wait()
    for i in range(n - 1):
        change_from(i).wait()
    chg_out.start()
    finish(seqs - 1)
    chg_out.wait()

    def end(s, carry):
        ga.drain(s)
        for copy in sequence_outs(s) + row_outs(s):
            copy.wait()
        return carry

    lax.fori_loop(0, seqs, end, 0)


def feed_kernel(n, seqs, units, *refs):
    (
        len_ref, mid_ref, nrm_ref, pre_ref, rstd_ref, par, change_ref, w1_ref, b1_ref, w2_ref, un_ref, ua_ref,
        out_o, dlow_o, dres_o, dw1_o, dw2_o, rowsum_o, unitsum_o,
        midf, dffn, w1, w2, act, inner, slope, own, psend, precv, xsend, xrecv,
        nrm, pre, rstd, change, dtwo, dsend, fout, dlow, dres, wide, grad, sums, unit_sums, ugate_ref,
        in_sem, out_sem, grad_sem, *sems,
    ) = refs
    g = Group(n)
    rows = SLOT // n
    half = SLOT // 2
    g1, r1, g2, r2 = sems[:7], sems[7:11], sems[11:18], sems[18:]
    seq = lambda s: pl.ds(pl.multiple_of(s * SLOT, SLOT), SLOT)
    own_rows = lambda s: pl.ds(pl.multiple_of(s * rows, rows), rows)
    spot = lambda s, h: pl.ds(pl.multiple_of(s * SLOT + g.slot(h) * rows, rows), rows)
    gm = Gather(g, g1, lambda s: mid_ref.at[own_rows(s), :], lambda s, h: midf.at[spot(s, h), :])
    gd = Gather(g, g2, lambda s: dsend.at[own_rows(s), :], lambda s, h: dffn.at[spot(s, h), :])
    rf = Reduce(g, r1, psend, precv, own, xsend, xrecv)
    rb = Reduce(g, r2, psend, precv, own, xsend, xrecv)
    loads = [
        pltpu.make_async_copy(w1_ref, w1, in_sem.at[0]),
        pltpu.make_async_copy(w2_ref, w2, in_sem.at[1]),
        pltpu.make_async_copy(nrm_ref, nrm, in_sem.at[2]),
        pltpu.make_async_copy(change_ref, change, in_sem.at[3]),
        pltpu.make_async_copy(pre_ref, pre, in_sem.at[4]),
        pltpu.make_async_copy(rstd_ref, rstd, in_sem.at[5]),
    ]

    meet(g.near_peers())

    def begin(s, carry):
        gm.start(s)
        return carry

    lax.fori_loop(0, seqs, begin, 0)
    for load in loads:
        load.start()
    sums[...] = jnp.zeros_like(sums)
    unit_sums[...] = jnp.zeros_like(unit_sums)
    ugate_ref[...] = gate_value(un_ref[...], part_of(ua_ref, g.me, units))
    gm.relay(0)
    for load in loads:
        load.wait()

    def finish_forward(s):
        rf.arrive(s)
        length = len_ref[lax.axis_index("dp") * seqs + s]

        def block(i, carry):
            at = pl.ds(pl.multiple_of(i * RB, RB), RB)
            here = pl.ds(pl.multiple_of(s * rows + i * RB, RB), RB)
            ffn_pre = rf.total(s, at) + par[4:5, :]
            middle = nrm[here, :] * par[2:3, :] + par[3:4, :]
            residual = middle + ffn_pre * par[1:2, :]
            centered = residual - mean_of(residual)
            row_rstd = lax.rsqrt(mean_of(centered * centered) + EPS)
            normed = centered * row_rstd
            final = normed * par[5:6, :] + par[6:7, :]
            fout[here, :] = final.astype(BF)
            place = g.slot(g.me) * rows + i * RB + lax.broadcasted_iota(jnp.int32, (RB, 1), 0)
            live = jnp.where(place < length, 1.0, 0.0)
            d_final = live * (change[here, :].astype(F32) + final)
            sums[0] += fold(d_final * normed)
            sums[1] += fold(d_final)
            d_normed = d_final * par[5:6, :]
            d_two = row_rstd * (d_normed - mean_of(d_normed) - normed * mean_of(d_normed * normed))
            sums[2] += fold(d_two * ffn_pre)
            d_ffn = d_two * par[1:2, :]
            sums[3] += fold(d_ffn)
            dtwo[here, :] = d_two
            dsend[here, :] = d_ffn.astype(BF)
            return carry

        lax.fori_loop(0, rows // RB, block, 0, unroll=4)
        gd.start(s)

    def forward(s, carry):
        gm.wait(s)
        here = seq(s)

        def part(b, carry):
            cols = pl.ds(pl.multiple_of(b * NB, NB), NB)
            wide[...] = nn(midf[here, :], w1[:, cols])
            bias = b1_ref[:, cols]
            gate = ugate_ref[:, cols]

            def block(i, carry):
                at = pl.ds(pl.multiple_of(i * 32, 32), 32)
                row = pl.ds(pl.multiple_of(s * SLOT + i * 32, 32), 32)
                v = wide[at, :] + bias
                phi = 0.5 * (1.0 + lax.erf(v * ROOT_HALF))
                activated = v * phi
                act[row, cols] = activated.astype(BF)
                inner[row, cols] = (activated * gate).astype(BF)
                steep = phi + v * jnp.exp(-0.5 * v * v) * (1.0 / ROOT_TWO_PI)
                slope[row, cols] = (gate * steep).astype(BF)
                return carry

            lax.fori_loop(0, SLOT // 32, block, 0, unroll=8)
            return carry

        lax.fori_loop(0, units // NB, part, 0)

        @pl.when(s + 1 < seqs)
        def _():
            gm.relay(s + 1)

        @pl.when(s > 0)
        def _():
            rf.cross(s - 1)

        there = pl.ds(pl.multiple_of(s * SLOT + (1 - g.c) * half, half), half)
        psend[s] = nn(inner[there, :], w2[...]).astype(BF).reshape(n // 2, rows, D)
        rf.start(s)
        mine = pl.ds(pl.multiple_of(s * SLOT + g.c * half, half), half)
        own[s] = nn(inner[mine, :], w2[...]).reshape(n // 2, rows, D)

        @pl.when(s > 1)
        def _():
            finish_forward(s - 2)

        return carry

    lax.fori_loop(0, seqs, forward, 0)
    rf.cross(seqs - 1)
    gd.relay(0)

    def row_outs(s):
        return [
            pltpu.make_async_copy(fout.at[own_rows(s), :], out_o.at[own_rows(s), :], out_sem.at[s, 0]),
            pltpu.make_async_copy(dlow.at[own_rows(s), :], dlow_o.at[own_rows(s), :], out_sem.at[s, 1]),
            pltpu.make_async_copy(dres.at[own_rows(s), :], dres_o.at[own_rows(s), :], out_sem.at[s, 2]),
        ]

    def finish_backward(s):
        rb.arrive(s)

        def block(i, carry):
            at = pl.ds(pl.multiple_of(i * RB, RB), RB)
            here = pl.ds(pl.multiple_of(s * rows + i * RB, RB), RB)
            normed = nrm[here, :]
            d_middle = dtwo[here, :] + rb.total(s, at)
            sums[4] += fold(d_middle * normed)
            sums[5] += fold(d_middle)
            d_normed = d_middle * par[2:3, :]
            d_one = rstd[here, 0:1] * (
                d_normed - mean_of(d_normed) - normed * mean_of(d_normed * normed)
            )
            sums[2] += fold(d_one * pre[here, :])
            d_attn = d_one * par[1:2, :]
            sums[6] += fold(d_attn)
            dres[here, :] = d_one
            dlow[here, :] = d_attn.astype(BF)
            return carry

        lax.fori_loop(0, rows // RB, block, 0, unroll=4)
        for copy in row_outs(s):
            copy.start()

    def backward(s, carry):
        gd.wait(s)
        here = seq(s)

        def part(b, carry):
            cols = pl.ds(pl.multiple_of(b * NB, NB), NB)
            wide[...] = nt(dffn[here, :], w2[cols, :])

            def block(i, sums_here):
                unit_part, bias_part = sums_here
                at = pl.ds(pl.multiple_of(i * 32, 32), 32)
                row = pl.ds(pl.multiple_of(s * SLOT + i * 32, 32), 32)
                d_inner = wide[at, :]
                d_pre = (d_inner * slope[row, cols].astype(F32)).astype(BF)
                unit_part = unit_part + fold(d_inner * act[row, cols].astype(F32))
                bias_part = bias_part + fold(d_pre.astype(F32))
                slope[row, cols] = d_pre
                return (unit_part, bias_part)

            zero = jnp.zeros((8, NB), F32)
            unit_part, bias_part = lax.fori_loop(0, SLOT // 32, block, (zero, zero), unroll=8)
            unit_sums[0, :, cols] += unit_part
            unit_sums[1, :, cols] += bias_part
            return carry

        lax.fori_loop(0, units // NB, part, 0)

        @pl.when(s < 2)
        def _():
            finish_forward(seqs - 2 + s)

        @pl.when(s + 1 < seqs)
        def _():
            gd.relay(s + 1)

        @pl.when(s > 0)
        def _():
            rb.cross(s - 1)

        there = pl.ds(pl.multiple_of(s * SLOT + (1 - g.c) * half, half), half)
        psend[s] = nt(slope[there, :], w1[...]).astype(BF).reshape(n // 2, rows, D)
        rb.start(s)
        mine = pl.ds(pl.multiple_of(s * SLOT + g.c * half, half), half)
        own[s] = nt(slope[mine, :], w1[...]).reshape(n // 2, rows, D)

        @pl.when(s > 1)
        def _():
            finish_backward(s - 2)

        return carry

    lax.fori_loop(0, seqs, backward, 0)
    rb.cross(seqs - 1)

    def grad_out(k, b):
        target = (dw2_o, dw1_o)[k]
        at = pl.ds(pl.multiple_of(b * NB, NB), NB)
        return pltpu.make_async_copy(grad.at[b], target.at[at, :], grad_sem.at[k, b])

    def down_grad(b, carry):
        cols = pl.ds(pl.multiple_of(b * NB, NB), NB)
        grad[b] = tn(inner[:, cols], dffn[...]).astype(BF)
        grad_out(0, b).start()
        return carry

    lax.fori_loop(0, units // NB, down_grad, 0)
    finish_backward(seqs - 2)
    for b in range(units // NB):
        grad_out(0, b).wait()

    def inner_grad(b, carry):
        cols = pl.ds(pl.multiple_of(b * NB, NB), NB)
        grad[b, :, 0:units] = tn(midf[:, cols], slope[...]).astype(BF)
        pltpu.make_async_copy(
            grad.at[b, :, pl.ds(0, units)], dw1_o.at[cols, :], grad_sem.at[1, b]
        ).start()
        return carry

    lax.fori_loop(0, D // NB, inner_grad, 0)
    finish_backward(seqs - 1)
    for k in range(7):
        rowsum_o[k : k + 1, :] = jnp.sum(sums[k], axis=0, keepdims=True)
    rowsum_o[7:8, :] = jnp.zeros((1, D), F32)
    for k in range(2):
        unitsum_o[k : k + 1, :] = jnp.sum(unit_sums[k], axis=0, keepdims=True)
    for b in range(D // NB):
        at = pl.ds(b * NB, NB)
        pltpu.make_async_copy(
            grad.at[b, :, pl.ds(0, units)], dw1_o.at[at, :], grad_sem.at[1, b]
        ).wait()

    def end(s, carry):
        gm.drain(s)
        gd.drain(s)
        for copy in row_outs(s):
            copy.wait()
        return carry

    lax.fori_loop(0, seqs, end, 0)


def attend_back_kernel(n, seqs, heads, size, *refs):
    (
        len_ref, dlow_ref, dres_ref, full_ref, qkv_ref, prob_ref, ctx_ref, gat_ref,
        wq_ref, wk_ref, wv_ref, wo_ref, dw1_ref, dw2_ref, out_ref, teacher_ref, gate_ref, row_ref, unit_ref,
        tgrad_o, dwq_o, dwk_o, dwv_o, dwo_o, dw1_o, dw2_o, output_o, small_o, units_o,
        dattn, dres, full, qkv, prob, ctx, gat, wqkv, wo, dctx, dqkv, dprob, dscore, acc,
        block_f, own, psend, precv, xsend, xrecv, tgrad, moved, sums, dw1, dw2,
        dwq, dwk, dwv, dwo, teacher, parts, small, rbuf, sbuf, ubuf,
        in_sem, out_sem, move_send, move_recv, r_send, r_recv, s_send, s_recv, u_send, u_recv, *sems,
    ) = refs
    g = Group(n)
    cycle = Cycle(size)
    rings = []
    grads = ((dw1, dw1_o), (dw2, dw2_o), (dwq, dwq_o), (dwk, dwk_o), (dwv, dwv_o), (dwo, dwo_o))
    for data, target in grads:
        for way in (1, -1):
            i = 11 + 7 * len(rings)
            rings.append(Ring(cycle, data, target, way, sems[i : i + 7]))
    ticks = rings[0].ticks

    def tick(t, which):
        for ring in rings[2 * which : 2 * which + 2]:
            ring.tick(t)

    def slot_tick(s, place):
        served = [0, heads // 2, heads // 2 + 1, heads + 1]
        if place in served:
            k = served.index(place)
            tick(2 + s * 2 + k // 2, k % 2)

    def row_to(i):
        to = lax.rem(g.me + 1 + i, n)
        return remote(parts.at[:, cols_of(to)], rbuf.at[i], r_send.at[i], r_recv.at[i], to)

    def small_to(i):
        to = {"dp": lax.rem(cycle.me + 1 + i, size)}
        return remote(small, sbuf.at[i], s_send.at[i], s_recv.at[i], to)

    def units_to(i):
        to = {"dp": lax.rem(cycle.me + 1 + i, size)}
        return remote(unit_ref, ubuf.at[i], u_send.at[i], u_recv.at[i], to)

    def move_to(i):
        to = lax.rem(g.me + 1 + i, n)
        return remote(
            out_ref.at[:, :, cols_of(to)], moved.at[:, g.slot(g.me)], move_send.at[i], move_recv.at[i], to
        )

    def move_from(i):
        to = lax.rem(g.me + 1 + i, n)
        frm = lax.rem(g.me - 1 - i + n, n)
        return remote(
            out_ref.at[:, :, cols_of(to)], moved.at[:, g.slot(frm)], move_send.at[i], move_recv.at[i], to
        )

    width = heads * HD
    rows = SLOT // n
    gsems, rsems = sems[:7], sems[7:11]
    cols_of = lambda h: pl.ds(pl.multiple_of(h * width, width), width)
    seq = lambda s: pl.ds(pl.multiple_of(s * SLOT, SLOT), SLOT)
    own_rows = lambda s: pl.ds(pl.multiple_of(s * rows, rows), rows)
    spot = lambda s, h: pl.ds(pl.multiple_of(s * SLOT + g.slot(h) * rows, rows), rows)
    ga = Gather(g, gsems, lambda s: dlow_ref.at[own_rows(s), :], lambda s, h: dattn.at[spot(s, h), :])
    re = Reduce(g, rsems, psend, precv, own, xsend, xrecv)
    loads = [
        pltpu.make_async_copy(wo_ref, wo, in_sem.at[0]),
        pltpu.make_async_copy(ctx_ref, ctx, in_sem.at[1]),
        pltpu.make_async_copy(qkv_ref, qkv, in_sem.at[2]),
        pltpu.make_async_copy(prob_ref, prob, in_sem.at[3]),
        pltpu.make_async_copy(wq_ref, wqkv.at[:, pl.ds(0, width)], in_sem.at[4]),
        pltpu.make_async_copy(wk_ref, wqkv.at[:, pl.ds(width, width)], in_sem.at[5]),
        pltpu.make_async_copy(wv_ref, wqkv.at[:, pl.ds(2 * width, width)], in_sem.at[6]),
        pltpu.make_async_copy(dres_ref, dres, in_sem.at[7]),
        pltpu.make_async_copy(full_ref, full, in_sem.at[8]),
        pltpu.make_async_copy(gat_ref, gat, in_sem.at[9]),
        pltpu.make_async_copy(
            out_ref.at[:, :, cols_of(g.me)], moved.at[:, g.slot(g.me)], in_sem.at[11]
        ),
        pltpu.make_async_copy(teacher_ref, teacher, in_sem.at[10]),
    ]
    grads_in = [
        pltpu.make_async_copy(dw1_ref, dw1, in_sem.at[12]),
        pltpu.make_async_copy(dw2_ref, dw2, in_sem.at[13]),
    ]
    for load in grads_in:
        load.start()
    meet(g.all_peers() + [{"dp": lax.rem(cycle.me + 1 + i, size)} for i in range(size - 1)])

    def begin(s, carry):
        ga.start(s)
        return carry

    lax.fori_loop(0, seqs, begin, 0)
    for load in loads:
        load.start()
    sums[...] = jnp.zeros_like(sums)
    for load in grads_in:
        load.wait()
    for t in range(2):
        tick(t, 0)
        tick(t, 1)
    ga.relay(0)
    for load in loads[:8]:
        load.wait()

    lanes = lax.broadcasted_iota(jnp.int32, (1, width), 1)
    head_lanes = [
        jnp.where((lanes >= h * HD) & (lanes < (h + 1) * HD), 1.0, 0.0).astype(BF) for h in range(heads)
    ]

    def out(s):
        return pltpu.make_async_copy(tgrad.at[seq(s), :], tgrad_o.at[seq(s), :], out_sem.at[s])

    def finish(s):
        re.arrive(s)

        def block(i, carry):
            at = pl.ds(pl.multiple_of(i * 32, 32), 32)
            tgrad[pl.ds(pl.multiple_of(s * SLOT + i * 32, 32), 32), :] = re.total(s, at)
            return carry

        lax.fori_loop(0, SLOT // 32, block, 0, unroll=4)
        out(s).start()

    def token_block(s, h):
        cols = pl.ds(pl.multiple_of(h * width, width), width)
        block_f[...] = nt(dqkv[seq(s), :], wqkv[cols, :])
        mine = pl.ds(pl.multiple_of(g.slot(g.me) * rows, rows), rows)
        block_f[mine, :] += dres[own_rows(s), cols]

    def sequence(s, carry):
        ga.wait(s)
        here = seq(s)
        d_gated = nt(dattn[here, :], wo[...])
        sums[0] += fold(d_gated * ctx[here, :])
        dctx[...] = (d_gated * gate_ref[...]).astype(BF)
        slot_tick(s, 0)

        @pl.when(s + 1 < seqs)
        def _():
            ga.relay(s + 1)

        @pl.when(s > 0)
        def _():
            re.cross(s - 1)

        @pl.when(s == 1)
        def _():
            for i in range(n - 1):
                move_to(i).start()
            for i in range(size - 1):
                units_to(i).start()

        for h in range(heads):
            d_context = dctx[...] * head_lanes[h]
            dprob[...] = nt(d_context, qkv[here, 2 * width : 3 * width])

            def softmax(i, carry, h=h):
                at = pl.ds(pl.multiple_of(i * 64, 64), 64)
                p = prob[s, h, at, :].astype(F32)
                weighted = p * dprob[at, :]
                total = jnp.sum(weighted, axis=1, keepdims=True)
                dscore[at, :] = (weighted - p * total).astype(BF)
                return carry

            lax.fori_loop(0, SLOT // 64, softmax, 0, unroll=True)
            slot_tick(s, h + 1)
            terms = (
                nn(dscore[...], qkv[here, width : 2 * width] * head_lanes[h]),
                tn(dscore[...], qkv[here, 0:width] * head_lanes[h]),
                tn(prob[s, h], d_context),
            )
            for k in range(3):
                acc[k] = terms[k] if h == 0 else acc[k] + terms[k]
        scales = (HD**-0.5, HD**-0.5, 1.0)
        for k in range(3):
            rounded = (acc[k] * scales[k]).astype(BF)
            dqkv[here, k * width : (k + 1) * width] = rounded
            sums[1 + k] += fold(rounded.astype(F32))
        for chip in range(n // 2):
            token_block(s, 2 * chip + 1 - g.c)
            psend[s, chip] = block_f[...].astype(BF)
        re.start(s)
        slot_tick(s, heads + 1)
        for chip in range(n // 2):
            token_block(s, 2 * chip + g.c)
            own[s, chip] = block_f[...]

        @pl.when(s > 0)
        def _():
            finish(s - 1)

        return carry

    lax.fori_loop(0, seqs, sequence, 0)
    re.cross(seqs - 1)
    for load in loads[8:]:
        load.wait()

    def rest(t, carry):
        tick(t, 0)
        tick(t, 1)
        return carry

    def token_grad(b, carry):
        cols = pl.ds(pl.multiple_of(b * NB, NB), NB)
        term = tn(full[:, cols], dqkv[...])
        for k, grad in enumerate((dwq, dwk, dwv)):
            grad[cols, :] = term[:, k * width : (k + 1) * width].astype(BF)
        tick(2 + 2 * seqs + b, 0)
        tick(2 + 2 * seqs + b, 1)
        return carry

    lax.fori_loop(0, D // NB, token_grad, 0)
    for which in range(2, 5):
        tick(0, which)
    dwo[...] = tn(gat[...], dattn[...]).astype(BF)
    tick(0, 5)
    lax.fori_loop(2 + 2 * seqs + D // NB, ticks, rest, 0)
    for i in range(n - 1):
        move_from(i).wait()
    moved_out = pltpu.make_async_copy(moved, output_o, in_sem.at[14])
    moved_out.start()

    def squares(s, total):
        length = len_ref[cycle.me * seqs + s]

        def block(i, total):
            each = rows // 32
            at = pl.ds(pl.multiple_of(lax.rem(i, each) * 32, 32), 32)
            value = moved[s, lax.div(i, each), at, :].astype(F32)
            place = i * 32 + lax.broadcasted_iota(jnp.int32, (32, 1), 0)
            differ = value - teacher[pl.ds(pl.multiple_of(s * SLOT + i * 32, 32), 32), :].astype(F32)
            return total + fold(jnp.where(place < length, differ * differ, 0.0))

        return lax.fori_loop(0, SLOT // 32, block, total)

    square_sum = lax.fori_loop(0, seqs, squares, jnp.zeros((8, width), F32))
    parts[...] = row_ref[...]
    for h in range(n):
        parts[7:8, h * width : (h + 1) * width] = jnp.sum(square_sum, axis=0, keepdims=True)
    for i in range(n - 1):
        row_to(i).start()
    for which in range(2, 6):
        tick(1, which)
    finish(seqs - 1)
    total = parts[:, cols_of(g.me)]
    for i in range(n - 1):
        row_to(i).wait()
        total = total + rbuf[i]
    small[:, 0:width] = total
    for k in range(4):
        small[k : k + 1, width : 2 * width] = jnp.sum(sums[k], axis=0, keepdims=True)
    small[4:8, width : 2 * width] = jnp.zeros((4, width), F32)
    for i in range(size - 1):
        small_to(i).start()

    def last(t, carry):
        for which in range(2, 6):
            tick(t, which)
        return carry

    lax.fori_loop(2, ticks, last, 0)
    small_sum = small[...]
    unit_sum = unit_ref[...]
    for i in range(size - 1):
        small_to(i).wait()
        units_to(i).wait()
        small_sum = small_sum + sbuf[i]
        unit_sum = unit_sum + ubuf[i]
    small_o[...] = small_sum
    units_o[...] = unit_sum
    moved_out.wait()
    for ring in rings:
        ring.drain()

    def end(s, carry):
        ga.drain(s)
        out(s).wait()
        return carry

    lax.fori_loop(0, seqs, end, 0)


def complete_kernel(n, heads, units, *refs):
    (
        dw1_ref, dw2_ref, dwq_ref, dwk_ref, dwv_ref, dwo_ref, tgrad_ref, output_ref,
        small_ref, unit_ref, ha_ref, ua_ref, wa_ref, mult_ref, hn_ref, un_ref, wn_ref, len_ref,
        dw1_o, dw2_o, dwq_o, dwk_o, dwv_o, dwo_o, tgrad_o, output_o,
        qb_o, vb_o, ob_o, ag_o, as_o, db_o, fg_o, fs_o, b1_o, ha_o, ua_o, wa_o, mse_o, mult_o,
        dw1, dw2, dwq, dwk, dwv, dwo, tgrad, output, fw1, fw2, fwq, fwk, fwv, fwo, in_sem, out_sem,
    ) = refs
    width = heads * HD
    rank = lax.axis_index("hid")
    wide = (
        (dw1_ref, dw1, fw1, dw1_o), (dw2_ref, dw2, fw2, dw2_o), (dwq_ref, dwq, fwq, dwq_o),
        (dwk_ref, dwk, fwk, dwk_o), (dwv_ref, dwv, fwv, dwv_o), (dwo_ref, dwo, fwo, dwo_o),
        (tgrad_ref, tgrad, tgrad, tgrad_o), (output_ref, output, output, output_o),
    )
    parts = 4

    def piece(ref, p):
        rows = ref.shape[0] // parts
        return ref.at[pl.ds(pl.multiple_of(p * rows, rows), rows), :]

    def load(k, p):
        return pltpu.make_async_copy(piece(wide[k][0], p), piece(wide[k][1], p), in_sem.at[k, p])

    def store(k, p):
        return pltpu.make_async_copy(piece(wide[k][2], p), piece(wide[k][3], p), out_sem.at[k, p])

    for k in range(len(wide)):
        for p in range(parts):
            load(k, p).start()

    head_all = small_ref[:, width : 2 * width]
    for ref, row in ((ob_o, 6), (ag_o, 4), (as_o, 5), (db_o, 3), (fg_o, 0), (fs_o, 1)):
        ref[...] = small_ref[row : row + 1, 0:width]
    qb_o[...] = head_all[1:2, :]
    vb_o[...] = head_all[3:4, :]
    b1_o[...] = unit_ref[1:2, :]
    keeps = [keep_prob(ref[...]) for ref in (ha_ref, ua_ref, wa_ref)]
    heads_kept, units_kept, dims_kept = [jnp.sum(k, axis=1, keepdims=True) for k in keeps]
    full_size = 4.0 * D * D + 2.0 * D * FF
    gap = 1.0 - (4.0 * HD * heads_kept * dims_kept + 2.0 * units_kept * dims_kept) / full_size - TARGET
    pull = -(lane_of(mult_ref[...], 0) + 2.0 * lane_of(mult_ref[...], 1) * gap) / full_size
    slot = lax.broadcasted_iota(jnp.int32, (1, 2), 1)
    mult_o[...] = mult_ref[...] + ASCENT * jnp.where(slot == 0, gap, gap * gap)

    def pulled(alpha, factor):
        k = keep_prob(alpha)
        return pull * factor * k * (1.0 - k)

    unit_alpha = part_of(ua_ref, rank, units)
    ua_o[...] = unit_ref[0:1, :] * gate_slope(un_ref[...], unit_alpha) + pulled(unit_alpha, 2.0 * dims_kept)
    width_alpha = part_of(wa_ref, rank, width)
    wa_o[...] = small_ref[2:3, 0:width] * gate_slope(wn_ref[...], width_alpha) + pulled(
        width_alpha, 4.0 * HD * heads_kept + 2.0 * units_kept
    )
    noise_row, alpha_row = head_row(hn_ref, ha_ref, rank, heads)
    lanes = lax.broadcasted_iota(jnp.int32, (1, width), 1)
    per_lane = head_all[0:1, :] * gate_slope(noise_row, alpha_row)
    head_pulled = pulled(alpha_row, 4.0 * HD * dims_kept) * (1.0 / HD)
    for h in range(heads):
        here = (lanes >= h * HD) & (lanes < (h + 1) * HD)
        ha_o[:, h : h + 1] = jnp.sum(jnp.where(here, per_lane + head_pulled, 0.0), axis=1, keepdims=True)
    live = jnp.sum(len_ref[...].astype(F32), axis=1, keepdims=True)
    mse_o[...] = jnp.sum(small_ref[7:8, 0:width], axis=1, keepdims=True) / (live * D)

    for k, (_, low, high, _) in enumerate(wide):
        rows = low.shape[0] // parts
        for p in range(parts):
            load(k, p).wait()
            if low is not high:

                step = min(64, rows)

                def widen(i, carry, low=low, high=high, first=p * rows, step=step):
                    at = pl.ds(pl.multiple_of(first + i * step, step), step)
                    high[at, :] = low[at, :].astype(F32)
                    return carry

                lax.fori_loop(0, rows // step, widen, 0)
            store(k, p).start()
    for k in range(len(wide)):
        for p in range(parts):
            store(k, p).wait()


def hbm():
    return pl.BlockSpec(memory_space=pl.ANY)


def vmem():
    return pl.BlockSpec(memory_space=pltpu.VMEM)


def smem():
    return pl.BlockSpec(memory_space=pltpu.SMEM)


def call(kernel, name, ident, ins, outs, scratch, flops):
    return pl.pallas_call(
        kernel,
        name=name,
        out_shape=[jax.ShapeDtypeStruct(shape, dtype) for shape, dtype, _ in outs],
        in_specs=ins,
        out_specs=[spec for _, _, spec in outs],
        scratch_shapes=scratch,
        compiler_params=pltpu.CompilerParams(
            collective_id=ident, has_side_effects=True, vmem_limit_bytes=VMEM_LIMIT
        ),
        cost_estimate=pl.CostEstimate(flops=flops, bytes_accessed=30_000_000, transcendentals=0),
    )


def attend(n, seqs, heads, args):
    width, rows, nx, half = heads * HD, SLOT // n, n // 2, SLOT // 2
    tokens, owned = seqs * SLOT, seqs * rows
    v, dma = pltpu.VMEM, pltpu.SemaphoreType.DMA
    return call(
        functools.partial(attend_kernel, n, seqs, heads),
        "attend",
        0,
        [smem()] + [hbm()] * 3 + [vmem()] * 10 + [hbm()] * 3 + [vmem()] * 2 + [hbm()],
        [
            ((tokens, D), BF, hbm()),
            ((tokens, 3 * width), BF, hbm()),
            ((seqs, heads, SLOT, SLOT), BF, hbm()),
            ((tokens, width), F32, hbm()),
            ((tokens, width), BF, hbm()),
            ((owned, D), F32, hbm()),
            ((owned, D), F32, hbm()),
            ((owned, 128), F32, hbm()),
            ((owned, D), BF, hbm()),
            ((8, D), F32, vmem()),
            ((seqs, rows, D), BF, hbm()),
            ((1, width), F32, vmem()),
        ],
        [
            v((tokens, D), BF),
            v((D, 3 * width), BF),
            v((width, D), BF),
            v((tokens, 3 * width), BF),
            v((seqs, heads, SLOT, SLOT), BF),
            v((tokens, width), F32),
            v((tokens, width), BF),
            v((seqs, nx, rows, D), F32),
            v((seqs, nx, rows, D), BF),
            v((seqs, nx, rows, D), BF),
            v((seqs, nx - 1, rows, D), BF),
            v((seqs, nx - 1, rows, D), BF),
            v((owned, D), F32),
            v((owned, D), F32),
            v((owned, 128), F32),
            v((owned, D), BF),
            v((8, D), F32),
            v((seqs, rows, D), BF),
            v((tokens, width), BF),
            v((tokens, width), BF),
            v((seqs, n, rows, width), BF),
            v((8, width), F32),
            v((SLOT, SLOT), F32),
            dma((9,)),
            dma((seqs, 9)),
            dma((n - 1,)),
            dma((n - 1,)),
            dma((n - 1,)),
            dma((n - 1,)),
        ]
        + gather_sems(seqs, nx)
        + reduce_sems(seqs, nx),
        10_000_000_000,
    )(*args)


def feed(n, seqs, units, args):
    rows, nx = SLOT // n, n // 2
    tokens, owned = seqs * SLOT, seqs * rows
    v, dma = pltpu.VMEM, pltpu.SemaphoreType.DMA
    return call(
        functools.partial(feed_kernel, n, seqs, units),
        "feed",
        1,
        [smem(), hbm(), hbm(), hbm(), hbm(), vmem(), hbm(), hbm(), vmem(), hbm(), vmem(), vmem()],
        [
            ((owned, D), BF, hbm()),
            ((owned, D), BF, hbm()),
            ((owned, D), F32, hbm()),
            ((D, units), BF, hbm()),
            ((units, D), BF, hbm()),
            ((8, D), F32, vmem()),
            ((2, units), F32, vmem()),
        ],
        [
            v((tokens, D), BF),
            v((tokens, D), BF),
            v((D, units), BF),
            v((units, D), BF),
            v((tokens, units), BF),
            v((tokens, units), BF),
            v((tokens, units), BF),
            v((seqs, nx, rows, D), F32),
            v((seqs, nx, rows, D), BF),
            v((seqs, nx, rows, D), BF),
            v((seqs, nx - 1, rows, D), BF),
            v((seqs, nx - 1, rows, D), BF),
            v((owned, D), F32),
            v((owned, D), F32),
            v((owned, 128), F32),
            v((owned, D), BF),
            v((owned, D), F32),
            v((owned, D), BF),
            v((owned, D), BF),
            v((owned, D), BF),
            v((owned, D), F32),
            v((SLOT, NB), F32),
            v((D // NB, NB, D), BF),
            v((7, 8, D), F32),
            v((2, 8, units), F32),
            v((1, units), F32),
            dma((6,)),
            dma((seqs, 3)),
            dma((2, D // NB)),
        ]
        + (gather_sems(seqs, nx) + reduce_sems(seqs, nx)) * 2,
        30_000_000_000,
    )(*args)


def attend_back(n, seqs, heads, units, size, args):
    width, rows, nx = heads * HD, SLOT // n, n // 2
    tokens, owned = seqs * SLOT, seqs * rows
    v, dma = pltpu.VMEM, pltpu.SemaphoreType.DMA
    return call(
        functools.partial(attend_back_kernel, n, seqs, heads, size),
        "attend_back",
        2,
        [smem()] + [hbm()] * 15 + [vmem()] * 3,
        [
            ((tokens, width), F32, hbm()),
            ((D, width), BF, hbm()),
            ((D, width), BF, hbm()),
            ((D, width), BF, hbm()),
            ((width, D), BF, hbm()),
            ((D, units), BF, hbm()),
            ((units, D), BF, hbm()),
            ((seqs, n, rows, width), BF, hbm()),
            ((8, 2 * width), F32, vmem()),
            ((2, units), F32, vmem()),
        ],
        [
            v((tokens, D), BF),
            v((owned, D), F32),
            v((tokens, D), BF),
            v((tokens, 3 * width), BF),
            v((seqs, heads, SLOT, SLOT), BF),
            v((tokens, width), F32),
            v((tokens, width), BF),
            v((D, 3 * width), BF),
            v((width, D), BF),
            v((SLOT, width), BF),
            v((tokens, 3 * width), BF),
            v((SLOT, SLOT), F32),
            v((SLOT, SLOT), BF),
            v((3, SLOT, width), F32),
            v((SLOT, width), F32),
            v((seqs, nx, SLOT, width), F32),
            v((seqs, nx, SLOT, width), BF),
            v((seqs, nx, SLOT, width), BF),
            v((seqs, nx - 1, SLOT, width), BF),
            v((seqs, nx - 1, SLOT, width), BF),
            v((tokens, width), F32),
            v((seqs, n, rows, width), BF),
            v((4, 8, width), F32),
            v((D, units), BF),
            v((units, D), BF),
            v((D, width), BF),
            v((D, width), BF),
            v((D, width), BF),
            v((width, D), BF),
            v((tokens, width), BF),
            v((8, D), F32),
            v((8, 2 * width), F32),
            v((n - 1, 8, width), F32),
            v((size - 1, 8, 2 * width), F32),
            v((size - 1, 2, units), F32),
            dma((15,)),
            dma((seqs,)),
            dma((n - 1,)),
            dma((n - 1,)),
            dma((n - 1,)),
            dma((n - 1,)),
        ]
        + [dma((size - 1,))] * 4
        + gather_sems(seqs, nx)
        + reduce_sems(seqs, nx)
        + ring_scratch((D, units), size) * 2
        + ring_scratch((units, D), size) * 2
        + ring_scratch((D, width), size) * 6
        + ring_scratch((width, D), size) * 2,
        20_000_000_000,
    )(*args)


def complete(n, heads, units, tokens, args):
    v, dma, width = pltpu.VMEM, pltpu.SemaphoreType.DMA, heads * HD
    shapes = [(D, units), (units, D), (D, width), (D, width), (D, width), (width, D)]
    rows = [(width,)] * 8 + [(units,), (heads,), (units,), (width,), (1,), (2,)]
    return pl.pallas_call(
        functools.partial(complete_kernel, n, heads, units),
        name="complete",
        out_shape=[jax.ShapeDtypeStruct(shape, F32) for shape in shapes]
        + [jax.ShapeDtypeStruct((tokens, width), F32), jax.ShapeDtypeStruct((tokens, width), BF)]
        + [jax.ShapeDtypeStruct((1, count), F32) for (count,) in rows],
        in_specs=[hbm()] * 8 + [vmem()] * 10,
        out_specs=[hbm()] * 8 + [vmem()] * len(rows),
        scratch_shapes=[v(shape, BF) for shape in shapes]
        + [v((tokens, width), F32), v((tokens, width), BF)]
        + [v(shape, F32) for shape in shapes]
        + [dma((8, 4))] * 2,
        compiler_params=pltpu.CompilerParams(vmem_limit_bytes=VMEM_LIMIT),
        cost_estimate=pl.CostEstimate(flops=10_000_000, bytes_accessed=24_000_000, transcendentals=0),
    )(*args)


def on_device(
    n,
    size,
    tokens,
    query_weight,
    query_bias,
    key_weight,
    value_weight,
    value_bias,
    output_weight,
    output_bias,
    attention_gain,
    attention_shift,
    inner_weight,
    inner_bias,
    down_weight,
    down_bias,
    final_gain,
    final_shift,
    head_alpha,
    unit_alpha,
    width_alpha,
    multipliers,
    head_noise,
    unit_noise,
    width_noise,
    lengths,
    teacher,
    upstream,
):
    row_count, width = tokens.shape
    heads = width // HD
    units = inner_weight.shape[1]
    seqs = row_count // SLOT
    rows = SLOT // n
    flat = lambda vector: vector.reshape(1, vector.shape[0])
    head_alpha, unit_alpha, width_alpha = flat(head_alpha), flat(unit_alpha), flat(width_alpha)
    head_noise, unit_noise, width_noise = flat(head_noise), flat(unit_noise), flat(width_noise)
    full, qkv, prob, ctx, gat, nrm, pre, rstd, mid, par, change_rows, gate_row = attend(
        n,
        seqs,
        heads,
        (
            lengths,
            tokens,
            upstream,
            teacher,
            flat(output_bias),
            flat(attention_gain),
            flat(attention_shift),
            flat(down_bias),
            flat(final_gain),
            flat(final_shift),
            width_noise,
            width_alpha,
            head_noise,
            head_alpha,
            query_weight,
            key_weight,
            value_weight,
            flat(query_bias),
            flat(value_bias),
            output_weight,
        ),
    )
    out_rows, d_low, d_res, dw_inner, dw_down, row_sums, unit_sums = feed(
        n,
        seqs,
        units,
        (
            lengths,
            mid,
            nrm,
            pre,
            rstd,
            par,
            change_rows.reshape(seqs * rows, D),
            inner_weight,
            flat(inner_bias),
            down_weight,
            unit_noise,
            unit_alpha,
        ),
    )
    tokens_grad, dw_q, dw_k, dw_v, dw_o, dw_inner, dw_down, output, small, unit_all = attend_back(
        n,
        seqs,
        heads,
        units,
        size,
        (
            lengths,
            d_low,
            d_res,
            full,
            qkv,
            prob,
            ctx,
            gat,
            query_weight,
            key_weight,
            value_weight,
            output_weight,
            dw_inner,
            dw_down,
            out_rows.reshape(seqs, rows, D),
            teacher,
            gate_row,
            row_sums,
            unit_sums,
        ),
    )
    output = output.reshape(row_count, width)
    dw_inner, dw_down, dw_q, dw_k, dw_v, dw_o, tokens_grad, output, *vectors = complete(
        n,
        heads,
        units,
        row_count,
        (
            dw_inner,
            dw_down,
            dw_q,
            dw_k,
            dw_v,
            dw_o,
            tokens_grad,
            output,
            small,
            unit_all,
            head_alpha,
            unit_alpha,
            width_alpha,
            flat(multipliers),
            head_noise,
            unit_noise,
            width_noise,
            flat(lengths),
        ),
    )
    qb, vb, ob, ag, shift, db, fg, fs, b1, ha, ua, wa, mse, mult = [v.reshape(v.shape[1]) for v in vectors]
    return (
        output,
        tokens_grad,
        dw_q,
        qb,
        dw_k,
        dw_v,
        vb,
        dw_o,
        ob,
        ag,
        shift,
        dw_inner,
        b1,
        dw_down,
        db,
        fg,
        fs,
        ha,
        ua,
        wa,
        mse.reshape(()),
        mult,
    )


def solution(mesh):
    tall, wide, vec, rep = P("dp", "hid"), P(None, "hid"), P("hid"), P()
    deep = P("hid", None)
    return jax.shard_map(
        functools.partial(on_device, mesh.shape["hid"], mesh.shape["dp"]),
        mesh=mesh,
        in_specs=(tall, wide, vec, wide, wide, vec, deep, vec, vec, vec, wide, vec, deep)
        + (vec,) * 3
        + (rep,) * 4
        + (vec,) * 3
        + (rep, tall, tall),
        out_specs=(tall, tall, wide, vec, wide, wide, vec, deep, vec, vec, vec, wide, vec, deep)
        + (vec,) * 6
        + (rep, rep),
        check_vma=False,
    )
```

```python
import functools
import math

import jax
import jax.numpy as jnp
from jax import lax
from jax.experimental import pallas as pl
from jax.experimental.pallas import tpu as pltpu
from jax.sharding import PartitionSpec as P

D = 1024
HD = 64
FF = 4096
SLOT = 512

BETA = 2.0 / 3.0
GAMMA = -0.1
ZETA = 1.1
TARGET = 0.7
ASCENT = 1.0
EPS = 1e-12
MASKED = -1000000000.0
ROOT_HALF = 0.7071067811865476
ROOT_TWO_PI = 2.5066282746310002

MESH = pl.DeviceIdType.MESH
VMEM_LIMIT = 66_000_000
BF = jnp.bfloat16
F32 = jnp.float32
NB = 256
RB = 16


def gate_value(noise, alpha):
    logits = (jnp.log(noise) - jnp.log(1.0 - noise) + alpha) / BETA
    stretched = jax.nn.sigmoid(logits) * (ZETA - GAMMA) + GAMMA
    return jnp.clip(stretched, 0.0, 1.0)


def gate_slope(noise, alpha):
    s = jax.nn.sigmoid((jnp.log(noise) - jnp.log(1.0 - noise) + alpha) / BETA)
    stretched = s * (ZETA - GAMMA) + GAMMA
    free = (stretched > 0.0) & (stretched < 1.0)
    return jnp.where(free, (ZETA - GAMMA) / BETA * s * (1.0 - s), 0.0)


def keep_prob(alpha):
    return jax.nn.sigmoid(alpha - BETA * math.log(-GAMMA / ZETA))


def lane_of(row, place):
    lanes = lax.broadcasted_iota(jnp.int32, row.shape, 1)
    return jnp.sum(jnp.where(lanes == place, row, 0.0), axis=1, keepdims=True)


def head_row(noise_ref, alpha_ref, rank, heads):
    lanes = lax.broadcasted_iota(jnp.int32, (1, heads * HD), 1)
    noise = jnp.full((1, heads * HD), 0.5, F32)
    alpha = jnp.zeros((1, heads * HD), F32)
    for h in range(heads):
        here = (lanes >= h * HD) & (lanes < (h + 1) * HD)
        noise = jnp.where(here, lane_of(noise_ref[...], h), noise)
        alpha = jnp.where(here, lane_of(alpha_ref[...], rank * heads + h), alpha)
    return noise, alpha


def part_of(ref, rank, width):
    return ref[:, pl.ds(pl.multiple_of(rank * width, width), width)]


def nn(a, b):
    return jnp.dot(a, b, preferred_element_type=F32)


def nt(a, b):
    return lax.dot_general(a, b, (((1,), (1,)), ((), ())), preferred_element_type=F32)


def tn(a, b):
    return lax.dot_general(a, b, (((0,), (0,)), ((), ())), preferred_element_type=F32)


def fold(values):
    return jnp.sum(values.reshape(values.shape[0] // 8, 8, values.shape[1]), axis=0)


class Group:
    def __init__(self, n):
        self.n = n
        self.nx = n // 2
        self.me = lax.axis_index("hid")
        self.x = lax.div(self.me, 2)
        self.c = lax.rem(self.me, 2)
        self.partner = 2 * self.x + 1 - self.c

    def chip_ahead(self, j):
        return lax.rem(self.x + 1 + j, self.nx)

    def chip_behind(self, j):
        return lax.rem(self.x - 1 - j + self.nx, self.nx)

    def slot(self, h):
        return lax.rem(h, 2) * self.nx + lax.div(h, 2)

    def all_peers(self):
        return [{"hid": lax.rem(self.me + 1 + i, self.n)} for i in range(self.n - 1)]

    def near_peers(self):
        near = [self.partner] + [2 * self.chip_ahead(j) + self.c for j in range(self.nx - 1)]
        return [{"hid": peer} for peer in near]


def remote(src, dst, send_sem, recv_sem, to):
    return pltpu.make_async_remote_copy(
        src_ref=src,
        dst_ref=dst,
        send_sem=send_sem,
        recv_sem=recv_sem,
        device_id=to if isinstance(to, dict) else {"hid": to},
        device_id_type=MESH,
    )


def gather_sems(seqs, nx):
    wide = pltpu.SemaphoreType.DMA((seqs, nx - 1))
    return [wide] * 4 + [pltpu.SemaphoreType.DMA((seqs,))] * 3


def reduce_sems(seqs, nx):
    wide = pltpu.SemaphoreType.DMA((seqs, nx - 1))
    return [wide] * 2 + [pltpu.SemaphoreType.DMA((seqs,))] * 2


class Gather:
    def __init__(self, group, sems, source, region):
        self.g, self.source, self.region = group, source, region
        self.xs, self.xr, self.rs, self.rr, self.ps, self.pr, self.os = sems

    def _own(self, s):
        return pltpu.make_async_copy(self.source(s), self.region(s, self.g.me), self.os.at[s])

    def _cross(self, s, j):
        to = 2 * self.g.chip_ahead(j) + self.g.c
        return remote(
            self.source(s), self.region(s, self.g.me), self.xs.at[s, j], self.xr.at[s, j], to
        )

    def _crossed(self, s, j):
        to = 2 * self.g.chip_ahead(j) + self.g.c
        block = self.region(s, 2 * self.g.chip_behind(j) + self.g.c)
        return remote(self.source(s), block, self.xs.at[s, j], self.xr.at[s, j], to)

    def _pair(self, s):
        return remote(
            self.source(s),
            self.region(s, self.g.me),
            self.ps.at[s],
            self.pr.at[s],
            self.g.partner,
        )

    def _paired(self, s):
        block = self.region(s, self.g.partner)
        return remote(self.source(s), block, self.ps.at[s], self.pr.at[s], self.g.partner)

    def _relay(self, s, j):
        block = self.region(s, 2 * self.g.chip_behind(j) + self.g.c)
        return remote(block, block, self.rs.at[s, j], self.rr.at[s, j], self.g.partner)

    def _relayed(self, s, j):
        block = self.region(s, 2 * self.g.chip_behind(j) + 1 - self.g.c)
        return remote(block, block, self.rs.at[s, j], self.rr.at[s, j], self.g.partner)

    def start(self, s):
        for j in range(self.g.nx - 1):
            self._cross(s, j).start()
        self._pair(s).start()
        self._own(s).start()

    def relay(self, s):
        for j in range(self.g.nx - 1):
            self._crossed(s, j).wait_recv()
            self._relay(s, j).start()

    def wait(self, s):
        self._own(s).wait()
        self._paired(s).wait_recv()
        for j in range(self.g.nx - 1):
            self._relayed(s, j).wait_recv()

    def drain(self, s):
        self._pair(s).wait_send()
        for j in range(self.g.nx - 1):
            self._cross(s, j).wait_send()
            self._relay(s, j).wait_send()


class Reduce:
    def __init__(self, group, sems, psend, precv, own, xsend, xrecv):
        self.g = group
        self.psend, self.precv, self.own, self.xsend, self.xrecv = psend, precv, own, xsend, xrecv
        self.xs, self.xr, self.ps, self.pr = sems

    def _pair(self, s):
        return remote(
            self.psend.at[s], self.precv.at[s], self.ps.at[s], self.pr.at[s], self.g.partner
        )

    def _cross(self, s, j):
        to = 2 * self.g.chip_ahead(j) + self.g.c
        return remote(
            self.xsend.at[s, j], self.xrecv.at[s, j], self.xs.at[s, j], self.xr.at[s, j], to
        )

    def start(self, s):
        self._pair(s).start()

    def cross(self, s):
        self._pair(s).wait()
        rows = self.own.shape[2]
        for j in range(self.g.nx - 1):
            chip = self.g.chip_ahead(j)

            def add(i, carry, chip=chip, j=j):
                at = pl.ds(pl.multiple_of(i * RB, RB), RB)
                total = self.own[s, chip, at, :] + self.precv[s, chip, at, :].astype(F32)
                self.xsend[s, j, at, :] = total.astype(BF)
                return carry

            lax.fori_loop(0, rows // RB, add, 0, unroll=4)
            self._cross(s, j).start()

    def arrive(self, s):
        for j in range(self.g.nx - 1):
            self._cross(s, j).wait()

    def total(self, s, at):
        total = self.own[s, self.g.x, at, :] + self.precv[s, self.g.x, at, :].astype(F32)
        for j in range(self.g.nx - 1):
            total = total + self.xrecv[s, j, at, :].astype(F32)
        return total


class Cycle:
    def __init__(self, size):
        self.size = size
        self.me = lax.axis_index("dp")
        self.length = size // 2
        line, column = lax.div(self.me, 2), lax.rem(self.me, 2)
        self.place = line + column * (size - 1 - 2 * line)

    def device(self, place):
        column = lax.div(place, self.length)
        line = place + column * (self.size - 1 - 2 * place)
        return 2 * line + column

    def beside(self, way):
        return self.device(lax.rem(self.place + way + self.size, self.size))


def split(shape, size):
    tall = max(16, shape[0] // (2 * size))
    across = 2 * size * tall // shape[0]
    return tall, shape[1] // across, across


def ring_scratch(shape, size):
    tall, broad, _ = split(shape, size)
    step = pltpu.SemaphoreType.DMA((size - 1,))
    return [
        pltpu.VMEM((size - 1, tall, broad), BF),
        pltpu.SemaphoreType.DMA((size,)),
    ] + [step] * 4 + [pltpu.SemaphoreType.REGULAR]


class Ring:
    def __init__(self, cycle, data, target, way, scratch):
        self.cycle, self.data, self.target, self.way = cycle, data, target, way
        self.size = cycle.size
        self.recv, self.out_sem, self.ss, self.sr, self.gs, self.gr, self.free = scratch
        self.tall, self.broad, self.across = split(data.shape, self.size)
        self.to, self.frm = {"dp": cycle.beside(way)}, {"dp": cycle.beside(-way)}
        self.ticks = 2 * self.size - 1

    def block(self, number):
        place = lax.rem(self.cycle.place + self.way * number + 2 * self.size, self.size)
        index = 2 * place + (0 if self.way > 0 else 1)
        if self.across == 1:
            return pl.multiple_of(index * self.tall, self.tall), 0
        row = lax.div(index, self.across)
        column = lax.rem(index, self.across)
        return (
            pl.multiple_of(row * self.tall, self.tall),
            pl.multiple_of(column * self.broad, self.broad),
        )

    def view(self, number):
        row, column = self.block(number)
        return self.data.at[pl.ds(row, self.tall), pl.ds(column, self.broad)]

    def _add(self, t):
        return remote(self.view(-t), self.recv.at[t], self.ss.at[t], self.sr.at[t], self.to)

    def _pass(self, t):
        block = self.view(1 - t)
        return remote(block, block, self.gs.at[t], self.gr.at[t], self.to)

    def _passed(self, t):
        block = self.view(-t)
        return remote(block, block, self.gs.at[t], self.gr.at[t], self.to)

    def _sum(self, t):
        row, column = self.block(-t)

        def part(i, carry):
            at = pl.ds(pl.multiple_of(row + i * RB, RB), RB)
            cols = pl.ds(column, self.broad)
            arrived = self.recv[t - 1, pl.ds(pl.multiple_of(i * RB, RB), RB), :].astype(F32)
            self.data[at, cols] = (self.data[at, cols].astype(F32) + arrived).astype(BF)
            return carry

        lax.fori_loop(0, self.tall // RB, part, 0, unroll=True)

    def _out(self, number, count):
        row, column = self.block(number)
        place = self.target.at[pl.ds(row, self.tall), pl.ds(column, self.broad)]
        return pltpu.make_async_copy(self.view(number), place, self.out_sem.at[count])

    def tick(self, t):
        size = self.size

        @pl.when(t == 0)
        def _():
            self._add(0).start()

        @pl.when((t >= 1) & (t <= size - 1))
        def _():
            self._add(t - 1).wait_recv()
            self._sum(t)

        @pl.when((t >= 1) & (t < size - 1))
        def _():
            self._add(t).start()

        @pl.when((t >= 1) & (t <= size - 1))
        def _():
            self._add(t - 1).wait_send()
            pl.semaphore_signal(self.free, inc=1, device_id=self.frm, device_id_type=MESH)

        @pl.when(t == size - 1)
        def _():
            pl.semaphore_wait(self.free, 1)
            self._pass(0).start()
            self._out(1, 0).start()

        @pl.when((t > size - 1) & (t < 2 * size - 1))
        def _():
            u = t - size
            self._passed(u).wait_recv()

            @pl.when(t < 2 * size - 2)
            def _():
                pl.semaphore_wait(self.free, 1)
                self._pass(u + 1).start()

            self._out(-u, u + 1).start()

    def drain(self):
        self._out(1, 0).wait()

        def step(t, carry):
            self._pass(t).wait_send()
            self._out(-t, t + 1).wait()
            return carry

        lax.fori_loop(0, self.size - 1, step, 0)


def meet(peers):
    barrier = pltpu.get_barrier_semaphore()
    for peer in peers:
        pl.semaphore_signal(barrier, inc=1, device_id=peer, device_id_type=MESH)
    pl.semaphore_wait(barrier, len(peers))


def mean_of(values):
    return jnp.sum(values, axis=1, keepdims=True) * (1.0 / D)


def attend_kernel(n, seqs, heads, *refs):
    (
        len_ref, tok_ref, up_ref, tea_ref, ob_ref, ag_ref, as_ref, db_ref, fg_ref, fs_ref,
        wn_ref, wa_ref, hn_ref, ha_ref, wq_ref, wk_ref, wv_ref, qb_ref, vb_ref, wo_ref,
        full_o, qkv_o, prob_o, ctx_o, gat_o, nrm_o, pre_o, rstd_o, mid_o, par_o, change_o, gate_o,
        full, wqkv, wo, qkv, prob, ctx, gat, own, psend, precv, xsend, xrecv,
        nrm, pre, rstd, mid, par, chg, up, tea, change, vec, score, in_sem, out_sem, vec_send, vec_recv, ch_send, ch_recv, *sems,
    ) = refs
    g = Group(n)
    width = heads * HD
    rows = SLOT // n
    gsems, rsems = sems[:7], sems[7:]
    cols = lambda h: pl.ds(pl.multiple_of(h * width, width), width)
    seq = lambda s: pl.ds(pl.multiple_of(s * SLOT, SLOT), SLOT)
    own_rows = lambda s: pl.ds(pl.multiple_of(s * rows, rows), rows)
    ga = Gather(g, gsems, lambda s: tok_ref.at[seq(s), :], lambda s, h: full.at[seq(s), cols(h)])
    re = Reduce(g, rsems, psend, precv, own, xsend, xrecv)

    def vec_to(i):
        to = lax.rem(g.me + 1 + i, n)
        return remote(vec, par.at[:, cols(g.me)], vec_send.at[i], vec_recv.at[i], to)

    def vec_from(i):
        to = lax.rem(g.me + 1 + i, n)
        frm = lax.rem(g.me - 1 - i + n, n)
        return remote(vec, par.at[:, cols(frm)], vec_send.at[i], vec_recv.at[i], to)

    def change_to(i):
        to = lax.rem(g.me + 1 + i, n)
        return remote(
            change.at[:, g.slot(to)], chg.at[:, :, cols(g.me)], ch_send.at[i], ch_recv.at[i], to
        )

    def change_from(i):
        to = lax.rem(g.me + 1 + i, n)
        frm = lax.rem(g.me - 1 - i + n, n)
        return remote(
            change.at[:, g.slot(to)], chg.at[:, :, cols(frm)], ch_send.at[i], ch_recv.at[i], to
        )

    loads = [
        pltpu.make_async_copy(wq_ref, wqkv.at[:, pl.ds(0, width)], in_sem.at[0]),
        pltpu.make_async_copy(wk_ref, wqkv.at[:, pl.ds(width, width)], in_sem.at[1]),
        pltpu.make_async_copy(wv_ref, wqkv.at[:, pl.ds(2 * width, width)], in_sem.at[2]),
        pltpu.make_async_copy(wo_ref, wo, in_sem.at[3]),
        pltpu.make_async_copy(up_ref, up, in_sem.at[4]),
        pltpu.make_async_copy(tea_ref, tea, in_sem.at[5]),
    ]
    par_own = pltpu.make_async_copy(vec, par.at[:, cols(g.me)], in_sem.at[7])
    change_own = pltpu.make_async_copy(
        change.at[:, g.slot(g.me)], chg.at[:, :, cols(g.me)], in_sem.at[8]
    )
    chg_out = pltpu.make_async_copy(chg, change_o, in_sem.at[6])

    def sequence_outs(s):
        return [
            pltpu.make_async_copy(full.at[seq(s), :], full_o.at[seq(s), :], out_sem.at[s, 0]),
            pltpu.make_async_copy(qkv.at[seq(s), :], qkv_o.at[seq(s), :], out_sem.at[s, 1]),
            pltpu.make_async_copy(prob.at[s], prob_o.at[s], out_sem.at[s, 2]),
            pltpu.make_async_copy(ctx.at[seq(s), :], ctx_o.at[seq(s), :], out_sem.at[s, 3]),
            pltpu.make_async_copy(gat.at[seq(s), :], gat_o.at[seq(s), :], out_sem.at[s, 4]),
        ]

    def row_outs(s):
        return [
            pltpu.make_async_copy(nrm.at[own_rows(s), :], nrm_o.at[own_rows(s), :], out_sem.at[s, 5]),
            pltpu.make_async_copy(pre.at[own_rows(s), :], pre_o.at[own_rows(s), :], out_sem.at[s, 6]),
            pltpu.make_async_copy(rstd.at[own_rows(s), :], rstd_o.at[own_rows(s), :], out_sem.at[s, 7]),
            pltpu.make_async_copy(mid.at[own_rows(s), :], mid_o.at[own_rows(s), :], out_sem.at[s, 8]),
        ]

    for load in loads:
        load.start()
    for row, ref in ((0, ob_ref), (2, ag_ref), (3, as_ref), (4, db_ref), (5, fg_ref), (6, fs_ref)):
        vec[row : row + 1, :] = ref[...]
    vec[1:2, :] = gate_value(wn_ref[...], part_of(wa_ref, g.me, width))
    vec[7:8, :] = jnp.zeros((1, width), F32)
    meet(g.all_peers())

    def begin(s, carry):
        ga.start(s)
        return carry

    for i in range(n - 1):
        vec_to(i).start()
    lax.fori_loop(0, seqs, begin, 0)
    par_own.start()
    gate_row = gate_value(*head_row(hn_ref, ha_ref, g.me, heads))
    gate_o[...] = gate_row
    for load in loads:
        load.wait()

    def differ(i, carry):
        at = pl.ds(pl.multiple_of(i * 32, 32), 32)
        value = (up[at, :].astype(F32) - tea[at, :].astype(F32)).astype(BF)
        each = SLOT // n // 32
        s, q = lax.div(i, SLOT // 32), lax.rem(i, SLOT // 32)
        change[s, lax.div(q, each), pl.ds(pl.multiple_of(lax.rem(q, each) * 32, 32), 32), :] = value
        return carry

    lax.fori_loop(0, seqs * SLOT // 32, differ, 0)
    change_own.start()
    ga.relay(0)
    par_own.wait()
    for i in range(n - 1):
        vec_from(i).wait()
    par_o[...] = par[...]

    lanes = lax.broadcasted_iota(jnp.int32, (1, width), 1)
    head_lanes = [
        jnp.where((lanes >= h * HD) & (lanes < (h + 1) * HD), 1.0, 0.0).astype(BF) for h in range(heads)
    ]

    scaled_lanes = [lane * HD**-0.5 for lane in head_lanes]

    def finish(s):
        re.arrive(s)

        def block(i, carry):
            at = pl.ds(pl.multiple_of(i * RB, RB), RB)
            here = pl.ds(pl.multiple_of(s * rows + i * RB, RB), RB)
            token_row = pl.multiple_of(s * SLOT + g.slot(g.me) * rows + i * RB, RB)
            attention_pre = re.total(s, at) + par[0:1, :]
            residual = full[pl.ds(token_row, RB), :].astype(F32) + attention_pre * par[1:2, :]
            centered = residual - mean_of(residual)
            row_rstd = lax.rsqrt(mean_of(centered * centered) + EPS)
            normed = centered * row_rstd
            middle = normed * par[2:3, :] + par[3:4, :]
            nrm[here, :] = normed
            pre[here, :] = attention_pre
            rstd[here, :] = jnp.broadcast_to(row_rstd, (RB, 128))
            mid[here, :] = middle.astype(BF)
            return carry

        lax.fori_loop(0, rows // RB, block, 0, unroll=4)
        for copy in row_outs(s):
            copy.start()

    def sequence(s, carry):
        ga.wait(s)
        here = seq(s)
        projected = nn(full[here, :], wqkv[...])
        qkv[here, 0:width] = (projected[:, 0:width] + qb_ref[...]).astype(BF)
        qkv[here, width : 2 * width] = projected[:, width : 2 * width].astype(BF)
        qkv[here, 2 * width : 3 * width] = (projected[:, 2 * width : 3 * width] + vb_ref[...]).astype(BF)

        @pl.when(s + 1 < seqs)
        def _():
            ga.relay(s + 1)

        length = len_ref[lax.axis_index("dp") * seqs + s]
        bias = jnp.where(lax.broadcasted_iota(jnp.int32, (1, SLOT), 1) < length, 0.0, MASKED)
        for h in range(heads):
            score[...] = nt(qkv[here, 0:width] * scaled_lanes[h], qkv[here, width : 2 * width])

            def softmax(i, carry, h=h):
                at = pl.ds(pl.multiple_of(i * 64, 64), 64)
                scores = score[at, :] + bias
                exponent = jnp.exp(scores - jnp.max(scores, axis=1, keepdims=True))
                total = jnp.sum(exponent, axis=1, keepdims=True)
                prob[s, h, at, :] = (exponent * (1.0 / total)).astype(BF)
                return carry

            lax.fori_loop(0, SLOT // 64, softmax, 0, unroll=True)
            term = nn(prob[s, h], qkv[here, 2 * width : 3 * width] * head_lanes[h])
            ctx[here, :] = term if h == 0 else ctx[here, :] + term
        gat[here, :] = (ctx[here, :] * gate_row).astype(BF)
        for copy in sequence_outs(s):
            copy.start()
        half = SLOT // 2
        there = pl.ds(pl.multiple_of(s * SLOT + (1 - g.c) * half, half), half)
        psend[s] = nn(gat[there, :], wo[...]).astype(BF).reshape(n // 2, rows, D)
        re.start(s)
        mine = pl.ds(pl.multiple_of(s * SLOT + g.c * half, half), half)
        own[s] = nn(gat[mine, :], wo[...]).reshape(n // 2, rows, D)
        re.cross(s)

        @pl.when(s == seqs - 3)
        def _():
            for i in range(n - 1):
                change_to(i).start()

        @pl.when(s > 0)
        def _():
            finish(s - 1)

        return carry

    lax.fori_loop(0, seqs, sequence, 0)
    change_own.wait()
    for i in range(n - 1):
        change_from(i).wait()
    chg_out.start()
    finish(seqs - 1)
    chg_out.wait()

    def end(s, carry):
        ga.drain(s)
        for copy in sequence_outs(s) + row_outs(s):
            copy.wait()
        return carry

    lax.fori_loop(0, seqs, end, 0)


def feed_kernel(n, seqs, units, *refs):
    (
        len_ref, mid_ref, nrm_ref, pre_ref, rstd_ref, par, change_ref, w1_ref, b1_ref, w2_ref, un_ref, ua_ref,
        out_o, dlow_o, dres_o, dw1_o, dw2_o, rowsum_o, unitsum_o,
        midf, dffn, w1, w2, act, inner, slope, own, psend, precv, xsend, xrecv,
        nrm, pre, rstd, change, dtwo, dsend, fout, dlow, dres, wide, grad, sums, unit_sums, ugate_ref,
        in_sem, out_sem, grad_sem, *sems,
    ) = refs
    g = Group(n)
    rows = SLOT // n
    half = SLOT // 2
    g1, r1, g2, r2 = sems[:7], sems[7:11], sems[11:18], sems[18:]
    seq = lambda s: pl.ds(pl.multiple_of(s * SLOT, SLOT), SLOT)
    own_rows = lambda s: pl.ds(pl.multiple_of(s * rows, rows), rows)
    spot = lambda s, h: pl.ds(pl.multiple_of(s * SLOT + g.slot(h) * rows, rows), rows)
    gm = Gather(g, g1, lambda s: mid_ref.at[own_rows(s), :], lambda s, h: midf.at[spot(s, h), :])
    gd = Gather(g, g2, lambda s: dsend.at[own_rows(s), :], lambda s, h: dffn.at[spot(s, h), :])
    rf = Reduce(g, r1, psend, precv, own, xsend, xrecv)
    rb = Reduce(g, r2, psend, precv, own, xsend, xrecv)
    loads = [
        pltpu.make_async_copy(w1_ref, w1, in_sem.at[0]),
        pltpu.make_async_copy(w2_ref, w2, in_sem.at[1]),
        pltpu.make_async_copy(nrm_ref, nrm, in_sem.at[2]),
        pltpu.make_async_copy(change_ref, change, in_sem.at[3]),
        pltpu.make_async_copy(pre_ref, pre, in_sem.at[4]),
        pltpu.make_async_copy(rstd_ref, rstd, in_sem.at[5]),
    ]

    meet(g.near_peers())

    def begin(s, carry):
        gm.start(s)
        return carry

    lax.fori_loop(0, seqs, begin, 0)
    for load in loads:
        load.start()
    sums[...] = jnp.zeros_like(sums)
    unit_sums[...] = jnp.zeros_like(unit_sums)
    ugate_ref[...] = gate_value(un_ref[...], part_of(ua_ref, g.me, units))
    gm.relay(0)
    for load in loads:
        load.wait()

    def finish_forward(s):
        rf.arrive(s)
        length = len_ref[lax.axis_index("dp") * seqs + s]

        def block(i, carry):
            at = pl.ds(pl.multiple_of(i * RB, RB), RB)
            here = pl.ds(pl.multiple_of(s * rows + i * RB, RB), RB)
            ffn_pre = rf.total(s, at) + par[4:5, :]
            middle = nrm[here, :] * par[2:3, :] + par[3:4, :]
            residual = middle + ffn_pre * par[1:2, :]
            centered = residual - mean_of(residual)
            row_rstd = lax.rsqrt(mean_of(centered * centered) + EPS)
            normed = centered * row_rstd
            final = normed * par[5:6, :] + par[6:7, :]
            fout[here, :] = final.astype(BF)
            place = g.slot(g.me) * rows + i * RB + lax.broadcasted_iota(jnp.int32, (RB, 1), 0)
            live = jnp.where(place < length, 1.0, 0.0)
            d_final = live * (change[here, :].astype(F32) + final)
            sums[0] += fold(d_final * normed)
            sums[1] += fold(d_final)
            d_normed = d_final * par[5:6, :]
            d_two = row_rstd * (d_normed - mean_of(d_normed) - normed * mean_of(d_normed * normed))
            sums[2] += fold(d_two * ffn_pre)
            d_ffn = d_two * par[1:2, :]
            sums[3] += fold(d_ffn)
            dtwo[here, :] = d_two
            dsend[here, :] = d_ffn.astype(BF)
            return carry

        lax.fori_loop(0, rows // RB, block, 0, unroll=4)
        gd.start(s)

    def forward(s, carry):
        gm.wait(s)
        here = seq(s)

        def part(b, carry):
            cols = pl.ds(pl.multiple_of(b * NB, NB), NB)
            wide[...] = nn(midf[here, :], w1[:, cols])
            bias = b1_ref[:, cols]
            gate = ugate_ref[:, cols]

            def block(i, carry):
                at = pl.ds(pl.multiple_of(i * 32, 32), 32)
                row = pl.ds(pl.multiple_of(s * SLOT + i * 32, 32), 32)
                v = wide[at, :] + bias
                phi = 0.5 * (1.0 + lax.erf(v * ROOT_HALF))
                activated = v * phi
                act[row, cols] = activated.astype(BF)
                inner[row, cols] = (activated * gate).astype(BF)
                steep = phi + v * jnp.exp(-0.5 * v * v) * (1.0 / ROOT_TWO_PI)
                slope[row, cols] = (gate * steep).astype(BF)
                return carry

            lax.fori_loop(0, SLOT // 32, block, 0, unroll=8)
            return carry

        lax.fori_loop(0, units // NB, part, 0)

        @pl.when(s + 1 < seqs)
        def _():
            gm.relay(s + 1)

        @pl.when(s > 0)
        def _():
            rf.cross(s - 1)

        there = pl.ds(pl.multiple_of(s * SLOT + (1 - g.c) * half, half), half)
        psend[s] = nn(inner[there, :], w2[...]).astype(BF).reshape(n // 2, rows, D)
        rf.start(s)
        mine = pl.ds(pl.multiple_of(s * SLOT + g.c * half, half), half)
        own[s] = nn(inner[mine, :], w2[...]).reshape(n // 2, rows, D)

        @pl.when(s > 1)
        def _():
            finish_forward(s - 2)

        return carry

    lax.fori_loop(0, seqs, forward, 0)
    rf.cross(seqs - 1)
    gd.relay(0)

    def row_outs(s):
        return [
            pltpu.make_async_copy(fout.at[own_rows(s), :], out_o.at[own_rows(s), :], out_sem.at[s, 0]),
            pltpu.make_async_copy(dlow.at[own_rows(s), :], dlow_o.at[own_rows(s), :], out_sem.at[s, 1]),
            pltpu.make_async_copy(dres.at[own_rows(s), :], dres_o.at[own_rows(s), :], out_sem.at[s, 2]),
        ]

    def finish_backward(s):
        rb.arrive(s)

        def block(i, carry):
            at = pl.ds(pl.multiple_of(i * RB, RB), RB)
            here = pl.ds(pl.multiple_of(s * rows + i * RB, RB), RB)
            normed = nrm[here, :]
            d_middle = dtwo[here, :] + rb.total(s, at)
            sums[4] += fold(d_middle * normed)
            sums[5] += fold(d_middle)
            d_normed = d_middle * par[2:3, :]
            d_one = rstd[here, 0:1] * (
                d_normed - mean_of(d_normed) - normed * mean_of(d_normed * normed)
            )
            sums[2] += fold(d_one * pre[here, :])
            d_attn = d_one * par[1:2, :]
            sums[6] += fold(d_attn)
            dres[here, :] = d_one
            dlow[here, :] = d_attn.astype(BF)
            return carry

        lax.fori_loop(0, rows // RB, block, 0, unroll=4)
        for copy in row_outs(s):
            copy.start()

    def backward(s, carry):
        gd.wait(s)
        here = seq(s)

        def part(b, carry):
            cols = pl.ds(pl.multiple_of(b * NB, NB), NB)
            wide[...] = nt(dffn[here, :], w2[cols, :])

            def block(i, sums_here):
                unit_part, bias_part = sums_here
                at = pl.ds(pl.multiple_of(i * 32, 32), 32)
                row = pl.ds(pl.multiple_of(s * SLOT + i * 32, 32), 32)
                d_inner = wide[at, :]
                d_pre = (d_inner * slope[row, cols].astype(F32)).astype(BF)
                unit_part = unit_part + fold(d_inner * act[row, cols].astype(F32))
                bias_part = bias_part + fold(d_pre.astype(F32))
                slope[row, cols] = d_pre
                return (unit_part, bias_part)

            zero = jnp.zeros((8, NB), F32)
            unit_part, bias_part = lax.fori_loop(0, SLOT // 32, block, (zero, zero), unroll=8)
            unit_sums[0, :, cols] += unit_part
            unit_sums[1, :, cols] += bias_part
            return carry

        lax.fori_loop(0, units // NB, part, 0)

        @pl.when(s < 2)
        def _():
            finish_forward(seqs - 2 + s)

        @pl.when(s + 1 < seqs)
        def _():
            gd.relay(s + 1)

        @pl.when(s > 0)
        def _():
            rb.cross(s - 1)

        there = pl.ds(pl.multiple_of(s * SLOT + (1 - g.c) * half, half), half)
        psend[s] = nt(slope[there, :], w1[...]).astype(BF).reshape(n // 2, rows, D)
        rb.start(s)
        mine = pl.ds(pl.multiple_of(s * SLOT + g.c * half, half), half)
        own[s] = nt(slope[mine, :], w1[...]).reshape(n // 2, rows, D)

        @pl.when(s > 1)
        def _():
            finish_backward(s - 2)

        return carry

    lax.fori_loop(0, seqs, backward, 0)
    rb.cross(seqs - 1)

    def grad_out(k, b):
        target = (dw2_o, dw1_o)[k]
        at = pl.ds(pl.multiple_of(b * NB, NB), NB)
        return pltpu.make_async_copy(grad.at[b], target.at[at, :], grad_sem.at[k, b])

    def down_grad(b, carry):
        cols = pl.ds(pl.multiple_of(b * NB, NB), NB)
        grad[b] = tn(inner[:, cols], dffn[...]).astype(BF)
        grad_out(0, b).start()
        return carry

    lax.fori_loop(0, units // NB, down_grad, 0)
    finish_backward(seqs - 2)
    for b in range(units // NB):
        grad_out(0, b).wait()

    def inner_grad(b, carry):
        cols = pl.ds(pl.multiple_of(b * NB, NB), NB)
        grad[b, :, 0:units] = tn(midf[:, cols], slope[...]).astype(BF)
        pltpu.make_async_copy(
            grad.at[b, :, pl.ds(0, units)], dw1_o.at[cols, :], grad_sem.at[1, b]
        ).start()
        return carry

    lax.fori_loop(0, D // NB, inner_grad, 0)
    finish_backward(seqs - 1)
    for k in range(7):
        rowsum_o[k : k + 1, :] = jnp.sum(sums[k], axis=0, keepdims=True)
    rowsum_o[7:8, :] = jnp.zeros((1, D), F32)
    for k in range(2):
        unitsum_o[k : k + 1, :] = jnp.sum(unit_sums[k], axis=0, keepdims=True)
    for b in range(D // NB):
        at = pl.ds(b * NB, NB)
        pltpu.make_async_copy(
            grad.at[b, :, pl.ds(0, units)], dw1_o.at[at, :], grad_sem.at[1, b]
        ).wait()

    def end(s, carry):
        gm.drain(s)
        gd.drain(s)
        for copy in row_outs(s):
            copy.wait()
        return carry

    lax.fori_loop(0, seqs, end, 0)


def attend_back_kernel(n, seqs, heads, size, *refs):
    (
        len_ref, dlow_ref, dres_ref, full_ref, qkv_ref, prob_ref, ctx_ref, gat_ref,
        wq_ref, wk_ref, wv_ref, wo_ref, dw1_ref, dw2_ref, out_ref, teacher_ref, gate_ref, row_ref, unit_ref,
        tgrad_o, dwq_o, dwk_o, dwv_o, dwo_o, dw1_o, dw2_o, output_o, small_o, units_o,
        dattn, dres, full, qkv, prob, ctx, gat, wqkv, wo, dctx, dqkv, dprob, dscore, acc,
        block_f, own, psend, precv, xsend, xrecv, tgrad, moved, sums, dw1, dw2,
        dwq, dwk, dwv, dwo, teacher, parts, small, rbuf, sbuf, ubuf,
        in_sem, out_sem, move_send, move_recv, r_send, r_recv, s_send, s_recv, u_send, u_recv, *sems,
    ) = refs
    g = Group(n)
    cycle = Cycle(size)
    rings = []
    grads = ((dw1, dw1_o), (dw2, dw2_o), (dwq, dwq_o), (dwk, dwk_o), (dwv, dwv_o), (dwo, dwo_o))
    for data, target in grads:
        for way in (1, -1):
            i = 11 + 7 * len(rings)
            rings.append(Ring(cycle, data, target, way, sems[i : i + 7]))
    ticks = rings[0].ticks

    def tick(t, which):
        for ring in rings[2 * which : 2 * which + 2]:
            ring.tick(t)

    def slot_tick(s, place):
        served = [0, heads // 2, heads // 2 + 1, heads + 1]
        if place in served:
            k = served.index(place)
            tick(2 + s * 2 + k // 2, k % 2)

    def row_to(i):
        to = lax.rem(g.me + 1 + i, n)
        return remote(parts.at[:, cols_of(to)], rbuf.at[i], r_send.at[i], r_recv.at[i], to)

    def small_to(i):
        to = {"dp": lax.rem(cycle.me + 1 + i, size)}
        return remote(small, sbuf.at[i], s_send.at[i], s_recv.at[i], to)

    def units_to(i):
        to = {"dp": lax.rem(cycle.me + 1 + i, size)}
        return remote(unit_ref, ubuf.at[i], u_send.at[i], u_recv.at[i], to)

    def move_to(i):
        to = lax.rem(g.me + 1 + i, n)
        return remote(
            out_ref.at[:, :, cols_of(to)], moved.at[:, g.slot(g.me)], move_send.at[i], move_recv.at[i], to
        )

    def move_from(i):
        to = lax.rem(g.me + 1 + i, n)
        frm = lax.rem(g.me - 1 - i + n, n)
        return remote(
            out_ref.at[:, :, cols_of(to)], moved.at[:, g.slot(frm)], move_send.at[i], move_recv.at[i], to
        )

    width = heads * HD
    rows = SLOT // n
    gsems, rsems = sems[:7], sems[7:11]
    cols_of = lambda h: pl.ds(pl.multiple_of(h * width, width), width)
    seq = lambda s: pl.ds(pl.multiple_of(s * SLOT, SLOT), SLOT)
    own_rows = lambda s: pl.ds(pl.multiple_of(s * rows, rows), rows)
    spot = lambda s, h: pl.ds(pl.multiple_of(s * SLOT + g.slot(h) * rows, rows), rows)
    ga = Gather(g, gsems, lambda s: dlow_ref.at[own_rows(s), :], lambda s, h: dattn.at[spot(s, h), :])
    re = Reduce(g, rsems, psend, precv, own, xsend, xrecv)
    loads = [
        pltpu.make_async_copy(wo_ref, wo, in_sem.at[0]),
        pltpu.make_async_copy(ctx_ref, ctx, in_sem.at[1]),
        pltpu.make_async_copy(qkv_ref, qkv, in_sem.at[2]),
        pltpu.make_async_copy(prob_ref, prob, in_sem.at[3]),
        pltpu.make_async_copy(wq_ref, wqkv.at[:, pl.ds(0, width)], in_sem.at[4]),
        pltpu.make_async_copy(wk_ref, wqkv.at[:, pl.ds(width, width)], in_sem.at[5]),
        pltpu.make_async_copy(wv_ref, wqkv.at[:, pl.ds(2 * width, width)], in_sem.at[6]),
        pltpu.make_async_copy(dres_ref, dres, in_sem.at[7]),
        pltpu.make_async_copy(full_ref, full, in_sem.at[8]),
        pltpu.make_async_copy(gat_ref, gat, in_sem.at[9]),
        pltpu.make_async_copy(
            out_ref.at[:, :, cols_of(g.me)], moved.at[:, g.slot(g.me)], in_sem.at[11]
        ),
        pltpu.make_async_copy(teacher_ref, teacher, in_sem.at[10]),
    ]
    grads_in = [
        pltpu.make_async_copy(dw1_ref, dw1, in_sem.at[12]),
        pltpu.make_async_copy(dw2_ref, dw2, in_sem.at[13]),
    ]
    for load in grads_in:
        load.start()
    meet(g.all_peers() + [{"dp": lax.rem(cycle.me + 1 + i, size)} for i in range(size - 1)])

    def begin(s, carry):
        ga.start(s)
        return carry

    lax.fori_loop(0, seqs, begin, 0)
    for load in loads:
        load.start()
    sums[...] = jnp.zeros_like(sums)
    for load in grads_in:
        load.wait()
    for t in range(2):
        tick(t, 0)
        tick(t, 1)
    ga.relay(0)
    for load in loads[:8]:
        load.wait()

    lanes = lax.broadcasted_iota(jnp.int32, (1, width), 1)
    head_lanes = [
        jnp.where((lanes >= h * HD) & (lanes < (h + 1) * HD), 1.0, 0.0).astype(BF) for h in range(heads)
    ]

    def out(s):
        return pltpu.make_async_copy(tgrad.at[seq(s), :], tgrad_o.at[seq(s), :], out_sem.at[s])

    def finish(s):
        re.arrive(s)

        def block(i, carry):
            at = pl.ds(pl.multiple_of(i * 32, 32), 32)
            tgrad[pl.ds(pl.multiple_of(s * SLOT + i * 32, 32), 32), :] = re.total(s, at)
            return carry

        lax.fori_loop(0, SLOT // 32, block, 0, unroll=4)
        out(s).start()

    def token_block(s, h):
        cols = pl.ds(pl.multiple_of(h * width, width), width)
        block_f[...] = nt(dqkv[seq(s), :], wqkv[cols, :])
        mine = pl.ds(pl.multiple_of(g.slot(g.me) * rows, rows), rows)
        block_f[mine, :] += dres[own_rows(s), cols]

    def sequence(s, carry):
        ga.wait(s)
        here = seq(s)
        d_gated = nt(dattn[here, :], wo[...])
        sums[0] += fold(d_gated * ctx[here, :])
        dctx[...] = (d_gated * gate_ref[...]).astype(BF)
        slot_tick(s, 0)

        @pl.when(s + 1 < seqs)
        def _():
            ga.relay(s + 1)

        @pl.when(s > 0)
        def _():
            re.cross(s - 1)

        @pl.when(s == 1)
        def _():
            for i in range(n - 1):
                move_to(i).start()
            for i in range(size - 1):
                units_to(i).start()

        for h in range(heads):
            d_context = dctx[...] * head_lanes[h]
            dprob[...] = nt(d_context, qkv[here, 2 * width : 3 * width])

            def softmax(i, carry, h=h):
                at = pl.ds(pl.multiple_of(i * 64, 64), 64)
                p = prob[s, h, at, :].astype(F32)
                weighted = p * dprob[at, :]
                total = jnp.sum(weighted, axis=1, keepdims=True)
                dscore[at, :] = (weighted - p * total).astype(BF)
                return carry

            lax.fori_loop(0, SLOT // 64, softmax, 0, unroll=True)
            slot_tick(s, h + 1)
            terms = (
                nn(dscore[...], qkv[here, width : 2 * width] * head_lanes[h]),
                tn(dscore[...], qkv[here, 0:width] * head_lanes[h]),
                tn(prob[s, h], d_context),
            )
            for k in range(3):
                acc[k] = terms[k] if h == 0 else acc[k] + terms[k]
        scales = (HD**-0.5, HD**-0.5, 1.0)
        for k in range(3):
            rounded = (acc[k] * scales[k]).astype(BF)
            dqkv[here, k * width : (k + 1) * width] = rounded
            sums[1 + k] += fold(rounded.astype(F32))
        for chip in range(n // 2):
            token_block(s, 2 * chip + 1 - g.c)
            psend[s, chip] = block_f[...].astype(BF)
        re.start(s)
        slot_tick(s, heads + 1)
        for chip in range(n // 2):
            token_block(s, 2 * chip + g.c)
            own[s, chip] = block_f[...]

        @pl.when(s > 0)
        def _():
            finish(s - 1)

        return carry

    lax.fori_loop(0, seqs, sequence, 0)
    re.cross(seqs - 1)
    for load in loads[8:]:
        load.wait()

    def rest(t, carry):
        tick(t, 0)
        tick(t, 1)
        return carry

    def token_grad(b, carry):
        cols = pl.ds(pl.multiple_of(b * NB, NB), NB)
        term = tn(full[:, cols], dqkv[...])
        for k, grad in enumerate((dwq, dwk, dwv)):
            grad[cols, :] = term[:, k * width : (k + 1) * width].astype(BF)
        tick(2 + 2 * seqs + b, 0)
        tick(2 + 2 * seqs + b, 1)
        return carry

    lax.fori_loop(0, D // NB, token_grad, 0)
    for which in range(2, 5):
        tick(0, which)
    dwo[...] = tn(gat[...], dattn[...]).astype(BF)
    tick(0, 5)
    lax.fori_loop(2 + 2 * seqs + D // NB, ticks, rest, 0)
    for i in range(n - 1):
        move_from(i).wait()
    moved_out = pltpu.make_async_copy(moved, output_o, in_sem.at[14])
    moved_out.start()

    def squares(s, total):
        length = len_ref[cycle.me * seqs + s]

        def block(i, total):
            each = rows // 32
            at = pl.ds(pl.multiple_of(lax.rem(i, each) * 32, 32), 32)
            value = moved[s, lax.div(i, each), at, :].astype(F32)
            place = i * 32 + lax.broadcasted_iota(jnp.int32, (32, 1), 0)
            differ = value - teacher[pl.ds(pl.multiple_of(s * SLOT + i * 32, 32), 32), :].astype(F32)
            return total + fold(jnp.where(place < length, differ * differ, 0.0))

        return lax.fori_loop(0, SLOT // 32, block, total)

    square_sum = lax.fori_loop(0, seqs, squares, jnp.zeros((8, width), F32))
    parts[...] = row_ref[...]
    for h in range(n):
        parts[7:8, h * width : (h + 1) * width] = jnp.sum(square_sum, axis=0, keepdims=True)
    for i in range(n - 1):
        row_to(i).start()
    for which in range(2, 6):
        tick(1, which)
    finish(seqs - 1)
    total = parts[:, cols_of(g.me)]
    for i in range(n - 1):
        row_to(i).wait()
        total = total + rbuf[i]
    small[:, 0:width] = total
    for k in range(4):
        small[k : k + 1, width : 2 * width] = jnp.sum(sums[k], axis=0, keepdims=True)
    small[4:8, width : 2 * width] = jnp.zeros((4, width), F32)
    for i in range(size - 1):
        small_to(i).start()

    def last(t, carry):
        for which in range(2, 6):
            tick(t, which)
        return carry

    lax.fori_loop(2, ticks, last, 0)
    small_sum = small[...]
    unit_sum = unit_ref[...]
    for i in range(size - 1):
        small_to(i).wait()
        units_to(i).wait()
        small_sum = small_sum + sbuf[i]
        unit_sum = unit_sum + ubuf[i]
    small_o[...] = small_sum
    units_o[...] = unit_sum
    moved_out.wait()
    for ring in rings:
        ring.drain()

    def end(s, carry):
        ga.drain(s)
        out(s).wait()
        return carry

    lax.fori_loop(0, seqs, end, 0)


def complete_kernel(n, heads, units, *refs):
    (
        dw1_ref, dw2_ref, dwq_ref, dwk_ref, dwv_ref, dwo_ref, tgrad_ref, output_ref,
        small_ref, unit_ref, ha_ref, ua_ref, wa_ref, mult_ref, hn_ref, un_ref, wn_ref, len_ref,
        dw1_o, dw2_o, dwq_o, dwk_o, dwv_o, dwo_o, tgrad_o, output_o,
        qb_o, vb_o, ob_o, ag_o, as_o, db_o, fg_o, fs_o, b1_o, ha_o, ua_o, wa_o, mse_o, mult_o,
        dw1, dw2, dwq, dwk, dwv, dwo, tgrad, output, fw1, fw2, fwq, fwk, fwv, fwo, in_sem, out_sem,
    ) = refs
    width = heads * HD
    rank = lax.axis_index("hid")
    wide = (
        (dw1_ref, dw1, fw1, dw1_o), (dw2_ref, dw2, fw2, dw2_o), (dwq_ref, dwq, fwq, dwq_o),
        (dwk_ref, dwk, fwk, dwk_o), (dwv_ref, dwv, fwv, dwv_o), (dwo_ref, dwo, fwo, dwo_o),
        (tgrad_ref, tgrad, tgrad, tgrad_o), (output_ref, output, output, output_o),
    )
    parts = 4

    def piece(ref, p):
        rows = ref.shape[0] // parts
        return ref.at[pl.ds(pl.multiple_of(p * rows, rows), rows), :]

    def load(k, p):
        return pltpu.make_async_copy(piece(wide[k][0], p), piece(wide[k][1], p), in_sem.at[k, p])

    def store(k, p):
        return pltpu.make_async_copy(piece(wide[k][2], p), piece(wide[k][3], p), out_sem.at[k, p])

    for k in range(len(wide)):
        for p in range(parts):
            load(k, p).start()

    head_all = small_ref[:, width : 2 * width]
    for ref, row in ((ob_o, 6), (ag_o, 4), (as_o, 5), (db_o, 3), (fg_o, 0), (fs_o, 1)):
        ref[...] = small_ref[row : row + 1, 0:width]
    qb_o[...] = head_all[1:2, :]
    vb_o[...] = head_all[3:4, :]
    b1_o[...] = unit_ref[1:2, :]
    keeps = [keep_prob(ref[...]) for ref in (ha_ref, ua_ref, wa_ref)]
    heads_kept, units_kept, dims_kept = [jnp.sum(k, axis=1, keepdims=True) for k in keeps]
    full_size = 4.0 * D * D + 2.0 * D * FF
    gap = 1.0 - (4.0 * HD * heads_kept * dims_kept + 2.0 * units_kept * dims_kept) / full_size - TARGET
    pull = -(lane_of(mult_ref[...], 0) + 2.0 * lane_of(mult_ref[...], 1) * gap) / full_size
    slot = lax.broadcasted_iota(jnp.int32, (1, 2), 1)
    mult_o[...] = mult_ref[...] + ASCENT * jnp.where(slot == 0, gap, gap * gap)

    def pulled(alpha, factor):
        k = keep_prob(alpha)
        return pull * factor * k * (1.0 - k)

    unit_alpha = part_of(ua_ref, rank, units)
    ua_o[...] = unit_ref[0:1, :] * gate_slope(un_ref[...], unit_alpha) + pulled(unit_alpha, 2.0 * dims_kept)
    width_alpha = part_of(wa_ref, rank, width)
    wa_o[...] = small_ref[2:3, 0:width] * gate_slope(wn_ref[...], width_alpha) + pulled(
        width_alpha, 4.0 * HD * heads_kept + 2.0 * units_kept
    )
    noise_row, alpha_row = head_row(hn_ref, ha_ref, rank, heads)
    lanes = lax.broadcasted_iota(jnp.int32, (1, width), 1)
    per_lane = head_all[0:1, :] * gate_slope(noise_row, alpha_row)
    head_pulled = pulled(alpha_row, 4.0 * HD * dims_kept) * (1.0 / HD)
    for h in range(heads):
        here = (lanes >= h * HD) & (lanes < (h + 1) * HD)
        ha_o[:, h : h + 1] = jnp.sum(jnp.where(here, per_lane + head_pulled, 0.0), axis=1, keepdims=True)
    live = jnp.sum(len_ref[...].astype(F32), axis=1, keepdims=True)
    mse_o[...] = jnp.sum(small_ref[7:8, 0:width], axis=1, keepdims=True) / (live * D)

    for k, (_, low, high, _) in enumerate(wide):
        rows = low.shape[0] // parts
        for p in range(parts):
            load(k, p).wait()
            if low is not high:

                step = min(64, rows)

                def widen(i, carry, low=low, high=high, first=p * rows, step=step):
                    at = pl.ds(pl.multiple_of(first + i * step, step), step)
                    high[at, :] = low[at, :].astype(F32)
                    return carry

                lax.fori_loop(0, rows // step, widen, 0)
            store(k, p).start()
    for k in range(len(wide)):
        for p in range(parts):
            store(k, p).wait()


def hbm():
    return pl.BlockSpec(memory_space=pl.ANY)


def vmem():
    return pl.BlockSpec(memory_space=pltpu.VMEM)


def smem():
    return pl.BlockSpec(memory_space=pltpu.SMEM)


def call(kernel, name, ident, ins, outs, scratch, flops):
    return pl.pallas_call(
        kernel,
        name=name,
        out_shape=[jax.ShapeDtypeStruct(shape, dtype) for shape, dtype, _ in outs],
        in_specs=ins,
        out_specs=[spec for _, _, spec in outs],
        scratch_shapes=scratch,
        compiler_params=pltpu.CompilerParams(
            collective_id=ident, has_side_effects=True, vmem_limit_bytes=VMEM_LIMIT
        ),
        cost_estimate=pl.CostEstimate(flops=flops, bytes_accessed=30_000_000, transcendentals=0),
    )


def attend(n, seqs, heads, args):
    width, rows, nx, half = heads * HD, SLOT // n, n // 2, SLOT // 2
    tokens, owned = seqs * SLOT, seqs * rows
    v, dma = pltpu.VMEM, pltpu.SemaphoreType.DMA
    return call(
        functools.partial(attend_kernel, n, seqs, heads),
        "attend",
        0,
        [smem()] + [hbm()] * 3 + [vmem()] * 10 + [hbm()] * 3 + [vmem()] * 2 + [hbm()],
        [
            ((tokens, D), BF, hbm()),
            ((tokens, 3 * width), BF, hbm()),
            ((seqs, heads, SLOT, SLOT), BF, hbm()),
            ((tokens, width), F32, hbm()),
            ((tokens, width), BF, hbm()),
            ((owned, D), F32, hbm()),
            ((owned, D), F32, hbm()),
            ((owned, 128), F32, hbm()),
            ((owned, D), BF, hbm()),
            ((8, D), F32, vmem()),
            ((seqs, rows, D), BF, hbm()),
            ((1, width), F32, vmem()),
        ],
        [
            v((tokens, D), BF),
            v((D, 3 * width), BF),
            v((width, D), BF),
            v((tokens, 3 * width), BF),
            v((seqs, heads, SLOT, SLOT), BF),
            v((tokens, width), F32),
            v((tokens, width), BF),
            v((seqs, nx, rows, D), F32),
            v((seqs, nx, rows, D), BF),
            v((seqs, nx, rows, D), BF),
            v((seqs, nx - 1, rows, D), BF),
            v((seqs, nx - 1, rows, D), BF),
            v((owned, D), F32),
            v((owned, D), F32),
            v((owned, 128), F32),
            v((owned, D), BF),
            v((8, D), F32),
            v((seqs, rows, D), BF),
            v((tokens, width), BF),
            v((tokens, width), BF),
            v((seqs, n, rows, width), BF),
            v((8, width), F32),
            v((SLOT, SLOT), F32),
            dma((9,)),
            dma((seqs, 9)),
            dma((n - 1,)),
            dma((n - 1,)),
            dma((n - 1,)),
            dma((n - 1,)),
        ]
        + gather_sems(seqs, nx)
        + reduce_sems(seqs, nx),
        10_000_000_000,
    )(*args)


def feed(n, seqs, units, args):
    rows, nx = SLOT // n, n // 2
    tokens, owned = seqs * SLOT, seqs * rows
    v, dma = pltpu.VMEM, pltpu.SemaphoreType.DMA
    return call(
        functools.partial(feed_kernel, n, seqs, units),
        "feed",
        1,
        [smem(), hbm(), hbm(), hbm(), hbm(), vmem(), hbm(), hbm(), vmem(), hbm(), vmem(), vmem()],
        [
            ((owned, D), BF, hbm()),
            ((owned, D), BF, hbm()),
            ((owned, D), F32, hbm()),
            ((D, units), BF, hbm()),
            ((units, D), BF, hbm()),
            ((8, D), F32, vmem()),
            ((2, units), F32, vmem()),
        ],
        [
            v((tokens, D), BF),
            v((tokens, D), BF),
            v((D, units), BF),
            v((units, D), BF),
            v((tokens, units), BF),
            v((tokens, units), BF),
            v((tokens, units), BF),
            v((seqs, nx, rows, D), F32),
            v((seqs, nx, rows, D), BF),
            v((seqs, nx, rows, D), BF),
            v((seqs, nx - 1, rows, D), BF),
            v((seqs, nx - 1, rows, D), BF),
            v((owned, D), F32),
            v((owned, D), F32),
            v((owned, 128), F32),
            v((owned, D), BF),
            v((owned, D), F32),
            v((owned, D), BF),
            v((owned, D), BF),
            v((owned, D), BF),
            v((owned, D), F32),
            v((SLOT, NB), F32),
            v((D // NB, NB, D), BF),
            v((7, 8, D), F32),
            v((2, 8, units), F32),
            v((1, units), F32),
            dma((6,)),
            dma((seqs, 3)),
            dma((2, D // NB)),
        ]
        + (gather_sems(seqs, nx) + reduce_sems(seqs, nx)) * 2,
        30_000_000_000,
    )(*args)


def attend_back(n, seqs, heads, units, size, args):
    width, rows, nx = heads * HD, SLOT // n, n // 2
    tokens, owned = seqs * SLOT, seqs * rows
    v, dma = pltpu.VMEM, pltpu.SemaphoreType.DMA
    return call(
        functools.partial(attend_back_kernel, n, seqs, heads, size),
        "attend_back",
        2,
        [smem()] + [hbm()] * 15 + [vmem()] * 3,
        [
            ((tokens, width), F32, hbm()),
            ((D, width), BF, hbm()),
            ((D, width), BF, hbm()),
            ((D, width), BF, hbm()),
            ((width, D), BF, hbm()),
            ((D, units), BF, hbm()),
            ((units, D), BF, hbm()),
            ((seqs, n, rows, width), BF, hbm()),
            ((8, 2 * width), F32, vmem()),
            ((2, units), F32, vmem()),
        ],
        [
            v((tokens, D), BF),
            v((owned, D), F32),
            v((tokens, D), BF),
            v((tokens, 3 * width), BF),
            v((seqs, heads, SLOT, SLOT), BF),
            v((tokens, width), F32),
            v((tokens, width), BF),
            v((D, 3 * width), BF),
            v((width, D), BF),
            v((SLOT, width), BF),
            v((tokens, 3 * width), BF),
            v((SLOT, SLOT), F32),
            v((SLOT, SLOT), BF),
            v((3, SLOT, width), F32),
            v((SLOT, width), F32),
            v((seqs, nx, SLOT, width), F32),
            v((seqs, nx, SLOT, width), BF),
            v((seqs, nx, SLOT, width), BF),
            v((seqs, nx - 1, SLOT, width), BF),
            v((seqs, nx - 1, SLOT, width), BF),
            v((tokens, width), F32),
            v((seqs, n, rows, width), BF),
            v((4, 8, width), F32),
            v((D, units), BF),
            v((units, D), BF),
            v((D, width), BF),
            v((D, width), BF),
            v((D, width), BF),
            v((width, D), BF),
            v((tokens, width), BF),
            v((8, D), F32),
            v((8, 2 * width), F32),
            v((n - 1, 8, width), F32),
            v((size - 1, 8, 2 * width), F32),
            v((size - 1, 2, units), F32),
            dma((15,)),
            dma((seqs,)),
            dma((n - 1,)),
            dma((n - 1,)),
            dma((n - 1,)),
            dma((n - 1,)),
        ]
        + [dma((size - 1,))] * 4
        + gather_sems(seqs, nx)
        + reduce_sems(seqs, nx)
        + ring_scratch((D, units), size) * 2
        + ring_scratch((units, D), size) * 2
        + ring_scratch((D, width), size) * 6
        + ring_scratch((width, D), size) * 2,
        20_000_000_000,
    )(*args)


def complete(n, heads, units, tokens, args):
    v, dma, width = pltpu.VMEM, pltpu.SemaphoreType.DMA, heads * HD
    shapes = [(D, units), (units, D), (D, width), (D, width), (D, width), (width, D)]
    rows = [(width,)] * 8 + [(units,), (heads,), (units,), (width,), (1,), (2,)]
    return pl.pallas_call(
        functools.partial(complete_kernel, n, heads, units),
        name="complete",
        out_shape=[jax.ShapeDtypeStruct(shape, F32) for shape in shapes]
        + [jax.ShapeDtypeStruct((tokens, width), F32), jax.ShapeDtypeStruct((tokens, width), BF)]
        + [jax.ShapeDtypeStruct((1, count), F32) for (count,) in rows],
        in_specs=[hbm()] * 8 + [vmem()] * 10,
        out_specs=[hbm()] * 8 + [vmem()] * len(rows),
        scratch_shapes=[v(shape, BF) for shape in shapes]
        + [v((tokens, width), F32), v((tokens, width), BF)]
        + [v(shape, F32) for shape in shapes]
        + [dma((8, 4))] * 2,
        compiler_params=pltpu.CompilerParams(vmem_limit_bytes=VMEM_LIMIT),
        cost_estimate=pl.CostEstimate(flops=10_000_000, bytes_accessed=24_000_000, transcendentals=0),
    )(*args)


def on_device(
    n,
    size,
    tokens,
    query_weight,
    query_bias,
    key_weight,
    value_weight,
    value_bias,
    output_weight,
    output_bias,
    attention_gain,
    attention_shift,
    inner_weight,
    inner_bias,
    down_weight,
    down_bias,
    final_gain,
    final_shift,
    head_alpha,
    unit_alpha,
    width_alpha,
    multipliers,
    head_noise,
    unit_noise,
    width_noise,
    lengths,
    teacher,
    upstream,
):
    row_count, width = tokens.shape
    heads = width // HD
    units = inner_weight.shape[1]
    seqs = row_count // SLOT
    rows = SLOT // n
    flat = lambda vector: vector.reshape(1, vector.shape[0])
    head_alpha, unit_alpha, width_alpha = flat(head_alpha), flat(unit_alpha), flat(width_alpha)
    head_noise, unit_noise, width_noise = flat(head_noise), flat(unit_noise), flat(width_noise)
    full, qkv, prob, ctx, gat, nrm, pre, rstd, mid, par, change_rows, gate_row = attend(
        n,
        seqs,
        heads,
        (
            lengths,
            tokens,
            upstream,
            teacher,
            flat(output_bias),
            flat(attention_gain),
            flat(attention_shift),
            flat(down_bias),
            flat(final_gain),
            flat(final_shift),
            width_noise,
            width_alpha,
            head_noise,
            head_alpha,
            query_weight,
            key_weight,
            value_weight,
            flat(query_bias),
            flat(value_bias),
            output_weight,
        ),
    )
    out_rows, d_low, d_res, dw_inner, dw_down, row_sums, unit_sums = feed(
        n,
        seqs,
        units,
        (
            lengths,
            mid,
            nrm,
            pre,
            rstd,
            par,
            change_rows.reshape(seqs * rows, D),
            inner_weight,
            flat(inner_bias),
            down_weight,
            unit_noise,
            unit_alpha,
        ),
    )
    tokens_grad, dw_q, dw_k, dw_v, dw_o, dw_inner, dw_down, output, small, unit_all = attend_back(
        n,
        seqs,
        heads,
        units,
        size,
        (
            lengths,
            d_low,
            d_res,
            full,
            qkv,
            prob,
            ctx,
            gat,
            query_weight,
            key_weight,
            value_weight,
            output_weight,
            dw_inner,
            dw_down,
            out_rows.reshape(seqs, rows, D),
            teacher,
            gate_row,
            row_sums,
            unit_sums,
        ),
    )
    output = output.reshape(row_count, width)
    dw_inner, dw_down, dw_q, dw_k, dw_v, dw_o, tokens_grad, output, *vectors = complete(
        n,
        heads,
        units,
        row_count,
        (
            dw_inner,
            dw_down,
            dw_q,
            dw_k,
            dw_v,
            dw_o,
            tokens_grad,
            output,
            small,
            unit_all,
            head_alpha,
            unit_alpha,
            width_alpha,
            flat(multipliers),
            head_noise,
            unit_noise,
            width_noise,
            flat(lengths),
        ),
    )
    qb, vb, ob, ag, shift, db, fg, fs, b1, ha, ua, wa, mse, mult = [v.reshape(v.shape[1]) for v in vectors]
    return (
        output,
        tokens_grad,
        dw_q,
        qb,
        dw_k,
        dw_v,
        vb,
        dw_o,
        ob,
        ag,
        shift,
        dw_inner,
        b1,
        dw_down,
        db,
        fg,
        fs,
        ha,
        ua,
        wa,
        mse.reshape(()),
        mult,
    )


def solution(mesh):
    tall, wide, vec, rep = P("dp", "hid"), P(None, "hid"), P("hid"), P()
    deep = P("hid", None)
    return jax.shard_map(
        functools.partial(on_device, mesh.shape["hid"], mesh.shape["dp"]),
        mesh=mesh,
        in_specs=(tall, wide, vec, wide, wide, vec, deep, vec, vec, vec, wide, vec, deep)
        + (vec,) * 3
        + (rep,) * 4
        + (vec,) * 3
        + (rep, tall, tall),
        out_specs=(tall, tall, wide, vec, wide, wide, vec, deep, vec, vec, vec, wide, vec, deep)
        + (vec,) * 6
        + (rep, rep),
        check_vma=False,
    )
```
